32 devices in a mesh: dp: 4 (over z), mp: 8 (over y, x, core).
Axes of the slice: x: 2, y: 2, z: 4, core: 2. Of those that a mesh axis runs over, the one named last changes fastest.
Arguments:
- layer_input: bfloat16 [4096, 2048], P(('dp', 'mp')), may hold values from -6 to 6
- lengths: int32 [4, 4], P('dp'), may hold values from 1 to 512, 1024 in all within a row
- norm1_gain: float32 [2048], replicated, may hold values from 0.5 to 1.5
- norm1_bias: float32 [2048], replicated, may hold values from -3 to 3
- norm2_gain: float32 [2048], replicated, may hold values from 0.5 to 1.5
- norm2_bias: float32 [2048], replicated, may hold values from -3 to 3
- qkv_weight: bfloat16 [2048, 6144], P(None, 'mp'), may hold values from -0.125 to 0.125
- qkv_bias: float32 [6144], P('mp'), may hold values from -3 to 3
- out_weight: bfloat16 [2048, 2048], P('mp'), may hold values from -1 to 1
- out_bias: float32 [2048], replicated, may hold values from -3 to 3
- up_weight: bfloat16 [2048, 8192], P(None, 'mp'), may hold values from -0.125 to 0.125
- up_bias: float32 [8192], P('mp'), may hold values from -3 to 3
- down_weight: bfloat16 [8192, 2048], P('mp'), may hold values from -0.0625 to 0.0625
- down_bias: float32 [2048], replicated, may hold values from -3 to 3
- cotangent: bfloat16 [4096, 2048], P(('dp', 'mp')), may hold values from -6 to 6
Outputs:
- layer_output: bfloat16 [4096, 2048], P(('dp', 'mp'))
- input_grad: float32 [4096, 2048], P(('dp', 'mp'))
- norm1_gain_grad: float32 [2048], replicated
- norm1_bias_grad: float32 [2048], replicated
- norm2_gain_grad: float32 [2048], replicated
- norm2_bias_grad: float32 [2048], replicated
- qkv_weight_grad: float32 [2048, 6144], P(None, 'mp')
- qkv_bias_grad: float32 [6144], P('mp')
- out_weight_grad: float32 [2048, 2048], P('mp')
- out_bias_grad: float32 [2048], replicated
- up_weight_grad: float32 [2048, 8192], P(None, 'mp')
- up_bias_grad: float32 [8192], P('mp')
- down_weight_grad: float32 [8192, 2048], P('mp')
- down_bias_grad: float32 [2048], replicated
The draws below stay inside these ranges and needn't reach their ends.
Inputs may be any that keep to these rules, and one draw needn't show every extreme that they name: In each row of lengths the 4 entries sum to 1024 and the largest is 512.
All inputs are finite; a program needn't handle non-finite values.
Results may differ from the reference program's by a relative error of at most 0.012.
Values may be sent and summed in bfloat16 or wider, within the bound.
No kernel may reach another device: no remote copies, remote signals or barrier semaphores. Data moves between devices by JAX's collectives and lax.ppermute only.
A program may use at most 192 MiB of HBM per device.

```python
import math
import jax
import jax.numpy as jnp
import numpy as np
from jax import lax

D = 2048
FF = 8192
HEADS = 16
HEAD_DIM = 128
ROTARY = 32
SLOTS = 4
GROUPS = 4
GROUP_TOK = 1024
TOKENS = 4096
LONGEST = 512
N_DP = 4


def shard_levels(own_key, dims, pieces, smallest, largest):
    level = 1.0
    for dim, blocks in pieces:
        steps = jax.random.uniform(jax.random.fold_in(jax.random.fold_in(own_key, 6), dim), (blocks,), jnp.float32, smallest / len(pieces), largest / len(pieces))
        level = level * jnp.repeat(jnp.exp(steps), dims[dim] // blocks).reshape((-1,) + (1,) * (len(dims) - 1 - dim))
    return level


def split_up(count, total, bound, skew):
    loads = [(1 << 20) // math.isqrt(standing ** skew) + 1 for standing in range(2, count + 1)]
    rest, holding = total - bound - (count - 1), [1] * (count - 1)
    while rest > 0:
        candidates = [i for i in range(count - 1) if holding[i] < bound]
        whole, budget = sum([loads[i] for i in candidates]), rest
        for i in candidates:
            extra = min(bound - holding[i], max(1, budget * loads[i] // whole), rest)
            holding[i] = holding[i] + extra
            rest = rest - extra
    return np.array([bound] + holding)


def uneven(rng, amount, total, reach, skew):
    if amount == 2:
        one = jax.random.randint(rng, (), max(1, total - reach), min(reach, total - 1) + 1)
        return jnp.stack([one, total - one])
    sizes = jnp.asarray(split_up(amount, total, reach, skew), jnp.int32)
    twos = (amount - 1) // 2
    giver, receiver = sizes[1:1 + 2 * twos:2], sizes[2:2 + 2 * twos:2]
    slack = jnp.minimum(giver - 1, reach - receiver)
    shifted = jax.random.randint(jax.random.fold_in(rng, 1), (twos,), 0, 1 << 20) % (slack + 1)
    sizes = sizes.at[1:1 + 2 * twos:2].set(giver - shifted).at[2:2 + 2 * twos:2].set(receiver + shifted)
    return sizes[jax.random.permutation(jax.random.fold_in(rng, 2), amount)]


def scatter_about(rng, dims, width, most, shards=(), kind=jnp.bfloat16):
    level = shard_levels(rng, dims, shards, -0.22, 0.18) if shards else 1.0
    array = jax.random.normal(rng, dims, jnp.float32) * width * level
    return jnp.minimum(jnp.maximum(array, -most), most).astype(kind)


def setup_inputs(seed: int = 0) -> dict:
    key_of = jax.random.split(jax.random.key(seed), 16)
    layer_input = scatter_about(key_of[0], (TOKENS, D), 1.0, 6.0, ((0, 32),))
    lengths = jax.vmap(lambda own: uneven(own, SLOTS, GROUP_TOK, LONGEST, 2))(jax.random.split(key_of[1], GROUPS)).reshape((GROUPS, SLOTS)).astype(jnp.int32)
    norm1_gain = jnp.clip(1.0 + 0.1 * jax.random.normal(key_of[2], (D,), jnp.float32), 0.5, 1.5)
    norm1_bias = scatter_about(key_of[3], (D,), 0.5, 3.0, (), jnp.float32)
    norm2_gain = jnp.clip(1.0 + 0.1 * jax.random.normal(key_of[4], (D,), jnp.float32), 0.5, 1.5)
    norm2_bias = scatter_about(key_of[5], (D,), 0.5, 3.0, (), jnp.float32)
    qkv_weight = scatter_about(key_of[6], (D, 3 * D), D ** -0.5, 0.125, ((1, 8),))
    qkv_bias = scatter_about(key_of[7], (3 * D,), 0.5, 3.0, ((0, 8),), jnp.float32)
    out_weight = scatter_about(key_of[8], (D, D), (HEAD_DIM // 4) ** -0.5, 1.0, ((0, 8),))
    out_bias = scatter_about(key_of[9], (D,), 0.5, 3.0, (), jnp.float32)
    up_weight = scatter_about(key_of[10], (D, FF), D ** -0.5, 0.125, ((1, 8),))
    up_bias = scatter_about(key_of[11], (FF,), 0.5, 3.0, ((0, 8),), jnp.float32)
    down_weight = scatter_about(key_of[12], (FF, D), FF ** -0.5, 0.0625, ((0, 8),))
    down_bias = scatter_about(key_of[13], (D,), 0.5, 3.0, (), jnp.float32)
    cotangent = scatter_about(key_of[14], (TOKENS, D), 1.0, 6.0, ((0, 32),))
    return dict(layer_input=layer_input, lengths=lengths, norm1_gain=norm1_gain, norm1_bias=norm1_bias, norm2_gain=norm2_gain, norm2_bias=norm2_bias, qkv_weight=qkv_weight, qkv_bias=qkv_bias, out_weight=out_weight, out_bias=out_bias, up_weight=up_weight, up_bias=up_bias, down_weight=down_weight, down_bias=down_bias, cotangent=cotangent)


@jax.custom_vjp
def low(v):
    return lax.optimization_barrier(v.astype(jnp.bfloat16)).astype(jnp.float32)

@jax.custom_vjp
def low_back(v):
    return v

def low_keep(v):
    return (low(v), None)

def low_pass(kept, grad):
    return (grad,)

def back_keep(v):
    return (v, None)

def back_low(kept, grad):
    return (low(grad),)
low.defvjp(low_keep, low_pass)
low_back.defvjp(back_keep, back_low)
norm_eps = 1e-05
highest = lax.Precision.HIGHEST

def layer_norm(values_in, norm_gain, norm_bias):
    row_mean = lax.optimization_barrier(jnp.mean(values_in, axis=-1, keepdims=True))
    centred = values_in - row_mean
    variance = lax.optimization_barrier(jnp.mean(centred * centred, axis=-1, keepdims=True))
    return centred * lax.rsqrt(variance + norm_eps) * norm_gain + norm_bias

def layout(seq_lengths, group_rows):
    seq_ends = jnp.cumsum(seq_lengths).astype(jnp.int32)
    seq_starts = seq_ends - seq_lengths.astype(jnp.int32)
    places = jnp.arange(group_rows, dtype=jnp.int32)
    segment = lax.optimization_barrier(jnp.sum((places[:, None] >= seq_ends[None, :]).astype(jnp.int32), axis=1))
    seq_first = lax.optimization_barrier(jnp.max(jnp.where(seq_starts[None, :] <= places[:, None], seq_starts[None, :], 0), axis=1))
    return (places, segment, (places - seq_first).astype(jnp.int32))

def rotary_tables(position):
    half_rot = ROTARY // 2
    frequency = 10000.0 ** (-2.0 * jnp.arange(half_rot, dtype=jnp.float32) / ROTARY)
    angles = position.astype(jnp.float32)[:, None] * frequency[None, :]
    cos_half = jnp.cos(angles)
    sine_half = jnp.sin(angles)
    return (jnp.concatenate([cos_half, cos_half], axis=1), jnp.concatenate([sine_half, sine_half], axis=1))

def rotate(values_in, cos_table, sine_table):
    half_rot = ROTARY // 2
    rot_part = values_in[..., :ROTARY]
    turned = jnp.concatenate([-rot_part[..., half_rot:], rot_part[..., :half_rot]], axis=-1)
    return jnp.concatenate([rot_part * cos_table + turned * sine_table, values_in[..., ROTARY:]], axis=-1)

def group_forward(layer_rows, seq_lengths, norm1_gain, norm1_bias, norm2_gain, norm2_bias, qkv_weight, qkv_bias, out_weight, out_bias, up_weight, up_bias, down_weight, down_bias):
    group_rows = layer_rows.shape[0]
    places, segment, position = layout(seq_lengths, group_rows)
    cos_table, sine_table = rotary_tables(position)
    allowed = (segment[:, None] == segment[None, :]) & (places[None, :] <= places[:, None])
    normed_one = low(layer_norm(layer_rows, norm1_gain, norm1_bias))
    normed_two = low(layer_norm(layer_rows, norm2_gain, norm2_bias))
    qkv_rows = low_back(jnp.dot(normed_one, qkv_weight, precision=highest) + qkv_bias)
    qkv_rows = qkv_rows.reshape(group_rows, HEADS, 3, HEAD_DIM)
    queries = low(rotate(qkv_rows[:, :, 0], cos_table[:, None, :], sine_table[:, None, :]))
    keys_all = low(rotate(qkv_rows[:, :, 1], cos_table[:, None, :], sine_table[:, None, :]))
    values = low(qkv_rows[:, :, 2])
    score_scale = HEAD_DIM ** (-0.5)

    def one_head(parts):
        query_rows, key_rows, value_rows = parts
        scores = low_back(jnp.dot(query_rows, key_rows.T, precision=highest) * score_scale)
        scores = jnp.where(allowed, scores, -1e+30)
        row_probs = jax.nn.softmax(scores, axis=-1)
        return low_back(low(jnp.dot(low(row_probs), value_rows, precision=highest)))
    attended = lax.map(jax.checkpoint(one_head), (jnp.transpose(queries, (1, 0, 2)), jnp.transpose(keys_all, (1, 0, 2)), jnp.transpose(values, (1, 0, 2))))
    attended = jnp.transpose(attended, (1, 0, 2)).reshape(group_rows, HEADS * HEAD_DIM)
    gate_pre = low_back(jnp.dot(normed_two, up_weight, precision=highest) + up_bias)
    hidden = low(jax.nn.gelu(gate_pre, approximate=False))
    attn_branch = jnp.dot(attended, out_weight, precision=highest) + out_bias
    mlp_branch = jnp.dot(hidden, down_weight, precision=highest) + down_bias
    return layer_rows + attn_branch + mlp_branch

def reference(layer_input, lengths, norm1_gain, norm1_bias, norm2_gain, norm2_bias, qkv_weight, qkv_bias, out_weight, out_bias, up_weight, up_bias, down_weight, down_bias, cotangent):
    params = tuple((weight_arg.astype(jnp.float32) for weight_arg in (norm1_gain, norm1_bias, norm2_gain, norm2_bias, qkv_weight, qkv_bias, out_weight, out_bias, up_weight, up_bias, down_weight, down_bias)))
    inputs = layer_input.reshape(N_DP, GROUP_TOK, D)
    grads_given = cotangent.reshape(N_DP, GROUP_TOK, D)

    def one_group(sums, group):
        group_input, seq_lengths, group_cot = group

        def forward(layer_rows, *weights):
            return group_forward(layer_rows, seq_lengths, *weights)
        result, pull = jax.vjp(forward, group_input.astype(jnp.float32), *params)
        grads = pull(group_cot.astype(jnp.float32))
        sums = tuple((total + part for total, part in zip(sums, grads[1:])))
        return (sums, (result.astype(jnp.bfloat16), grads[0]))
    start_sums = tuple((jnp.zeros_like(weight_arg) for weight_arg in params))
    sums, (outputs, input_grads) = lax.scan(one_group, start_sums, (inputs, lengths, grads_given))
    return (outputs.reshape(TOKENS, D), input_grads.reshape(TOKENS, D), sums[0], sums[1], sums[2], sums[3], sums[4], sums[5], sums[6], sums[7], sums[8], sums[9], sums[10], sums[11])
```

```python
import functools

import jax
import jax.numpy as jnp
from jax import lax
from jax.experimental import pallas as pl
from jax.experimental.pallas import tpu as pltpu
from jax.sharding import PartitionSpec as P

HEAD_DIM = 128
ROTARY = 32

norm_eps = 1e-05
masked_score = -1e30
inv_root_two = 0.7071067811865476
inv_root_tau = 0.3989422804014327
vmem_bytes = 60 << 20
gather_bytes = 128 << 20
bf16 = jnp.bfloat16
f32 = jnp.float32


def dot_plain(left, right):
    return jnp.dot(left, right, preferred_element_type=f32)


def contract_rows(left, right):
    return lax.dot_general(left, right, (((0,), (0,)), ((), ())), preferred_element_type=f32)


def contract_cols(left, right):
    return lax.dot_general(left, right, (((1,), (1,)), ((), ())), preferred_element_type=f32)


def swap(value, axis, count, bit):
    return lax.ppermute(value, axis, [(i, i ^ bit) for i in range(count)])


def turn(value, axis, count, step):
    return lax.ppermute(value, axis, [(i, (i + step) % count) for i in range(count)])


def chip_bits(count):
    return [1 << i for i in range(1, count.bit_length() - 1)]


def after(value, *earlier):
    return lax.optimization_barrier((value, *earlier))[0]


def halves(pair):
    rows = pair.shape[0] // 2
    return pair[:rows], pair[rows:]


class Spread:
    def __init__(self, arrays, a, b, names):
        self.arrays, self.a, self.b, self.names = arrays, a, b, names


def spread_sides(pair, count):
    return swap(pair, "mp", count, 2), swap(pair, "mp", count, 4)


def spread_corner(side_x, side_y, count):
    return swap(halves(side_x)[0], "mp", count, 4), swap(halves(side_y)[1], "mp", count, 2)


def spread_four(pair, sides, corner, count):
    rows = pair.shape[0] // 2
    arrays = [pair, *sides, *corner]
    arrays = arrays + [swap(array, "mp", count, 1) for array in arrays]
    a, b = {}, {}
    for core in range(2):
        base = 5 * core
        for i, name in enumerate((0, 2, 4)):
            a[name + core] = (base + i, 0)
            b[name + core] = (base + i, rows)
        a[6 + core] = (base + 3, 0)
        b[6 + core] = (base + 4, 0)
    return Spread(arrays, a, b, (0, 2, 4, 6, 1, 3, 5, 7))


def spread_any(pair, count):
    rows = pair.shape[0] // 2
    held, names = pair.reshape(1, 2, rows, -1), [0]
    for bit in chip_bits(count) + [1]:
        held = jnp.concatenate([held, swap(held, "mp", count, bit)], axis=0)
        names = names + [n ^ bit for n in names]
    arrays = [held.reshape(2 * rows * count, -1)]
    a = {n: (0, 2 * rows * i) for i, n in enumerate(names)}
    b = {n: (0, 2 * rows * i + rows) for i, n in enumerate(names)}
    return Spread(arrays, a, b, tuple(names))


def scatter_group(near, far, names, count, rows, rising):
    bits = chip_bits(count)
    came = swap(far, "mp", count, 1)
    names = names[: len(names) // 2]
    blocks = {n: near[i * rows : (i + 1) * rows] for i, n in enumerate(names)}
    adds = {n: came[i * rows : (i + 1) * rows] for i, n in enumerate(names)}
    for bit in bits if rising else bits[::-1]:
        stay = [n for n in blocks if not n & bit]

        def total(n):
            return (blocks[n].astype(f32) + adds[n].astype(f32)).astype(bf16)

        sent = jnp.concatenate([total(n | bit) for n in stay], axis=0)
        came = swap(sent, "mp", count, bit)
        blocks = {n: total(n) for n in stay}
        adds = {n: came[i * rows : (i + 1) * rows] for i, n in enumerate(stay)}
    return blocks[0].astype(f32) + adds[0].astype(f32)


def call(body, name, flops, moved, **kwargs):
    return pl.pallas_call(
        body,
        name=name,
        compiler_params=pltpu.CompilerParams(vmem_limit_bytes=vmem_bytes),
        cost_estimate=pl.CostEstimate(flops=flops, bytes_accessed=moved, transcendentals=0),
        **kwargs,
    )


def block_copies(spread, which, refs, buffer, sems, rows, block):
    copies = []
    for i, name in enumerate(spread.names):
        array, first = getattr(spread, which)[name]
        copies.append(
            pltpu.make_async_copy(
                refs[array].at[first : first + rows, :],
                buffer.at[i * rows : (i + 1) * rows, :],
                sems.at[i],
            )
        )
    per = block // rows
    return [copies[i : i + per] for i in range(0, len(copies), per)]


def out_copies(buffer, ref, sems, block):
    count = buffer.shape[0] // block
    return [
        pltpu.make_async_copy(
            buffer.at[i * block : (i + 1) * block, :],
            ref.at[i * block : (i + 1) * block, :],
            sems.at[i],
        )
        for i in range(count)
    ]


def entry_body(*refs, spread, rows, block):
    count = len(spread.arrays)
    arrays = refs[:count]
    (gain1, bias1, gain2, bias2, qkv_ref, out_weight_ref) = refs[count : count + 6]
    (one_ref, two_ref, hat_ref, raw_ref, grad_ref, cot_ref) = refs[count + 6 : count + 12]
    x_buf, c_buf, sem_x, sem_c, sem_out = refs[count + 12 :]
    step = pl.program_id(0)
    x_copies = block_copies(spread, "a", arrays, x_buf, sem_x, rows, block)
    c_copies = block_copies(spread, "b", arrays, c_buf, sem_c, rows, block)
    outs = out_copies(c_buf, cot_ref, sem_out, block)

    @pl.when(step == 0)
    def _():
        for x_list, c_list in zip(x_copies, c_copies):
            for copy in x_list + c_list:
                copy.start()

    for i in range(len(outs)):

        @pl.when(step == i)
        def _(i=i):
            for copy in x_copies[i] + c_copies[i]:
                copy.wait()
            outs[i].start()

    here = pl.ds(pl.multiple_of(step * block, block), block)
    values = x_buf[here, :].astype(f32)
    centred = values - jnp.mean(values, axis=1, keepdims=True)
    hat = centred * lax.rsqrt(jnp.mean(centred * centred, axis=1, keepdims=True) + norm_eps)
    hat_ref[...] = hat.astype(bf16)
    one_ref[...] = (hat * gain1[...] + bias1[...]).astype(bf16)
    two_ref[...] = (hat * gain2[...] + bias2[...]).astype(bf16)
    raw_ref[...] = dot_plain(one_ref[...], qkv_ref[...])
    grad_ref[...] = contract_cols(c_buf[here, :], out_weight_ref[...]).astype(bf16)

    @pl.when(step == len(outs) - 1)
    def _():
        for copy in outs:
            copy.wait()


def entry(spread, rows, gains, qkv_weight, out_weight):
    group_rows = rows * len(spread.names)
    width, deep = qkv_weight.shape
    units = out_weight.shape[0]
    block = min(256, group_rows)
    steps = group_rows // block
    blocks = len(spread.names)
    once = pl.Buffered(1)
    full = pl.BlockSpec((block, width), lambda i: (i, 0))
    row = pl.BlockSpec((1, width), lambda i: (0, 0))
    anywhere = pl.BlockSpec(memory_space=pl.ANY)
    wide = jax.ShapeDtypeStruct((group_rows, width), bf16)
    return call(
        functools.partial(entry_body, spread=spread, rows=rows, block=block),
        "entry",
        2 * group_rows * width * (deep + units),
        12 * group_rows * width,
        grid=(steps,),
        in_specs=[anywhere] * len(spread.arrays)
        + [row] * 4
        + [
            pl.BlockSpec(qkv_weight.shape, lambda i: (0, 0), pipeline_mode=once),
            pl.BlockSpec(out_weight.shape, lambda i: (0, 0), pipeline_mode=once),
        ],
        out_specs=[
            full,
            full,
            full,
            pl.BlockSpec((block, deep), lambda i: (i, 0)),
            pl.BlockSpec((block, units), lambda i: (i, 0)),
            anywhere,
        ],
        out_shape=[
            wide,
            wide,
            wide,
            jax.ShapeDtypeStruct((group_rows, deep), f32),
            jax.ShapeDtypeStruct((group_rows, units), bf16),
            wide,
        ],
        scratch_shapes=[
            pltpu.VMEM((group_rows, width), bf16),
            pltpu.VMEM((group_rows, width), bf16),
            pltpu.SemaphoreType.DMA((blocks,)),
            pltpu.SemaphoreType.DMA((blocks,)),
            pltpu.SemaphoreType.DMA((steps,)),
        ],
    )(*spread.arrays, *gains, qkv_weight, out_weight)


def mlp_body(*refs, spread, rows, block, tile, keep):
    count = len(spread.arrays)
    arrays = refs[:count]
    up_ref, shift_ref, down_ref, hidden_ref, grad_ref, sum_ref = refs[count : count + 6]
    rest = refs[count + 6 :]
    if keep:
        rows_ref, cot_ref = rest[:2]
        rest = rest[2:]
    x_buf, c_buf, u_buf, d_buf, sem_x, sem_c, sem_u, sem_d, sem_ox, sem_oc = rest
    step = pl.program_id(0)
    units = u_buf.shape[1]
    x_copies = block_copies(spread, "a", arrays, x_buf, sem_x, rows, block)
    c_copies = block_copies(spread, "b", arrays, c_buf, sem_c, rows, block)
    tiles = [slice(i, i + tile) for i in range(0, units, tile)]
    u_copies = [
        pltpu.make_async_copy(up_ref.at[:, t], u_buf.at[:, t], sem_u.at[i])
        for i, t in enumerate(tiles)
    ]
    d_copies = [
        pltpu.make_async_copy(down_ref.at[t, :], d_buf.at[t, :], sem_d.at[i])
        for i, t in enumerate(tiles)
    ]
    outs = []
    if keep:
        outs = list(
            zip(
                out_copies(x_buf, rows_ref, sem_ox, block),
                out_copies(c_buf, cot_ref, sem_oc, block),
            )
        )

    @pl.when(step == 0)
    def _():
        for copy in x_copies[0] + u_copies[:1] + c_copies[0] + d_copies[:1]:
            copy.start()
        for pair in zip(u_copies[1:], d_copies[1:]):
            for copy in pair:
                copy.start()
        for x_list, c_list in zip(x_copies[1:], c_copies[1:]):
            for copy in x_list + c_list:
                copy.start()
        sum_ref[...] = jnp.zeros_like(sum_ref)

    for i in range(len(x_copies)):

        @pl.when(step == i)
        def _(i=i):
            for copy in x_copies[i] + c_copies[i]:
                copy.wait()
            if keep:
                outs[i][0].start()
                outs[i][1].start()

    here = pl.ds(pl.multiple_of(step * block, block), block)
    for i, part in enumerate(tiles):

        @pl.when(step == 0)
        def _(i=i):
            u_copies[i].wait()
            d_copies[i].wait()

        gate = dot_plain(x_buf[here, :], u_buf[:, part]) + shift_ref[:, part]
        grad_hidden = contract_cols(c_buf[here, :], d_buf[part, :])
        below = 0.5 * (1.0 + lax.erf(gate * inv_root_two))
        hidden_ref[:, part] = (gate * below).astype(bf16)
        slope = below + gate * jnp.exp(-0.5 * gate * gate) * inv_root_tau
        grad = (grad_hidden * slope).astype(bf16)
        grad_ref[:, part] = grad
        sum_ref[:, part] += jnp.sum(grad.astype(f32), axis=0, keepdims=True)

    if keep:

        @pl.when(step == len(x_copies) - 1)
        def _():
            for pair in outs:
                for copy in pair:
                    copy.wait()


def mlp(spread, rows, up_weight, up_bias, down_weight, keep):
    width, units = up_weight.shape
    group_rows = rows * len(spread.names)
    block = min(512, group_rows)
    tile = min(512, units)
    steps, tiles, blocks = group_rows // block, units // tile, len(spread.names)
    anywhere = pl.BlockSpec(memory_space=pl.ANY)
    part = pl.BlockSpec((block, units), lambda i: (i, 0))
    low = jax.ShapeDtypeStruct((group_rows, units), bf16)
    wide = jax.ShapeDtypeStruct((group_rows, width), bf16)
    dma = pltpu.SemaphoreType.DMA
    return call(
        functools.partial(mlp_body, spread=spread, rows=rows, block=block, tile=tile, keep=keep),
        "mlp",
        4 * group_rows * width * units,
        8 * group_rows * width + 4 * width * units,
        grid=(steps,),
        in_specs=[anywhere] * len(spread.arrays)
        + [anywhere, pl.BlockSpec((1, units), lambda i: (0, 0)), anywhere],
        out_specs=[part, part, pl.BlockSpec((1, units), lambda i: (0, 0))]
        + [anywhere] * (2 * keep),
        out_shape=[low, low, jax.ShapeDtypeStruct((1, units), f32)] + [wide] * (2 * keep),
        scratch_shapes=[
            pltpu.VMEM((group_rows, width), bf16),
            pltpu.VMEM((group_rows, width), bf16),
            pltpu.VMEM((width, units), bf16),
            pltpu.VMEM((units, width), bf16),
            dma((blocks,)),
            dma((blocks,)),
            dma((tiles,)),
            dma((tiles,)),
            dma((steps,)),
            dma((steps,)),
        ],
    )(*spread.arrays, up_weight, up_bias, down_weight)


def weight_body(*refs, pieces):
    out_ref = refs[2 * pieces]
    total = contract_rows(refs[0][...], refs[pieces][...])
    for piece in range(1, pieces):
        total = total + contract_rows(refs[piece][...], refs[pieces + piece][...])
    out_ref[...] = total.astype(out_ref.dtype)


def weight_product(lefts, rights, tile_left, kind):
    wide, deep = lefts[0].shape[1], rights[0].shape[1]
    tile = min(512, wide if tile_left else deep)
    once = pl.Buffered(1)

    def spec(piece, tiled):
        if tiled:
            return pl.BlockSpec((piece.shape[0], tile), lambda i: (0, i))
        return pl.BlockSpec(piece.shape, lambda i: (0, 0), pipeline_mode=once)

    rows = sum(piece.shape[0] for piece in lefts)
    return call(
        functools.partial(weight_body, pieces=len(lefts)),
        "weight_product",
        2 * rows * wide * deep,
        2 * rows * (wide + deep) + 4 * wide * deep,
        grid=((wide if tile_left else deep) // tile,),
        in_specs=[spec(p, tile_left) for p in lefts] + [spec(p, not tile_left) for p in rights],
        out_specs=(
            pl.BlockSpec((tile, deep), lambda i: (i, 0))
            if tile_left
            else pl.BlockSpec((wide, tile), lambda i: (0, i))
        ),
        out_shape=jax.ShapeDtypeStruct((wide, deep), kind),
    )(*lefts, *rights)


def branch_body(attended_ref, hidden_ref, out_ref, down_ref, near_ref, far_ref):
    middle = near_ref.shape[0]
    total = dot_plain(attended_ref[...], out_ref[...]) + dot_plain(hidden_ref[...], down_ref[...])
    near_ref[...] = total[:middle].astype(bf16)
    far_ref[...] = total[middle:].astype(bf16)


def branch_sum(attended, hidden, out_weight, down_weight):
    group_rows = attended.shape[0]
    width = out_weight.shape[1]
    tile = min(512, width)
    once = pl.Buffered(1)
    half = pl.BlockSpec((group_rows // 2, tile), lambda i: (0, i))
    depth = attended.shape[1] + hidden.shape[1]
    return call(
        branch_body,
        "branch_sum",
        2 * group_rows * width * depth,
        2 * (group_rows * depth + width * depth + group_rows * width),
        grid=(width // tile,),
        in_specs=[
            pl.BlockSpec(attended.shape, lambda i: (0, 0), pipeline_mode=once),
            pl.BlockSpec(hidden.shape, lambda i: (0, 0), pipeline_mode=once),
            pl.BlockSpec((out_weight.shape[0], tile), lambda i: (0, i)),
            pl.BlockSpec((down_weight.shape[0], tile), lambda i: (0, i)),
        ],
        out_specs=[half, half],
        out_shape=[jax.ShapeDtypeStruct((group_rows // 2, width), bf16)] * 2,
    )(attended, hidden, out_weight, down_weight)


def input_body(
    qkv_grad_ref, gate_grad_ref, qkv_ref, up_ref, gain1, gain2, hat_ref, near_ref, far_ref, sum_ref
):
    middle = near_ref.shape[0]
    hat = hat_ref[...].astype(f32)
    first = contract_cols(qkv_grad_ref[...], qkv_ref[...])
    second = contract_cols(gate_grad_ref[...], up_ref[...])
    both = first * gain1[...] + second * gain2[...]
    near_ref[...] = both[:middle].astype(bf16)
    far_ref[...] = both[middle:].astype(bf16)
    sum_ref[0:1, :] = jnp.sum(first * hat, axis=0, keepdims=True)
    sum_ref[1:2, :] = jnp.sum(first, axis=0, keepdims=True)
    sum_ref[2:3, :] = jnp.sum(second * hat, axis=0, keepdims=True)
    sum_ref[3:4, :] = jnp.sum(second, axis=0, keepdims=True)


def input_sums(grad_qkv, grad_gate, qkv_weight, up_weight, gain1, gain2, hat):
    group_rows = grad_qkv.shape[0]
    width = qkv_weight.shape[0]
    tile = min(256, width)
    once = pl.Buffered(1)
    half = pl.BlockSpec((group_rows // 2, tile), lambda i: (0, i))
    row = pl.BlockSpec((1, tile), lambda i: (0, i))
    depth = grad_qkv.shape[1] + grad_gate.shape[1]
    return call(
        input_body,
        "input_sums",
        2 * group_rows * width * depth,
        2 * (group_rows * depth + width * depth + 2 * group_rows * width),
        grid=(width // tile,),
        in_specs=[
            pl.BlockSpec(grad_qkv.shape, lambda i: (0, 0), pipeline_mode=once),
            pl.BlockSpec(grad_gate.shape, lambda i: (0, 0), pipeline_mode=once),
            pl.BlockSpec((tile, qkv_weight.shape[1]), lambda i: (i, 0)),
            pl.BlockSpec((tile, up_weight.shape[1]), lambda i: (i, 0)),
            row,
            row,
            pl.BlockSpec((group_rows, tile), lambda i: (0, i)),
        ],
        out_specs=[half, half, pl.BlockSpec((4, tile), lambda i: (0, i))],
        out_shape=[jax.ShapeDtypeStruct((group_rows // 2, width), bf16)] * 2
        + [jax.ShapeDtypeStruct((4, width), f32)],
    )(grad_qkv, grad_gate, qkv_weight, up_weight, gain1, gain2, hat)


def attention_body(
    own_ref,
    starts_ref,
    raw_ref,
    bias_ref,
    cos_ref,
    sine_ref,
    slope_in_ref,
    attended_ref,
    grad_qkv_ref,
    bias_grad_ref,
    query_ref,
    key_ref,
    value_ref,
    slope_ref,
    query_sum_ref,
    key_sum_ref,
    value_sum_ref,
    *,
    rows,
    names,
    block_rows,
    longest,
):
    own = own_ref[0]
    group_rows = rows * len(names)
    lane = lax.broadcasted_iota(jnp.int32, (rows, HEAD_DIM), 1)
    half = ROTARY // 2
    scale = HEAD_DIM ** (-0.5)

    def turned(u):
        return jnp.where(lane < half, pltpu.roll(u, HEAD_DIM - half, 1), pltpu.roll(u, half, 1))

    def far_rows(name):
        return pl.ds(pl.multiple_of((own ^ name) * rows, rows), rows)

    for i, name in enumerate(names):
        near = slice(i * rows, (i + 1) * rows)
        far = far_rows(name)
        raw = raw_ref[near, :] + bias_ref[...]
        cos_table = cos_ref[near, :]
        sine_table = sine_ref[near, :]
        query = raw[:, :HEAD_DIM]
        key = raw[:, HEAD_DIM : 2 * HEAD_DIM]
        query_ref[far, :] = (query * cos_table + turned(query) * sine_table).astype(bf16)
        key_ref[far, :] = (key * cos_table + turned(key) * sine_table).astype(bf16)
        value_ref[far, :] = raw[:, 2 * HEAD_DIM :].astype(bf16)
        slope_ref[far, :] = slope_in_ref[near, :]
    key_sum_ref[...] = jnp.zeros_like(key_sum_ref)
    value_sum_ref[...] = jnp.zeros_like(value_sum_ref)
    for first in range(0, group_rows, block_rows):
        last = first + block_rows
        low = max(0, (first - longest + 1) // 128 * 128)
        query = query_ref[first:last, :]
        keys = key_ref[low:last, :]
        values = value_ref[low:last, :]
        slope = slope_ref[first:last, :]
        scores = contract_cols(query, keys) * scale
        row = first + lax.broadcasted_iota(jnp.int32, (block_rows, 1), 0)
        begin = jnp.zeros((block_rows, 1), jnp.int32)
        for slot in range(starts_ref.shape[0]):
            begin = jnp.where(starts_ref[slot] <= row, starts_ref[slot], begin)
        column = low + lax.broadcasted_iota(jnp.int32, scores.shape, 1)
        scores = jnp.where((column >= begin) & (column <= row), scores, masked_score)
        peak = jnp.max(scores, axis=1, keepdims=True)
        raised = jnp.exp(scores - peak)
        probs = raised * (1.0 / jnp.sum(raised, axis=1, keepdims=True))
        probs_low = probs.astype(bf16)
        query_ref[first:last, :] = dot_plain(probs_low, values).astype(bf16)
        grad_probs = contract_cols(slope, values)
        delta = jnp.sum(grad_probs * probs, axis=1, keepdims=True)
        grad_score = (probs * (grad_probs - delta)).astype(bf16)
        query_sum_ref[first:last, :] = dot_plain(grad_score, keys) * scale
        key_sum_ref[low:last, :] += contract_rows(grad_score, query) * scale
        value_sum_ref[low:last, :] += contract_rows(probs_low, slope)
    bias_grad = jnp.zeros(bias_grad_ref.shape, f32)
    for i, name in enumerate(names):
        near = slice(i * rows, (i + 1) * rows)
        far = far_rows(name)
        cos_table = cos_ref[near, :]
        sine_table = sine_ref[near, :]
        query_grad = query_sum_ref[far, :]
        key_grad = key_sum_ref[far, :]
        grads = jnp.concatenate(
            [
                query_grad * cos_table - turned(query_grad) * sine_table,
                key_grad * cos_table - turned(key_grad) * sine_table,
                value_sum_ref[far, :],
            ],
            axis=1,
        ).astype(bf16)
        grad_qkv_ref[near, :] = grads
        bias_grad = bias_grad + jnp.sum(grads.astype(f32), axis=0, keepdims=True)
        attended_ref[near, :] = query_ref[far, :]
    bias_grad_ref[...] = bias_grad


def attention(own, starts, raw, bias, cos_table, sine_table, slope, rows, names):
    group_rows, width = raw.shape
    part = 3 * HEAD_DIM
    heads = width // part
    whole = pl.BlockSpec((group_rows, HEAD_DIM), lambda h: (0, 0))
    scalars = pl.BlockSpec(memory_space=pltpu.SMEM)
    low = pltpu.VMEM((group_rows, HEAD_DIM), bf16)
    wide = pltpu.VMEM((group_rows, HEAD_DIM), f32)
    longest = group_rows // 2
    return pl.pallas_call(
        functools.partial(
            attention_body,
            rows=rows,
            names=names,
            block_rows=min(256, group_rows),
            longest=longest,
        ),
        grid=(heads,),
        in_specs=[
            scalars,
            scalars,
            pl.BlockSpec((group_rows, part), lambda h: (0, h)),
            pl.BlockSpec((1, part), lambda h: (0, h)),
            whole,
            whole,
            pl.BlockSpec((group_rows, HEAD_DIM), lambda h: (0, h)),
        ],
        out_specs=[
            pl.BlockSpec((group_rows, HEAD_DIM), lambda h: (0, h)),
            pl.BlockSpec((group_rows, part), lambda h: (0, h)),
            pl.BlockSpec((1, part), lambda h: (0, h)),
        ],
        out_shape=[
            jax.ShapeDtypeStruct((group_rows, heads * HEAD_DIM), bf16),
            jax.ShapeDtypeStruct((group_rows, width), bf16),
            jax.ShapeDtypeStruct((1, width), f32),
        ],
        scratch_shapes=[low, low, low, low, wide, wide, wide],
        compiler_params=pltpu.CompilerParams(vmem_limit_bytes=vmem_bytes),
        cost_estimate=pl.CostEstimate(
            flops=12 * heads * group_rows * longest * HEAD_DIM,
            bytes_accessed=12 * group_rows * width,
            transcendentals=heads * group_rows * longest,
        ),
        name="attention",
    )(own, starts, raw, bias, cos_table, sine_table, slope)


def rotary_tables(position):
    half_rot = ROTARY // 2
    frequency = 10000.0 ** (-2.0 * jnp.arange(half_rot, dtype=f32) / ROTARY)
    angles = position.astype(f32)[:, None] * frequency[None, :]
    cos_half = jnp.cos(angles)
    sine_half = jnp.sin(angles)
    rest = (position.shape[0], HEAD_DIM - ROTARY)
    return (
        jnp.concatenate([cos_half, cos_half, jnp.ones(rest, f32)], axis=1),
        jnp.concatenate([-sine_half, sine_half, jnp.zeros(rest, f32)], axis=1),
    )


def per_device(
    layer_input,
    lengths,
    norm1_gain,
    norm1_bias,
    norm2_gain,
    norm2_bias,
    qkv_weight,
    qkv_bias,
    out_weight,
    out_bias,
    up_weight,
    up_bias,
    down_weight,
    down_bias,
    cotangent,
):
    dp = lax.axis_size("dp")
    mp = lax.axis_size("mp")
    own = lax.axis_index("mp")
    rows = layer_input.shape[0]
    group_rows = rows * mp
    four = mp == 8
    up_row = up_bias[None, :]
    width = layer_input.shape[1]

    pair = jnp.concatenate([layer_input, cotangent], axis=0)
    if four:
        sides = spread_sides(pair, mp)
    input_float = layer_input.astype(f32)
    centred = input_float - jnp.mean(input_float, axis=-1, keepdims=True)
    inv_std = lax.rsqrt(jnp.mean(centred * centred, axis=-1, keepdims=True) + norm_eps)
    xhat = centred * inv_std
    second_own = (xhat * norm2_gain + norm2_bias).astype(bf16)
    shared = jnp.concatenate([second_own, cotangent], axis=0)
    ring = []
    ahead = behind = shared
    lean = dp * group_rows * (width + up_weight.shape[1]) * 4 > gather_bytes
    for step in range(1, 0 if lean else dp // 2 + 1):
        if four and step == 2:
            ahead = after(ahead, sides[0])
        ahead = turn(ahead, "dp", dp, 1)
        ring.append(ahead)
        if 2 * step < dp:
            behind = turn(behind, "dp", dp, -1)
            ring.append(behind)
    if four:
        corner = spread_corner(*sides, mp)
        spread = spread_four(pair, sides, corner, mp)
    else:
        spread = spread_any(pair, mp)
    names = spread.names

    seq_ends = jnp.cumsum(lengths[0])
    seq_starts = seq_ends - lengths[0]
    places = (
        (own ^ jnp.array(names, jnp.int32))[:, None] * rows
        + jnp.arange(rows, dtype=jnp.int32)[None, :]
    ).reshape(group_rows)
    seq_first = jnp.max(
        jnp.where(seq_starts[None, :] <= places[:, None], seq_starts[None, :], 0), axis=1
    )
    cos_table, sine_table = rotary_tables(places - seq_first)
    gains = (norm1_gain[None, :], norm1_bias[None, :], norm2_gain[None, :], norm2_bias[None, :])
    first_all, second_all, hat, raw, grad_attended, grad_out = entry(
        spread, rows, gains, qkv_weight, out_weight
    )
    attended, grad_qkv, qkv_bias_part = attention(
        own.reshape(1),
        seq_starts,
        raw,
        qkv_bias[None, :],
        cos_table,
        sine_table,
        grad_attended,
        rows,
        names,
    )
    qkv_part = weight_product([first_all], [grad_qkv], True, bf16)
    out_part = weight_product([attended], [grad_out], False, bf16)
    qkv_sum, out_sum = lax.psum((qkv_part, out_part), "dp")

    plain = {n: (0, i * rows) for i, n in enumerate(names)}
    far = {n: (1, i * rows) for i, n in enumerate(names)}
    whole = Spread([second_all, grad_out], plain, far, names)
    hidden, grad_gate, gate_sum = mlp(whole, rows, up_weight, up_row, down_weight, False)
    branch = branch_sum(attended, hidden, out_weight, down_weight)
    scaled = input_sums(
        grad_qkv, grad_gate, qkv_weight, up_weight, gains[0], gains[2], hat
    )
    own_branch = scatter_group(*branch, names, mp, rows, True)
    own_scaled = scatter_group(*scaled[:2], names, mp, rows, False)
    layer_output = (input_float + own_branch + out_bias + down_bias).astype(bf16)
    input_grad = cotangent.astype(f32) + inv_std * (
        own_scaled
        - jnp.mean(own_scaled, axis=-1, keepdims=True)
        - xhat * jnp.mean(own_scaled * xhat, axis=-1, keepdims=True)
    )
    cot_sum = jnp.sum(cotangent.astype(f32), axis=0)
    small = jnp.concatenate([scaled[2].reshape(-1), cot_sum, qkv_bias_part.reshape(-1)])
    small = small.reshape(-1, 128)
    bit = 1
    while bit < dp:
        small = small + swap(small, "dp", dp, bit)
        bit *= 2
    small = small.reshape(-1)
    qkv_bias_grad = small[5 * width :]
    small = small[: 5 * width].reshape(-1, 128)
    bit = 1
    while bit < mp:
        small = small + swap(small, "mp", mp, bit)
        bit *= 2
    small = small.reshape(5, width)

    xhats, cots, hiddens, grads, sums = [second_all], [grad_out], [hidden], [grad_gate], [gate_sum]
    tie = corner if four else ()
    for pair in ring:
        if four:
            pair = after(pair, *tie)
            sides = spread_sides(pair, mp)
            tie = corner = spread_corner(*sides, mp)
            spread = spread_four(pair, sides, corner, mp)
        else:
            spread = spread_any(pair, mp)
        hidden, grad_gate, gate_sum, other_rows, other_cot = mlp(
            spread, rows, up_weight, up_row, down_weight, True
        )
        xhats.append(other_rows)
        cots.append(other_cot)
        hiddens.append(hidden)
        grads.append(grad_gate)
        sums.append(gate_sum)
    up_weight_grad = weight_product(xhats, grads, True, f32)
    down_weight_grad = weight_product(hiddens, cots, False, f32)
    up_bias_grad = sum(sums)[0]
    if lean:
        up_weight_grad, down_weight_grad, up_bias_grad = lax.psum(
            (up_weight_grad, down_weight_grad, up_bias_grad), "dp"
        )
    return (
        layer_output,
        input_grad,
        small[0],
        small[1],
        small[2],
        small[3],
        qkv_sum.astype(f32),
        qkv_bias_grad,
        out_sum.astype(f32),
        small[4],
        up_weight_grad,
        up_bias_grad,
        down_weight_grad,
        small[4],
    )


def solution(mesh):
    in_specs = (
        P(("dp", "mp"), None),
        P("dp", None),
        P(),
        P(),
        P(),
        P(),
        P(None, "mp"),
        P("mp"),
        P("mp", None),
        P(),
        P(None, "mp"),
        P("mp"),
        P("mp", None),
        P(),
        P(("dp", "mp"), None),
    )
    out_specs = (
        P(("dp", "mp"), None),
        P(("dp", "mp"), None),
        P(),
        P(),
        P(),
        P(),
        P(None, "mp"),
        P("mp"),
        P("mp", None),
        P(),
        P(None, "mp"),
        P("mp"),
        P("mp", None),
        P(),
    )
    return jax.shard_map(
        per_device, mesh=mesh, in_specs=in_specs, out_specs=out_specs, check_vma=False
    )
```

```python
import functools

import jax
import jax.numpy as jnp
from jax import lax
from jax.experimental import pallas as pl
from jax.experimental.pallas import tpu as pltpu
from jax.sharding import PartitionSpec as P

HEAD_DIM = 128
ROTARY = 32

norm_eps = 1e-05
masked_score = -1e30
inv_root_two = 0.7071067811865476
inv_root_tau = 0.3989422804014327
vmem_bytes = 60 << 20
most_gathered = 128 << 20
bf16 = jnp.bfloat16
f32 = jnp.float32


def dot_plain(left, right):
    return jnp.dot(left, right, preferred_element_type=f32)


def contract_rows(left, right):
    return lax.dot_general(left, right, (((0,), (0,)), ((), ())), preferred_element_type=f32)


def contract_cols(left, right):
    return lax.dot_general(left, right, (((1,), (1,)), ((), ())), preferred_element_type=f32)


def swap(value, axis, count, bit):
    return lax.ppermute(value, axis, [(i, i ^ bit) for i in range(count)])


def turn(value, axis, count, step):
    return lax.ppermute(value, axis, [(i, (i + step) % count) for i in range(count)])


def chip_bits(count):
    return [1 << i for i in range(1, count.bit_length() - 1)]


def after(value, *earlier):
    return lax.optimization_barrier((value, *earlier))[0]


def halves(pair):
    rows = pair.shape[0] // 2
    return pair[:rows], pair[rows:]


class Spread:
    def __init__(self, arrays, a, b, names):
        self.arrays, self.a, self.b, self.names = arrays, a, b, names


four_names = (0, 2, 4, 6, 1, 3, 5, 7)


def spread_sides(pair, count):
    return [swap(pair, "mp", count, 2), swap(pair, "mp", count, 4)]


def spread_corner(sides, count):
    side_x, side_y = sides
    return [swap(halves(side_x)[0], "mp", count, 4), swap(halves(side_y)[1], "mp", count, 2)]


def spread_core(arrays, count):
    return [swap(array, "mp", count, 1) for array in arrays]


def spread_four(near, far):
    rows = near[0].shape[0] // 2
    a, b = {}, {}
    for core in range(2):
        base = 5 * core
        for i, name in enumerate((0, 2, 4)):
            a[name + core] = (base + i, 0)
            b[name + core] = (base + i, rows)
        a[6 + core] = (base + 3, 0)
        b[6 + core] = (base + 4, 0)
    return Spread(near + far, a, b, four_names)


def spread_any(pair, count):
    rows = pair.shape[0] // 2
    held, names = pair.reshape(1, 2, rows, -1), [0]
    for bit in chip_bits(count) + [1]:
        held = jnp.concatenate([held, swap(held, "mp", count, bit)], axis=0)
        names = names + [n ^ bit for n in names]
    arrays = [held.reshape(2 * rows * count, -1)]
    a = {n: (0, 2 * rows * i) for i, n in enumerate(names)}
    b = {n: (0, 2 * rows * i + rows) for i, n in enumerate(names)}
    return Spread(arrays, a, b, tuple(names))


class Scatter:
    def __init__(self, near, came, names, count, rows, rising):
        self.count, self.rows = count, rows
        names = names[: len(names) // 2]
        self.blocks = {n: near[i * rows : (i + 1) * rows] for i, n in enumerate(names)}
        self.adds = {n: came[i * rows : (i + 1) * rows] for i, n in enumerate(names)}
        bits = chip_bits(count)
        self.bits = bits if rising else bits[::-1]

    def total(self, n):
        return self.blocks[n].astype(f32) + self.adds[n].astype(f32)

    def sent(self):
        bit = self.bits[0]
        stay = [n for n in self.blocks if not n & bit]
        going = jnp.concatenate([self.total(n | bit).astype(bf16) for n in stay], axis=0)
        return going, [self.total(n).astype(bf16) for n in stay]

    def step(self, going, kept):
        bit, self.bits = self.bits[0], self.bits[1:]
        came = swap(going, "mp", self.count, bit)
        stay = [n for n in self.blocks if not n & bit]
        self.blocks = dict(zip(stay, kept))
        self.adds = {n: came[i * self.rows : (i + 1) * self.rows] for i, n in enumerate(stay)}


def scatter_group(near, far, names, count, rows, rising):
    scatter = Scatter(near, swap(far, "mp", count, 1), names, count, rows, rising)
    while scatter.bits:
        scatter.step(*scatter.sent())
    return scatter.total(0)


def call(body, name, **kwargs):
    return pl.pallas_call(
        body,
        name=name,
        compiler_params=pltpu.CompilerParams(vmem_limit_bytes=vmem_bytes),
        cost_estimate=pl.CostEstimate(flops=1, bytes_accessed=1, transcendentals=0),
        **kwargs,
    )


def block_copies(spread, which, refs, buffer, sems, rows, block):
    copies = []
    for i, name in enumerate(spread.names):
        array, first = getattr(spread, which)[name]
        copies.append(
            pltpu.make_async_copy(
                refs[array].at[first : first + rows, :],
                buffer.at[i * rows : (i + 1) * rows, :],
                sems.at[i],
            )
        )
    per = block // rows
    return [copies[i : i + per] for i in range(0, len(copies), per)]


def out_copies(buffer, ref, sems, block):
    count = buffer.shape[0] // block
    return [
        pltpu.make_async_copy(
            buffer.at[i * block : (i + 1) * block, :],
            ref.at[i * block : (i + 1) * block, :],
            sems.at[i],
        )
        for i in range(count)
    ]


def entry_body(*refs, spread, rows, block):
    count = len(spread.arrays)
    arrays = refs[:count]
    (gain1, bias1, gain2, bias2, qkv_ref, out_weight_ref) = refs[count : count + 6]
    (one_ref, two_ref, hat_ref, raw_ref, grad_ref, cot_ref) = refs[count + 6 : count + 12]
    x_buf, c_buf, sem_x, sem_c, sem_out = refs[count + 12 :]
    step = pl.program_id(0)
    x_copies = block_copies(spread, "a", arrays, x_buf, sem_x, rows, block)
    c_copies = block_copies(spread, "b", arrays, c_buf, sem_c, rows, block)
    outs = out_copies(c_buf, cot_ref, sem_out, block)

    @pl.when(step == 0)
    def _():
        for x_list, c_list in zip(x_copies, c_copies):
            for copy in x_list + c_list:
                copy.start()

    for i in range(len(outs)):

        @pl.when(step == i)
        def _(i=i):
            for copy in x_copies[i] + c_copies[i]:
                copy.wait()
            outs[i].start()

    here = pl.ds(pl.multiple_of(step * block, block), block)
    values = x_buf[here, :].astype(f32)
    centred = values - jnp.mean(values, axis=1, keepdims=True)
    hat = centred * lax.rsqrt(jnp.mean(centred * centred, axis=1, keepdims=True) + norm_eps)
    hat_ref[...] = hat.astype(bf16)
    one_ref[...] = (hat * gain1[...] + bias1[...]).astype(bf16)
    two_ref[...] = (hat * gain2[...] + bias2[...]).astype(bf16)
    raw_ref[...] = dot_plain(one_ref[...], qkv_ref[...])
    grad_ref[...] = contract_cols(c_buf[here, :], out_weight_ref[...]).astype(bf16)

    @pl.when(step == len(outs) - 1)
    def _():
        for copy in outs:
            copy.wait()


def entry(spread, rows, gains, qkv_weight, out_weight):
    group_rows = rows * len(spread.names)
    width, deep = qkv_weight.shape
    units = out_weight.shape[0]
    block = min(256, group_rows)
    steps = group_rows // block
    blocks = len(spread.names)
    once = pl.Buffered(1)
    full = pl.BlockSpec((block, width), lambda i: (i, 0))
    row = pl.BlockSpec((1, width), lambda i: (0, 0))
    anywhere = pl.BlockSpec(memory_space=pl.ANY)
    wide = jax.ShapeDtypeStruct((group_rows, width), bf16)
    return call(
        functools.partial(entry_body, spread=spread, rows=rows, block=block),
        "entry",
        grid=(steps,),
        in_specs=[anywhere] * len(spread.arrays)
        + [row] * 4
        + [
            pl.BlockSpec(qkv_weight.shape, lambda i: (0, 0), pipeline_mode=once),
            pl.BlockSpec(out_weight.shape, lambda i: (0, 0), pipeline_mode=once),
        ],
        out_specs=[
            full,
            full,
            full,
            pl.BlockSpec((block, deep), lambda i: (i, 0)),
            pl.BlockSpec((block, units), lambda i: (i, 0)),
            anywhere,
        ],
        out_shape=[
            wide,
            wide,
            wide,
            jax.ShapeDtypeStruct((group_rows, deep), f32),
            jax.ShapeDtypeStruct((group_rows, units), bf16),
            wide,
        ],
        scratch_shapes=[
            pltpu.VMEM((group_rows, width), bf16),
            pltpu.VMEM((group_rows, width), bf16),
            pltpu.SemaphoreType.DMA((blocks,)),
            pltpu.SemaphoreType.DMA((blocks,)),
            pltpu.SemaphoreType.DMA((steps,)),
        ],
    )(*spread.arrays, *gains, qkv_weight, out_weight)


def mlp_body(*refs, spread, rows, block, tile, keep):
    count = len(spread.arrays)
    arrays = refs[:count]
    up_ref, shift_ref, down_ref, hidden_ref, grad_ref, sum_ref = refs[count : count + 6]
    rest = refs[count + 6 :]
    if keep:
        rows_ref, cot_ref = rest[:2]
        rest = rest[2:]
    x_buf, c_buf, u_buf, d_buf, sem_x, sem_c, sem_u, sem_d, sem_ox, sem_oc = rest
    step = pl.program_id(0)
    units = u_buf.shape[1]
    x_copies = block_copies(spread, "a", arrays, x_buf, sem_x, rows, block)
    c_copies = block_copies(spread, "b", arrays, c_buf, sem_c, rows, block)
    tiles = [slice(i, i + tile) for i in range(0, units, tile)]
    u_copies = [
        pltpu.make_async_copy(up_ref.at[:, t], u_buf.at[:, t], sem_u.at[i])
        for i, t in enumerate(tiles)
    ]
    d_copies = [
        pltpu.make_async_copy(down_ref.at[t, :], d_buf.at[t, :], sem_d.at[i])
        for i, t in enumerate(tiles)
    ]
    outs = []
    if keep:
        outs = list(
            zip(
                out_copies(x_buf, rows_ref, sem_ox, block),
                out_copies(c_buf, cot_ref, sem_oc, block),
            )
        )

    @pl.when(step == 0)
    def _():
        for copy in x_copies[0] + u_copies[:1] + c_copies[0] + d_copies[:1]:
            copy.start()
        for pair in zip(u_copies[1:], d_copies[1:]):
            for copy in pair:
                copy.start()
        for x_list, c_list in zip(x_copies[1:], c_copies[1:]):
            for copy in x_list + c_list:
                copy.start()
        sum_ref[...] = jnp.zeros_like(sum_ref)

    for i in range(len(x_copies)):

        @pl.when(step == i)
        def _(i=i):
            for copy in x_copies[i] + c_copies[i]:
                copy.wait()
            if keep:
                outs[i][0].start()
                outs[i][1].start()

    here = pl.ds(pl.multiple_of(step * block, block), block)
    for i, part in enumerate(tiles):

        @pl.when(step == 0)
        def _(i=i):
            u_copies[i].wait()
            d_copies[i].wait()

        gate = dot_plain(x_buf[here, :], u_buf[:, part]) + shift_ref[:, part]
        grad_hidden = contract_cols(c_buf[here, :], d_buf[part, :])
        below = 0.5 * (1.0 + lax.erf(gate * inv_root_two))
        hidden_ref[:, part] = (gate * below).astype(bf16)
        slope = below + gate * jnp.exp(-0.5 * gate * gate) * inv_root_tau
        grad = (grad_hidden * slope).astype(bf16)
        grad_ref[:, part] = grad
        sum_ref[:, part] += jnp.sum(grad.astype(f32), axis=0, keepdims=True)

    if keep:

        @pl.when(step == len(x_copies) - 1)
        def _():
            for pair in outs:
                for copy in pair:
                    copy.wait()


def mlp(spread, rows, up_weight, up_bias, down_weight, keep):
    width, units = up_weight.shape
    group_rows = rows * len(spread.names)
    block = min(512, group_rows)
    tile = min(512, units)
    steps, tiles, blocks = group_rows // block, units // tile, len(spread.names)
    anywhere = pl.BlockSpec(memory_space=pl.ANY)
    part = pl.BlockSpec((block, units), lambda i: (i, 0))
    low = jax.ShapeDtypeStruct((group_rows, units), bf16)
    wide = jax.ShapeDtypeStruct((group_rows, width), bf16)
    dma = pltpu.SemaphoreType.DMA
    return call(
        functools.partial(mlp_body, spread=spread, rows=rows, block=block, tile=tile, keep=keep),
        "mlp",
        grid=(steps,),
        in_specs=[anywhere] * len(spread.arrays)
        + [anywhere, pl.BlockSpec((1, units), lambda i: (0, 0)), anywhere],
        out_specs=[part, part, pl.BlockSpec((1, units), lambda i: (0, 0))]
        + [anywhere] * (2 * keep),
        out_shape=[low, low, jax.ShapeDtypeStruct((1, units), f32)] + [wide] * (2 * keep),
        scratch_shapes=[
            pltpu.VMEM((group_rows, width), bf16),
            pltpu.VMEM((group_rows, width), bf16),
            pltpu.VMEM((width, units), bf16),
            pltpu.VMEM((units, width), bf16),
            dma((blocks,)),
            dma((blocks,)),
            dma((tiles,)),
            dma((tiles,)),
            dma((steps,)),
            dma((steps,)),
        ],
    )(*spread.arrays, up_weight, up_bias, down_weight)


def weight_body(*refs, pieces):
    out_ref = refs[2 * pieces]
    total = contract_rows(refs[0][...], refs[pieces][...])
    for piece in range(1, pieces):
        total = total + contract_rows(refs[piece][...], refs[pieces + piece][...])
    out_ref[...] = total.astype(out_ref.dtype)


def weight_product(lefts, rights, tile_left, kind):
    wide, deep = lefts[0].shape[1], rights[0].shape[1]
    tile = min(512, wide if tile_left else deep)
    once = pl.Buffered(1)

    def spec(piece, tiled):
        if tiled:
            return pl.BlockSpec((piece.shape[0], tile), lambda i: (0, i))
        return pl.BlockSpec(piece.shape, lambda i: (0, 0), pipeline_mode=once)

    return call(
        functools.partial(weight_body, pieces=len(lefts)),
        "weight_product",
        grid=((wide if tile_left else deep) // tile,),
        in_specs=[spec(p, tile_left) for p in lefts] + [spec(p, not tile_left) for p in rights],
        out_specs=(
            pl.BlockSpec((tile, deep), lambda i: (i, 0))
            if tile_left
            else pl.BlockSpec((wide, tile), lambda i: (0, i))
        ),
        out_shape=jax.ShapeDtypeStruct((wide, deep), kind),
    )(*lefts, *rights)


def attention_weights_body(normed_ref, grad_qkv_ref, attended_ref, grad_out_ref, sum_ref):
    deep = grad_qkv_ref.shape[1]
    sum_ref[:, :deep] = contract_rows(normed_ref[...], grad_qkv_ref[...]).astype(bf16)
    sum_ref[:, deep:] = contract_rows(attended_ref[...], grad_out_ref[...]).astype(bf16)


def attention_weights(normed, grad_qkv, attended, grad_out):
    group_rows, width = normed.shape
    deep, units = grad_qkv.shape[1], attended.shape[1]
    once = pl.Buffered(1)
    block = pl.BlockSpec((group_rows, units), lambda i: (0, i))
    return call(
        attention_weights_body,
        "attention_weights",
        grid=(width // units,),
        in_specs=[
            block,
            pl.BlockSpec(grad_qkv.shape, lambda i: (0, 0), pipeline_mode=once),
            pl.BlockSpec(attended.shape, lambda i: (0, 0), pipeline_mode=once),
            block,
        ],
        out_specs=pl.BlockSpec((units, deep + units), lambda i: (i, 0)),
        out_shape=jax.ShapeDtypeStruct((width, deep + units), bf16),
    )(normed, grad_qkv, attended, grad_out)


def widen_body(sum_ref, qkv_ref, out_ref):
    deep = qkv_ref.shape[1]
    qkv_ref[...] = sum_ref[:, :deep].astype(f32)
    out_ref[...] = sum_ref[:, deep:].astype(f32)


def widen(total, deep, units):
    width = total.shape[0]
    return call(
        widen_body,
        "widen",
        grid=(width // units,),
        in_specs=[pl.BlockSpec((units, deep + units), lambda i: (i, 0))],
        out_specs=[
            pl.BlockSpec((units, deep), lambda i: (i, 0)),
            pl.BlockSpec((units, units), lambda i: (0, i)),
        ],
        out_shape=[
            jax.ShapeDtypeStruct((width, deep), f32),
            jax.ShapeDtypeStruct((units, width), f32),
        ],
    )(total)


def branch_body(attended_ref, hidden_ref, out_ref, down_ref, near_ref, far_ref):
    middle = near_ref.shape[0]
    total = dot_plain(attended_ref[...], out_ref[...]) + dot_plain(hidden_ref[...], down_ref[...])
    near_ref[...] = total[:middle].astype(bf16)
    far_ref[...] = total[middle:].astype(bf16)


def branch_sum(attended, hidden, out_weight, down_weight):
    group_rows = attended.shape[0]
    width = out_weight.shape[1]
    tile = min(512, width)
    once = pl.Buffered(1)
    half = pl.BlockSpec((group_rows // 2, tile), lambda i: (0, i))
    return call(
        branch_body,
        "branch_sum",
        grid=(width // tile,),
        in_specs=[
            pl.BlockSpec(attended.shape, lambda i: (0, 0), pipeline_mode=once),
            pl.BlockSpec(hidden.shape, lambda i: (0, 0), pipeline_mode=once),
            pl.BlockSpec((out_weight.shape[0], tile), lambda i: (0, i)),
            pl.BlockSpec((down_weight.shape[0], tile), lambda i: (0, i)),
        ],
        out_specs=[half, half],
        out_shape=[jax.ShapeDtypeStruct((group_rows // 2, width), bf16)] * 2,
    )(attended, hidden, out_weight, down_weight)


def input_body(
    qkv_grad_ref, gate_grad_ref, qkv_ref, up_ref, gain1, gain2, hat_ref, near_ref, far_ref, sum_ref
):
    middle = near_ref.shape[0]
    hat = hat_ref[...].astype(f32)
    first = contract_cols(qkv_grad_ref[...], qkv_ref[...])
    second = contract_cols(gate_grad_ref[...], up_ref[...])
    both = first * gain1[...] + second * gain2[...]
    near_ref[...] = both[:middle].astype(bf16)
    far_ref[...] = both[middle:].astype(bf16)
    sum_ref[0:1, :] = jnp.sum(first * hat, axis=0, keepdims=True)
    sum_ref[1:2, :] = jnp.sum(first, axis=0, keepdims=True)
    sum_ref[2:3, :] = jnp.sum(second * hat, axis=0, keepdims=True)
    sum_ref[3:4, :] = jnp.sum(second, axis=0, keepdims=True)


def input_sums(grad_qkv, grad_gate, qkv_weight, up_weight, gain1, gain2, hat):
    group_rows = grad_qkv.shape[0]
    width = qkv_weight.shape[0]
    tile = min(256, width)
    once = pl.Buffered(1)
    half = pl.BlockSpec((group_rows // 2, tile), lambda i: (0, i))
    row = pl.BlockSpec((1, tile), lambda i: (0, i))
    return call(
        input_body,
        "input_sums",
        grid=(width // tile,),
        in_specs=[
            pl.BlockSpec(grad_qkv.shape, lambda i: (0, 0), pipeline_mode=once),
            pl.BlockSpec(grad_gate.shape, lambda i: (0, 0), pipeline_mode=once),
            pl.BlockSpec((tile, qkv_weight.shape[1]), lambda i: (i, 0)),
            pl.BlockSpec((tile, up_weight.shape[1]), lambda i: (i, 0)),
            row,
            row,
            pl.BlockSpec((group_rows, tile), lambda i: (0, i)),
        ],
        out_specs=[half, half, pl.BlockSpec((4, tile), lambda i: (0, i))],
        out_shape=[jax.ShapeDtypeStruct((group_rows // 2, width), bf16)] * 2
        + [jax.ShapeDtypeStruct((4, width), f32)],
    )(grad_qkv, grad_gate, qkv_weight, up_weight, gain1, gain2, hat)


def attention_body(
    own_ref,
    starts_ref,
    raw_ref,
    bias_ref,
    cos_ref,
    sine_ref,
    slope_in_ref,
    attended_ref,
    grad_qkv_ref,
    bias_grad_ref,
    query_ref,
    key_ref,
    value_ref,
    slope_ref,
    query_sum_ref,
    key_sum_ref,
    value_sum_ref,
    *,
    rows,
    names,
    block_rows,
    longest,
):
    own = own_ref[0]
    group_rows = rows * len(names)
    lane = lax.broadcasted_iota(jnp.int32, (rows, HEAD_DIM), 1)
    half = ROTARY // 2
    scale = HEAD_DIM ** (-0.5)

    def turned(u):
        return jnp.where(lane < half, pltpu.roll(u, HEAD_DIM - half, 1), pltpu.roll(u, half, 1))

    def far_rows(name):
        return pl.ds(pl.multiple_of((own ^ name) * rows, rows), rows)

    for i, name in enumerate(names):
        near = slice(i * rows, (i + 1) * rows)
        far = far_rows(name)
        raw = raw_ref[near, :] + bias_ref[...]
        cos_table = cos_ref[near, :]
        sine_table = sine_ref[near, :]
        query = raw[:, :HEAD_DIM]
        key = raw[:, HEAD_DIM : 2 * HEAD_DIM]
        query_ref[far, :] = (query * cos_table + turned(query) * sine_table).astype(bf16)
        key_ref[far, :] = (key * cos_table + turned(key) * sine_table).astype(bf16)
        value_ref[far, :] = raw[:, 2 * HEAD_DIM :].astype(bf16)
        slope_ref[far, :] = slope_in_ref[near, :]
    key_sum_ref[...] = jnp.zeros_like(key_sum_ref)
    value_sum_ref[...] = jnp.zeros_like(value_sum_ref)
    for first in range(0, group_rows, block_rows):
        last = first + block_rows
        low = max(0, (first - longest + 1) // 128 * 128)
        query = query_ref[first:last, :]
        keys = key_ref[low:last, :]
        values = value_ref[low:last, :]
        slope = slope_ref[first:last, :]
        scores = contract_cols(query, keys) * scale
        row = first + lax.broadcasted_iota(jnp.int32, (block_rows, 1), 0)
        begin = jnp.zeros((block_rows, 1), jnp.int32)
        for slot in range(starts_ref.shape[0]):
            begin = jnp.where(starts_ref[slot] <= row, starts_ref[slot], begin)
        column = low + lax.broadcasted_iota(jnp.int32, scores.shape, 1)
        scores = jnp.where((column >= begin) & (column <= row), scores, masked_score)
        peak = jnp.max(scores, axis=1, keepdims=True)
        raised = jnp.exp(scores - peak)
        probs = raised * (1.0 / jnp.sum(raised, axis=1, keepdims=True))
        probs_low = probs.astype(bf16)
        query_ref[first:last, :] = dot_plain(probs_low, values).astype(bf16)
        grad_probs = contract_cols(slope, values)
        delta = jnp.sum(grad_probs * probs, axis=1, keepdims=True)
        grad_score = (probs * (grad_probs - delta)).astype(bf16)
        query_sum_ref[first:last, :] = dot_plain(grad_score, keys) * scale
        key_sum_ref[low:last, :] += contract_rows(grad_score, query) * scale
        value_sum_ref[low:last, :] += contract_rows(probs_low, slope)
    bias_grad = jnp.zeros(bias_grad_ref.shape, f32)
    for i, name in enumerate(names):
        near = slice(i * rows, (i + 1) * rows)
        far = far_rows(name)
        cos_table = cos_ref[near, :]
        sine_table = sine_ref[near, :]
        query_grad = query_sum_ref[far, :]
        key_grad = key_sum_ref[far, :]
        grads = jnp.concatenate(
            [
                query_grad * cos_table - turned(query_grad) * sine_table,
                key_grad * cos_table - turned(key_grad) * sine_table,
                value_sum_ref[far, :],
            ],
            axis=1,
        ).astype(bf16)
        grad_qkv_ref[near, :] = grads
        bias_grad = bias_grad + jnp.sum(grads.astype(f32), axis=0, keepdims=True)
        attended_ref[near, :] = query_ref[far, :]
    bias_grad_ref[...] = bias_grad


def attention(own, starts, raw, bias, cos_table, sine_table, slope, rows, names):
    group_rows, width = raw.shape
    part = 3 * HEAD_DIM
    heads = width // part
    whole = pl.BlockSpec((group_rows, HEAD_DIM), lambda h: (0, 0))
    scalars = pl.BlockSpec(memory_space=pltpu.SMEM)
    low = pltpu.VMEM((group_rows, HEAD_DIM), bf16)
    wide = pltpu.VMEM((group_rows, HEAD_DIM), f32)
    longest = group_rows // 2
    return pl.pallas_call(
        functools.partial(
            attention_body,
            rows=rows,
            names=names,
            block_rows=min(256, group_rows),
            longest=longest,
        ),
        grid=(heads,),
        in_specs=[
            scalars,
            scalars,
            pl.BlockSpec((group_rows, part), lambda h: (0, h)),
            pl.BlockSpec((1, part), lambda h: (0, h)),
            whole,
            whole,
            pl.BlockSpec((group_rows, HEAD_DIM), lambda h: (0, h)),
        ],
        out_specs=[
            pl.BlockSpec((group_rows, HEAD_DIM), lambda h: (0, h)),
            pl.BlockSpec((group_rows, part), lambda h: (0, h)),
            pl.BlockSpec((1, part), lambda h: (0, h)),
        ],
        out_shape=[
            jax.ShapeDtypeStruct((group_rows, heads * HEAD_DIM), bf16),
            jax.ShapeDtypeStruct((group_rows, width), bf16),
            jax.ShapeDtypeStruct((1, width), f32),
        ],
        scratch_shapes=[low, low, low, low, wide, wide, wide],
        compiler_params=pltpu.CompilerParams(vmem_limit_bytes=vmem_bytes),
        cost_estimate=pl.CostEstimate(flops=1, bytes_accessed=1, transcendentals=0),
        name="attention",
    )(own, starts, raw, bias, cos_table, sine_table, slope)


def rotary_tables(position):
    half_rot = ROTARY // 2
    frequency = 10000.0 ** (-2.0 * jnp.arange(half_rot, dtype=f32) / ROTARY)
    angles = position.astype(f32)[:, None] * frequency[None, :]
    cos_half = jnp.cos(angles)
    sine_half = jnp.sin(angles)
    rest = (position.shape[0], HEAD_DIM - ROTARY)
    return (
        jnp.concatenate([cos_half, cos_half, jnp.ones(rest, f32)], axis=1),
        jnp.concatenate([-sine_half, sine_half, jnp.zeros(rest, f32)], axis=1),
    )


def butterfly(value, axis, count, bit):
    return value + swap(value, axis, count, bit)


def fence(*values):
    return lax.optimization_barrier(values)


def norm_own(layer_input):
    values = layer_input.astype(f32)
    centred = values - jnp.mean(values, axis=-1, keepdims=True)
    inv_std = lax.rsqrt(jnp.mean(centred * centred, axis=-1, keepdims=True) + norm_eps)
    return centred * inv_std, inv_std


def tables(own, lengths, names, rows):
    seq_ends = jnp.cumsum(lengths)
    seq_starts = seq_ends - lengths
    places = (
        (own ^ jnp.array(names, jnp.int32))[:, None] * rows
        + jnp.arange(rows, dtype=jnp.int32)[None, :]
    ).reshape(-1)
    seq_first = jnp.max(
        jnp.where(seq_starts[None, :] <= places[:, None], seq_starts[None, :], 0), axis=1
    )
    return (seq_starts, *rotary_tables(places - seq_first))


def contiguous(first, second, names, rows):
    places = [{n: (which, i * rows) for i, n in enumerate(names)} for which in range(2)]
    return Spread([first, second], *places, names)


def ends(layer_input, cotangent, xhat, inv_std, branch, scaled, biases):
    layer_output = (layer_input.astype(f32) + branch + biases).astype(bf16)
    input_grad = cotangent.astype(f32) + inv_std * (
        scaled
        - jnp.mean(scaled, axis=-1, keepdims=True)
        - xhat * jnp.mean(scaled * xhat, axis=-1, keepdims=True)
    )
    return layer_output, input_grad


def per_device(
    layer_input,
    lengths,
    norm1_gain,
    norm1_bias,
    norm2_gain,
    norm2_bias,
    qkv_weight,
    qkv_bias,
    out_weight,
    out_bias,
    up_weight,
    up_bias,
    down_weight,
    down_bias,
    cotangent,
):
    dp = lax.axis_size("dp")
    mp = lax.axis_size("mp")
    own = lax.axis_index("mp")
    rows, width = layer_input.shape
    up_row = up_bias[None, :]
    gains = (norm1_gain[None, :], norm1_bias[None, :], norm2_gain[None, :], norm2_bias[None, :])
    gather_all = mp == 8 and dp == 4 and 4 * rows * mp * dp * (width + up_bias.shape[0]) < most_gathered

    pair = jnp.concatenate([layer_input, cotangent], axis=0)
    if gather_all:
        names = four_names
        sides = spread_sides(pair, mp)
        xhat, inv_std = norm_own(layer_input)
        second_own = (xhat * norm2_gain + norm2_bias).astype(bf16)
        shared = jnp.concatenate([second_own, cotangent], axis=0)
        group_a = turn(shared, "dp", dp, 1)
        placed = tables(own, lengths[0], names, rows)
        shared, pair, sides, placed = fence(shared, pair, sides, placed)
        corner = spread_corner(sides, mp)
        near = [pair, *sides]
        far = spread_core(near, mp)
        near, far, corner, group_a = fence(near, far, corner, group_a)
        near, far = near + corner, far + spread_core(corner, mp)
        near, far, group_a, shared = fence(near, far, group_a, shared)
        spread = spread_four(near, far)
    else:
        spread = spread_any(pair, mp)
        names = spread.names
        xhat, inv_std = norm_own(layer_input)
        placed = tables(own, lengths[0], names, rows)
    seq_starts, cos_table, sine_table = placed

    first_all, second_all, hat, raw, grad_attended, grad_out = entry(
        spread, rows, gains, qkv_weight, out_weight
    )
    attended, grad_qkv, qkv_bias_part = attention(
        own.reshape(1),
        seq_starts,
        raw,
        qkv_bias[None, :],
        cos_table,
        sine_table,
        grad_attended,
        rows,
        names,
    )
    if gather_all:
        sides_a = spread_sides(group_a, mp)
        far_a = spread_core([group_a], mp)
        group_b = turn(shared, "dp", dp, -1)
        (first_all, second_all, hat, grad_out, attended, grad_qkv), near_a, far_a, group_b = fence(
            (first_all, second_all, hat, grad_out, attended, grad_qkv),
            [group_a, *sides_a],
            far_a,
            group_b,
        )

    weights_part = attention_weights(first_all, grad_qkv, attended, grad_out)
    weights_sum = lax.psum_scatter(weights_part, "dp", scatter_dimension=0, tiled=True)
    if gather_all:
        corner_a = spread_corner(near_a[1:], mp)
        far_a = far_a + spread_core(near_a[1:], mp)
        group_c = turn(near_a[0], "dp", dp, 1)
        weights_part, second_all, hat, grad_out, attended, near_a, corner_a, far_a, group_b = fence(
            weights_part, second_all, hat, grad_out, attended, near_a, corner_a, far_a, group_b
        )

    own_spread = contiguous(second_all, grad_out, names, rows)
    hidden, grad_gate, gate_sum = mlp(own_spread, rows, up_weight, up_row, down_weight, False)
    branch = branch_sum(attended, hidden, out_weight, down_weight)
    if gather_all:
        sides_b = spread_sides(group_b, mp)
        far_b = spread_core([group_b], mp)
        far_a = far_a + spread_core(corner_a, mp)
        near_a = near_a + corner_a
        (hidden, grad_gate, branch, grad_qkv, hat), near_a, far_a, near_b, far_b, group_c = fence(
            (hidden, grad_gate, branch, grad_qkv, hat),
            near_a,
            far_a,
            [group_b, *sides_b],
            far_b,
            group_c,
        )

    scaled = input_sums(grad_qkv, grad_gate, qkv_weight, up_weight, gains[0], gains[2], hat)
    cot_sum = jnp.sum(cotangent.astype(f32), axis=0)
    small = jnp.concatenate([scaled[2].reshape(-1), cot_sum, qkv_bias_part.reshape(-1)])
    small = small.reshape(-1, 128)
    five = 5 * width // 128
    biases = out_bias + down_bias
    if not gather_all:
        own_branch = scatter_group(*branch, names, mp, rows, True)
        own_scaled = scatter_group(*scaled[:2], names, mp, rows, False)
        layer_output, input_grad = ends(
            layer_input, cotangent, xhat, inv_std, own_branch, own_scaled, biases
        )
        for bit in (1 << i for i in range(dp.bit_length() - 1)):
            small = butterfly(small, "dp", dp, bit)
        small, qkv_bias_grad = small[:five], small[five:]
        for bit in (1 << i for i in range(mp.bit_length() - 1)):
            small = butterfly(small, "mp", mp, bit)
        weights_sum = lax.all_gather(weights_sum, "dp", axis=0, tiled=True)
        up_weight_grad, down_weight_grad, up_bias_grad = lax.psum(
            (
                weight_product([second_all], [grad_gate], True, f32),
                weight_product([hidden], [grad_out], False, f32),
                gate_sum[0],
            ),
            "dp",
        )
    else:
        corner_b = spread_corner(near_b[1:], mp)
        far_b = far_b + spread_core(near_b[1:], mp)
        branch_came = swap(branch[1], "mp", mp, 1)
        scaled, small, near_a, far_a, near_b, far_b, corner_b, branch_came, group_c = fence(
            scaled, small, near_a, far_a, near_b, far_b, corner_b, branch_came, group_c
        )

        hidden_a, gate_a, sum_a, rows_a, cot_a = mlp(
            spread_four(near_a, far_a), rows, up_weight, up_row, down_weight, True
        )
        sides_c = spread_sides(group_c, mp)
        far_c = spread_core([group_c], mp)
        far_b = far_b + spread_core(corner_b, mp)
        near_b = near_b + corner_b
        scaled_came = swap(scaled[1], "mp", mp, 1)
        small = butterfly(small, "dp", dp, 1)
        own_branch = Scatter(branch[0], branch_came, names, mp, rows, True)
        branch_sent = own_branch.sent()
        done_a, near_b, far_b, near_c, far_c, scaled_came, small, branch_sent = fence(
            (hidden_a, gate_a, rows_a, cot_a),
            near_b,
            far_b,
            [group_c, *sides_c],
            far_c,
            scaled_came,
            small,
            branch_sent,
        )

        hidden_b, gate_b, sum_b, rows_b, cot_b = mlp(
            spread_four(near_b, far_b), rows, up_weight, up_row, down_weight, True
        )
        corner_c = spread_corner(near_c[1:], mp)
        far_c = far_c + spread_core(near_c[1:], mp)
        small = butterfly(small, "dp", dp, 2)
        (
            done_b,
            near_c,
            far_c,
            corner_c,
            small,
            branch_sent,
            scaled_near,
            scaled_came,
            weights_sum,
        ) = fence(
            (hidden_b, gate_b, rows_b, cot_b),
            near_c,
            far_c,
            corner_c,
            small,
            branch_sent,
            scaled[0],
            scaled_came,
            weights_sum,
        )
        weights_sum = lax.all_gather(weights_sum, "dp", axis=0, tiled=True)

        far_c = far_c + spread_core(corner_c, mp)
        near_c = near_c + corner_c
        own_scaled = Scatter(scaled_near, scaled_came, names, mp, rows, False)
        near_c, far_c, scaled_sent, branch_sent, small = fence(
            near_c, far_c, own_scaled.sent(), branch_sent, small
        )

        hidden_c, gate_c, sum_c, rows_c, cot_c = mlp(
            spread_four(near_c, far_c), rows, up_weight, up_row, down_weight, True
        )
        own_branch.step(*branch_sent)
        own_scaled.step(*scaled_sent)
        small, qkv_bias_grad = small[:five], small[five:]
        small = butterfly(small, "mp", mp, 1)
        done_c, branch_sent, scaled_sent, small = fence(
            (hidden_c, gate_c, rows_c, cot_c), own_branch.sent(), own_scaled.sent(), small
        )

        hiddens, gates, all_rows, all_cots = zip(done_a, done_b, done_c)
        up_weight_grad = weight_product([second_all, *all_rows], [grad_gate, *gates], True, f32)
        own_branch.step(*branch_sent)
        own_scaled.step(*scaled_sent)
        small = butterfly(small, "mp", mp, 2)
        up_weight_grad, hiddens, branch_total, scaled_total, small = fence(
            up_weight_grad, hiddens, own_branch.total(0), own_scaled.total(0), small
        )

        down_weight_grad = weight_product([hidden, *hiddens], [grad_out, *all_cots], False, f32)
        small = butterfly(small, "mp", mp, 4)
        layer_output, input_grad = ends(
            layer_input, cotangent, xhat, inv_std, branch_total, scaled_total, biases
        )
        up_bias_grad = (gate_sum + sum_a + sum_b + sum_c)[0]
        down_weight_grad, weights_sum, small, layer_output, input_grad = fence(
            down_weight_grad, weights_sum, small, layer_output, input_grad
        )
    small = small.reshape(5, width)
    qkv_weight_grad, out_weight_grad = widen(weights_sum, qkv_weight.shape[1], out_weight.shape[0])
    return (
        layer_output,
        input_grad,
        small[0],
        small[1],
        small[2],
        small[3],
        qkv_weight_grad,
        qkv_bias_grad.reshape(-1),
        out_weight_grad,
        small[4],
        up_weight_grad,
        up_bias_grad,
        down_weight_grad,
        small[4],
    )


def solution(mesh):
    in_specs = (
        P(("dp", "mp"), None),
        P("dp", None),
        P(),
        P(),
        P(),
        P(),
        P(None, "mp"),
        P("mp"),
        P("mp", None),
        P(),
        P(None, "mp"),
        P("mp"),
        P("mp", None),
        P(),
        P(("dp", "mp"), None),
    )
    out_specs = (
        P(("dp", "mp"), None),
        P(("dp", "mp"), None),
        P(),
        P(),
        P(),
        P(),
        P(None, "mp"),
        P("mp"),
        P("mp", None),
        P(),
        P(None, "mp"),
        P("mp"),
        P("mp", None),
        P(),
    )
    return jax.shard_map(
        per_device, mesh=mesh, in_specs=in_specs, out_specs=out_specs, check_vma=False
    )
```

```python
import functools

import jax
import jax.numpy as jnp
from jax import lax
from jax.experimental import pallas as pl
from jax.experimental.pallas import tpu as pltpu
from jax.sharding import PartitionSpec as P

HEAD_DIM = 128
ROTARY = 32

norm_eps = 1e-05
masked_score = -1e30
inv_root_two = 0.7071067811865476
inv_root_tau = 0.3989422804014327
vmem_bytes = 60 << 20
most_gathered = 128 << 20
bf16 = jnp.bfloat16
f32 = jnp.float32


def dot_plain(left, right):
    return jnp.dot(left, right, preferred_element_type=f32)


def contract_rows(left, right):
    return lax.dot_general(left, right, (((0,), (0,)), ((), ())), preferred_element_type=f32)


def contract_cols(left, right):
    return lax.dot_general(left, right, (((1,), (1,)), ((), ())), preferred_element_type=f32)


def swap(value, axis, count, bit):
    return lax.ppermute(value, axis, [(i, i ^ bit) for i in range(count)])


def turn(value, axis, count, step):
    return lax.ppermute(value, axis, [(i, (i + step) % count) for i in range(count)])


def chip_bits(count):
    return [1 << i for i in range(1, count.bit_length() - 1)]


def after(value, *earlier):
    return lax.optimization_barrier((value, *earlier))[0]


def halves(pair):
    rows = pair.shape[0] // 2
    return pair[:rows], pair[rows:]


class Spread:
    def __init__(self, arrays, a, b, names):
        self.arrays, self.a, self.b, self.names = arrays, a, b, names


four_names = (0, 2, 4, 6, 1, 3, 5, 7)


def spread_sides(pair, count):
    return [swap(pair, "mp", count, 2), swap(pair, "mp", count, 4)]


def spread_corner(sides, count):
    side_x, side_y = sides
    return [swap(halves(side_x)[0], "mp", count, 4), swap(halves(side_y)[1], "mp", count, 2)]


def spread_core(arrays, count):
    return [swap(array, "mp", count, 1) for array in arrays]


def spread_four(near, far):
    rows = near[0].shape[0] // 2
    a, b = {}, {}
    for core in range(2):
        base = 5 * core
        for i, name in enumerate((0, 2, 4)):
            a[name + core] = (base + i, 0)
            b[name + core] = (base + i, rows)
        a[6 + core] = (base + 3, 0)
        b[6 + core] = (base + 4, 0)
    return Spread(near + far, a, b, four_names)


def spread_any(pair, count):
    rows = pair.shape[0] // 2
    held, names = pair.reshape(1, 2, rows, -1), [0]
    for bit in chip_bits(count) + [1]:
        held = jnp.concatenate([held, swap(held, "mp", count, bit)], axis=0)
        names = names + [n ^ bit for n in names]
    arrays = [held.reshape(2 * rows * count, -1)]
    a = {n: (0, 2 * rows * i) for i, n in enumerate(names)}
    b = {n: (0, 2 * rows * i + rows) for i, n in enumerate(names)}
    return Spread(arrays, a, b, tuple(names))


class Scatter:
    def __init__(self, near, came, names, count, rows, rising):
        self.count, self.rows = count, rows
        names = names[: len(names) // 2]
        self.blocks = {n: near[i * rows : (i + 1) * rows] for i, n in enumerate(names)}
        self.adds = {n: came[i * rows : (i + 1) * rows] for i, n in enumerate(names)}
        bits = chip_bits(count)
        self.bits = bits if rising else bits[::-1]

    def total(self, n):
        return self.blocks[n].astype(f32) + self.adds[n].astype(f32)

    def sent(self):
        bit = self.bits[0]
        stay = [n for n in self.blocks if not n & bit]
        going = jnp.concatenate([self.total(n | bit).astype(bf16) for n in stay], axis=0)
        return going, [self.total(n).astype(bf16) for n in stay]

    def step(self, going, kept):
        bit, self.bits = self.bits[0], self.bits[1:]
        came = swap(going, "mp", self.count, bit)
        stay = [n for n in self.blocks if not n & bit]
        self.blocks = dict(zip(stay, kept))
        self.adds = {n: came[i * self.rows : (i + 1) * self.rows] for i, n in enumerate(stay)}


def scatter_group(near, far, names, count, rows, rising):
    scatter = Scatter(near, swap(far, "mp", count, 1), names, count, rows, rising)
    while scatter.bits:
        scatter.step(*scatter.sent())
    return scatter.total(0)


def call(body, name, **kwargs):
    return pl.pallas_call(
        body,
        name=name,
        compiler_params=pltpu.CompilerParams(vmem_limit_bytes=vmem_bytes),
        cost_estimate=pl.CostEstimate(flops=1, bytes_accessed=1, transcendentals=0),
        **kwargs,
    )


def block_copies(spread, which, refs, buffer, sems, rows, block):
    copies = []
    for i, name in enumerate(spread.names):
        array, first = getattr(spread, which)[name]
        copies.append(
            pltpu.make_async_copy(
                refs[array].at[first : first + rows, :],
                buffer.at[i * rows : (i + 1) * rows, :],
                sems.at[i],
            )
        )
    per = block // rows
    return [copies[i : i + per] for i in range(0, len(copies), per)]


def out_copies(buffer, ref, sems, block):
    count = buffer.shape[0] // block
    return [
        pltpu.make_async_copy(
            buffer.at[i * block : (i + 1) * block, :],
            ref.at[i * block : (i + 1) * block, :],
            sems.at[i],
        )
        for i in range(count)
    ]


def entry_body(*refs, spread, rows, block):
    count = len(spread.arrays)
    arrays = refs[:count]
    (gain1, bias1, gain2, bias2, qkv_ref, out_weight_ref) = refs[count : count + 6]
    (one_ref, two_ref, hat_ref, raw_ref, grad_ref, cot_ref) = refs[count + 6 : count + 12]
    x_buf, c_buf, sem_x, sem_c, sem_out = refs[count + 12 :]
    step = pl.program_id(0)
    x_copies = block_copies(spread, "a", arrays, x_buf, sem_x, rows, block)
    c_copies = block_copies(spread, "b", arrays, c_buf, sem_c, rows, block)
    outs = out_copies(c_buf, cot_ref, sem_out, block)

    @pl.when(step == 0)
    def _():
        for x_list, c_list in zip(x_copies, c_copies):
            for copy in x_list + c_list:
                copy.start()

    for i in range(len(outs)):

        @pl.when(step == i)
        def _(i=i):
            for copy in x_copies[i] + c_copies[i]:
                copy.wait()
            outs[i].start()

    here = pl.ds(pl.multiple_of(step * block, block), block)
    values = x_buf[here, :].astype(f32)
    centred = values - jnp.mean(values, axis=1, keepdims=True)
    hat = centred * lax.rsqrt(jnp.mean(centred * centred, axis=1, keepdims=True) + norm_eps)
    hat_ref[...] = hat.astype(bf16)
    one_ref[...] = (hat * gain1[...] + bias1[...]).astype(bf16)
    two_ref[...] = (hat * gain2[...] + bias2[...]).astype(bf16)
    raw_ref[...] = dot_plain(one_ref[...], qkv_ref[...])
    grad_ref[...] = contract_cols(c_buf[here, :], out_weight_ref[...]).astype(bf16)

    @pl.when(step == len(outs) - 1)
    def _():
        for copy in outs:
            copy.wait()


def entry(spread, rows, gains, qkv_weight, out_weight):
    group_rows = rows * len(spread.names)
    width, deep = qkv_weight.shape
    units = out_weight.shape[0]
    block = min(256, group_rows)
    steps = group_rows // block
    blocks = len(spread.names)
    once = pl.Buffered(1)
    full = pl.BlockSpec((block, width), lambda i: (i, 0))
    row = pl.BlockSpec((1, width), lambda i: (0, 0))
    anywhere = pl.BlockSpec(memory_space=pl.ANY)
    wide = jax.ShapeDtypeStruct((group_rows, width), bf16)
    return call(
        functools.partial(entry_body, spread=spread, rows=rows, block=block),
        "entry",
        grid=(steps,),
        in_specs=[anywhere] * len(spread.arrays)
        + [row] * 4
        + [
            pl.BlockSpec(qkv_weight.shape, lambda i: (0, 0), pipeline_mode=once),
            pl.BlockSpec(out_weight.shape, lambda i: (0, 0), pipeline_mode=once),
        ],
        out_specs=[
            full,
            full,
            full,
            pl.BlockSpec((block, deep), lambda i: (i, 0)),
            pl.BlockSpec((block, units), lambda i: (i, 0)),
            anywhere,
        ],
        out_shape=[
            wide,
            wide,
            wide,
            jax.ShapeDtypeStruct((group_rows, deep), f32),
            jax.ShapeDtypeStruct((group_rows, units), bf16),
            wide,
        ],
        scratch_shapes=[
            pltpu.VMEM((group_rows, width), bf16),
            pltpu.VMEM((group_rows, width), bf16),
            pltpu.SemaphoreType.DMA((blocks,)),
            pltpu.SemaphoreType.DMA((blocks,)),
            pltpu.SemaphoreType.DMA((steps,)),
        ],
    )(*spread.arrays, *gains, qkv_weight, out_weight)


def mlp_body(*refs, spread, rows, block, tile, keep):
    count = len(spread.arrays)
    arrays = refs[:count]
    up_ref, shift_ref, down_ref, hidden_ref, grad_ref, sum_ref = refs[count : count + 6]
    rest = refs[count + 6 :]
    if keep:
        rows_ref, cot_ref = rest[:2]
        rest = rest[2:]
    x_buf, c_buf, u_buf, d_buf, *rest = rest
    gates, slopes = rest[:2], rest[2:4]
    sem_x, sem_c, sem_u, sem_d, sem_ox, sem_oc = rest[4:]
    step = pl.program_id(0)
    units = u_buf.shape[1]
    x_copies = block_copies(spread, "a", arrays, x_buf, sem_x, rows, block)
    c_copies = block_copies(spread, "b", arrays, c_buf, sem_c, rows, block)
    tiles = [slice(i, i + tile) for i in range(0, units, tile)]
    u_copies = [
        pltpu.make_async_copy(up_ref.at[:, t], u_buf.at[:, t], sem_u.at[i])
        for i, t in enumerate(tiles)
    ]
    d_copies = [
        pltpu.make_async_copy(down_ref.at[t, :], d_buf.at[t, :], sem_d.at[i])
        for i, t in enumerate(tiles)
    ]
    outs = []
    if keep:
        outs = list(
            zip(
                out_copies(x_buf, rows_ref, sem_ox, block),
                out_copies(c_buf, cot_ref, sem_oc, block),
            )
        )

    @pl.when(step == 0)
    def _():
        for copy in x_copies[0] + u_copies[:1] + c_copies[0] + d_copies[:1]:
            copy.start()
        for pair in zip(u_copies[1:], d_copies[1:]):
            for copy in pair:
                copy.start()
        for x_list, c_list in zip(x_copies[1:], c_copies[1:]):
            for copy in x_list + c_list:
                copy.start()
        sum_ref[...] = jnp.zeros_like(sum_ref)

    for i in range(len(x_copies)):

        @pl.when(step == i)
        def _(i=i):
            for copy in x_copies[i] + c_copies[i]:
                copy.wait()
            if keep:
                outs[i][0].start()
                outs[i][1].start()

    here = pl.ds(pl.multiple_of(step * block, block), block)

    def finish(part, gate, grad_hidden):
        gate = gate[...] + shift_ref[:, part]
        below = 0.5 * (1.0 + lax.erf(gate * inv_root_two))
        hidden_ref[:, part] = (gate * below).astype(bf16)
        slope = below + gate * jnp.exp(-0.5 * gate * gate) * inv_root_tau
        grad = (grad_hidden[...] * slope).astype(bf16)
        grad_ref[:, part] = grad
        sum_ref[:, part] += jnp.sum(grad.astype(f32), axis=0, keepdims=True)

    for i, part in enumerate(tiles):

        @pl.when(step == 0)
        def _(i=i):
            u_copies[i].wait()
            d_copies[i].wait()

        gates[i % 2][...] = dot_plain(x_buf[here, :], u_buf[:, part])
        slopes[i % 2][...] = contract_cols(c_buf[here, :], d_buf[part, :])
        if i:
            finish(tiles[i - 1], gates[(i - 1) % 2], slopes[(i - 1) % 2])
    finish(tiles[-1], gates[(len(tiles) - 1) % 2], slopes[(len(tiles) - 1) % 2])

    if keep:

        @pl.when(step == len(x_copies) - 1)
        def _():
            for pair in outs:
                for copy in pair:
                    copy.wait()


def mlp(spread, rows, up_weight, up_bias, down_weight, keep):
    width, units = up_weight.shape
    group_rows = rows * len(spread.names)
    block = min(512, group_rows)
    tile = min(256, units)
    steps, tiles, blocks = group_rows // block, units // tile, len(spread.names)
    anywhere = pl.BlockSpec(memory_space=pl.ANY)
    part = pl.BlockSpec((block, units), lambda i: (i, 0))
    low = jax.ShapeDtypeStruct((group_rows, units), bf16)
    wide = jax.ShapeDtypeStruct((group_rows, width), bf16)
    dma = pltpu.SemaphoreType.DMA
    return call(
        functools.partial(mlp_body, spread=spread, rows=rows, block=block, tile=tile, keep=keep),
        "mlp",
        grid=(steps,),
        in_specs=[anywhere] * len(spread.arrays)
        + [anywhere, pl.BlockSpec((1, units), lambda i: (0, 0)), anywhere],
        out_specs=[part, part, pl.BlockSpec((1, units), lambda i: (0, 0))]
        + [anywhere] * (2 * keep),
        out_shape=[low, low, jax.ShapeDtypeStruct((1, units), f32)] + [wide] * (2 * keep),
        scratch_shapes=[
            pltpu.VMEM((group_rows, width), bf16),
            pltpu.VMEM((group_rows, width), bf16),
            pltpu.VMEM((width, units), bf16),
            pltpu.VMEM((units, width), bf16),
            *[pltpu.VMEM((block, tile), f32)] * 4,
            dma((blocks,)),
            dma((blocks,)),
            dma((tiles,)),
            dma((tiles,)),
            dma((steps,)),
            dma((steps,)),
        ],
    )(*spread.arrays, up_weight, up_bias, down_weight)


def widen_body(sum_ref, qkv_ref, out_ref):
    units, deep = out_ref.shape[0], qkv_ref.shape[1]
    qkv_ref[...] = sum_ref[:, :deep].astype(f32)
    for first in range(0, sum_ref.shape[0], units):
        out_ref[:, first : first + units] = sum_ref[first : first + units, deep:].astype(f32)


def weight_body(*refs, pieces):
    if len(refs) > 2 * pieces + 1:
        widen_body(refs[2 * pieces], *refs[-2:])
        refs = refs[: 2 * pieces] + (refs[2 * pieces + 1],)
    out_ref = refs[2 * pieces]
    total = contract_rows(refs[0][...], refs[pieces][...])
    for piece in range(1, pieces):
        total = total + contract_rows(refs[piece][...], refs[pieces + piece][...])
    out_ref[...] = total.astype(out_ref.dtype)


def weight_product(lefts, rights, tile_left, total=None, deep_units=()):
    wide, deep = lefts[0].shape[1], rights[0].shape[1]
    tile = min(512, wide if tile_left else deep)
    once = pl.Buffered(1)
    steps = (wide if tile_left else deep) // tile

    def spec(piece, tiled):
        if tiled:
            return pl.BlockSpec((piece.shape[0], tile), lambda i: (0, i))
        return pl.BlockSpec(piece.shape, lambda i: (0, 0), pipeline_mode=once)

    extra = ([], [], [])
    if total is not None:
        extra = widen_specs(total, *deep_units, total.shape[0] // steps)
    out_spec = (
        pl.BlockSpec((tile, deep), lambda i: (i, 0))
        if tile_left
        else pl.BlockSpec((wide, tile), lambda i: (0, i))
    )
    return call(
        functools.partial(weight_body, pieces=len(lefts)),
        "weight_product",
        grid=(steps,),
        in_specs=[spec(p, tile_left) for p in lefts]
        + [spec(p, not tile_left) for p in rights]
        + extra[0],
        out_specs=[out_spec] + extra[1],
        out_shape=[jax.ShapeDtypeStruct((wide, deep), f32)] + extra[2],
    )(*lefts, *rights, *([] if total is None else [total]))


def attention_weights_body(normed_ref, grad_qkv_ref, attended_ref, grad_out_ref, sum_ref):
    deep = grad_qkv_ref.shape[1]
    sum_ref[:, :deep] = contract_rows(normed_ref[...], grad_qkv_ref[...]).astype(bf16)
    sum_ref[:, deep:] = contract_rows(attended_ref[...], grad_out_ref[...]).astype(bf16)


def attention_weights(normed, grad_qkv, attended, grad_out):
    group_rows, width = normed.shape
    deep, units = grad_qkv.shape[1], attended.shape[1]
    once = pl.Buffered(1)
    block = pl.BlockSpec((group_rows, units), lambda i: (0, i))
    return call(
        attention_weights_body,
        "attention_weights",
        grid=(width // units,),
        in_specs=[
            block,
            pl.BlockSpec(grad_qkv.shape, lambda i: (0, 0), pipeline_mode=once),
            pl.BlockSpec(attended.shape, lambda i: (0, 0), pipeline_mode=once),
            block,
        ],
        out_specs=pl.BlockSpec((units, deep + units), lambda i: (i, 0)),
        out_shape=jax.ShapeDtypeStruct((width, deep + units), bf16),
    )(normed, grad_qkv, attended, grad_out)


def widen_specs(total, deep, units, block):
    width = total.shape[0]
    return (
        [pl.BlockSpec((block, deep + units), lambda i: (i, 0))],
        [
            pl.BlockSpec((block, deep), lambda i: (i, 0)),
            pl.BlockSpec((units, block), lambda i: (0, i)),
        ],
        [
            jax.ShapeDtypeStruct((width, deep), f32),
            jax.ShapeDtypeStruct((units, width), f32),
        ],
    )


def widen(total, deep, units):
    in_specs, out_specs, out_shape = widen_specs(total, deep, units, units)
    return call(
        widen_body,
        "widen",
        grid=(total.shape[0] // units,),
        in_specs=in_specs,
        out_specs=out_specs,
        out_shape=out_shape,
    )(total)


def branch_body(attended_ref, hidden_ref, out_ref, down_ref, near_ref, far_ref):
    middle = near_ref.shape[0]
    total = dot_plain(attended_ref[...], out_ref[...]) + dot_plain(hidden_ref[...], down_ref[...])
    near_ref[...] = total[:middle].astype(bf16)
    far_ref[...] = total[middle:].astype(bf16)


def branch_sum(attended, hidden, out_weight, down_weight):
    group_rows = attended.shape[0]
    width = out_weight.shape[1]
    tile = min(512, width)
    once = pl.Buffered(1)
    half = pl.BlockSpec((group_rows // 2, tile), lambda i: (0, i))
    return call(
        branch_body,
        "branch_sum",
        grid=(width // tile,),
        in_specs=[
            pl.BlockSpec(attended.shape, lambda i: (0, 0), pipeline_mode=once),
            pl.BlockSpec(hidden.shape, lambda i: (0, 0), pipeline_mode=once),
            pl.BlockSpec((out_weight.shape[0], tile), lambda i: (0, i)),
            pl.BlockSpec((down_weight.shape[0], tile), lambda i: (0, i)),
        ],
        out_specs=[half, half],
        out_shape=[jax.ShapeDtypeStruct((group_rows // 2, width), bf16)] * 2,
    )(attended, hidden, out_weight, down_weight)


def input_body(
    qkv_grad_ref, gate_grad_ref, qkv_ref, up_ref, gain1, gain2, hat_ref, near_ref, far_ref, sum_ref
):
    middle = near_ref.shape[0]
    hat = hat_ref[...].astype(f32)
    first = contract_cols(qkv_grad_ref[...], qkv_ref[...])
    second = contract_cols(gate_grad_ref[...], up_ref[...])
    both = first * gain1[...] + second * gain2[...]
    near_ref[...] = both[:middle].astype(bf16)
    far_ref[...] = both[middle:].astype(bf16)
    sum_ref[0:1, :] = jnp.sum(first * hat, axis=0, keepdims=True)
    sum_ref[1:2, :] = jnp.sum(first, axis=0, keepdims=True)
    sum_ref[2:3, :] = jnp.sum(second * hat, axis=0, keepdims=True)
    sum_ref[3:4, :] = jnp.sum(second, axis=0, keepdims=True)


def input_sums(grad_qkv, grad_gate, qkv_weight, up_weight, gain1, gain2, hat):
    group_rows = grad_qkv.shape[0]
    width = qkv_weight.shape[0]
    tile = min(256, width)
    once = pl.Buffered(1)
    half = pl.BlockSpec((group_rows // 2, tile), lambda i: (0, i))
    row = pl.BlockSpec((1, tile), lambda i: (0, i))
    return call(
        input_body,
        "input_sums",
        grid=(width // tile,),
        in_specs=[
            pl.BlockSpec(grad_qkv.shape, lambda i: (0, 0), pipeline_mode=once),
            pl.BlockSpec(grad_gate.shape, lambda i: (0, 0), pipeline_mode=once),
            pl.BlockSpec((tile, qkv_weight.shape[1]), lambda i: (i, 0)),
            pl.BlockSpec((tile, up_weight.shape[1]), lambda i: (i, 0)),
            row,
            row,
            pl.BlockSpec((group_rows, tile), lambda i: (0, i)),
        ],
        out_specs=[half, half, pl.BlockSpec((4, tile), lambda i: (0, i))],
        out_shape=[jax.ShapeDtypeStruct((group_rows // 2, width), bf16)] * 2
        + [jax.ShapeDtypeStruct((4, width), f32)],
    )(grad_qkv, grad_gate, qkv_weight, up_weight, gain1, gain2, hat)


def attention_body(
    own_ref,
    starts_ref,
    raw_ref,
    bias_ref,
    cos_ref,
    sine_ref,
    slope_in_ref,
    attended_ref,
    grad_qkv_ref,
    bias_grad_ref,
    query_ref,
    key_ref,
    value_ref,
    slope_ref,
    query_sum_ref,
    key_sum_ref,
    value_sum_ref,
    *,
    rows,
    names,
    block_rows,
    longest,
):
    own = own_ref[0]
    group_rows = rows * len(names)
    lane = lax.broadcasted_iota(jnp.int32, (rows, HEAD_DIM), 1)
    half = ROTARY // 2
    scale = HEAD_DIM ** (-0.5)

    def turned(u):
        return jnp.where(lane < half, pltpu.roll(u, HEAD_DIM - half, 1), pltpu.roll(u, half, 1))

    def far_rows(name):
        return pl.ds(pl.multiple_of((own ^ name) * rows, rows), rows)

    for i, name in enumerate(names):
        near = slice(i * rows, (i + 1) * rows)
        far = far_rows(name)
        raw = raw_ref[near, :] + bias_ref[...]
        cos_table = cos_ref[near, :]
        sine_table = sine_ref[near, :]
        query = raw[:, :HEAD_DIM]
        key = raw[:, HEAD_DIM : 2 * HEAD_DIM]
        query_ref[far, :] = (query * cos_table + turned(query) * sine_table).astype(bf16)
        key_ref[far, :] = (key * cos_table + turned(key) * sine_table).astype(bf16)
        value_ref[far, :] = raw[:, 2 * HEAD_DIM :].astype(bf16)
        slope_ref[far, :] = slope_in_ref[near, :]
    key_sum_ref[...] = jnp.zeros_like(key_sum_ref)
    value_sum_ref[...] = jnp.zeros_like(value_sum_ref)
    for first in range(0, group_rows, block_rows):
        last = first + block_rows
        low = max(0, (first - longest + 1) // 128 * 128)
        query = query_ref[first:last, :]
        keys = key_ref[low:last, :]
        values = value_ref[low:last, :]
        slope = slope_ref[first:last, :]
        scores = contract_cols(query, keys) * scale
        row = first + lax.broadcasted_iota(jnp.int32, (block_rows, 1), 0)
        begin = jnp.zeros((block_rows, 1), jnp.int32)
        for slot in range(starts_ref.shape[0]):
            begin = jnp.where(starts_ref[slot] <= row, starts_ref[slot], begin)
        column = low + lax.broadcasted_iota(jnp.int32, scores.shape, 1)
        scores = jnp.where((column >= begin) & (column <= row), scores, masked_score)
        peak = jnp.max(scores, axis=1, keepdims=True)
        raised = jnp.exp(scores - peak)
        probs = raised * (1.0 / jnp.sum(raised, axis=1, keepdims=True))
        probs_low = probs.astype(bf16)
        query_ref[first:last, :] = dot_plain(probs_low, values).astype(bf16)
        grad_probs = contract_cols(slope, values)
        delta = jnp.sum(grad_probs * probs, axis=1, keepdims=True)
        grad_score = (probs * (grad_probs - delta)).astype(bf16)
        query_sum_ref[first:last, :] = dot_plain(grad_score, keys) * scale
        key_sum_ref[low:last, :] += contract_rows(grad_score, query) * scale
        value_sum_ref[low:last, :] += contract_rows(probs_low, slope)
    bias_grad = jnp.zeros(bias_grad_ref.shape, f32)
    for i, name in enumerate(names):
        near = slice(i * rows, (i + 1) * rows)
        far = far_rows(name)
        cos_table = cos_ref[near, :]
        sine_table = sine_ref[near, :]
        query_grad = query_sum_ref[far, :]
        key_grad = key_sum_ref[far, :]
        grads = jnp.concatenate(
            [
                query_grad * cos_table - turned(query_grad) * sine_table,
                key_grad * cos_table - turned(key_grad) * sine_table,
                value_sum_ref[far, :],
            ],
            axis=1,
        ).astype(bf16)
        grad_qkv_ref[near, :] = grads
        bias_grad = bias_grad + jnp.sum(grads.astype(f32), axis=0, keepdims=True)
        attended_ref[near, :] = query_ref[far, :]
    bias_grad_ref[...] = bias_grad


def attention(own, starts, raw, bias, cos_table, sine_table, slope, rows, names):
    group_rows, width = raw.shape
    part = 3 * HEAD_DIM
    heads = width // part
    whole = pl.BlockSpec((group_rows, HEAD_DIM), lambda h: (0, 0))
    scalars = pl.BlockSpec(memory_space=pltpu.SMEM)
    low = pltpu.VMEM((group_rows, HEAD_DIM), bf16)
    wide = pltpu.VMEM((group_rows, HEAD_DIM), f32)
    longest = group_rows // 2
    return pl.pallas_call(
        functools.partial(
            attention_body,
            rows=rows,
            names=names,
            block_rows=min(256, group_rows),
            longest=longest,
        ),
        grid=(heads,),
        in_specs=[
            scalars,
            scalars,
            pl.BlockSpec((group_rows, part), lambda h: (0, h)),
            pl.BlockSpec((1, part), lambda h: (0, h)),
            whole,
            whole,
            pl.BlockSpec((group_rows, HEAD_DIM), lambda h: (0, h)),
        ],
        out_specs=[
            pl.BlockSpec((group_rows, HEAD_DIM), lambda h: (0, h)),
            pl.BlockSpec((group_rows, part), lambda h: (0, h)),
            pl.BlockSpec((1, part), lambda h: (0, h)),
        ],
        out_shape=[
            jax.ShapeDtypeStruct((group_rows, heads * HEAD_DIM), bf16),
            jax.ShapeDtypeStruct((group_rows, width), bf16),
            jax.ShapeDtypeStruct((1, width), f32),
        ],
        scratch_shapes=[low, low, low, low, wide, wide, wide],
        compiler_params=pltpu.CompilerParams(vmem_limit_bytes=vmem_bytes),
        cost_estimate=pl.CostEstimate(flops=1, bytes_accessed=1, transcendentals=0),
        name="attention",
    )(own, starts, raw, bias, cos_table, sine_table, slope)


def rotary_tables(position):
    half_rot = ROTARY // 2
    frequency = 10000.0 ** (-2.0 * jnp.arange(half_rot, dtype=f32) / ROTARY)
    angles = position.astype(f32)[:, None] * frequency[None, :]
    cos_half = jnp.cos(angles)
    sine_half = jnp.sin(angles)
    rest = (position.shape[0], HEAD_DIM - ROTARY)
    return (
        jnp.concatenate([cos_half, cos_half, jnp.ones(rest, f32)], axis=1),
        jnp.concatenate([-sine_half, sine_half, jnp.zeros(rest, f32)], axis=1),
    )


def butterfly(value, axis, count, bit):
    return value + swap(value, axis, count, bit)


def fence(*values):
    return lax.optimization_barrier(values)


def norm_own(layer_input):
    values = layer_input.astype(f32)
    centred = values - jnp.mean(values, axis=-1, keepdims=True)
    inv_std = lax.rsqrt(jnp.mean(centred * centred, axis=-1, keepdims=True) + norm_eps)
    return centred * inv_std, inv_std


def tables(own, lengths, names, rows):
    seq_ends = jnp.cumsum(lengths)
    seq_starts = seq_ends - lengths
    places = (
        (own ^ jnp.array(names, jnp.int32))[:, None] * rows
        + jnp.arange(rows, dtype=jnp.int32)[None, :]
    ).reshape(-1)
    seq_first = jnp.max(
        jnp.where(seq_starts[None, :] <= places[:, None], seq_starts[None, :], 0), axis=1
    )
    return (seq_starts, *rotary_tables(places - seq_first))


def contiguous(first, second, names, rows):
    places = [{n: (which, i * rows) for i, n in enumerate(names)} for which in range(2)]
    return Spread([first, second], *places, names)


def ends(layer_input, cotangent, xhat, inv_std, branch, scaled, biases):
    layer_output = (layer_input.astype(f32) + branch + biases).astype(bf16)
    input_grad = cotangent.astype(f32) + inv_std * (
        scaled
        - jnp.mean(scaled, axis=-1, keepdims=True)
        - xhat * jnp.mean(scaled * xhat, axis=-1, keepdims=True)
    )
    return layer_output, input_grad


def per_device(
    layer_input,
    lengths,
    norm1_gain,
    norm1_bias,
    norm2_gain,
    norm2_bias,
    qkv_weight,
    qkv_bias,
    out_weight,
    out_bias,
    up_weight,
    up_bias,
    down_weight,
    down_bias,
    cotangent,
):
    dp = lax.axis_size("dp")
    mp = lax.axis_size("mp")
    own = lax.axis_index("mp")
    rows, width = layer_input.shape
    up_row = up_bias[None, :]
    gains = (norm1_gain[None, :], norm1_bias[None, :], norm2_gain[None, :], norm2_bias[None, :])
    gather_all = mp == 8 and dp == 4 and 4 * rows * mp * dp * (width + up_bias.shape[0]) < most_gathered

    pair = jnp.concatenate([layer_input, cotangent], axis=0)
    if gather_all:
        names = four_names
        sides = spread_sides(pair, mp)
        xhat, inv_std = norm_own(layer_input)
        second_own = (xhat * norm2_gain + norm2_bias).astype(bf16)
        shared = jnp.concatenate([second_own, cotangent], axis=0)
        group_a = turn(shared, "dp", dp, 1)
        placed = tables(own, lengths[0], names, rows)
        far = spread_core([pair], mp)
        shared, pair, sides, placed, far = fence(shared, pair, sides, placed, far)
        group_b = turn(shared, "dp", dp, -1)
        corner = spread_corner(sides, mp)
        near = [pair, *sides]
        far = far + spread_core(sides, mp)
        near, far, corner, group_a = fence(near, far, corner, group_a)
        near, far = near + corner, far + spread_core(corner, mp)
        near, far, group_a = fence(near, far, group_a)
        spread = spread_four(near, far)
    else:
        spread = spread_any(pair, mp)
        names = spread.names
        xhat, inv_std = norm_own(layer_input)
        placed = tables(own, lengths[0], names, rows)
    seq_starts, cos_table, sine_table = placed

    first_all, second_all, hat, raw, grad_attended, grad_out = entry(
        spread, rows, gains, qkv_weight, out_weight
    )
    attended, grad_qkv, qkv_bias_part = attention(
        own.reshape(1),
        seq_starts,
        raw,
        qkv_bias[None, :],
        cos_table,
        sine_table,
        grad_attended,
        rows,
        names,
    )
    if gather_all:
        sides_a = spread_sides(group_a, mp)
        far_a = spread_core([group_a], mp)
        group_c = turn(group_a, "dp", dp, 1)
        (first_all, second_all, hat, grad_out, attended, grad_qkv), near_a, far_a, group_b, group_c = (
            fence(
                (first_all, second_all, hat, grad_out, attended, grad_qkv),
                [group_a, *sides_a],
                far_a,
                group_b,
                group_c,
            )
        )

    weights_part = attention_weights(first_all, grad_qkv, attended, grad_out)
    if gather_all:
        corner_a = spread_corner(near_a[1:], mp)
        far_a = far_a + spread_core(near_a[1:], mp)
        weights_part, second_all, hat, grad_out, attended, near_a, corner_a, far_a, group_b = fence(
            weights_part, second_all, hat, grad_out, attended, near_a, corner_a, far_a, group_b
        )
    weights_sum = lax.psum_scatter(weights_part, "dp", scatter_dimension=0, tiled=True)

    own_spread = contiguous(second_all, grad_out, names, rows)
    hidden, grad_gate, gate_sum = mlp(own_spread, rows, up_weight, up_row, down_weight, False)
    branch = branch_sum(attended, hidden, out_weight, down_weight)
    if gather_all:
        sides_b = spread_sides(group_b, mp)
        far_b = spread_core([group_b], mp)
        far_a = far_a + spread_core(corner_a, mp)
        near_a = near_a + corner_a
        (hidden, grad_gate, branch, grad_qkv, hat), near_a, far_a, near_b, far_b, group_c = fence(
            (hidden, grad_gate, branch, grad_qkv, hat),
            near_a,
            far_a,
            [group_b, *sides_b],
            far_b,
            group_c,
        )

    scaled = input_sums(grad_qkv, grad_gate, qkv_weight, up_weight, gains[0], gains[2], hat)
    cot_sum = jnp.sum(cotangent.astype(f32), axis=0)
    small = jnp.concatenate([scaled[2].reshape(-1), cot_sum, qkv_bias_part.reshape(-1)])
    small = small.reshape(-1, 128)
    five = 5 * width // 128
    biases = out_bias + down_bias

    def over_mp(both, bit):
        return jnp.concatenate([butterfly(both[:five], "mp", mp, bit), both[five:]], axis=0)

    if not gather_all:
        own_branch = scatter_group(*branch, names, mp, rows, True)
        own_scaled = scatter_group(*scaled[:2], names, mp, rows, False)
        layer_output, input_grad = ends(
            layer_input, cotangent, xhat, inv_std, own_branch, own_scaled, biases
        )
        for bit in (1 << i for i in range(dp.bit_length() - 1)):
            small = butterfly(small, "dp", dp, bit)
        small, qkv_bias_grad = small[:five], small[five:]
        for bit in (1 << i for i in range(mp.bit_length() - 1)):
            small = butterfly(small, "mp", mp, bit)
        qkv_weight_grad, out_weight_grad = widen(
            lax.all_gather(weights_sum, "dp", axis=0, tiled=True),
            qkv_weight.shape[1],
            out_weight.shape[0],
        )
        up_weight_grad, down_weight_grad, up_bias_grad = lax.psum(
            (
                weight_product([second_all], [grad_gate], True)[0],
                weight_product([hidden], [grad_out], False)[0],
                gate_sum[0],
            ),
            "dp",
        )
    else:
        corner_b = spread_corner(near_b[1:], mp)
        far_b = far_b + spread_core(near_b[1:], mp)
        branch_came = swap(branch[1], "mp", mp, 1)
        scaled, small, near_a, far_a, near_b, far_b, corner_b, branch_came, group_c = fence(
            scaled, small, near_a, far_a, near_b, far_b, corner_b, branch_came, group_c
        )

        hidden_a, gate_a, sum_a, rows_a, cot_a = mlp(
            spread_four(near_a, far_a), rows, up_weight, up_row, down_weight, True
        )
        sides_c = spread_sides(group_c, mp)
        far_c = spread_core([group_c], mp)
        far_b = far_b + spread_core(corner_b, mp)
        near_b = near_b + corner_b
        scaled_came = swap(scaled[1], "mp", mp, 1)
        small = over_mp(small, 1)
        own_branch = Scatter(branch[0], branch_came, names, mp, rows, True)
        branch_sent = own_branch.sent()
        done_a, near_b, far_b, near_c, far_c, scaled_came, small, branch_sent, weights_sum = fence(
            (hidden_a, gate_a, rows_a, cot_a),
            near_b,
            far_b,
            [group_c, *sides_c],
            far_c,
            scaled_came,
            small,
            branch_sent,
            weights_sum,
        )
        weights_sum = lax.all_gather(weights_sum, "dp", axis=0, tiled=True)

        hidden_b, gate_b, sum_b, rows_b, cot_b = mlp(
            spread_four(near_b, far_b), rows, up_weight, up_row, down_weight, True
        )
        corner_c = spread_corner(near_c[1:], mp)
        far_c = far_c + spread_core(near_c[1:], mp)
        small = over_mp(small, 2)
        (
            done_b,
            near_c,
            far_c,
            corner_c,
            small,
            branch_sent,
            scaled_near,
            scaled_came,
        ) = fence(
            (hidden_b, gate_b, rows_b, cot_b),
            near_c,
            far_c,
            corner_c,
            small,
            branch_sent,
            scaled[0],
            scaled_came,
        )

        far_c = far_c + spread_core(corner_c, mp)
        near_c = near_c + corner_c
        own_scaled = Scatter(scaled_near, scaled_came, names, mp, rows, False)
        near_c, far_c, scaled_sent, branch_sent, small = fence(
            near_c, far_c, own_scaled.sent(), branch_sent, small
        )

        hidden_c, gate_c, sum_c, rows_c, cot_c = mlp(
            spread_four(near_c, far_c), rows, up_weight, up_row, down_weight, True
        )
        own_branch.step(*branch_sent)
        own_scaled.step(*scaled_sent)
        small = over_mp(small, 4)
        done_c, branch_sent, scaled_sent, small = fence(
            (hidden_c, gate_c, rows_c, cot_c), own_branch.sent(), own_scaled.sent(), small
        )

        hiddens, gates, all_rows, all_cots = zip(done_a, done_b, done_c)
        (up_weight_grad,) = weight_product([second_all, *all_rows], [grad_gate, *gates], True)
        own_branch.step(*branch_sent)
        own_scaled.step(*scaled_sent)
        small = butterfly(small, "dp", dp, 1)
        up_weight_grad, hiddens, branch_total, scaled_total, small, weights_sum = fence(
            up_weight_grad, hiddens, own_branch.total(0), own_scaled.total(0), small, weights_sum
        )

        down_weight_grad, qkv_weight_grad, out_weight_grad = weight_product(
            [hidden, *hiddens],
            [grad_out, *all_cots],
            False,
            weights_sum,
            (qkv_weight.shape[1], out_weight.shape[0]),
        )
        small = butterfly(small, "dp", dp, 2)
        layer_output, input_grad = ends(
            layer_input, cotangent, xhat, inv_std, branch_total, scaled_total, biases
        )
        up_bias_grad = (gate_sum + sum_a + sum_b + sum_c)[0]
        down_weight_grad, qkv_bias_grad, small, layer_output, input_grad = fence(
            down_weight_grad, small[five:], small[:five], layer_output, input_grad
        )
    small = small.reshape(5, width)
    return (
        layer_output,
        input_grad,
        small[0],
        small[1],
        small[2],
        small[3],
        qkv_weight_grad,
        qkv_bias_grad.reshape(-1),
        out_weight_grad,
        small[4],
        up_weight_grad,
        up_bias_grad,
        down_weight_grad,
        small[4],
    )


def solution(mesh):
    in_specs = (
        P(("dp", "mp"), None),
        P("dp", None),
        P(),
        P(),
        P(),
        P(),
        P(None, "mp"),
        P("mp"),
        P("mp", None),
        P(),
        P(None, "mp"),
        P("mp"),
        P("mp", None),
        P(),
        P(("dp", "mp"), None),
    )
    out_specs = (
        P(("dp", "mp"), None),
        P(("dp", "mp"), None),
        P(),
        P(),
        P(),
        P(),
        P(None, "mp"),
        P("mp"),
        P("mp", None),
        P(),
        P(None, "mp"),
        P("mp"),
        P("mp", None),
        P(),
    )
    return jax.shard_map(
        per_device, mesh=mesh, in_specs=in_specs, out_specs=out_specs, check_vma=False
    )
```

```python
import functools

import jax
import jax.numpy as jnp
from jax import lax
from jax.experimental import pallas as pl
from jax.experimental.pallas import tpu as pltpu
from jax.sharding import PartitionSpec as P

HEAD_DIM = 128
ROTARY = 32

norm_eps = 1e-05
masked_score = -1e30
inv_root_two = 0.7071067811865476
inv_root_tau = 0.3989422804014327
vmem_bytes = 60 << 20
most_gathered = 128 << 20
bf16 = jnp.bfloat16
f32 = jnp.float32


def dot_plain(left, right):
    return jnp.dot(left, right, preferred_element_type=f32)


def contract_rows(left, right):
    return lax.dot_general(left, right, (((0,), (0,)), ((), ())), preferred_element_type=f32)


def contract_cols(left, right):
    return lax.dot_general(left, right, (((1,), (1,)), ((), ())), preferred_element_type=f32)


def swap(value, axis, count, bit):
    return lax.ppermute(value, axis, [(i, i ^ bit) for i in range(count)])


def turn(value, axis, count, step):
    return lax.ppermute(value, axis, [(i, (i + step) % count) for i in range(count)])


def chip_bits(count):
    return [1 << i for i in range(1, count.bit_length() - 1)]


def after(value, *earlier):
    return lax.optimization_barrier((value, *earlier))[0]


def halves(pair):
    rows = pair.shape[0] // 2
    return pair[:rows], pair[rows:]


class Spread:
    def __init__(self, arrays, a, b, names):
        self.arrays, self.a, self.b, self.names = arrays, a, b, names


four_names = (0, 2, 4, 6, 1, 3, 5, 7)


def spread_sides(pair, count):
    return [swap(pair, "mp", count, 2), swap(pair, "mp", count, 4)]


def spread_corner(sides, count):
    side_x, side_y = sides
    return [swap(halves(side_x)[0], "mp", count, 4), swap(halves(side_y)[1], "mp", count, 2)]


def spread_core(arrays, count):
    return [swap(array, "mp", count, 1) for array in arrays]


def spread_four(near, far):
    rows = near[0].shape[0] // 2
    a, b = {}, {}
    for core in range(2):
        base = len(near) * core
        for i, name in enumerate((0, 2, 4)):
            a[name + core] = (base + i, 0)
            b[name + core] = (base + i, rows)
        a[6 + core] = (base + 3, 0)
        b[6 + core] = (base + 4, 0)
    return Spread(near + far, a, b, four_names)


def spread_any(pair, count):
    rows = pair.shape[0] // 2
    held, names = pair.reshape(1, 2, rows, -1), [0]
    for bit in chip_bits(count) + [1]:
        held = jnp.concatenate([held, swap(held, "mp", count, bit)], axis=0)
        names = names + [n ^ bit for n in names]
    arrays = [held.reshape(2 * rows * count, -1)]
    a = {n: (0, 2 * rows * i) for i, n in enumerate(names)}
    b = {n: (0, 2 * rows * i + rows) for i, n in enumerate(names)}
    return Spread(arrays, a, b, tuple(names))


class Scatter:
    def __init__(self, near, came, names, count, rows, rising):
        self.count, self.rows = count, rows
        names = names[: len(names) // 2]
        self.blocks = {n: near[i * rows : (i + 1) * rows] for i, n in enumerate(names)}
        self.adds = {n: came[i * rows : (i + 1) * rows] for i, n in enumerate(names)}
        bits = chip_bits(count)
        self.bits = bits if rising else bits[::-1]

    def total(self, n):
        return self.blocks[n].astype(f32) + self.adds[n].astype(f32)

    def folded(self, near, came):
        bit, order = self.bits[0], list(self.blocks)
        going = [i for i, n in enumerate(order) if n & bit]
        kept = [i for i, n in enumerate(order) if not n & bit]
        going, kept = fold(near, came, self.rows, going, kept)
        return going, [kept[i * self.rows : (i + 1) * self.rows] for i in range(len(order) // 2)]

    def sent(self):
        bit = self.bits[0]
        stay = [n for n in self.blocks if not n & bit]
        going = jnp.concatenate([self.total(n | bit).astype(bf16) for n in stay], axis=0)
        return going, [self.total(n).astype(bf16) for n in stay]

    def step(self, going, kept):
        bit, self.bits = self.bits[0], self.bits[1:]
        came = swap(going, "mp", self.count, bit)
        stay = [n for n in self.blocks if not n & bit]
        self.blocks = dict(zip(stay, kept))
        self.adds = {n: came[i * self.rows : (i + 1) * self.rows] for i, n in enumerate(stay)}


def scatter_group(near, far, names, count, rows, rising):
    scatter = Scatter(near, swap(far, "mp", count, 1), names, count, rows, rising)
    while scatter.bits:
        scatter.step(*scatter.sent())
    return scatter.total(0)


def call(body, name, **kwargs):
    return pl.pallas_call(
        body,
        name=name,
        compiler_params=pltpu.CompilerParams(vmem_limit_bytes=vmem_bytes),
        cost_estimate=pl.CostEstimate(flops=1, bytes_accessed=1, transcendentals=0),
        **kwargs,
    )


def block_copies(spread, which, refs, buffer, sems, rows, block, blocks):
    per = block // rows
    listed = []
    for at in blocks:
        listed.append([])
        for i in range(at * per, (at + 1) * per):
            array, first = getattr(spread, which)[spread.names[i]]
            listed[-1].append(
                pltpu.make_async_copy(
                    refs[array].at[first : first + rows, :],
                    buffer.at[i * rows : (i + 1) * rows, :],
                    sems.at[i],
                )
            )
    return listed


def out_copies(buffer, ref, sems, block, blocks):
    return [
        pltpu.make_async_copy(
            buffer.at[i * block : (i + 1) * block, :],
            ref.at[i * block : (i + 1) * block, :],
            sems.at[i],
        )
        for i in blocks
    ]


def entry_body(*refs, spread, rows, block, blocks, earlier):
    count = len(spread.arrays)
    arrays = refs[:count]
    (gain1, bias1, gain2, bias2, qkv_ref, out_weight_ref) = refs[count : count + 6]
    count += 6 + earlier
    (one_ref, two_ref, hat_ref, raw_ref, grad_ref, cot_ref) = refs[count : count + 6]
    x_buf, c_buf, sem_x, sem_c, sem_out = refs[count + 6 :]
    step = pl.program_id(0)
    x_copies = block_copies(spread, "a", arrays, x_buf, sem_x, rows, block, blocks)
    c_copies = block_copies(spread, "b", arrays, c_buf, sem_c, rows, block, blocks)
    outs = out_copies(c_buf, cot_ref, sem_out, block, blocks)

    @pl.when(step == 0)
    def _():
        for x_list, c_list in zip(x_copies, c_copies):
            for copy in x_list + c_list:
                copy.start()

    for i in range(len(outs)):

        @pl.when(step == i)
        def _(i=i):
            for copy in x_copies[i] + c_copies[i]:
                copy.wait()
            outs[i].start()

    here = pl.ds(pl.multiple_of((step * blocks.step + blocks.start) * block, block), block)
    values = x_buf[here, :].astype(f32)
    centred = values - jnp.mean(values, axis=1, keepdims=True)
    hat = centred * lax.rsqrt(jnp.mean(centred * centred, axis=1, keepdims=True) + norm_eps)
    hat_ref[...] = hat.astype(bf16)
    one_ref[...] = (hat * gain1[...] + bias1[...]).astype(bf16)
    two_ref[...] = (hat * gain2[...] + bias2[...]).astype(bf16)
    raw_ref[...] = dot_plain(one_ref[...], qkv_ref[...])
    grad_ref[...] = contract_cols(c_buf[here, :], out_weight_ref[...]).astype(bf16)

    @pl.when(step == len(outs) - 1)
    def _():
        for copy in outs:
            copy.wait()


def entry(spread, rows, gains, qkv_weight, out_weight, begin=0, stride=1, earlier=()):
    group_rows = rows * len(spread.names)
    width, deep = qkv_weight.shape
    units = out_weight.shape[0]
    block = min(256, group_rows)
    steps = group_rows // block
    per_group = len(spread.names)
    blocks = range(begin, steps, stride)
    once = pl.Buffered(1)

    def out_block(columns):
        return pl.BlockSpec((block, columns), lambda i: (i * stride + begin, 0))

    row = pl.BlockSpec((1, width), lambda i: (0, 0))
    anywhere = pl.BlockSpec(memory_space=pl.ANY)
    wide = jax.ShapeDtypeStruct((group_rows, width), bf16)
    first = len(spread.arrays) + 6
    return call(
        functools.partial(
            entry_body, spread=spread, rows=rows, block=block, blocks=blocks, earlier=len(earlier)
        ),
        "entry",
        grid=(len(blocks),),
        in_specs=[anywhere] * len(spread.arrays)
        + [row] * 4
        + [
            pl.BlockSpec(qkv_weight.shape, lambda i: (0, 0), pipeline_mode=once),
            pl.BlockSpec(out_weight.shape, lambda i: (0, 0), pipeline_mode=once),
        ]
        + [anywhere] * len(earlier),
        out_specs=[
            out_block(width),
            out_block(width),
            out_block(width),
            out_block(deep),
            out_block(units),
            anywhere,
        ],
        out_shape=[
            wide,
            wide,
            wide,
            jax.ShapeDtypeStruct((group_rows, deep), f32),
            jax.ShapeDtypeStruct((group_rows, units), bf16),
            wide,
        ],
        input_output_aliases={first + i: i for i in range(len(earlier))},
        scratch_shapes=[
            pltpu.VMEM((group_rows, width), bf16),
            pltpu.VMEM((group_rows, width), bf16),
            pltpu.SemaphoreType.DMA((per_group,)),
            pltpu.SemaphoreType.DMA((per_group,)),
            pltpu.SemaphoreType.DMA((steps,)),
        ],
    )(*spread.arrays, *gains, qkv_weight, out_weight, *earlier)


def pairs_body(input_ref, cot_ref, gain_ref, bias_ref, pair_ref, shared_ref):
    rows = input_ref.shape[0]
    values = input_ref[...].astype(f32)
    centred = values - jnp.mean(values, axis=1, keepdims=True)
    hat = centred * lax.rsqrt(jnp.mean(centred * centred, axis=1, keepdims=True) + norm_eps)
    pair_ref[:rows, :] = input_ref[...]
    pair_ref[rows:, :] = cot_ref[...]
    shared_ref[:rows, :] = (hat * gain_ref[...] + bias_ref[...]).astype(bf16)
    shared_ref[rows:, :] = cot_ref[...]


def pairs(layer_input, cotangent, gain, bias):
    rows, width = layer_input.shape
    return call(
        pairs_body,
        "pairs",
        out_shape=[jax.ShapeDtypeStruct((2 * rows, width), bf16)] * 2,
    )(layer_input, cotangent, gain, bias)


def fold_body(near_ref, came_ref, going_ref, kept_ref, *, rows, going, kept):
    for ref, places in ((going_ref, going), (kept_ref, kept)):
        for i, at in enumerate(places):
            here = slice(at * rows, (at + 1) * rows)
            total = near_ref[here, :].astype(f32) + came_ref[here, :].astype(f32)
            ref[i * rows : (i + 1) * rows, :] = total.astype(bf16)


def fold(near, came, rows, going, kept):
    width = near.shape[1]
    tile = min(512, width)
    half = len(going) * rows
    return call(
        functools.partial(fold_body, rows=rows, going=going, kept=kept),
        "fold",
        grid=(width // tile,),
        in_specs=[pl.BlockSpec((near.shape[0], tile), lambda i: (0, i))] * 2,
        out_specs=[pl.BlockSpec((half, tile), lambda i: (0, i))] * 2,
        out_shape=[jax.ShapeDtypeStruct((half, width), bf16)] * 2,
    )(near, came)


def mlp_body(*refs, spread, rows, block, tile, keep):
    count = len(spread.arrays)
    arrays = refs[:count]
    up_ref, shift_ref, down_ref, hidden_ref, grad_ref, sum_ref = refs[count : count + 6]
    rest = refs[count + 6 :]
    if keep:
        rows_ref, cot_ref = rest[:2]
        rest = rest[2:]
    x_buf, c_buf, u_buf, d_buf, sem_x, sem_c, sem_u, sem_d, sem_ox, sem_oc = rest
    step = pl.program_id(0)
    units = u_buf.shape[1]
    every = range(x_buf.shape[0] // block)
    x_copies = block_copies(spread, "a", arrays, x_buf, sem_x, rows, block, every)
    c_copies = block_copies(spread, "b", arrays, c_buf, sem_c, rows, block, every)
    tiles = [slice(i, i + tile) for i in range(0, units, tile)]
    u_copies = [
        pltpu.make_async_copy(up_ref.at[:, t], u_buf.at[:, t], sem_u.at[i])
        for i, t in enumerate(tiles)
    ]
    d_copies = [
        pltpu.make_async_copy(down_ref.at[t, :], d_buf.at[t, :], sem_d.at[i])
        for i, t in enumerate(tiles)
    ]
    outs = [(), ()]
    if keep:
        outs = [
            out_copies(x_buf, rows_ref, sem_ox, block, every),
            out_copies(c_buf, cot_ref, sem_oc, block, every),
        ]

    def start(copies):
        for copy in copies:
            copy.start()

    def wait(copies):
        for copy in copies:
            copy.wait()

    needs = [[u] for u in u_copies], [[d] for d in d_copies]
    needs = [need for two in zip(*needs) for need in two]
    needs[0] = x_copies[0] + needs[0]
    needs[1] = c_copies[0] + needs[1]

    @pl.when(step == 0)
    def _():
        start(needs[0])
        sum_ref[...] = jnp.zeros_like(sum_ref)
        wait(needs[0])
        start(needs[1])
        for need in needs[2:3]:
            start(need)
        start(outs[0][:1])

    for i in every[1:]:

        @pl.when(step == i)
        def _(i=i):
            wait(x_copies[i] + c_copies[i])
            start(outs[0][i : i + 1] + outs[1][i : i + 1] if keep else [])

    here = pl.ds(pl.multiple_of(step * block, block), block)
    for i, part in enumerate(tiles):
        gate = dot_plain(x_buf[here, :], u_buf[:, part]) + shift_ref[:, part]

        @pl.when(step == 0)
        def _(i=i):
            wait(needs[2 * i + 1])
            for need in needs[2 * i + 2 : 2 * i + 3]:
                wait(need)
            for need in needs[2 * i + 3 : 2 * i + 5]:
                start(need)
            if i == 0:
                start(outs[1][:1])
                for later in every[1:]:
                    start(x_copies[later] + c_copies[later])

        grad_hidden = contract_cols(c_buf[here, :], d_buf[part, :])
        below = 0.5 * (1.0 + lax.erf(gate * inv_root_two))
        hidden_ref[:, part] = (gate * below).astype(bf16)
        slope = below + gate * jnp.exp(-0.5 * gate * gate) * inv_root_tau
        grad = (grad_hidden * slope).astype(bf16)
        grad_ref[:, part] = grad
        sum_ref[:, part] += jnp.sum(grad.astype(f32), axis=0, keepdims=True)

    if keep:

        @pl.when(step == len(x_copies) - 1)
        def _():
            wait(outs[0] + outs[1])


def mlp(spread, rows, up_weight, up_bias, down_weight, keep):
    width, units = up_weight.shape
    group_rows = rows * len(spread.names)
    block = min(512, group_rows)
    tile = min(512, units)
    steps, tiles, blocks = group_rows // block, units // tile, len(spread.names)
    anywhere = pl.BlockSpec(memory_space=pl.ANY)
    part = pl.BlockSpec((block, units), lambda i: (i, 0))
    low = jax.ShapeDtypeStruct((group_rows, units), bf16)
    wide = jax.ShapeDtypeStruct((group_rows, width), bf16)
    dma = pltpu.SemaphoreType.DMA
    return call(
        functools.partial(mlp_body, spread=spread, rows=rows, block=block, tile=tile, keep=keep),
        "mlp",
        grid=(steps,),
        in_specs=[anywhere] * len(spread.arrays)
        + [anywhere, pl.BlockSpec((1, units), lambda i: (0, 0)), anywhere],
        out_specs=[part, part, pl.BlockSpec((1, units), lambda i: (0, 0))]
        + [anywhere] * (2 * keep),
        out_shape=[low, low, jax.ShapeDtypeStruct((1, units), f32)] + [wide] * (2 * keep),
        scratch_shapes=[
            pltpu.VMEM((group_rows, width), bf16),
            pltpu.VMEM((group_rows, width), bf16),
            pltpu.VMEM((width, units), bf16),
            pltpu.VMEM((units, width), bf16),
            dma((blocks,)),
            dma((blocks,)),
            dma((tiles,)),
            dma((tiles,)),
            dma((steps,)),
            dma((steps,)),
        ],
    )(*spread.arrays, up_weight, up_bias, down_weight)


def widen_body(sum_ref, qkv_ref, out_ref):
    units, deep = out_ref.shape[0], qkv_ref.shape[1]
    qkv_ref[...] = sum_ref[:, :deep].astype(f32)
    for first in range(0, sum_ref.shape[0], units):
        out_ref[:, first : first + units] = sum_ref[first : first + units, deep:].astype(f32)


def weight_body(*refs, pieces, tile_left, widened):
    inputs, refs = refs[: 2 * pieces], refs[2 * pieces :]
    if widened:
        widen_body(refs[0], *refs[2:4])
        refs = refs[1:2] + refs[4:]
    out_ref, *buffers, sems = refs
    whole = inputs[pieces:] if tile_left else inputs[:pieces]
    copies = [
        pltpu.make_async_copy(ref, buffer, sems.at[i])
        for i, (ref, buffer) in enumerate(zip(whole, buffers))
    ]
    step = pl.program_id(0)

    for piece in range(pieces):

        @pl.when(step == 0)
        def _(piece=piece):
            if piece == 0:
                for copy in copies[:2]:
                    copy.start()
            copies[piece].wait()
            for copy in copies[piece + 2 : piece + 3]:
                copy.start()

        left, right = inputs[piece], inputs[pieces + piece]
        if tile_left:
            right = buffers[piece]
        else:
            left = buffers[piece]
        product = contract_rows(left[...], right[...])
        if piece == 0:
            out_ref[...] = product
        else:
            out_ref[...] += product


def weight_product(lefts, rights, tile_left, total=None, deep_units=()):
    wide, deep = lefts[0].shape[1], rights[0].shape[1]
    tile = min(512, wide if tile_left else deep)
    steps = (wide if tile_left else deep) // tile

    def spec(piece, tiled):
        if tiled:
            return pl.BlockSpec((piece.shape[0], tile), lambda i: (0, i))
        return pl.BlockSpec(memory_space=pl.ANY)

    whole = rights if tile_left else lefts
    extra = ([], [], [])
    if total is not None:
        extra = widen_specs(total, *deep_units, total.shape[0] // steps)
    out_spec = (
        pl.BlockSpec((tile, deep), lambda i: (i, 0))
        if tile_left
        else pl.BlockSpec((wide, tile), lambda i: (0, i))
    )
    return call(
        functools.partial(
            weight_body, pieces=len(lefts), tile_left=tile_left, widened=total is not None
        ),
        "weight_product",
        grid=(steps,),
        in_specs=[spec(p, tile_left) for p in lefts]
        + [spec(p, not tile_left) for p in rights]
        + extra[0],
        out_specs=[out_spec] + extra[1],
        out_shape=[jax.ShapeDtypeStruct((wide, deep), f32)] + extra[2],
        scratch_shapes=[pltpu.VMEM(piece.shape, piece.dtype) for piece in whole]
        + [pltpu.SemaphoreType.DMA((len(whole),))],
    )(*lefts, *rights, *([] if total is None else [total]))


def attention_weights_body(normed_ref, grad_qkv_ref, attended_ref, grad_out_ref, sum_ref):
    deep = grad_qkv_ref.shape[1]
    sum_ref[:, :deep] = contract_rows(normed_ref[...], grad_qkv_ref[...]).astype(bf16)
    sum_ref[:, deep:] = contract_rows(attended_ref[...], grad_out_ref[...]).astype(bf16)


def attention_weights(normed, grad_qkv, attended, grad_out):
    group_rows, width = normed.shape
    deep, units = grad_qkv.shape[1], attended.shape[1]
    once = pl.Buffered(1)
    block = pl.BlockSpec((group_rows, units), lambda i: (0, i))
    return call(
        attention_weights_body,
        "attention_weights",
        grid=(width // units,),
        in_specs=[
            block,
            pl.BlockSpec(grad_qkv.shape, lambda i: (0, 0), pipeline_mode=once),
            pl.BlockSpec(attended.shape, lambda i: (0, 0), pipeline_mode=once),
            block,
        ],
        out_specs=pl.BlockSpec((units, deep + units), lambda i: (i, 0)),
        out_shape=jax.ShapeDtypeStruct((width, deep + units), bf16),
    )(normed, grad_qkv, attended, grad_out)


def widen_specs(total, deep, units, block):
    width = total.shape[0]
    return (
        [pl.BlockSpec((block, deep + units), lambda i: (i, 0))],
        [
            pl.BlockSpec((block, deep), lambda i: (i, 0)),
            pl.BlockSpec((units, block), lambda i: (0, i)),
        ],
        [
            jax.ShapeDtypeStruct((width, deep), f32),
            jax.ShapeDtypeStruct((units, width), f32),
        ],
    )


def widen(total, deep, units):
    in_specs, out_specs, out_shape = widen_specs(total, deep, units, units)
    return call(
        widen_body,
        "widen",
        grid=(total.shape[0] // units,),
        in_specs=in_specs,
        out_specs=out_specs,
        out_shape=out_shape,
    )(total)


def branch_body(attended_ref, hidden_ref, out_ref, down_ref, near_ref, far_ref):
    middle = near_ref.shape[0]
    total = dot_plain(attended_ref[...], out_ref[...]) + dot_plain(hidden_ref[...], down_ref[...])
    near_ref[...] = total[:middle].astype(bf16)
    far_ref[...] = total[middle:].astype(bf16)


def branch_sum(attended, hidden, out_weight, down_weight):
    group_rows = attended.shape[0]
    width = out_weight.shape[1]
    tile = min(512, width)
    once = pl.Buffered(1)
    half = pl.BlockSpec((group_rows // 2, tile), lambda i: (0, i))
    return call(
        branch_body,
        "branch_sum",
        grid=(width // tile,),
        in_specs=[
            pl.BlockSpec(attended.shape, lambda i: (0, 0), pipeline_mode=once),
            pl.BlockSpec(hidden.shape, lambda i: (0, 0), pipeline_mode=once),
            pl.BlockSpec((out_weight.shape[0], tile), lambda i: (0, i)),
            pl.BlockSpec((down_weight.shape[0], tile), lambda i: (0, i)),
        ],
        out_specs=[half, half],
        out_shape=[jax.ShapeDtypeStruct((group_rows // 2, width), bf16)] * 2,
    )(attended, hidden, out_weight, down_weight)


def input_body(
    qkv_grad_ref, gate_grad_ref, qkv_ref, up_ref, gain1, gain2, hat_ref, near_ref, far_ref, sum_ref
):
    middle = near_ref.shape[0]
    hat = hat_ref[...].astype(f32)
    first = contract_cols(qkv_grad_ref[...], qkv_ref[...])
    second = contract_cols(gate_grad_ref[...], up_ref[...])
    both = first * gain1[...] + second * gain2[...]
    near_ref[...] = both[:middle].astype(bf16)
    far_ref[...] = both[middle:].astype(bf16)
    sum_ref[0:1, :] = jnp.sum(first * hat, axis=0, keepdims=True)
    sum_ref[1:2, :] = jnp.sum(first, axis=0, keepdims=True)
    sum_ref[2:3, :] = jnp.sum(second * hat, axis=0, keepdims=True)
    sum_ref[3:4, :] = jnp.sum(second, axis=0, keepdims=True)


def input_sums(grad_qkv, grad_gate, qkv_weight, up_weight, gain1, gain2, hat):
    group_rows = grad_qkv.shape[0]
    width = qkv_weight.shape[0]
    tile = min(256, width)
    once = pl.Buffered(1)
    half = pl.BlockSpec((group_rows // 2, tile), lambda i: (0, i))
    row = pl.BlockSpec((1, tile), lambda i: (0, i))
    return call(
        input_body,
        "input_sums",
        grid=(width // tile,),
        in_specs=[
            pl.BlockSpec(grad_qkv.shape, lambda i: (0, 0), pipeline_mode=once),
            pl.BlockSpec(grad_gate.shape, lambda i: (0, 0), pipeline_mode=once),
            pl.BlockSpec((tile, qkv_weight.shape[1]), lambda i: (i, 0)),
            pl.BlockSpec((tile, up_weight.shape[1]), lambda i: (i, 0)),
            row,
            row,
            pl.BlockSpec((group_rows, tile), lambda i: (0, i)),
        ],
        out_specs=[half, half, pl.BlockSpec((4, tile), lambda i: (0, i))],
        out_shape=[jax.ShapeDtypeStruct((group_rows // 2, width), bf16)] * 2
        + [jax.ShapeDtypeStruct((4, width), f32)],
    )(grad_qkv, grad_gate, qkv_weight, up_weight, gain1, gain2, hat)


def attention_body(
    own_ref,
    starts_ref,
    raw_ref,
    bias_ref,
    cos_ref,
    sine_ref,
    slope_in_ref,
    attended_ref,
    grad_qkv_ref,
    bias_grad_ref,
    query_ref,
    key_ref,
    value_ref,
    slope_ref,
    query_sum_ref,
    key_sum_ref,
    value_sum_ref,
    *,
    rows,
    names,
    block_rows,
    longest,
):
    own = own_ref[0]
    group_rows = rows * len(names)
    lane = lax.broadcasted_iota(jnp.int32, (rows, HEAD_DIM), 1)
    half = ROTARY // 2
    scale = HEAD_DIM ** (-0.5)

    def turned(u):
        return jnp.where(lane < half, pltpu.roll(u, HEAD_DIM - half, 1), pltpu.roll(u, half, 1))

    def far_rows(name):
        return pl.ds(pl.multiple_of((own ^ name) * rows, rows), rows)

    for i, name in enumerate(names):
        near = slice(i * rows, (i + 1) * rows)
        far = far_rows(name)
        raw = raw_ref[near, :] + bias_ref[...]
        cos_table = cos_ref[near, :]
        sine_table = sine_ref[near, :]
        query = raw[:, :HEAD_DIM]
        key = raw[:, HEAD_DIM : 2 * HEAD_DIM]
        query_ref[far, :] = (query * cos_table + turned(query) * sine_table).astype(bf16)
        key_ref[far, :] = (key * cos_table + turned(key) * sine_table).astype(bf16)
        value_ref[far, :] = raw[:, 2 * HEAD_DIM :].astype(bf16)
        slope_ref[far, :] = slope_in_ref[near, :]
    key_sum_ref[...] = jnp.zeros_like(key_sum_ref)
    value_sum_ref[...] = jnp.zeros_like(value_sum_ref)
    for first in range(0, group_rows, block_rows):
        last = first + block_rows
        low = max(0, (first - longest + 1) // 128 * 128)
        query = query_ref[first:last, :]
        keys = key_ref[low:last, :]
        values = value_ref[low:last, :]
        slope = slope_ref[first:last, :]
        scores = contract_cols(query, keys) * scale
        row = first + lax.broadcasted_iota(jnp.int32, (block_rows, 1), 0)
        begin = jnp.zeros((block_rows, 1), jnp.int32)
        for slot in range(starts_ref.shape[0]):
            begin = jnp.where(starts_ref[slot] <= row, starts_ref[slot], begin)
        column = low + lax.broadcasted_iota(jnp.int32, scores.shape, 1)
        scores = jnp.where((column >= begin) & (column <= row), scores, masked_score)
        peak = jnp.max(scores, axis=1, keepdims=True)
        raised = jnp.exp(scores - peak)
        probs = raised * (1.0 / jnp.sum(raised, axis=1, keepdims=True))
        probs_low = probs.astype(bf16)
        query_ref[first:last, :] = dot_plain(probs_low, values).astype(bf16)
        grad_probs = contract_cols(slope, values)
        delta = jnp.sum(grad_probs * probs, axis=1, keepdims=True)
        grad_score = (probs * (grad_probs - delta)).astype(bf16)
        query_sum_ref[first:last, :] = dot_plain(grad_score, keys) * scale
        key_sum_ref[low:last, :] += contract_rows(grad_score, query) * scale
        value_sum_ref[low:last, :] += contract_rows(probs_low, slope)
    bias_grad = jnp.zeros(bias_grad_ref.shape, f32)
    for i, name in enumerate(names):
        near = slice(i * rows, (i + 1) * rows)
        far = far_rows(name)
        cos_table = cos_ref[near, :]
        sine_table = sine_ref[near, :]
        query_grad = query_sum_ref[far, :]
        key_grad = key_sum_ref[far, :]
        grads = jnp.concatenate(
            [
                query_grad * cos_table - turned(query_grad) * sine_table,
                key_grad * cos_table - turned(key_grad) * sine_table,
                value_sum_ref[far, :],
            ],
            axis=1,
        ).astype(bf16)
        grad_qkv_ref[near, :] = grads
        bias_grad = bias_grad + jnp.sum(grads.astype(f32), axis=0, keepdims=True)
        attended_ref[near, :] = query_ref[far, :]
    bias_grad_ref[...] = bias_grad


def attention(own, starts, raw, bias, cos_table, sine_table, slope, rows, names):
    group_rows, width = raw.shape
    part = 3 * HEAD_DIM
    heads = width // part
    whole = pl.BlockSpec((group_rows, HEAD_DIM), lambda h: (0, 0))
    scalars = pl.BlockSpec(memory_space=pltpu.SMEM)
    low = pltpu.VMEM((group_rows, HEAD_DIM), bf16)
    wide = pltpu.VMEM((group_rows, HEAD_DIM), f32)
    longest = group_rows // 2
    return pl.pallas_call(
        functools.partial(
            attention_body,
            rows=rows,
            names=names,
            block_rows=min(256, group_rows),
            longest=longest,
        ),
        grid=(heads,),
        in_specs=[
            scalars,
            scalars,
            pl.BlockSpec((group_rows, part), lambda h: (0, h)),
            pl.BlockSpec((1, part), lambda h: (0, h)),
            whole,
            whole,
            pl.BlockSpec((group_rows, HEAD_DIM), lambda h: (0, h)),
        ],
        out_specs=[
            pl.BlockSpec((group_rows, HEAD_DIM), lambda h: (0, h)),
            pl.BlockSpec((group_rows, part), lambda h: (0, h)),
            pl.BlockSpec((1, part), lambda h: (0, h)),
        ],
        out_shape=[
            jax.ShapeDtypeStruct((group_rows, heads * HEAD_DIM), bf16),
            jax.ShapeDtypeStruct((group_rows, width), bf16),
            jax.ShapeDtypeStruct((1, width), f32),
        ],
        scratch_shapes=[low, low, low, low, wide, wide, wide],
        compiler_params=pltpu.CompilerParams(vmem_limit_bytes=vmem_bytes),
        cost_estimate=pl.CostEstimate(flops=1, bytes_accessed=1, transcendentals=0),
        name="attention",
    )(own, starts, raw, bias, cos_table, sine_table, slope)


def rotary_tables(position):
    half_rot = ROTARY // 2
    frequency = 10000.0 ** (-2.0 * jnp.arange(half_rot, dtype=f32) / ROTARY)
    angles = position.astype(f32)[:, None] * frequency[None, :]
    cos_half = jnp.cos(angles)
    sine_half = jnp.sin(angles)
    rest = (position.shape[0], HEAD_DIM - ROTARY)
    return (
        jnp.concatenate([cos_half, cos_half, jnp.ones(rest, f32)], axis=1),
        jnp.concatenate([-sine_half, sine_half, jnp.zeros(rest, f32)], axis=1),
    )


def butterfly(value, axis, count, bit):
    return value + swap(value, axis, count, bit)


def fence(*values):
    return lax.optimization_barrier(values)


def norm_own(layer_input):
    values = layer_input.astype(f32)
    centred = values - jnp.mean(values, axis=-1, keepdims=True)
    inv_std = lax.rsqrt(jnp.mean(centred * centred, axis=-1, keepdims=True) + norm_eps)
    return centred * inv_std, inv_std


def tables(own, lengths, names, rows):
    seq_ends = jnp.cumsum(lengths)
    seq_starts = seq_ends - lengths
    places = (
        (own ^ jnp.array(names, jnp.int32))[:, None] * rows
        + jnp.arange(rows, dtype=jnp.int32)[None, :]
    ).reshape(-1)
    seq_first = jnp.max(
        jnp.where(seq_starts[None, :] <= places[:, None], seq_starts[None, :], 0), axis=1
    )
    return (seq_starts, *rotary_tables(places - seq_first))


def contiguous(first, second, names, rows):
    places = [{n: (which, i * rows) for i, n in enumerate(names)} for which in range(2)]
    return Spread([first, second], *places, names)


def ends(layer_input, cotangent, xhat, inv_std, branch, scaled, biases):
    layer_output = (layer_input.astype(f32) + branch + biases).astype(bf16)
    input_grad = cotangent.astype(f32) + inv_std * (
        scaled
        - jnp.mean(scaled, axis=-1, keepdims=True)
        - xhat * jnp.mean(scaled * xhat, axis=-1, keepdims=True)
    )
    return layer_output, input_grad


def per_device(
    layer_input,
    lengths,
    norm1_gain,
    norm1_bias,
    norm2_gain,
    norm2_bias,
    qkv_weight,
    qkv_bias,
    out_weight,
    out_bias,
    up_weight,
    up_bias,
    down_weight,
    down_bias,
    cotangent,
):
    dp = lax.axis_size("dp")
    mp = lax.axis_size("mp")
    own = lax.axis_index("mp")
    rows, width = layer_input.shape
    up_row = up_bias[None, :]
    gains = (norm1_gain[None, :], norm1_bias[None, :], norm2_gain[None, :], norm2_bias[None, :])
    gather_all = mp == 8 and dp == 4 and 4 * rows * mp * dp * (width + up_bias.shape[0]) < most_gathered

    pair, shared = pairs(layer_input, cotangent, *gains[2:])
    if gather_all:
        names = four_names
        sides = spread_sides(pair, mp)
        group_a = turn(shared, "dp", dp, 1)
        placed = tables(own, lengths[0], names, rows)
        far = spread_core([pair], mp)
        shared, pair, sides, placed, far, group_a = fence(shared, pair, sides, placed, far, group_a)
        group_b = turn(shared, "dp", dp, -1)
        corner = spread_corner(sides, mp)
        near = [pair, *sides]
        far = far + spread_core(sides, mp)
        begun = entry(spread_four(near, far), rows, gains, qkv_weight, out_weight, 0, 2)
        near, far, corner, group_a, begun = fence(near, far, corner, group_a, begun)
        near, far = near + corner, far + spread_core(corner, mp)
        sides_a = spread_sides(group_a, mp)
        entered = entry(spread_four(near, far), rows, gains, qkv_weight, out_weight, 1, 2, begun)
        entered, group_b, group_a = fence(entered, group_b, group_a)
        far_a = spread_core([group_a], mp)
        group_c = turn(group_a, "dp", dp, 1)
    else:
        spread = spread_any(pair, mp)
        names = spread.names
        placed = tables(own, lengths[0], names, rows)
        entered = entry(spread, rows, gains, qkv_weight, out_weight)
    seq_starts, cos_table, sine_table = placed

    first_all, second_all, hat, raw, grad_attended, grad_out = entered
    attended, grad_qkv, qkv_bias_part = attention(
        own.reshape(1),
        seq_starts,
        raw,
        qkv_bias[None, :],
        cos_table,
        sine_table,
        grad_attended,
        rows,
        names,
    )
    if gather_all:
        (first_all, second_all, hat, grad_out, attended, grad_qkv), near_a, far_a, group_b = fence(
            (first_all, second_all, hat, grad_out, attended, grad_qkv),
            [group_a, *sides_a],
            far_a,
            group_b,
        )

    weights_part = attention_weights(first_all, grad_qkv, attended, grad_out)
    if gather_all:
        corner_a = spread_corner(near_a[1:], mp)
        far_a = far_a + spread_core(near_a[1:], mp)
        (weights_part, second_all, hat, grad_out, attended), near_a, corner_a, far_a, group_b, group_c = (
            fence(
                (weights_part, second_all, hat, grad_out, attended),
                near_a,
                corner_a,
                far_a,
                group_b,
                group_c,
            )
        )
    weights_sum = lax.psum_scatter(weights_part, "dp", scatter_dimension=0, tiled=True)

    own_spread = contiguous(second_all, grad_out, names, rows)
    hidden, grad_gate, gate_sum = mlp(own_spread, rows, up_weight, up_row, down_weight, False)
    branch = branch_sum(attended, hidden, out_weight, down_weight)
    if gather_all:
        sides_b = spread_sides(group_b, mp)
        far_b = spread_core([group_b], mp)
        far_a = far_a + spread_core(corner_a, mp)
        near_a = near_a + corner_a
        (hidden, grad_gate, branch, grad_qkv, hat), near_a, far_a, near_b, far_b, group_c = fence(
            (hidden, grad_gate, branch, grad_qkv, hat),
            near_a,
            far_a,
            [group_b, *sides_b],
            far_b,
            group_c,
        )

    scaled = input_sums(grad_qkv, grad_gate, qkv_weight, up_weight, gains[0], gains[2], hat)
    cot_sum = jnp.sum(cotangent.astype(f32), axis=0)
    small = jnp.concatenate([scaled[2].reshape(-1), cot_sum, qkv_bias_part.reshape(-1)])
    small = small.reshape(-1, 128)
    five = 5 * width // 128
    biases = out_bias + down_bias
    xhat, inv_std = norm_own(layer_input)

    def over_mp(both, bit):
        return jnp.concatenate([butterfly(both[:five], "mp", mp, bit), both[five:]], axis=0)

    if not gather_all:
        own_branch = scatter_group(*branch, names, mp, rows, True)
        own_scaled = scatter_group(*scaled[:2], names, mp, rows, False)
        layer_output, input_grad = ends(
            layer_input, cotangent, xhat, inv_std, own_branch, own_scaled, biases
        )
        for bit in (1 << i for i in range(dp.bit_length() - 1)):
            small = butterfly(small, "dp", dp, bit)
        small, qkv_bias_grad = small[:five], small[five:]
        for bit in (1 << i for i in range(mp.bit_length() - 1)):
            small = butterfly(small, "mp", mp, bit)
        qkv_weight_grad, out_weight_grad = widen(
            lax.all_gather(weights_sum, "dp", axis=0, tiled=True),
            qkv_weight.shape[1],
            out_weight.shape[0],
        )
        up_weight_grad, down_weight_grad, up_bias_grad = lax.psum(
            (
                weight_product([second_all], [grad_gate], True)[0],
                weight_product([hidden], [grad_out], False)[0],
                gate_sum[0],
            ),
            "dp",
        )
    else:
        corner_b = spread_corner(near_b[1:], mp)
        far_b = far_b + spread_core(near_b[1:], mp)
        branch_came = swap(branch[1], "mp", mp, 1)
        scaled, small, near_a, far_a, near_b, far_b, corner_b, branch_came, group_c = fence(
            scaled, small, near_a, far_a, near_b, far_b, corner_b, branch_came, group_c
        )

        hidden_a, gate_a, sum_a, rows_a, cot_a = mlp(
            spread_four(near_a, far_a), rows, up_weight, up_row, down_weight, True
        )
        sides_c = spread_sides(group_c, mp)
        far_c = spread_core([group_c], mp)
        far_b = far_b + spread_core(corner_b, mp)
        near_b = near_b + corner_b
        scaled_came = swap(scaled[1], "mp", mp, 1)
        small = over_mp(small, 1)
        own_branch = Scatter(branch[0], branch_came, names, mp, rows, True)
        branch_sent = own_branch.folded(branch[0], branch_came)
        done_a, near_b, far_b, near_c, far_c, scaled_came, small, branch_sent, weights_sum = fence(
            (hidden_a, gate_a, rows_a, cot_a),
            near_b,
            far_b,
            [group_c, *sides_c],
            far_c,
            scaled_came,
            small,
            branch_sent,
            weights_sum,
        )
        weights_sum = lax.all_gather(weights_sum, "dp", axis=0, tiled=True)

        hidden_b, gate_b, sum_b, rows_b, cot_b = mlp(
            spread_four(near_b, far_b), rows, up_weight, up_row, down_weight, True
        )
        corner_c = spread_corner(near_c[1:], mp)
        far_c = far_c + spread_core(near_c[1:], mp)
        small = over_mp(small, 2)
        (
            done_b,
            near_c,
            far_c,
            corner_c,
            small,
            branch_sent,
            scaled_near,
            scaled_came,
        ) = fence(
            (hidden_b, gate_b, rows_b, cot_b),
            near_c,
            far_c,
            corner_c,
            small,
            branch_sent,
            scaled[0],
            scaled_came,
        )

        far_c = far_c + spread_core(corner_c, mp)
        near_c = near_c + corner_c
        own_scaled = Scatter(scaled_near, scaled_came, names, mp, rows, False)
        near_c, far_c, scaled_sent, branch_sent, small = fence(
            near_c, far_c, own_scaled.folded(scaled_near, scaled_came), branch_sent, small
        )

        hidden_c, gate_c, sum_c, rows_c, cot_c = mlp(
            spread_four(near_c, far_c), rows, up_weight, up_row, down_weight, True
        )
        own_branch.step(*branch_sent)
        own_scaled.step(*scaled_sent)
        small = over_mp(small, 4)
        done_c, branch_sent, scaled_sent, small = fence(
            (hidden_c, gate_c, rows_c, cot_c), own_branch.sent(), own_scaled.sent(), small
        )

        hiddens, gates, all_rows, all_cots = zip(done_a, done_b, done_c)
        (up_weight_grad,) = weight_product([second_all, *all_rows], [grad_gate, *gates], True)
        own_branch.step(*branch_sent)
        own_scaled.step(*scaled_sent)
        small = butterfly(small, "dp", dp, 1)
        up_weight_grad, hiddens, branch_total, scaled_total, small, weights_sum = fence(
            up_weight_grad, hiddens, own_branch.total(0), own_scaled.total(0), small, weights_sum
        )

        down_weight_grad, qkv_weight_grad, out_weight_grad = weight_product(
            [hidden, *hiddens],
            [grad_out, *all_cots],
            False,
            weights_sum,
            (qkv_weight.shape[1], out_weight.shape[0]),
        )
        small = butterfly(small, "dp", dp, 2)
        layer_output, input_grad = ends(
            layer_input, cotangent, xhat, inv_std, branch_total, scaled_total, biases
        )
        up_bias_grad = (gate_sum + sum_a + sum_b + sum_c)[0]
        down_weight_grad, qkv_bias_grad, small, layer_output, input_grad = fence(
            down_weight_grad, small[five:], small[:five], layer_output, input_grad
        )
    small = small.reshape(5, width)
    return (
        layer_output,
        input_grad,
        small[0],
        small[1],
        small[2],
        small[3],
        qkv_weight_grad,
        qkv_bias_grad.reshape(-1),
        out_weight_grad,
        small[4],
        up_weight_grad,
        up_bias_grad,
        down_weight_grad,
        small[4],
    )


def solution(mesh):
    in_specs = (
        P(("dp", "mp"), None),
        P("dp", None),
        P(),
        P(),
        P(),
        P(),
        P(None, "mp"),
        P("mp"),
        P("mp", None),
        P(),
        P(None, "mp"),
        P("mp"),
        P("mp", None),
        P(),
        P(("dp", "mp"), None),
    )
    out_specs = (
        P(("dp", "mp"), None),
        P(("dp", "mp"), None),
        P(),
        P(),
        P(),
        P(),
        P(None, "mp"),
        P("mp"),
        P("mp", None),
        P(),
        P(None, "mp"),
        P("mp"),
        P("mp", None),
        P(),
    )
    return jax.shard_map(
        per_device, mesh=mesh, in_specs=in_specs, out_specs=out_specs, check_vma=False
    )
```

```python
import functools

import jax
import jax.numpy as jnp
from jax import lax
from jax.experimental import pallas as pl
from jax.experimental.pallas import tpu as pltpu
from jax.sharding import PartitionSpec as P

HEAD_DIM = 128
ROTARY = 32

norm_eps = 1e-05
masked_score = -1e30
inv_root_two = 0.7071067811865476
inv_root_tau = 0.3989422804014327
vmem_bytes = 60 << 20
most_gathered = 128 << 20
bf16 = jnp.bfloat16
f32 = jnp.float32


def dot_plain(left, right):
    return jnp.dot(left, right, preferred_element_type=f32)


def contract_rows(left, right):
    return lax.dot_general(left, right, (((0,), (0,)), ((), ())), preferred_element_type=f32)


def contract_cols(left, right):
    return lax.dot_general(left, right, (((1,), (1,)), ((), ())), preferred_element_type=f32)


def swap(value, axis, count, bit):
    return lax.ppermute(value, axis, [(i, i ^ bit) for i in range(count)])


def turn(value, axis, count, step):
    return lax.ppermute(value, axis, [(i, (i + step) % count) for i in range(count)])


def chip_bits(count):
    return [1 << i for i in range(1, count.bit_length() - 1)]


def after(value, *earlier):
    return lax.optimization_barrier((value, *earlier))[0]


def halves(pair):
    rows = pair.shape[0] // 2
    return pair[:rows], pair[rows:]


class Spread:
    def __init__(self, arrays, a, b, names):
        self.arrays, self.a, self.b, self.names = arrays, a, b, names


four_names = (0, 2, 4, 6, 1, 3, 5, 7)


def spread_sides(pair, count):
    return [swap(pair, "mp", count, 2), swap(pair, "mp", count, 4)]


def spread_corner(sides, count):
    side_x, side_y = sides
    return [swap(halves(side_x)[0], "mp", count, 4), swap(halves(side_y)[1], "mp", count, 2)]


def spread_core(arrays, count):
    return [swap(array, "mp", count, 1) for array in arrays]


def spread_four(near, far):
    rows = near[0].shape[0] // 2
    a, b = {}, {}
    for core in range(2):
        base = len(near) * core
        for i, name in enumerate((0, 2, 4)):
            a[name + core] = (base + i, 0)
            b[name + core] = (base + i, rows)
        a[6 + core] = (base + 3, 0)
        b[6 + core] = (base + 4, 0)
    return Spread(near + far, a, b, four_names)


def spread_any(pair, count):
    rows = pair.shape[0] // 2
    held, names = pair.reshape(1, 2, rows, -1), [0]
    for bit in chip_bits(count) + [1]:
        held = jnp.concatenate([held, swap(held, "mp", count, bit)], axis=0)
        names = names + [n ^ bit for n in names]
    arrays = [held.reshape(2 * rows * count, -1)]
    a = {n: (0, 2 * rows * i) for i, n in enumerate(names)}
    b = {n: (0, 2 * rows * i + rows) for i, n in enumerate(names)}
    return Spread(arrays, a, b, tuple(names))


class Scatter:
    def __init__(self, near, came, names, count, rows):
        self.count, self.rows = count, rows
        names = names[: len(names) // 2]
        self.blocks = {n: near[i * rows : (i + 1) * rows] for i, n in enumerate(names)}
        self.adds = {n: came[i * rows : (i + 1) * rows] for i, n in enumerate(names)}
        self.bits = chip_bits(count)

    def total(self, n):
        return self.blocks[n].astype(f32) + self.adds[n].astype(f32)

    def folded(self, near, came):
        bit, order = self.bits[0], list(self.blocks)
        going = [i for i, n in enumerate(order) if n & bit]
        kept = [i for i, n in enumerate(order) if not n & bit]
        going, kept = fold(near, came, self.rows, going, kept)
        return going, [kept[i * self.rows : (i + 1) * self.rows] for i in range(len(order) // 2)]

    def sent(self):
        bit = self.bits[0]
        stay = [n for n in self.blocks if not n & bit]
        going = jnp.concatenate([self.total(n | bit).astype(bf16) for n in stay], axis=0)
        return going, [self.total(n).astype(bf16) for n in stay]

    def step(self, going, kept):
        bit, self.bits = self.bits[0], self.bits[1:]
        came = swap(going, "mp", self.count, bit)
        stay = [n for n in self.blocks if not n & bit]
        self.blocks = dict(zip(stay, kept))
        self.adds = {n: came[i * self.rows : (i + 1) * self.rows] for i, n in enumerate(stay)}


def scatter_group(near, far, names, count, rows):
    scatter = Scatter(near, swap(far, "mp", count, 1), names, count, rows)
    while scatter.bits:
        scatter.step(*scatter.sent())
    return scatter.total(0)


def call(body, name, **kwargs):
    return pl.pallas_call(
        body,
        name=name,
        compiler_params=pltpu.CompilerParams(vmem_limit_bytes=vmem_bytes),
        cost_estimate=pl.CostEstimate(flops=1, bytes_accessed=1, transcendentals=0),
        **kwargs,
    )


def block_copies(spread, which, refs, buffer, sems, rows, block, blocks):
    per = block // rows
    listed = []
    for at in blocks:
        listed.append([])
        for i in range(at * per, (at + 1) * per):
            array, first = getattr(spread, which)[spread.names[i]]
            listed[-1].append(
                pltpu.make_async_copy(
                    refs[array].at[first : first + rows, :],
                    buffer.at[i * rows : (i + 1) * rows, :],
                    sems.at[i],
                )
            )
    return listed


def out_copies(buffer, ref, sems, block, blocks):
    return [
        pltpu.make_async_copy(
            buffer.at[i * block : (i + 1) * block, :],
            ref.at[i * block : (i + 1) * block, :],
            sems.at[i],
        )
        for i in blocks
    ]


def entry_body(*refs, spread, rows, block, blocks, earlier):
    count = len(spread.arrays)
    arrays = refs[:count]
    (gain1, bias1, gain2, bias2, qkv_ref, out_weight_ref) = refs[count : count + 6]
    count += 6 + earlier
    (one_ref, two_ref, hat_ref, raw_ref, grad_ref, cot_ref) = refs[count : count + 6]
    x_buf, c_buf, sem_x, sem_c, sem_out = refs[count + 6 :]
    step = pl.program_id(0)
    x_copies = block_copies(spread, "a", arrays, x_buf, sem_x, rows, block, blocks)
    c_copies = block_copies(spread, "b", arrays, c_buf, sem_c, rows, block, blocks)
    outs = out_copies(c_buf, cot_ref, sem_out, block, blocks)

    @pl.when(step == 0)
    def _():
        for x_list, c_list in zip(x_copies, c_copies):
            for copy in x_list + c_list:
                copy.start()

    for i in range(len(outs)):

        @pl.when(step == i)
        def _(i=i):
            for copy in x_copies[i] + c_copies[i]:
                copy.wait()
            outs[i].start()

    here = pl.ds(pl.multiple_of((step * blocks.step + blocks.start) * block, block), block)
    values = x_buf[here, :].astype(f32)
    centred = values - jnp.mean(values, axis=1, keepdims=True)
    hat = centred * lax.rsqrt(jnp.mean(centred * centred, axis=1, keepdims=True) + norm_eps)
    hat_ref[...] = hat.astype(bf16)
    one_ref[...] = (hat * gain1[...] + bias1[...]).astype(bf16)
    two_ref[...] = (hat * gain2[...] + bias2[...]).astype(bf16)
    raw_ref[...] = dot_plain(one_ref[...], qkv_ref[...])
    grad_ref[...] = contract_cols(c_buf[here, :], out_weight_ref[...]).astype(bf16)

    @pl.when(step == len(outs) - 1)
    def _():
        for copy in outs:
            copy.wait()


def entry(spread, rows, gains, qkv_weight, out_weight, begin=0, stride=1, earlier=()):
    group_rows = rows * len(spread.names)
    width, deep = qkv_weight.shape
    units = out_weight.shape[0]
    block = min(256, group_rows)
    steps = group_rows // block
    per_group = len(spread.names)
    blocks = range(begin, steps, stride)
    once = pl.Buffered(1)

    def out_block(columns):
        return pl.BlockSpec((block, columns), lambda i: (i * stride + begin, 0))

    row = pl.BlockSpec((1, width), lambda i: (0, 0))
    anywhere = pl.BlockSpec(memory_space=pl.ANY)
    wide = jax.ShapeDtypeStruct((group_rows, width), bf16)
    first = len(spread.arrays) + 6
    return call(
        functools.partial(
            entry_body, spread=spread, rows=rows, block=block, blocks=blocks, earlier=len(earlier)
        ),
        "entry",
        grid=(len(blocks),),
        in_specs=[anywhere] * len(spread.arrays)
        + [row] * 4
        + [
            pl.BlockSpec(qkv_weight.shape, lambda i: (0, 0), pipeline_mode=once),
            pl.BlockSpec(out_weight.shape, lambda i: (0, 0), pipeline_mode=once),
        ]
        + [anywhere] * len(earlier),
        out_specs=[
            out_block(width),
            out_block(width),
            out_block(width),
            out_block(deep),
            out_block(units),
            anywhere,
        ],
        out_shape=[
            wide,
            wide,
            wide,
            jax.ShapeDtypeStruct((group_rows, deep), f32),
            jax.ShapeDtypeStruct((group_rows, units), bf16),
            wide,
        ],
        input_output_aliases={first + i: i for i in range(len(earlier))},
        scratch_shapes=[
            pltpu.VMEM((group_rows, width), bf16),
            pltpu.VMEM((group_rows, width), bf16),
            pltpu.SemaphoreType.DMA((per_group,)),
            pltpu.SemaphoreType.DMA((per_group,)),
            pltpu.SemaphoreType.DMA((steps,)),
        ],
    )(*spread.arrays, *gains, qkv_weight, out_weight, *earlier)


def pairs_body(input_ref, cot_ref, gain_ref, bias_ref, pair_ref, shared_ref):
    rows = input_ref.shape[0]
    values = input_ref[...].astype(f32)
    centred = values - jnp.mean(values, axis=1, keepdims=True)
    hat = centred * lax.rsqrt(jnp.mean(centred * centred, axis=1, keepdims=True) + norm_eps)
    pair_ref[:rows, :] = input_ref[...]
    pair_ref[rows:, :] = cot_ref[...]
    shared_ref[:rows, :] = (hat * gain_ref[...] + bias_ref[...]).astype(bf16)
    shared_ref[rows:, :] = cot_ref[...]


def pairs(layer_input, cotangent, gain, bias):
    rows, width = layer_input.shape
    return call(
        pairs_body,
        "pairs",
        out_shape=[jax.ShapeDtypeStruct((2 * rows, width), bf16)] * 2,
    )(layer_input, cotangent, gain, bias)


def fold_body(near_ref, came_ref, going_ref, kept_ref, *, rows, going, kept):
    for ref, places in ((going_ref, going), (kept_ref, kept)):
        for i, at in enumerate(places):
            here = slice(at * rows, (at + 1) * rows)
            total = near_ref[here, :].astype(f32) + came_ref[here, :].astype(f32)
            ref[i * rows : (i + 1) * rows, :] = total.astype(bf16)


def fold(near, came, rows, going, kept):
    width = near.shape[1]
    tile = min(512, width)
    half = len(going) * rows
    return call(
        functools.partial(fold_body, rows=rows, going=going, kept=kept),
        "fold",
        grid=(width // tile,),
        in_specs=[pl.BlockSpec((near.shape[0], tile), lambda i: (0, i))] * 2,
        out_specs=[pl.BlockSpec((half, tile), lambda i: (0, i))] * 2,
        out_shape=[jax.ShapeDtypeStruct((half, width), bf16)] * 2,
    )(near, came)


def start(copies):
    for copy in copies:
        copy.start()


def wait(copies):
    for copy in copies:
        copy.wait()


class Branch:
    def __init__(self, arrays, weights, buffers, sems, spread, rows, block, tile):
        self.up_ref, self.shift_ref, self.down_ref = weights
        self.x_buf, self.c_buf, self.u_buf, self.d_buf = buffers
        sem_x, sem_c, sem_u, sem_d = sems
        self.block = block
        self.every = range(self.x_buf.shape[0] // block)
        units = self.u_buf.shape[1]
        self.x_copies = block_copies(spread, "a", arrays, self.x_buf, sem_x, rows, block, self.every)
        self.c_copies = block_copies(spread, "b", arrays, self.c_buf, sem_c, rows, block, self.every)
        self.tiles = [slice(i, i + tile) for i in range(0, units, tile)]
        self.needs = []
        for i, t in enumerate(self.tiles):
            for ref, buf, sem, at in (
                (self.up_ref, self.u_buf, sem_u, (slice(None), t)),
                (self.down_ref, self.d_buf, sem_d, (t, slice(None))),
            ):
                self.needs.append([pltpu.make_async_copy(ref.at[at], buf.at[at], sem.at[i])])
        self.needs[0] = self.x_copies[0] + self.needs[0]
        self.needs[1] = self.c_copies[0] + self.needs[1]

    def block_step(self, step, hidden_ref, grad_ref, sum_ref, to_rows, extra=()):
        @pl.when(step == 0)
        def _():
            start(self.needs[0])
            sum_ref[...] = jnp.zeros_like(sum_ref)
            wait(self.needs[0])
            for need in self.needs[1:3]:
                start(need)

        for i in self.every[1:]:

            @pl.when(step == i)
            def _(i=i):
                wait(self.x_copies[i] + self.c_copies[i])

        here = pl.ds(pl.multiple_of(step * self.block, self.block), self.block)
        there = here if to_rows else slice(None)
        for i, part in enumerate(self.tiles):
            gate = dot_plain(self.x_buf[here, :], self.u_buf[:, part]) + self.shift_ref[:, part]

            @pl.when(step == 0)
            def _(i=i):
                for need in self.needs[2 * i + 1 : 2 * i + 3]:
                    wait(need)
                for need in self.needs[2 * i + 3 : 2 * i + 5]:
                    start(need)
                if i == 0:
                    for later in self.every[1:]:
                        start(self.x_copies[later] + self.c_copies[later])
                if i == len(self.tiles) - 1:
                    start(extra)

            grad_hidden = contract_cols(self.c_buf[here, :], self.d_buf[part, :])
            below = 0.5 * (1.0 + lax.erf(gate * inv_root_two))
            hidden_ref[there, part] = (gate * below).astype(bf16)
            slope = below + gate * jnp.exp(-0.5 * gate * gate) * inv_root_tau
            grad = (grad_hidden * slope).astype(bf16)
            grad_ref[there, part] = grad
            sum_ref[:, part] += jnp.sum(grad.astype(f32), axis=0, keepdims=True)


def branch_scratch(group_rows, width, units, blocks, tiles):
    dma = pltpu.SemaphoreType.DMA
    return [
        pltpu.VMEM((group_rows, width), bf16),
        pltpu.VMEM((group_rows, width), bf16),
        pltpu.VMEM((width, units), bf16),
        pltpu.VMEM((units, width), bf16),
        dma((blocks,)),
        dma((blocks,)),
        dma((tiles,)),
        dma((tiles,)),
    ]


def mlp_body(*refs, spread, rows, block, tile):
    count = len(spread.arrays)
    hidden_ref, grad_ref, sum_ref = refs[count + 3 : count + 6]
    scratch = refs[count + 6 :]
    branch = Branch(
        refs[:count], refs[count : count + 3], scratch[:4], scratch[4:], spread, rows, block, tile
    )
    branch.block_step(pl.program_id(0), hidden_ref, grad_ref, sum_ref, False)


def mlp(spread, rows, up_weight, up_bias, down_weight):
    width, units = up_weight.shape
    group_rows = rows * len(spread.names)
    block = min(512, group_rows)
    tile = min(512, units)
    steps, tiles, blocks = group_rows // block, units // tile, len(spread.names)
    anywhere = pl.BlockSpec(memory_space=pl.ANY)
    part = pl.BlockSpec((block, units), lambda i: (i, 0))
    low = jax.ShapeDtypeStruct((group_rows, units), bf16)
    row = pl.BlockSpec((1, units), lambda i: (0, 0))
    return call(
        functools.partial(mlp_body, spread=spread, rows=rows, block=block, tile=tile),
        "mlp",
        grid=(steps,),
        in_specs=[anywhere] * len(spread.arrays) + [anywhere, row, anywhere],
        out_specs=[part, part, row],
        out_shape=[low, low, jax.ShapeDtypeStruct((1, units), f32)],
        scratch_shapes=branch_scratch(group_rows, width, units, blocks, tiles),
    )(*spread.arrays, up_weight, up_bias, down_weight)


def group_body(*refs, spread, rows, block, tile, steps, ups, adds, more):
    count = len(spread.arrays)
    arrays, weights, refs = refs[:count], refs[count : count + 3], refs[count + 3 :]
    added, refs = refs[: 2 * adds], refs[2 * adds :]
    own, refs = refs[: 4 * more], refs[4 * more :]
    up_out, down_out, sum_ref = refs[:3]
    buffers, sems, (hidden_buf, grad_buf), refs = refs[3:7], refs[7:11], refs[11:13], refs[13:]
    branch = Branch(arrays, weights, buffers, sems, spread, rows, block, tile)
    step = pl.program_id(0)
    at = jnp.where(step < steps + ups, step - steps, step - steps - ups)
    at = jnp.maximum(at, 0)
    here = pl.ds(pl.multiple_of(at * tile, tile), tile)
    later = []
    if adds:
        sum_up, sum_down, sem_sum_up, sem_sum_down, *refs = refs

        def up_copy(i):
            first = pl.multiple_of(i * tile, tile)
            return pltpu.make_async_copy(
                added[0].at[pl.ds(first, tile), :], sum_up.at[i % 2], sem_sum_up.at[i % 2]
            )

        def down_copy(i):
            first = pl.multiple_of(i * tile, tile)
            return pltpu.make_async_copy(
                added[1].at[:, pl.ds(first, tile)], sum_down.at[i % 2], sem_sum_down.at[i % 2]
            )

        later = later + [up_copy(0)]
    if more:
        own_bufs, sem_own = refs[:4], refs[4]
        own_copies = [
            pltpu.make_async_copy(ref, buf, sem_own.at[i])
            for i, (ref, buf) in enumerate(zip(own, own_bufs))
        ]
        later = later + own_copies
        rows_own, cot_own, hidden_own, grad_own = own_bufs

    @pl.when(step < steps)
    def _():
        branch.block_step(step, hidden_buf, grad_buf, sum_ref, True, later)

    if more:

        @pl.when(step == steps)
        def _():
            wait(own_copies)

    @pl.when((step >= steps) & (step < steps + ups))
    def _():
        if adds:

            @pl.when(at + 1 < ups)
            def _():
                up_copy(at + 1).start()

            @pl.when(at + 1 == ups)
            def _():
                down_copy(0).start()

            up_copy(at).wait()
        total = contract_rows(branch.x_buf[:, here], grad_buf[...])
        if more:
            total = total + contract_rows(rows_own[:, here], grad_own[...])
        if adds:
            total = total + sum_up[at % 2]
        up_out[...] = total

    @pl.when(step >= steps + ups)
    def _():
        if adds:

            @pl.when(at + 1 < ups)
            def _():
                down_copy(at + 1).start()

            down_copy(at).wait()
        total = contract_rows(hidden_buf[...], branch.c_buf[:, here])
        if more:
            total = total + contract_rows(hidden_own[...], cot_own[:, here])
        if adds:
            total = total + sum_down[at % 2]
        down_out[...] = total


def group(spread, rows, up_weight, up_bias, down_weight, added=(), own=()):
    width, units = up_weight.shape
    group_rows = rows * len(spread.names)
    block = min(512, group_rows)
    tile = min(512, units)
    steps, tiles, blocks = group_rows // block, units // tile, len(spread.names)
    ups = width // tile
    anywhere = pl.BlockSpec(memory_space=pl.ANY)
    row = pl.BlockSpec((1, units), lambda i: (0, 0))
    dma = pltpu.SemaphoreType.DMA
    scratch = branch_scratch(group_rows, width, units, blocks, tiles)
    scratch += [pltpu.VMEM((group_rows, units), bf16)] * 2
    if added:
        scratch += [
            pltpu.VMEM((2, tile, units), f32),
            pltpu.VMEM((2, units, tile), f32),
            dma((2,)),
            dma((2,)),
        ]
    if own:
        scratch += [pltpu.VMEM(array.shape, bf16) for array in own] + [dma((4,))]
    return call(
        functools.partial(
            group_body,
            spread=spread,
            rows=rows,
            block=block,
            tile=tile,
            steps=steps,
            ups=ups,
            adds=bool(added),
            more=bool(own),
        ),
        "group",
        grid=(steps + 2 * ups,),
        in_specs=[anywhere] * len(spread.arrays)
        + [anywhere, row, anywhere]
        + [anywhere] * (len(added) + len(own)),
        out_specs=[
            pl.BlockSpec((tile, units), lambda i: (jnp.clip(i - steps, 0, ups - 1), 0)),
            pl.BlockSpec((units, tile), lambda i: (0, jnp.clip(i - steps - ups, 0, ups - 1))),
            row,
        ],
        out_shape=[
            jax.ShapeDtypeStruct((width, units), f32),
            jax.ShapeDtypeStruct((units, width), f32),
            jax.ShapeDtypeStruct((1, units), f32),
        ],
        scratch_shapes=scratch,
    )(*spread.arrays, up_weight, up_bias, down_weight, *added, *own)


def weight_body(left_ref, right_ref, out_ref):
    out_ref[...] = contract_rows(left_ref[...], right_ref[...])


def weight_product(left, right):
    wide, deep = left.shape[1], right.shape[1]
    tile = min(512, wide)
    return call(
        weight_body,
        "weight_product",
        grid=(wide // tile,),
        in_specs=[
            pl.BlockSpec((left.shape[0], tile), lambda i: (0, i)),
            pl.BlockSpec(right.shape, lambda i: (0, 0), pipeline_mode=pl.Buffered(1)),
        ],
        out_specs=pl.BlockSpec((tile, deep), lambda i: (i, 0)),
        out_shape=jax.ShapeDtypeStruct((wide, deep), f32),
    )(left, right)


def attention_weights_body(normed_ref, grad_qkv_ref, attended_ref, grad_out_ref, sum_ref):
    deep = grad_qkv_ref.shape[1]
    sum_ref[:, :deep] = contract_rows(normed_ref[...], grad_qkv_ref[...]).astype(bf16)
    sum_ref[:, deep:] = contract_rows(attended_ref[...], grad_out_ref[...]).astype(bf16)


def attention_weights(normed, grad_qkv, attended, grad_out):
    group_rows, width = normed.shape
    deep, units = grad_qkv.shape[1], attended.shape[1]
    once = pl.Buffered(1)
    block = pl.BlockSpec((group_rows, units), lambda i: (0, i))
    return call(
        attention_weights_body,
        "attention_weights",
        grid=(width // units,),
        in_specs=[
            block,
            pl.BlockSpec(grad_qkv.shape, lambda i: (0, 0), pipeline_mode=once),
            pl.BlockSpec(attended.shape, lambda i: (0, 0), pipeline_mode=once),
            block,
        ],
        out_specs=pl.BlockSpec((units, deep + units), lambda i: (i, 0)),
        out_shape=jax.ShapeDtypeStruct((width, deep + units), bf16),
    )(normed, grad_qkv, attended, grad_out)


def widen_body(sum_ref, qkv_ref, out_ref):
    units, deep = out_ref.shape[0], qkv_ref.shape[1]
    qkv_ref[...] = sum_ref[:, :deep].astype(f32)
    for first in range(0, sum_ref.shape[0], units):
        out_ref[:, first : first + units] = sum_ref[first : first + units, deep:].astype(f32)


def widen(total, deep, units):
    width = total.shape[0]
    block = min(2 * units, width)
    return call(
        widen_body,
        "widen",
        grid=(width // block,),
        in_specs=[pl.BlockSpec((block, deep + units), lambda i: (i, 0))],
        out_specs=[
            pl.BlockSpec((block, deep), lambda i: (i, 0)),
            pl.BlockSpec((units, block), lambda i: (0, i)),
        ],
        out_shape=[
            jax.ShapeDtypeStruct((width, deep), f32),
            jax.ShapeDtypeStruct((units, width), f32),
        ],
    )(total)


def branch_body(attended_ref, hidden_ref, out_ref, down_ref, near_ref, far_ref):
    middle = near_ref.shape[0]
    total = dot_plain(attended_ref[...], out_ref[...]) + dot_plain(hidden_ref[...], down_ref[...])
    near_ref[...] = total[:middle].astype(bf16)
    far_ref[...] = total[middle:].astype(bf16)


def branch_sum(attended, hidden, out_weight, down_weight):
    group_rows = attended.shape[0]
    width = out_weight.shape[1]
    tile = min(512, width)
    once = pl.Buffered(1)
    half = pl.BlockSpec((group_rows // 2, tile), lambda i: (0, i))
    return call(
        branch_body,
        "branch_sum",
        grid=(width // tile,),
        in_specs=[
            pl.BlockSpec(attended.shape, lambda i: (0, 0), pipeline_mode=once),
            pl.BlockSpec(hidden.shape, lambda i: (0, 0), pipeline_mode=once),
            pl.BlockSpec((out_weight.shape[0], tile), lambda i: (0, i)),
            pl.BlockSpec((down_weight.shape[0], tile), lambda i: (0, i)),
        ],
        out_specs=[half, half],
        out_shape=[jax.ShapeDtypeStruct((group_rows // 2, width), bf16)] * 2,
    )(attended, hidden, out_weight, down_weight)


def input_body(
    qkv_grad_ref, gate_grad_ref, qkv_ref, up_ref, gain1, gain2, hat_ref, near_ref, far_ref, sum_ref
):
    middle = near_ref.shape[0]
    hat = hat_ref[...].astype(f32)
    first = contract_cols(qkv_grad_ref[...], qkv_ref[...])
    second = contract_cols(gate_grad_ref[...], up_ref[...])
    both = first * gain1[...] + second * gain2[...]
    near_ref[...] = both[:middle].astype(bf16)
    far_ref[...] = both[middle:].astype(bf16)
    sum_ref[0:1, :] = jnp.sum(first * hat, axis=0, keepdims=True)
    sum_ref[1:2, :] = jnp.sum(first, axis=0, keepdims=True)
    sum_ref[2:3, :] = jnp.sum(second * hat, axis=0, keepdims=True)
    sum_ref[3:4, :] = jnp.sum(second, axis=0, keepdims=True)


def input_sums(grad_qkv, grad_gate, qkv_weight, up_weight, gain1, gain2, hat):
    group_rows = grad_qkv.shape[0]
    width = qkv_weight.shape[0]
    tile = min(256, width)
    once = pl.Buffered(1)
    half = pl.BlockSpec((group_rows // 2, tile), lambda i: (0, i))
    row = pl.BlockSpec((1, tile), lambda i: (0, i))
    return call(
        input_body,
        "input_sums",
        grid=(width // tile,),
        in_specs=[
            pl.BlockSpec(grad_qkv.shape, lambda i: (0, 0), pipeline_mode=once),
            pl.BlockSpec(grad_gate.shape, lambda i: (0, 0), pipeline_mode=once),
            pl.BlockSpec((tile, qkv_weight.shape[1]), lambda i: (i, 0)),
            pl.BlockSpec((tile, up_weight.shape[1]), lambda i: (i, 0)),
            row,
            row,
            pl.BlockSpec((group_rows, tile), lambda i: (0, i)),
        ],
        out_specs=[half, half, pl.BlockSpec((4, tile), lambda i: (0, i))],
        out_shape=[jax.ShapeDtypeStruct((group_rows // 2, width), bf16)] * 2
        + [jax.ShapeDtypeStruct((4, width), f32)],
    )(grad_qkv, grad_gate, qkv_weight, up_weight, gain1, gain2, hat)


def attention_body(
    own_ref,
    starts_ref,
    raw_ref,
    bias_ref,
    cos_ref,
    sine_ref,
    slope_in_ref,
    attended_ref,
    grad_qkv_ref,
    bias_grad_ref,
    query_ref,
    key_ref,
    value_ref,
    slope_ref,
    query_sum_ref,
    key_sum_ref,
    value_sum_ref,
    *,
    rows,
    names,
    block_rows,
    longest,
):
    own = own_ref[0]
    group_rows = rows * len(names)
    lane = lax.broadcasted_iota(jnp.int32, (rows, HEAD_DIM), 1)
    half = ROTARY // 2
    scale = HEAD_DIM ** (-0.5)

    def turned(u):
        return jnp.where(lane < half, pltpu.roll(u, HEAD_DIM - half, 1), pltpu.roll(u, half, 1))

    def far_rows(name):
        return pl.ds(pl.multiple_of((own ^ name) * rows, rows), rows)

    for i, name in enumerate(names):
        near = slice(i * rows, (i + 1) * rows)
        far = far_rows(name)
        raw = raw_ref[near, :] + bias_ref[...]
        cos_table = cos_ref[near, :]
        sine_table = sine_ref[near, :]
        query = raw[:, :HEAD_DIM]
        key = raw[:, HEAD_DIM : 2 * HEAD_DIM]
        query_ref[far, :] = (query * cos_table + turned(query) * sine_table).astype(bf16)
        key_ref[far, :] = (key * cos_table + turned(key) * sine_table).astype(bf16)
        value_ref[far, :] = raw[:, 2 * HEAD_DIM :].astype(bf16)
        slope_ref[far, :] = slope_in_ref[near, :]
    key_sum_ref[...] = jnp.zeros_like(key_sum_ref)
    value_sum_ref[...] = jnp.zeros_like(value_sum_ref)
    for first in range(0, group_rows, block_rows):
        last = first + block_rows
        low = max(0, (first - longest + 1) // 128 * 128)
        query = query_ref[first:last, :]
        keys = key_ref[low:last, :]
        values = value_ref[low:last, :]
        slope = slope_ref[first:last, :]
        scores = contract_cols(query, keys) * scale
        row = first + lax.broadcasted_iota(jnp.int32, (block_rows, 1), 0)
        begin = jnp.zeros((block_rows, 1), jnp.int32)
        for slot in range(starts_ref.shape[0]):
            begin = jnp.where(starts_ref[slot] <= row, starts_ref[slot], begin)
        column = low + lax.broadcasted_iota(jnp.int32, scores.shape, 1)
        scores = jnp.where((column >= begin) & (column <= row), scores, masked_score)
        peak = jnp.max(scores, axis=1, keepdims=True)
        raised = jnp.exp(scores - peak)
        probs = raised * (1.0 / jnp.sum(raised, axis=1, keepdims=True))
        probs_low = probs.astype(bf16)
        query_ref[first:last, :] = dot_plain(probs_low, values).astype(bf16)
        grad_probs = contract_cols(slope, values)
        delta = jnp.sum(grad_probs * probs, axis=1, keepdims=True)
        grad_score = (probs * (grad_probs - delta)).astype(bf16)
        query_sum_ref[first:last, :] = dot_plain(grad_score, keys) * scale
        key_sum_ref[low:last, :] += contract_rows(grad_score, query) * scale
        value_sum_ref[low:last, :] += contract_rows(probs_low, slope)
    bias_grad = jnp.zeros(bias_grad_ref.shape, f32)
    for i, name in enumerate(names):
        near = slice(i * rows, (i + 1) * rows)
        far = far_rows(name)
        cos_table = cos_ref[near, :]
        sine_table = sine_ref[near, :]
        query_grad = query_sum_ref[far, :]
        key_grad = key_sum_ref[far, :]
        grads = jnp.concatenate(
            [
                query_grad * cos_table - turned(query_grad) * sine_table,
                key_grad * cos_table - turned(key_grad) * sine_table,
                value_sum_ref[far, :],
            ],
            axis=1,
        ).astype(bf16)
        grad_qkv_ref[near, :] = grads
        bias_grad = bias_grad + jnp.sum(grads.astype(f32), axis=0, keepdims=True)
        attended_ref[near, :] = query_ref[far, :]
    bias_grad_ref[...] = bias_grad


def attention(own, starts, raw, bias, cos_table, sine_table, slope, rows, names):
    group_rows, width = raw.shape
    part = 3 * HEAD_DIM
    heads = width // part
    whole = pl.BlockSpec((group_rows, HEAD_DIM), lambda h: (0, 0))
    scalars = pl.BlockSpec(memory_space=pltpu.SMEM)
    low = pltpu.VMEM((group_rows, HEAD_DIM), bf16)
    wide = pltpu.VMEM((group_rows, HEAD_DIM), f32)
    longest = group_rows // 2
    return pl.pallas_call(
        functools.partial(
            attention_body,
            rows=rows,
            names=names,
            block_rows=min(256, group_rows),
            longest=longest,
        ),
        grid=(heads,),
        in_specs=[
            scalars,
            scalars,
            pl.BlockSpec((group_rows, part), lambda h: (0, h)),
            pl.BlockSpec((1, part), lambda h: (0, h)),
            whole,
            whole,
            pl.BlockSpec((group_rows, HEAD_DIM), lambda h: (0, h)),
        ],
        out_specs=[
            pl.BlockSpec((group_rows, HEAD_DIM), lambda h: (0, h)),
            pl.BlockSpec((group_rows, part), lambda h: (0, h)),
            pl.BlockSpec((1, part), lambda h: (0, h)),
        ],
        out_shape=[
            jax.ShapeDtypeStruct((group_rows, heads * HEAD_DIM), bf16),
            jax.ShapeDtypeStruct((group_rows, width), bf16),
            jax.ShapeDtypeStruct((1, width), f32),
        ],
        scratch_shapes=[low, low, low, low, wide, wide, wide],
        compiler_params=pltpu.CompilerParams(vmem_limit_bytes=vmem_bytes),
        cost_estimate=pl.CostEstimate(flops=1, bytes_accessed=1, transcendentals=0),
        name="attention",
    )(own, starts, raw, bias, cos_table, sine_table, slope)


def rotary_tables(position):
    half_rot = ROTARY // 2
    frequency = 10000.0 ** (-2.0 * jnp.arange(half_rot, dtype=f32) / ROTARY)
    angles = position.astype(f32)[:, None] * frequency[None, :]
    cos_half = jnp.cos(angles)
    sine_half = jnp.sin(angles)
    rest = (position.shape[0], HEAD_DIM - ROTARY)
    return (
        jnp.concatenate([cos_half, cos_half, jnp.ones(rest, f32)], axis=1),
        jnp.concatenate([-sine_half, sine_half, jnp.zeros(rest, f32)], axis=1),
    )


def butterfly(value, axis, count, bit):
    return value + swap(value, axis, count, bit)


def fence(*values):
    return lax.optimization_barrier(values)


def norm_own(layer_input):
    values = layer_input.astype(f32)
    centred = values - jnp.mean(values, axis=-1, keepdims=True)
    inv_std = lax.rsqrt(jnp.mean(centred * centred, axis=-1, keepdims=True) + norm_eps)
    return centred * inv_std, inv_std


def tables(own, lengths, names, rows):
    seq_ends = jnp.cumsum(lengths)
    seq_starts = seq_ends - lengths
    places = (
        (own ^ jnp.array(names, jnp.int32))[:, None] * rows
        + jnp.arange(rows, dtype=jnp.int32)[None, :]
    ).reshape(-1)
    seq_first = jnp.max(
        jnp.where(seq_starts[None, :] <= places[:, None], seq_starts[None, :], 0), axis=1
    )
    return (seq_starts, *rotary_tables(places - seq_first))


def contiguous(first, second, names, rows):
    places = [{n: (which, i * rows) for i, n in enumerate(names)} for which in range(2)]
    return Spread([first, second], *places, names)


def ends(layer_input, cotangent, xhat, inv_std, branch, scaled, biases):
    layer_output = (layer_input.astype(f32) + branch + biases).astype(bf16)
    input_grad = cotangent.astype(f32) + inv_std * (
        scaled
        - jnp.mean(scaled, axis=-1, keepdims=True)
        - xhat * jnp.mean(scaled * xhat, axis=-1, keepdims=True)
    )
    return layer_output, input_grad


def per_device(
    layer_input,
    lengths,
    norm1_gain,
    norm1_bias,
    norm2_gain,
    norm2_bias,
    qkv_weight,
    qkv_bias,
    out_weight,
    out_bias,
    up_weight,
    up_bias,
    down_weight,
    down_bias,
    cotangent,
):
    dp = lax.axis_size("dp")
    mp = lax.axis_size("mp")
    own = lax.axis_index("mp")
    rows, width = layer_input.shape
    up_row = up_bias[None, :]
    gains = (norm1_gain[None, :], norm1_bias[None, :], norm2_gain[None, :], norm2_bias[None, :])
    gather_all = mp == 8 and dp == 4 and 4 * rows * mp * dp * (width + up_bias.shape[0]) < most_gathered

    pair, shared = pairs(layer_input, cotangent, *gains[2:])
    if gather_all:
        names = four_names
        sides = spread_sides(pair, mp)
        group_a = turn(shared, "dp", dp, 1)
        placed = tables(own, lengths[0], names, rows)
        far = spread_core([pair], mp)
        shared, pair, sides, placed, far, group_a = fence(shared, pair, sides, placed, far, group_a)
        group_b = turn(shared, "dp", dp, -1)
        corner = spread_corner(sides, mp)
        near = [pair, *sides]
        far = far + spread_core(sides, mp)
        begun = entry(spread_four(near, far), rows, gains, qkv_weight, out_weight, 0, 2)
        near, far, corner, group_a, begun = fence(near, far, corner, group_a, begun)
        near, far = near + corner, far + spread_core(corner, mp)
        sides_a = spread_sides(group_a, mp)
        entered = entry(spread_four(near, far), rows, gains, qkv_weight, out_weight, 1, 2, begun)
        entered, group_b, group_a = fence(entered, group_b, group_a)
        far_a = spread_core([group_a], mp)
        group_c = turn(group_a, "dp", dp, 1)
    else:
        spread = spread_any(pair, mp)
        names = spread.names
        placed = tables(own, lengths[0], names, rows)
        entered = entry(spread, rows, gains, qkv_weight, out_weight)
    seq_starts, cos_table, sine_table = placed

    first_all, second_all, hat, raw, grad_attended, grad_out = entered
    attended, grad_qkv, qkv_bias_part = attention(
        own.reshape(1),
        seq_starts,
        raw,
        qkv_bias[None, :],
        cos_table,
        sine_table,
        grad_attended,
        rows,
        names,
    )
    if gather_all:
        (first_all, second_all, hat, grad_out, attended, grad_qkv), near_a, far_a, group_b = fence(
            (first_all, second_all, hat, grad_out, attended, grad_qkv),
            [group_a, *sides_a],
            far_a,
            group_b,
        )

    weights_part = attention_weights(first_all, grad_qkv, attended, grad_out)
    if gather_all:
        corner_a = spread_corner(near_a[1:], mp)
        far_a = far_a + spread_core(near_a[1:], mp)
        (weights_part, second_all, hat, grad_out, attended), near_a, corner_a, far_a, group_b, group_c = (
            fence(
                (weights_part, second_all, hat, grad_out, attended),
                near_a,
                corner_a,
                far_a,
                group_b,
                group_c,
            )
        )
    weights_sum = lax.psum_scatter(weights_part, "dp", scatter_dimension=0, tiled=True)

    own_spread = contiguous(second_all, grad_out, names, rows)
    hidden, grad_gate, gate_sum = mlp(own_spread, rows, up_weight, up_row, down_weight)
    if gather_all:
        sides_b = spread_sides(group_b, mp)
        far_b = spread_core([group_b], mp)
        far_a = far_a + spread_core(corner_a, mp)
        near_a = near_a + corner_a
        (hidden, grad_gate, attended, grad_qkv, hat), near_a, far_a, near_b, far_b, group_c = fence(
            (hidden, grad_gate, attended, grad_qkv, hat),
            near_a,
            far_a,
            [group_b, *sides_b],
            far_b,
            group_c,
        )

    branch = branch_sum(attended, hidden, out_weight, down_weight)
    if gather_all:
        corner_b = spread_corner(near_b[1:], mp)
        far_b = far_b + spread_core(near_b[1:], mp)
        far_c = spread_core([group_c], mp)
        branch, hidden, grad_gate, grad_qkv, hat, near_b, far_b, corner_b, group_c, far_c = fence(
            branch, hidden, grad_gate, grad_qkv, hat, near_b, far_b, corner_b, group_c, far_c
        )

    scaled = input_sums(grad_qkv, grad_gate, qkv_weight, up_weight, gains[0], gains[2], hat)
    cot_sum = jnp.sum(cotangent.astype(f32), axis=0)
    small = jnp.concatenate([scaled[2].reshape(-1), cot_sum, qkv_bias_part.reshape(-1)])
    small = small.reshape(-1, 128)
    five = 5 * width // 128
    biases = out_bias + down_bias
    xhat, inv_std = norm_own(layer_input)

    def over_mp(both, bit):
        return jnp.concatenate([butterfly(both[:five], "mp", mp, bit), both[five:]], axis=0)

    if not gather_all:
        own_branch = scatter_group(*branch, names, mp, rows)
        own_scaled = scatter_group(*scaled[:2], names, mp, rows)
        layer_output, input_grad = ends(
            layer_input, cotangent, xhat, inv_std, own_branch, own_scaled, biases
        )
        for bit in (1 << i for i in range(dp.bit_length() - 1)):
            small = butterfly(small, "dp", dp, bit)
        small, qkv_bias_grad = small[:five], small[five:]
        for bit in (1 << i for i in range(mp.bit_length() - 1)):
            small = butterfly(small, "mp", mp, bit)
        weights_sum = lax.all_gather(weights_sum, "dp", axis=0, tiled=True)
        up_weight_grad, down_weight_grad, up_bias_grad = lax.psum(
            (weight_product(second_all, grad_gate), weight_product(hidden, grad_out), gate_sum[0]),
            "dp",
        )
    else:
        sides_c = spread_sides(group_c, mp)
        far_b = far_b + spread_core(corner_b, mp)
        near_b = near_b + corner_b
        branch_came = swap(branch[1], "mp", mp, 1)
        scaled, small, near_a, far_a, near_b, far_b, near_c, far_c, branch_came = fence(
            scaled, small, near_a, far_a, near_b, far_b, [group_c, *sides_c], far_c, branch_came
        )

        own_branch = Scatter(branch[0], branch_came, names, mp, rows)
        branch_sent = own_branch.folded(branch[0], branch_came)
        scaled_came = swap(scaled[1], "mp", mp, 1)
        small = over_mp(small, 1)
        up_sum, down_sum, sum_a = group(
            spread_four(near_a, far_a), rows, up_weight, up_row, down_weight
        )
        own_branch.step(*branch_sent)
        corner_c = spread_corner(near_c[1:], mp)
        sums, near_b, far_b, near_c, far_c, corner_c, branch_sent, scaled_came, small, weights_sum = (
            fence(
                (up_sum, down_sum),
                near_b,
                far_b,
                near_c,
                far_c,
                corner_c,
                own_branch.sent(),
                scaled_came,
                small,
                weights_sum,
            )
        )

        weights_sum = lax.all_gather(weights_sum, "dp", axis=0, tiled=True)
        own_scaled = Scatter(scaled[0], scaled_came, names, mp, rows)
        scaled_sent = own_scaled.folded(scaled[0], scaled_came)
        up_sum, down_sum, sum_b = group(
            spread_four(near_b, far_b), rows, up_weight, up_row, down_weight, sums
        )
        far_c = far_c + spread_core(near_c[1:] + corner_c, mp)
        near_c = near_c + corner_c
        own_branch.step(*branch_sent)
        own_scaled.step(*scaled_sent)
        small = over_mp(small, 2)
        sums, near_c, far_c, branch_total, scaled_sent, small = fence(
            (up_sum, down_sum), near_c, far_c, own_branch.total(0), own_scaled.sent(), small
        )

        up_weight_grad, down_weight_grad, sum_c = group(
            spread_four(near_c, far_c),
            rows,
            up_weight,
            up_row,
            down_weight,
            sums,
            (second_all, grad_out, hidden, grad_gate),
        )
        own_scaled.step(*scaled_sent)
        small = over_mp(small, 4)
        up_weight_grad, scaled_total, small = fence(up_weight_grad, own_scaled.total(0), small)

        small = butterfly(small, "dp", dp, 1)
        layer_output, input_grad = ends(
            layer_input, cotangent, xhat, inv_std, branch_total, scaled_total, biases
        )
        small = butterfly(small, "dp", dp, 2)
        up_bias_grad = (gate_sum + sum_a + sum_b + sum_c)[0]
        small, qkv_bias_grad = small[:five], small[five:]
    qkv_weight_grad, out_weight_grad = widen(weights_sum, qkv_weight.shape[1], out_weight.shape[0])
    small = small.reshape(5, width)
    return (
        layer_output,
        input_grad,
        small[0],
        small[1],
        small[2],
        small[3],
        qkv_weight_grad,
        qkv_bias_grad.reshape(-1),
        out_weight_grad,
        small[4],
        up_weight_grad,
        up_bias_grad,
        down_weight_grad,
        small[4],
    )


def solution(mesh):
    in_specs = (
        P(("dp", "mp"), None),
        P("dp", None),
        P(),
        P(),
        P(),
        P(),
        P(None, "mp"),
        P("mp"),
        P("mp", None),
        P(),
        P(None, "mp"),
        P("mp"),
        P("mp", None),
        P(),
        P(("dp", "mp"), None),
    )
    out_specs = (
        P(("dp", "mp"), None),
        P(("dp", "mp"), None),
        P(),
        P(),
        P(),
        P(),
        P(None, "mp"),
        P("mp"),
        P("mp", None),
        P(),
        P(None, "mp"),
        P("mp"),
        P("mp", None),
        P(),
    )
    return jax.shard_map(
        per_device, mesh=mesh, in_specs=in_specs, out_specs=out_specs, check_vma=False
    )
```

```python
import functools

import jax
import jax.numpy as jnp
from jax import lax
from jax.experimental import pallas as pl
from jax.experimental.pallas import tpu as pltpu
from jax.sharding import PartitionSpec as P

HEAD_DIM = 128
ROTARY = 32

norm_eps = 1e-05
masked_score = -1e30
inv_root_two = 0.7071067811865476
inv_root_tau = 0.3989422804014327
vmem_bytes = 60 << 20
most_gathered = 128 << 20
bf16 = jnp.bfloat16
f32 = jnp.float32


def dot_plain(left, right):
    return jnp.dot(left, right, preferred_element_type=f32)


def contract_rows(left, right):
    return lax.dot_general(left, right, (((0,), (0,)), ((), ())), preferred_element_type=f32)


def contract_cols(left, right):
    return lax.dot_general(left, right, (((1,), (1,)), ((), ())), preferred_element_type=f32)


def swap(value, axis, count, bit):
    return lax.ppermute(value, axis, [(i, i ^ bit) for i in range(count)])


def turn(value, axis, count, step):
    return lax.ppermute(value, axis, [(i, (i + step) % count) for i in range(count)])


def chip_bits(count):
    return [1 << i for i in range(1, count.bit_length() - 1)]


def after(value, *earlier):
    return lax.optimization_barrier((value, *earlier))[0]


def halves(pair):
    rows = pair.shape[0] // 2
    return pair[:rows], pair[rows:]


class Spread:
    def __init__(self, arrays, a, b, names):
        self.arrays, self.a, self.b, self.names = arrays, a, b, names


four_names = (0, 2, 4, 6, 1, 3, 5, 7)


def spread_sides(pair, count):
    return [swap(pair, "mp", count, 2), swap(pair, "mp", count, 4)]


def spread_corner(sides, count):
    side_x, side_y = sides
    return [swap(halves(side_x)[0], "mp", count, 4), swap(halves(side_y)[1], "mp", count, 2)]


def spread_core(arrays, count):
    return [swap(array, "mp", count, 1) for array in arrays]


def spread_four(near, far):
    rows = near[0].shape[0] // 2
    a, b = {}, {}
    for core in range(2):
        base = len(near) * core
        for i, name in enumerate((0, 2, 4)):
            a[name + core] = (base + i, 0)
            b[name + core] = (base + i, rows)
        a[6 + core] = (base + 3, 0)
        b[6 + core] = (base + 4, 0)
    return Spread(near + far, a, b, four_names)


def spread_any(pair, count):
    rows = pair.shape[0] // 2
    held, names = pair.reshape(1, 2, rows, -1), [0]
    for bit in chip_bits(count) + [1]:
        held = jnp.concatenate([held, swap(held, "mp", count, bit)], axis=0)
        names = names + [n ^ bit for n in names]
    arrays = [held.reshape(2 * rows * count, -1)]
    a = {n: (0, 2 * rows * i) for i, n in enumerate(names)}
    b = {n: (0, 2 * rows * i + rows) for i, n in enumerate(names)}
    return Spread(arrays, a, b, tuple(names))


class Scatter:
    def __init__(self, near, came, names, count, rows, rising):
        self.count, self.rows = count, rows
        names = names[: len(names) // 2]
        self.blocks = {n: near[i * rows : (i + 1) * rows] for i, n in enumerate(names)}
        self.adds = {n: came[i * rows : (i + 1) * rows] for i, n in enumerate(names)}
        bits = chip_bits(count)
        self.bits = bits if rising else bits[::-1]

    def total(self, n):
        return self.blocks[n].astype(f32) + self.adds[n].astype(f32)

    def places(self):
        bit, order = self.bits[0], list(self.blocks)
        going = [i for i, n in enumerate(order) if n & bit]
        return going, [i for i, n in enumerate(order) if not n & bit]

    def listed(self, kept):
        return [kept[i : i + self.rows] for i in range(0, kept.shape[0], self.rows)]

    def sent(self):
        bit = self.bits[0]
        stay = [n for n in self.blocks if not n & bit]
        going = jnp.concatenate([self.total(n | bit).astype(bf16) for n in stay], axis=0)
        return going, [self.total(n).astype(bf16) for n in stay]

    def swapped(self, going):
        return swap(going, "mp", self.count, self.bits[0])

    def take(self, kept, came):
        bit, self.bits = self.bits[0], self.bits[1:]
        stay = [n for n in self.blocks if not n & bit]
        self.blocks = dict(zip(stay, kept))
        self.adds = {n: came[i * self.rows : (i + 1) * self.rows] for i, n in enumerate(stay)}


def scatter_group(near, far, names, count, rows):
    scatter = Scatter(near, swap(far, "mp", count, 1), names, count, rows, True)
    while scatter.bits:
        going, kept = scatter.sent()
        scatter.take(kept, scatter.swapped(going))
    return scatter.total(0)


def call(body, name, **kwargs):
    return pl.pallas_call(
        body,
        name=name,
        compiler_params=pltpu.CompilerParams(vmem_limit_bytes=vmem_bytes),
        cost_estimate=pl.CostEstimate(flops=1, bytes_accessed=1, transcendentals=0),
        **kwargs,
    )


def block_copies(spread, which, refs, buffer, sems, rows, block, blocks):
    per = block // rows
    listed = []
    for at in blocks:
        listed.append([])
        for i in range(at * per, (at + 1) * per):
            array, first = getattr(spread, which)[spread.names[i]]
            listed[-1].append(
                pltpu.make_async_copy(
                    refs[array].at[first : first + rows, :],
                    buffer.at[i * rows : (i + 1) * rows, :],
                    sems.at[i],
                )
            )
    return listed


def out_copies(buffer, ref, sems, block, blocks):
    return [
        pltpu.make_async_copy(
            buffer.at[i * block : (i + 1) * block, :],
            ref.at[i * block : (i + 1) * block, :],
            sems.at[i],
        )
        for i in blocks
    ]


def entry_body(*refs, spread, rows, block, blocks, earlier):
    count = len(spread.arrays)
    arrays = refs[:count]
    (gain1, bias1, gain2, bias2, qkv_ref, out_weight_ref) = refs[count : count + 6]
    count += 6 + earlier
    (one_ref, two_ref, hat_ref, raw_ref, grad_ref, cot_ref) = refs[count : count + 6]
    x_buf, c_buf, sem_x, sem_c, sem_out = refs[count + 6 :]
    step = pl.program_id(0)
    x_copies = block_copies(spread, "a", arrays, x_buf, sem_x, rows, block, blocks)
    c_copies = block_copies(spread, "b", arrays, c_buf, sem_c, rows, block, blocks)
    outs = out_copies(c_buf, cot_ref, sem_out, block, blocks)

    @pl.when(step == 0)
    def _():
        for x_list, c_list in zip(x_copies, c_copies):
            for copy in x_list + c_list:
                copy.start()

    for i in range(len(outs)):

        @pl.when(step == i)
        def _(i=i):
            for copy in x_copies[i] + c_copies[i]:
                copy.wait()
            outs[i].start()

    here = pl.ds(pl.multiple_of((step * blocks.step + blocks.start) * block, block), block)
    values = x_buf[here, :].astype(f32)
    centred = values - jnp.mean(values, axis=1, keepdims=True)
    hat = centred * lax.rsqrt(jnp.mean(centred * centred, axis=1, keepdims=True) + norm_eps)
    hat_ref[...] = hat.astype(bf16)
    one_ref[...] = (hat * gain1[...] + bias1[...]).astype(bf16)
    two_ref[...] = (hat * gain2[...] + bias2[...]).astype(bf16)
    raw_ref[...] = dot_plain(one_ref[...], qkv_ref[...])
    grad_ref[...] = contract_cols(c_buf[here, :], out_weight_ref[...]).astype(bf16)

    @pl.when(step == len(outs) - 1)
    def _():
        for copy in outs:
            copy.wait()


def entry(spread, rows, gains, qkv_weight, out_weight, begin=0, stride=1, earlier=()):
    group_rows = rows * len(spread.names)
    width, deep = qkv_weight.shape
    units = out_weight.shape[0]
    block = min(256, group_rows)
    steps = group_rows // block
    per_group = len(spread.names)
    blocks = range(begin, steps, stride)
    once = pl.Buffered(1)

    def out_block(columns):
        return pl.BlockSpec((block, columns), lambda i: (i * stride + begin, 0))

    row = pl.BlockSpec((1, width), lambda i: (0, 0))
    anywhere = pl.BlockSpec(memory_space=pl.ANY)
    wide = jax.ShapeDtypeStruct((group_rows, width), bf16)
    first = len(spread.arrays) + 6
    return call(
        functools.partial(
            entry_body, spread=spread, rows=rows, block=block, blocks=blocks, earlier=len(earlier)
        ),
        "entry",
        grid=(len(blocks),),
        in_specs=[anywhere] * len(spread.arrays)
        + [row] * 4
        + [
            pl.BlockSpec(qkv_weight.shape, lambda i: (0, 0), pipeline_mode=once),
            pl.BlockSpec(out_weight.shape, lambda i: (0, 0), pipeline_mode=once),
        ]
        + [anywhere] * len(earlier),
        out_specs=[
            out_block(width),
            out_block(width),
            out_block(width),
            out_block(deep),
            out_block(units),
            anywhere,
        ],
        out_shape=[
            wide,
            wide,
            wide,
            jax.ShapeDtypeStruct((group_rows, deep), f32),
            jax.ShapeDtypeStruct((group_rows, units), bf16),
            wide,
        ],
        input_output_aliases={first + i: i for i in range(len(earlier))},
        scratch_shapes=[
            pltpu.VMEM((group_rows, width), bf16),
            pltpu.VMEM((group_rows, width), bf16),
            pltpu.SemaphoreType.DMA((per_group,)),
            pltpu.SemaphoreType.DMA((per_group,)),
            pltpu.SemaphoreType.DMA((steps,)),
        ],
    )(*spread.arrays, *gains, qkv_weight, out_weight, *earlier)


def pairs_body(input_ref, cot_ref, gain_ref, bias_ref, pair_ref, shared_ref):
    rows = input_ref.shape[0]
    values = input_ref[...].astype(f32)
    centred = values - jnp.mean(values, axis=1, keepdims=True)
    hat = centred * lax.rsqrt(jnp.mean(centred * centred, axis=1, keepdims=True) + norm_eps)
    pair_ref[:rows, :] = input_ref[...]
    pair_ref[rows:, :] = cot_ref[...]
    shared_ref[:rows, :] = (hat * gain_ref[...] + bias_ref[...]).astype(bf16)
    shared_ref[rows:, :] = cot_ref[...]


def pairs(layer_input, cotangent, gain, bias):
    rows, width = layer_input.shape
    return call(
        pairs_body,
        "pairs",
        out_shape=[jax.ShapeDtypeStruct((2 * rows, width), bf16)] * 2,
    )(layer_input, cotangent, gain, bias)


def fold_body(near_ref, came_ref, going_ref, kept_ref, *, rows, going, kept):
    for ref, places in ((going_ref, going), (kept_ref, kept)):
        for i, at in enumerate(places):
            here = slice(at * rows, (at + 1) * rows)
            total = near_ref[here, :].astype(f32) + came_ref[here, :].astype(f32)
            ref[i * rows : (i + 1) * rows, :] = total.astype(bf16)


def fold(near, came, rows, going, kept):
    width = near.shape[1]
    tile = min(512, width)
    half = len(going) * rows
    return call(
        functools.partial(fold_body, rows=rows, going=going, kept=kept),
        "fold",
        grid=(width // tile,),
        in_specs=[pl.BlockSpec((near.shape[0], tile), lambda i: (0, i))] * 2,
        out_specs=[pl.BlockSpec((half, tile), lambda i: (0, i))] * 2,
        out_shape=[jax.ShapeDtypeStruct((half, width), bf16)] * 2,
    )(near, came)


def start(copies):
    for copy in copies:
        copy.start()


def wait(copies):
    for copy in copies:
        copy.wait()


class Branch:
    def __init__(self, arrays, weights, buffers, sems, spread, rows, block, tile):
        self.up_ref, self.shift_ref, self.down_ref = weights
        self.x_buf, self.c_buf, self.u_buf, self.d_buf = buffers
        sem_x, sem_c, sem_u, sem_d = sems
        self.block = block
        self.every = range(self.x_buf.shape[0] // block)
        units = self.u_buf.shape[1]
        self.x_copies = block_copies(spread, "a", arrays, self.x_buf, sem_x, rows, block, self.every)
        self.c_copies = block_copies(spread, "b", arrays, self.c_buf, sem_c, rows, block, self.every)
        self.tiles = [slice(i, i + tile) for i in range(0, units, tile)]
        self.needs = []
        for i, t in enumerate(self.tiles):
            for ref, buf, sem, at in (
                (self.up_ref, self.u_buf, sem_u, (slice(None), t)),
                (self.down_ref, self.d_buf, sem_d, (t, slice(None))),
            ):
                self.needs.append([pltpu.make_async_copy(ref.at[at], buf.at[at], sem.at[i])])
        self.needs[0] = self.x_copies[0] + self.needs[0]
        self.needs[1] = self.c_copies[0] + self.needs[1]

    def block_step(self, step, hidden_ref, grad_ref, sum_ref, to_rows, extra=()):
        @pl.when(step == 0)
        def _():
            start(self.needs[0])
            sum_ref[...] = jnp.zeros_like(sum_ref)
            wait(self.needs[0])
            for need in self.needs[1:3]:
                start(need)

        for i in self.every[1:]:

            @pl.when(step == i)
            def _(i=i):
                wait(self.x_copies[i] + self.c_copies[i])

        here = pl.ds(pl.multiple_of(step * self.block, self.block), self.block)
        there = here if to_rows else slice(None)
        for i, part in enumerate(self.tiles):
            gate = dot_plain(self.x_buf[here, :], self.u_buf[:, part]) + self.shift_ref[:, part]

            @pl.when(step == 0)
            def _(i=i):
                for need in self.needs[2 * i + 1 : 2 * i + 3]:
                    wait(need)
                for need in self.needs[2 * i + 3 : 2 * i + 5]:
                    start(need)
                if i == 0:
                    for later in self.every[1:]:
                        start(self.x_copies[later] + self.c_copies[later])
                if i == len(self.tiles) - 1:
                    start(extra)

            grad_hidden = contract_cols(self.c_buf[here, :], self.d_buf[part, :])
            below = 0.5 * (1.0 + lax.erf(gate * inv_root_two))
            hidden_ref[there, part] = (gate * below).astype(bf16)
            slope = below + gate * jnp.exp(-0.5 * gate * gate) * inv_root_tau
            grad = (grad_hidden * slope).astype(bf16)
            grad_ref[there, part] = grad
            sum_ref[:, part] += jnp.sum(grad.astype(f32), axis=0, keepdims=True)


def branch_scratch(group_rows, width, units, blocks, tiles):
    dma = pltpu.SemaphoreType.DMA
    return [
        pltpu.VMEM((group_rows, width), bf16),
        pltpu.VMEM((group_rows, width), bf16),
        pltpu.VMEM((width, units), bf16),
        pltpu.VMEM((units, width), bf16),
        dma((blocks,)),
        dma((blocks,)),
        dma((tiles,)),
        dma((tiles,)),
    ]


def mlp_body(*refs, spread, rows, block, tile):
    count = len(spread.arrays)
    hidden_ref, grad_ref, sum_ref = refs[count + 3 : count + 6]
    scratch = refs[count + 6 :]
    branch = Branch(
        refs[:count], refs[count : count + 3], scratch[:4], scratch[4:], spread, rows, block, tile
    )
    branch.block_step(pl.program_id(0), hidden_ref, grad_ref, sum_ref, False)


def mlp(spread, rows, up_weight, up_bias, down_weight):
    width, units = up_weight.shape
    group_rows = rows * len(spread.names)
    block = min(512, group_rows)
    tile = min(512, units)
    steps, tiles, blocks = group_rows // block, units // tile, len(spread.names)
    anywhere = pl.BlockSpec(memory_space=pl.ANY)
    part = pl.BlockSpec((block, units), lambda i: (i, 0))
    low = jax.ShapeDtypeStruct((group_rows, units), bf16)
    row = pl.BlockSpec((1, units), lambda i: (0, 0))
    return call(
        functools.partial(mlp_body, spread=spread, rows=rows, block=block, tile=tile),
        "mlp",
        grid=(steps,),
        in_specs=[anywhere] * len(spread.arrays) + [anywhere, row, anywhere],
        out_specs=[part, part, row],
        out_shape=[low, low, jax.ShapeDtypeStruct((1, units), f32)],
        scratch_shapes=branch_scratch(group_rows, width, units, blocks, tiles),
    )(*spread.arrays, up_weight, up_bias, down_weight)


def group_body(*refs, spread, rows, block, tile, steps, ups, adds, more, places):
    count = len(spread.arrays)
    arrays, weights, refs = refs[:count], refs[count : count + 3], refs[count + 3 :]
    added, refs = refs[: 2 * adds], refs[2 * adds :]
    own, refs = refs[: 4 * more], refs[4 * more :]
    folds, refs = (refs[:2], refs[2:]) if places else ((), refs)
    up_out, down_out, sum_ref = refs[:3]
    folded, refs = (refs[3:5], refs[5:]) if places else ((), refs[3:])
    buffers, sems, (hidden_buf, grad_buf), refs = refs[:4], refs[4:8], refs[8:10], refs[10:]
    branch = Branch(arrays, weights, buffers, sems, spread, rows, block, tile)
    step = pl.program_id(0)
    at = jnp.where(step < steps + ups, step - steps, step - steps - ups)
    at = jnp.maximum(at, 0)
    here = pl.ds(pl.multiple_of(at * tile, tile), tile)
    later = []
    if adds:
        sum_up, sum_down, sem_sum_up, sem_sum_down, *refs = refs

        def up_copy(i):
            first = pl.multiple_of(i * tile, tile)
            return pltpu.make_async_copy(
                added[0].at[pl.ds(first, tile), :], sum_up.at[i % 2], sem_sum_up.at[i % 2]
            )

        def down_copy(i):
            first = pl.multiple_of(i * tile, tile)
            return pltpu.make_async_copy(
                added[1].at[:, pl.ds(first, tile)], sum_down.at[i % 2], sem_sum_down.at[i % 2]
            )

        later = later + [up_copy(0)]
    if more:
        own_bufs, sem_own = refs[:4], refs[4]
        own_copies = [
            pltpu.make_async_copy(ref, buf, sem_own.at[i])
            for i, (ref, buf) in enumerate(zip(own, own_bufs))
        ]
        later = later + own_copies
        rows_own, cot_own, hidden_own, grad_own = own_bufs

    @pl.when(step < steps)
    def _():
        branch.block_step(step, hidden_buf, grad_buf, sum_ref, True, later)

    if more:

        @pl.when(step == steps)
        def _():
            wait(own_copies)

    if places:

        @pl.when(step >= steps)
        def _():
            fold_body(*folds, *folded, rows=rows, going=places[0], kept=places[1])

    @pl.when((step >= steps) & (step < steps + ups))
    def _():
        if adds:

            @pl.when(at + 1 < ups)
            def _():
                up_copy(at + 1).start()

            @pl.when(at + 1 == ups)
            def _():
                down_copy(0).start()

            up_copy(at).wait()
        total = contract_rows(branch.x_buf[:, here], grad_buf[...])
        if more:
            total = total + contract_rows(rows_own[:, here], grad_own[...])
        if adds:
            total = total + sum_up[at % 2]
        up_out[...] = total

    @pl.when(step >= steps + ups)
    def _():
        if adds:

            @pl.when(at + 1 < ups)
            def _():
                down_copy(at + 1).start()

            down_copy(at).wait()
        total = contract_rows(hidden_buf[...], branch.c_buf[:, here])
        if more:
            total = total + contract_rows(hidden_own[...], cot_own[:, here])
        if adds:
            total = total + sum_down[at % 2]
        down_out[...] = total


def group(spread, rows, up_weight, up_bias, down_weight, added=(), own=(), folds=(), places=()):
    width, units = up_weight.shape
    group_rows = rows * len(spread.names)
    block = min(512, group_rows)
    tile = min(512, units)
    steps, tiles, blocks = group_rows // block, units // tile, len(spread.names)
    ups = width // tile
    anywhere = pl.BlockSpec(memory_space=pl.ANY)
    row = pl.BlockSpec((1, units), lambda i: (0, 0))
    dma = pltpu.SemaphoreType.DMA
    scratch = branch_scratch(group_rows, width, units, blocks, tiles)
    scratch += [pltpu.VMEM((group_rows, units), bf16)] * 2
    if added:
        scratch += [
            pltpu.VMEM((2, tile, units), f32),
            pltpu.VMEM((2, units, tile), f32),
            dma((2,)),
            dma((2,)),
        ]
    if own:
        scratch += [pltpu.VMEM(array.shape, bf16) for array in own] + [dma((4,))]
    fold_in, fold_out, fold_shape = [], [], []
    if folds:
        strip = width // (2 * ups)
        half = folds[0].shape[0] // 2

        def column(i):
            return 0, jnp.clip(i - steps, 0, 2 * ups - 1)

        fold_in = [pl.BlockSpec((2 * half, strip), column)] * 2
        fold_out = [pl.BlockSpec((half, strip), column)] * 2
        fold_shape = [jax.ShapeDtypeStruct((half, width), bf16)] * 2
    return call(
        functools.partial(
            group_body,
            spread=spread,
            rows=rows,
            block=block,
            tile=tile,
            steps=steps,
            ups=ups,
            adds=bool(added),
            more=bool(own),
            places=places,
        ),
        "group",
        grid=(steps + 2 * ups,),
        in_specs=[anywhere] * len(spread.arrays)
        + [anywhere, row, anywhere]
        + [anywhere] * (len(added) + len(own))
        + fold_in,
        out_specs=[
            pl.BlockSpec((tile, units), lambda i: (jnp.clip(i - steps, 0, ups - 1), 0)),
            pl.BlockSpec((units, tile), lambda i: (0, jnp.clip(i - steps - ups, 0, ups - 1))),
            row,
        ]
        + fold_out,
        out_shape=[
            jax.ShapeDtypeStruct((width, units), f32),
            jax.ShapeDtypeStruct((units, width), f32),
            jax.ShapeDtypeStruct((1, units), f32),
        ]
        + fold_shape,
        scratch_shapes=scratch,
    )(*spread.arrays, up_weight, up_bias, down_weight, *added, *own, *folds)


def weight_body(left_ref, right_ref, out_ref):
    out_ref[...] = contract_rows(left_ref[...], right_ref[...])


def weight_product(left, right):
    wide, deep = left.shape[1], right.shape[1]
    tile = min(512, wide)
    return call(
        weight_body,
        "weight_product",
        grid=(wide // tile,),
        in_specs=[
            pl.BlockSpec((left.shape[0], tile), lambda i: (0, i)),
            pl.BlockSpec(right.shape, lambda i: (0, 0), pipeline_mode=pl.Buffered(1)),
        ],
        out_specs=pl.BlockSpec((tile, deep), lambda i: (i, 0)),
        out_shape=jax.ShapeDtypeStruct((wide, deep), f32),
    )(left, right)


def attention_weights_body(normed_ref, grad_qkv_ref, attended_ref, grad_out_ref, sum_ref):
    deep = grad_qkv_ref.shape[1]
    sum_ref[:, :deep] = contract_rows(normed_ref[...], grad_qkv_ref[...]).astype(bf16)
    sum_ref[:, deep:] = contract_rows(attended_ref[...], grad_out_ref[...]).astype(bf16)


def attention_weights(normed, grad_qkv, attended, grad_out):
    group_rows, width = normed.shape
    deep, units = grad_qkv.shape[1], attended.shape[1]
    once = pl.Buffered(1)
    block = pl.BlockSpec((group_rows, units), lambda i: (0, i))
    return call(
        attention_weights_body,
        "attention_weights",
        grid=(width // units,),
        in_specs=[
            block,
            pl.BlockSpec(grad_qkv.shape, lambda i: (0, 0), pipeline_mode=once),
            pl.BlockSpec(attended.shape, lambda i: (0, 0), pipeline_mode=once),
            block,
        ],
        out_specs=pl.BlockSpec((units, deep + units), lambda i: (i, 0)),
        out_shape=jax.ShapeDtypeStruct((width, deep + units), bf16),
    )(normed, grad_qkv, attended, grad_out)


def widen_body(sum_ref, qkv_ref, out_ref):
    units, deep = out_ref.shape[0], qkv_ref.shape[1]
    qkv_ref[...] = sum_ref[:, :deep].astype(f32)
    for first in range(0, sum_ref.shape[0], units):
        out_ref[:, first : first + units] = sum_ref[first : first + units, deep:].astype(f32)


def widen(total, deep, units):
    width = total.shape[0]
    block = min(2 * units, width)
    return call(
        widen_body,
        "widen",
        grid=(width // block,),
        in_specs=[pl.BlockSpec((block, deep + units), lambda i: (i, 0))],
        out_specs=[
            pl.BlockSpec((block, deep), lambda i: (i, 0)),
            pl.BlockSpec((units, block), lambda i: (0, i)),
        ],
        out_shape=[
            jax.ShapeDtypeStruct((width, deep), f32),
            jax.ShapeDtypeStruct((units, width), f32),
        ],
    )(total)


def branch_body(attended_ref, hidden_ref, out_ref, down_ref, near_ref, far_ref):
    middle = near_ref.shape[0]
    total = dot_plain(attended_ref[...], out_ref[...]) + dot_plain(hidden_ref[...], down_ref[...])
    near_ref[...] = total[:middle].astype(bf16)
    far_ref[...] = total[middle:].astype(bf16)


def branch_sum(attended, hidden, out_weight, down_weight):
    group_rows = attended.shape[0]
    width = out_weight.shape[1]
    tile = min(512, width)
    once = pl.Buffered(1)
    half = pl.BlockSpec((group_rows // 2, tile), lambda i: (0, i))
    return call(
        branch_body,
        "branch_sum",
        grid=(width // tile,),
        in_specs=[
            pl.BlockSpec(attended.shape, lambda i: (0, 0), pipeline_mode=once),
            pl.BlockSpec(hidden.shape, lambda i: (0, 0), pipeline_mode=once),
            pl.BlockSpec((out_weight.shape[0], tile), lambda i: (0, i)),
            pl.BlockSpec((down_weight.shape[0], tile), lambda i: (0, i)),
        ],
        out_specs=[half, half],
        out_shape=[jax.ShapeDtypeStruct((group_rows // 2, width), bf16)] * 2,
    )(attended, hidden, out_weight, down_weight)


def input_body(
    qkv_grad_ref, gate_grad_ref, qkv_ref, up_ref, gain1, gain2, hat_ref, near_ref, far_ref, sum_ref
):
    middle = near_ref.shape[0]
    hat = hat_ref[...].astype(f32)
    first = contract_cols(qkv_grad_ref[...], qkv_ref[...])
    second = contract_cols(gate_grad_ref[...], up_ref[...])
    both = first * gain1[...] + second * gain2[...]
    near_ref[...] = both[:middle].astype(bf16)
    far_ref[...] = both[middle:].astype(bf16)
    sum_ref[0:1, :] = jnp.sum(first * hat, axis=0, keepdims=True)
    sum_ref[1:2, :] = jnp.sum(first, axis=0, keepdims=True)
    sum_ref[2:3, :] = jnp.sum(second * hat, axis=0, keepdims=True)
    sum_ref[3:4, :] = jnp.sum(second, axis=0, keepdims=True)


def input_sums(grad_qkv, grad_gate, qkv_weight, up_weight, gain1, gain2, hat):
    group_rows = grad_qkv.shape[0]
    width = qkv_weight.shape[0]
    tile = min(256, width)
    once = pl.Buffered(1)
    half = pl.BlockSpec((group_rows // 2, tile), lambda i: (0, i))
    row = pl.BlockSpec((1, tile), lambda i: (0, i))
    return call(
        input_body,
        "input_sums",
        grid=(width // tile,),
        in_specs=[
            pl.BlockSpec(grad_qkv.shape, lambda i: (0, 0), pipeline_mode=once),
            pl.BlockSpec(grad_gate.shape, lambda i: (0, 0), pipeline_mode=once),
            pl.BlockSpec((tile, qkv_weight.shape[1]), lambda i: (i, 0)),
            pl.BlockSpec((tile, up_weight.shape[1]), lambda i: (i, 0)),
            row,
            row,
            pl.BlockSpec((group_rows, tile), lambda i: (0, i)),
        ],
        out_specs=[half, half, pl.BlockSpec((4, tile), lambda i: (0, i))],
        out_shape=[jax.ShapeDtypeStruct((group_rows // 2, width), bf16)] * 2
        + [jax.ShapeDtypeStruct((4, width), f32)],
    )(grad_qkv, grad_gate, qkv_weight, up_weight, gain1, gain2, hat)


def attention_body(
    own_ref,
    starts_ref,
    raw_ref,
    bias_ref,
    cos_ref,
    sine_ref,
    slope_in_ref,
    attended_ref,
    grad_qkv_ref,
    bias_grad_ref,
    query_ref,
    key_ref,
    value_ref,
    slope_ref,
    query_sum_ref,
    key_sum_ref,
    value_sum_ref,
    *,
    rows,
    names,
    block_rows,
    longest,
):
    own = own_ref[0]
    group_rows = rows * len(names)
    lane = lax.broadcasted_iota(jnp.int32, (rows, HEAD_DIM), 1)
    half = ROTARY // 2
    scale = HEAD_DIM ** (-0.5)

    def turned(u):
        return jnp.where(lane < half, pltpu.roll(u, HEAD_DIM - half, 1), pltpu.roll(u, half, 1))

    def far_rows(name):
        return pl.ds(pl.multiple_of((own ^ name) * rows, rows), rows)

    for i, name in enumerate(names):
        near = slice(i * rows, (i + 1) * rows)
        far = far_rows(name)
        raw = raw_ref[near, :] + bias_ref[...]
        cos_table = cos_ref[near, :]
        sine_table = sine_ref[near, :]
        query = raw[:, :HEAD_DIM]
        key = raw[:, HEAD_DIM : 2 * HEAD_DIM]
        query_ref[far, :] = (query * cos_table + turned(query) * sine_table).astype(bf16)
        key_ref[far, :] = (key * cos_table + turned(key) * sine_table).astype(bf16)
        value_ref[far, :] = raw[:, 2 * HEAD_DIM :].astype(bf16)
        slope_ref[far, :] = slope_in_ref[near, :]
    key_sum_ref[...] = jnp.zeros_like(key_sum_ref)
    value_sum_ref[...] = jnp.zeros_like(value_sum_ref)
    for first in range(0, group_rows, block_rows):
        last = first + block_rows
        low = max(0, (first - longest + 1) // 128 * 128)
        query = query_ref[first:last, :]
        keys = key_ref[low:last, :]
        values = value_ref[low:last, :]
        slope = slope_ref[first:last, :]
        scores = contract_cols(query, keys) * scale
        row = first + lax.broadcasted_iota(jnp.int32, (block_rows, 1), 0)
        begin = jnp.zeros((block_rows, 1), jnp.int32)
        for slot in range(starts_ref.shape[0]):
            begin = jnp.where(starts_ref[slot] <= row, starts_ref[slot], begin)
        column = low + lax.broadcasted_iota(jnp.int32, scores.shape, 1)
        scores = jnp.where((column >= begin) & (column <= row), scores, masked_score)
        peak = jnp.max(scores, axis=1, keepdims=True)
        raised = jnp.exp(scores - peak)
        probs = raised * (1.0 / jnp.sum(raised, axis=1, keepdims=True))
        probs_low = probs.astype(bf16)
        query_ref[first:last, :] = dot_plain(probs_low, values).astype(bf16)
        grad_probs = contract_cols(slope, values)
        delta = jnp.sum(grad_probs * probs, axis=1, keepdims=True)
        grad_score = (probs * (grad_probs - delta)).astype(bf16)
        query_sum_ref[first:last, :] = dot_plain(grad_score, keys) * scale
        key_sum_ref[low:last, :] += contract_rows(grad_score, query) * scale
        value_sum_ref[low:last, :] += contract_rows(probs_low, slope)
    bias_grad = jnp.zeros(bias_grad_ref.shape, f32)
    for i, name in enumerate(names):
        near = slice(i * rows, (i + 1) * rows)
        far = far_rows(name)
        cos_table = cos_ref[near, :]
        sine_table = sine_ref[near, :]
        query_grad = query_sum_ref[far, :]
        key_grad = key_sum_ref[far, :]
        grads = jnp.concatenate(
            [
                query_grad * cos_table - turned(query_grad) * sine_table,
                key_grad * cos_table - turned(key_grad) * sine_table,
                value_sum_ref[far, :],
            ],
            axis=1,
        ).astype(bf16)
        grad_qkv_ref[near, :] = grads
        bias_grad = bias_grad + jnp.sum(grads.astype(f32), axis=0, keepdims=True)
        attended_ref[near, :] = query_ref[far, :]
    bias_grad_ref[...] = bias_grad


def attention(own, starts, raw, bias, cos_table, sine_table, slope, rows, names):
    group_rows, width = raw.shape
    part = 3 * HEAD_DIM
    heads = width // part
    whole = pl.BlockSpec((group_rows, HEAD_DIM), lambda h: (0, 0))
    scalars = pl.BlockSpec(memory_space=pltpu.SMEM)
    low = pltpu.VMEM((group_rows, HEAD_DIM), bf16)
    wide = pltpu.VMEM((group_rows, HEAD_DIM), f32)
    longest = group_rows // 2
    return pl.pallas_call(
        functools.partial(
            attention_body,
            rows=rows,
            names=names,
            block_rows=min(256, group_rows),
            longest=longest,
        ),
        grid=(heads,),
        in_specs=[
            scalars,
            scalars,
            pl.BlockSpec((group_rows, part), lambda h: (0, h)),
            pl.BlockSpec((1, part), lambda h: (0, h)),
            whole,
            whole,
            pl.BlockSpec((group_rows, HEAD_DIM), lambda h: (0, h)),
        ],
        out_specs=[
            pl.BlockSpec((group_rows, HEAD_DIM), lambda h: (0, h)),
            pl.BlockSpec((group_rows, part), lambda h: (0, h)),
            pl.BlockSpec((1, part), lambda h: (0, h)),
        ],
        out_shape=[
            jax.ShapeDtypeStruct((group_rows, heads * HEAD_DIM), bf16),
            jax.ShapeDtypeStruct((group_rows, width), bf16),
            jax.ShapeDtypeStruct((1, width), f32),
        ],
        scratch_shapes=[low, low, low, low, wide, wide, wide],
        compiler_params=pltpu.CompilerParams(vmem_limit_bytes=vmem_bytes),
        cost_estimate=pl.CostEstimate(flops=1, bytes_accessed=1, transcendentals=0),
        name="attention",
    )(own, starts, raw, bias, cos_table, sine_table, slope)


def rotary_tables(position):
    half_rot = ROTARY // 2
    frequency = 10000.0 ** (-2.0 * jnp.arange(half_rot, dtype=f32) / ROTARY)
    angles = position.astype(f32)[:, None] * frequency[None, :]
    cos_half = jnp.cos(angles)
    sine_half = jnp.sin(angles)
    rest = (position.shape[0], HEAD_DIM - ROTARY)
    return (
        jnp.concatenate([cos_half, cos_half, jnp.ones(rest, f32)], axis=1),
        jnp.concatenate([-sine_half, sine_half, jnp.zeros(rest, f32)], axis=1),
    )


def butterfly(value, axis, count, bit):
    return value + swap(value, axis, count, bit)


def fence(*values):
    return lax.optimization_barrier(values)


def norm_own(layer_input):
    values = layer_input.astype(f32)
    centred = values - jnp.mean(values, axis=-1, keepdims=True)
    inv_std = lax.rsqrt(jnp.mean(centred * centred, axis=-1, keepdims=True) + norm_eps)
    return centred * inv_std, inv_std


def tables(own, lengths, names, rows):
    seq_ends = jnp.cumsum(lengths)
    seq_starts = seq_ends - lengths
    places = (
        (own ^ jnp.array(names, jnp.int32))[:, None] * rows
        + jnp.arange(rows, dtype=jnp.int32)[None, :]
    ).reshape(-1)
    seq_first = jnp.max(
        jnp.where(seq_starts[None, :] <= places[:, None], seq_starts[None, :], 0), axis=1
    )
    return (seq_starts, *rotary_tables(places - seq_first))


def contiguous(first, second, names, rows):
    places = [{n: (which, i * rows) for i, n in enumerate(names)} for which in range(2)]
    return Spread([first, second], *places, names)


def ends(layer_input, cotangent, xhat, inv_std, branch, scaled, biases):
    layer_output = (layer_input.astype(f32) + branch + biases).astype(bf16)
    input_grad = cotangent.astype(f32) + inv_std * (
        scaled
        - jnp.mean(scaled, axis=-1, keepdims=True)
        - xhat * jnp.mean(scaled * xhat, axis=-1, keepdims=True)
    )
    return layer_output, input_grad


def per_device(
    layer_input,
    lengths,
    norm1_gain,
    norm1_bias,
    norm2_gain,
    norm2_bias,
    qkv_weight,
    qkv_bias,
    out_weight,
    out_bias,
    up_weight,
    up_bias,
    down_weight,
    down_bias,
    cotangent,
):
    dp = lax.axis_size("dp")
    mp = lax.axis_size("mp")
    own = lax.axis_index("mp")
    rows, width = layer_input.shape
    up_row = up_bias[None, :]
    gains = (norm1_gain[None, :], norm1_bias[None, :], norm2_gain[None, :], norm2_bias[None, :])
    gather_all = mp == 8 and dp == 4 and 4 * rows * mp * dp * (width + up_bias.shape[0]) < most_gathered

    pair, shared = pairs(layer_input, cotangent, *gains[2:])
    if gather_all:
        names = four_names
        sides = spread_sides(pair, mp)
        group_a = turn(shared, "dp", dp, 1)
        placed = tables(own, lengths[0], names, rows)
        far = spread_core([pair], mp)
        shared, pair, sides, placed, far, group_a = fence(shared, pair, sides, placed, far, group_a)
        group_b = turn(shared, "dp", dp, -1)
        corner = spread_corner(sides, mp)
        near = [pair, *sides]
        far = far + spread_core(sides, mp)
        begun = entry(spread_four(near, far), rows, gains, qkv_weight, out_weight, 0, 2)
        near, far, corner, group_a, begun = fence(near, far, corner, group_a, begun)
        near, far = near + corner, far + spread_core(corner, mp)
        sides_a = spread_sides(group_a, mp)
        entered = entry(spread_four(near, far), rows, gains, qkv_weight, out_weight, 1, 2, begun)
        entered, group_b, group_a = fence(entered, group_b, group_a)
        far_a = spread_core([group_a], mp)
        group_c = turn(group_a, "dp", dp, 1)
    else:
        spread = spread_any(pair, mp)
        names = spread.names
        placed = tables(own, lengths[0], names, rows)
        entered = entry(spread, rows, gains, qkv_weight, out_weight)
    seq_starts, cos_table, sine_table = placed

    first_all, second_all, hat, raw, grad_attended, grad_out = entered
    attended, grad_qkv, qkv_bias_part = attention(
        own.reshape(1),
        seq_starts,
        raw,
        qkv_bias[None, :],
        cos_table,
        sine_table,
        grad_attended,
        rows,
        names,
    )
    if gather_all:
        (first_all, second_all, hat, grad_out, attended, grad_qkv), near_a, far_a, group_b = fence(
            (first_all, second_all, hat, grad_out, attended, grad_qkv),
            [group_a, *sides_a],
            far_a,
            group_b,
        )

    weights_part = attention_weights(first_all, grad_qkv, attended, grad_out)
    if gather_all:
        corner_a = spread_corner(near_a[1:], mp)
        far_a = far_a + spread_core(near_a[1:], mp)
        (weights_part, second_all, hat, grad_out, attended), near_a, corner_a, far_a, group_b, group_c = (
            fence(
                (weights_part, second_all, hat, grad_out, attended),
                near_a,
                corner_a,
                far_a,
                group_b,
                group_c,
            )
        )
    weights_sum = lax.psum_scatter(weights_part, "dp", scatter_dimension=0, tiled=True)

    own_spread = contiguous(second_all, grad_out, names, rows)
    hidden, grad_gate, gate_sum = mlp(own_spread, rows, up_weight, up_row, down_weight)
    branch = branch_sum(attended, hidden, out_weight, down_weight)
    if gather_all:
        sides_b = spread_sides(group_b, mp)
        far_b = spread_core([group_b], mp)
        far_a = far_a + spread_core(corner_a, mp)
        near_a = near_a + corner_a
        (hidden, grad_gate, branch, grad_qkv, hat), near_a, far_a, near_b, far_b, group_c = fence(
            (hidden, grad_gate, branch, grad_qkv, hat),
            near_a,
            far_a,
            [group_b, *sides_b],
            far_b,
            group_c,
        )

    scaled = input_sums(grad_qkv, grad_gate, qkv_weight, up_weight, gains[0], gains[2], hat)
    cot_sum = jnp.sum(cotangent.astype(f32), axis=0)
    small = jnp.concatenate([scaled[2].reshape(-1), cot_sum, qkv_bias_part.reshape(-1)])
    small = small.reshape(-1, 128)
    five = 5 * width // 128
    biases = out_bias + down_bias
    xhat, inv_std = norm_own(layer_input)

    def over_mp(both, bit):
        return jnp.concatenate([butterfly(both[:five], "mp", mp, bit), both[five:]], axis=0)

    if not gather_all:
        own_branch = scatter_group(*branch, names, mp, rows)
        own_scaled = scatter_group(*scaled[:2], names, mp, rows)
        layer_output, input_grad = ends(
            layer_input, cotangent, xhat, inv_std, own_branch, own_scaled, biases
        )
        for bit in (1 << i for i in range(dp.bit_length() - 1)):
            small = butterfly(small, "dp", dp, bit)
        small, qkv_bias_grad = small[:five], small[five:]
        for bit in (1 << i for i in range(mp.bit_length() - 1)):
            small = butterfly(small, "mp", mp, bit)
        weights_sum = lax.all_gather(weights_sum, "dp", axis=0, tiled=True)
        up_weight_grad, down_weight_grad, up_bias_grad = lax.psum(
            (weight_product(second_all, grad_gate), weight_product(hidden, grad_out), gate_sum[0]),
            "dp",
        )
    else:
        corner_b = spread_corner(near_b[1:], mp)
        far_b = far_b + spread_core(near_b[1:], mp)
        branch_came = swap(branch[1], "mp", mp, 1)
        scaled, small, near_a, far_a, near_b, far_b, corner_b, branch_came, group_c = fence(
            scaled, small, near_a, far_a, near_b, far_b, corner_b, branch_came, group_c
        )

        own_branch = Scatter(branch[0], branch_came, names, mp, rows, True)
        small = over_mp(small, 1)
        sides_c = spread_sides(group_c, mp)
        scaled_came = swap(scaled[1], "mp", mp, 1)
        far_b = far_b + spread_core(corner_b, mp)
        near_b = near_b + corner_b
        up_sum, down_sum, sum_a, *branch_sent = group(
            spread_four(near_a, far_a),
            rows,
            up_weight,
            up_row,
            down_weight,
            folds=(branch[0], branch_came),
            places=own_branch.places(),
        )
        sums, near_b, far_b, near_c, branch_sent, scaled_came, small, weights_sum = fence(
            (up_sum, down_sum),
            near_b,
            far_b,
            [group_c, *sides_c],
            branch_sent,
            scaled_came,
            small,
            weights_sum,
        )

        weights_sum = lax.all_gather(weights_sum, "dp", axis=0, tiled=True)
        own_scaled = Scatter(scaled[0], scaled_came, names, mp, rows, False)
        scaled_sent = fold(scaled[0], scaled_came, rows, *own_scaled.places())
        far_c = spread_core(near_c[:1], mp)
        corner_c = spread_corner(near_c[1:], mp)
        small = over_mp(small, 2)
        scaled_sent, branch_sent, far_c, small, sums = fence(
            scaled_sent, branch_sent, far_c, small, sums
        )
        up_sum, down_sum, sum_b = group(
            spread_four(near_b, far_b), rows, up_weight, up_row, down_weight, sums
        )
        sums, near_c, far_c, corner_c, branch_came, branch_kept, scaled_came, scaled_kept, small = fence(
            (up_sum, down_sum),
            near_c,
            far_c,
            corner_c,
            own_branch.swapped(branch_sent[0]),
            branch_sent[1],
            own_scaled.swapped(scaled_sent[0]),
            scaled_sent[1],
            small,
        )

        far_c = far_c + spread_core(near_c[1:] + corner_c, mp)
        near_c = near_c + corner_c
        small = over_mp(small, 4)
        own_branch.take(own_branch.listed(branch_kept), branch_came)
        own_scaled.take(own_scaled.listed(scaled_kept), scaled_came)
        near_c, far_c, small, branch_sent, scaled_sent = fence(
            near_c, far_c, small, own_branch.sent(), own_scaled.sent()
        )
        up_weight_grad, down_weight_grad, sum_c = group(
            spread_four(near_c, far_c),
            rows,
            up_weight,
            up_row,
            down_weight,
            sums,
            (second_all, grad_out, hidden, grad_gate),
        )
        up_weight_grad, branch_came, branch_kept, scaled_came, scaled_kept, small_came, weights_sum = (
            fence(
                up_weight_grad,
                own_branch.swapped(branch_sent[0]),
                branch_sent[1],
                own_scaled.swapped(scaled_sent[0]),
                scaled_sent[1],
                swap(small, "dp", dp, 1),
                weights_sum,
            )
        )
        own_branch.take(branch_kept, branch_came)
        own_scaled.take(scaled_kept, scaled_came)
        branch_total, scaled_total = own_branch.total(0), own_scaled.total(0)
        small = small + small_came

        small = butterfly(small, "dp", dp, 2)
        layer_output, input_grad = ends(
            layer_input, cotangent, xhat, inv_std, branch_total, scaled_total, biases
        )
        up_bias_grad = (gate_sum + sum_a + sum_b + sum_c)[0]
        small, qkv_bias_grad = small[:five], small[five:]
    qkv_weight_grad, out_weight_grad = widen(weights_sum, qkv_weight.shape[1], out_weight.shape[0])
    small = small.reshape(5, width)
    return (
        layer_output,
        input_grad,
        small[0],
        small[1],
        small[2],
        small[3],
        qkv_weight_grad,
        qkv_bias_grad.reshape(-1),
        out_weight_grad,
        small[4],
        up_weight_grad,
        up_bias_grad,
        down_weight_grad,
        small[4],
    )


def solution(mesh):
    in_specs = (
        P(("dp", "mp"), None),
        P("dp", None),
        P(),
        P(),
        P(),
        P(),
        P(None, "mp"),
        P("mp"),
        P("mp", None),
        P(),
        P(None, "mp"),
        P("mp"),
        P("mp", None),
        P(),
        P(("dp", "mp"), None),
    )
    out_specs = (
        P(("dp", "mp"), None),
        P(("dp", "mp"), None),
        P(),
        P(),
        P(),
        P(),
        P(None, "mp"),
        P("mp"),
        P("mp", None),
        P(),
        P(None, "mp"),
        P("mp"),
        P("mp", None),
        P(),
    )
    return jax.shard_map(
        per_device, mesh=mesh, in_specs=in_specs, out_specs=out_specs, check_vma=False
    )
```

```python
import functools

import jax
import jax.numpy as jnp
from jax import lax
from jax.experimental import pallas as pl
from jax.experimental.pallas import tpu as pltpu
from jax.sharding import PartitionSpec as P

HEAD_DIM = 128
ROTARY = 32

norm_eps = 1e-05
masked_score = -1e30
inv_root_two = 0.7071067811865476
inv_root_tau = 0.3989422804014327
vmem_bytes = 60 << 20
most_gathered = 128 << 20
bf16 = jnp.bfloat16
f32 = jnp.float32


def dot_plain(left, right):
    return jnp.dot(left, right, preferred_element_type=f32)


def contract_rows(left, right):
    return lax.dot_general(left, right, (((0,), (0,)), ((), ())), preferred_element_type=f32)


def contract_cols(left, right):
    return lax.dot_general(left, right, (((1,), (1,)), ((), ())), preferred_element_type=f32)


def swap(value, axis, count, bit):
    return lax.ppermute(value, axis, [(i, i ^ bit) for i in range(count)])


def turn(value, axis, count, step):
    return lax.ppermute(value, axis, [(i, (i + step) % count) for i in range(count)])


def chip_bits(count):
    return [1 << i for i in range(1, count.bit_length() - 1)]


def after(value, *earlier):
    return lax.optimization_barrier((value, *earlier))[0]


class Spread:
    def __init__(self, arrays, a, b, names):
        self.arrays, self.a, self.b, self.names = arrays, a, b, names


four_names = (0, 2, 4, 6, 1, 3, 5, 7)


def spread_sides(pair, count):
    return [swap(pair, "mp", count, 2), swap(pair, "mp", count, 4)]


def spread_corner(sides, count):
    a, b = cut(*sides)
    return [swap(a, "mp", count, 4), swap(b, "mp", count, 2)]


def spread_core(arrays, count):
    return [swap(array, "mp", count, 1) for array in arrays]


def spread_four(near, far):
    rows = near[0].shape[0] // 2
    a, b = {}, {}
    for core in range(2):
        base = len(near) * core
        for i, name in enumerate((0, 2, 4)):
            a[name + core] = (base + i, 0)
            b[name + core] = (base + i, rows)
        a[6 + core] = (base + 3, 0)
        b[6 + core] = (base + 4, 0)
    return Spread(near + far, a, b, four_names)


def spread_any(pair, count):
    rows = pair.shape[0] // 2
    held, names = pair.reshape(1, 2, rows, -1), [0]
    for bit in chip_bits(count) + [1]:
        held = jnp.concatenate([held, swap(held, "mp", count, bit)], axis=0)
        names = names + [n ^ bit for n in names]
    arrays = [held.reshape(2 * rows * count, -1)]
    a = {n: (0, 2 * rows * i) for i, n in enumerate(names)}
    b = {n: (0, 2 * rows * i + rows) for i, n in enumerate(names)}
    return Spread(arrays, a, b, tuple(names))


class Scatter:
    def __init__(self, near, came, names, count, rows, rising):
        self.count, self.rows = count, rows
        names = names[: len(names) // 2]
        self.blocks = {n: near[i * rows : (i + 1) * rows] for i, n in enumerate(names)}
        self.adds = {n: came[i * rows : (i + 1) * rows] for i, n in enumerate(names)}
        bits = chip_bits(count)
        self.bits = bits if rising else bits[::-1]

    def total(self, n):
        return self.blocks[n].astype(f32) + self.adds[n].astype(f32)

    def places(self):
        bit, order = self.bits[0], list(self.blocks)
        going = [i for i, n in enumerate(order) if n & bit]
        return going, [i for i, n in enumerate(order) if not n & bit]

    def listed(self, kept):
        return [kept[i : i + self.rows] for i in range(0, kept.shape[0], self.rows)]

    def sent(self):
        bit = self.bits[0]
        stay = [n for n in self.blocks if not n & bit]
        going = jnp.concatenate([self.total(n | bit).astype(bf16) for n in stay], axis=0)
        return going, [self.total(n).astype(bf16) for n in stay]

    def swapped(self, going):
        return swap(going, "mp", self.count, self.bits[0])

    def take(self, kept, came):
        bit, self.bits = self.bits[0], self.bits[1:]
        stay = [n for n in self.blocks if not n & bit]
        self.blocks = dict(zip(stay, kept))
        self.adds = {n: came[i * self.rows : (i + 1) * self.rows] for i, n in enumerate(stay)}


def scatter_group(near, far, names, count, rows):
    scatter = Scatter(near, swap(far, "mp", count, 1), names, count, rows, True)
    while scatter.bits:
        going, kept = scatter.sent()
        scatter.take(kept, scatter.swapped(going))
    return scatter.total(0)


def call(body, name, **kwargs):
    return pl.pallas_call(
        body,
        name=name,
        compiler_params=pltpu.CompilerParams(vmem_limit_bytes=vmem_bytes),
        cost_estimate=pl.CostEstimate(flops=1, bytes_accessed=1, transcendentals=0),
        **kwargs,
    )


def block_copies(spread, which, refs, buffer, sems, rows, block, blocks):
    per = block // rows
    listed = []
    for at in blocks:
        listed.append([])
        for i in range(at * per, (at + 1) * per):
            array, first = getattr(spread, which)[spread.names[i]]
            listed[-1].append(
                pltpu.make_async_copy(
                    refs[array].at[first : first + rows, :],
                    buffer.at[i * rows : (i + 1) * rows, :],
                    sems.at[i],
                )
            )
    return listed


def out_copies(buffer, ref, sems, block, blocks):
    return [
        pltpu.make_async_copy(
            buffer.at[i * block : (i + 1) * block, :],
            ref.at[i * block : (i + 1) * block, :],
            sems.at[i],
        )
        for i in blocks
    ]


def entry_body(*refs, spread, rows, block, blocks, earlier):
    count = len(spread.arrays)
    arrays = refs[:count]
    (gain1, bias1, gain2, bias2, qkv_ref, out_weight_ref) = refs[count : count + 6]
    count += 6 + earlier
    (one_ref, two_ref, hat_ref, raw_ref, grad_ref, cot_ref) = refs[count : count + 6]
    x_buf, c_buf, sem_x, sem_c, sem_out = refs[count + 6 :]
    step = pl.program_id(0)
    x_copies = block_copies(spread, "a", arrays, x_buf, sem_x, rows, block, blocks)
    c_copies = block_copies(spread, "b", arrays, c_buf, sem_c, rows, block, blocks)
    outs = out_copies(c_buf, cot_ref, sem_out, block, blocks)

    @pl.when(step == 0)
    def _():
        for x_list, c_list in zip(x_copies, c_copies):
            for copy in x_list + c_list:
                copy.start()

    for i in range(len(outs)):

        @pl.when(step == i)
        def _(i=i):
            for copy in x_copies[i] + c_copies[i]:
                copy.wait()
            outs[i].start()

    here = pl.ds(pl.multiple_of((step * blocks.step + blocks.start) * block, block), block)
    values = x_buf[here, :].astype(f32)
    centred = values - jnp.mean(values, axis=1, keepdims=True)
    hat = centred * lax.rsqrt(jnp.mean(centred * centred, axis=1, keepdims=True) + norm_eps)
    hat_ref[...] = hat.astype(bf16)
    one_ref[...] = (hat * gain1[...] + bias1[...]).astype(bf16)
    two_ref[...] = (hat * gain2[...] + bias2[...]).astype(bf16)
    raw_ref[...] = dot_plain(one_ref[...], qkv_ref[...])
    grad_ref[...] = contract_cols(c_buf[here, :], out_weight_ref[...]).astype(bf16)

    @pl.when(step == len(outs) - 1)
    def _():
        for copy in outs:
            copy.wait()


def entry(spread, rows, gains, qkv_weight, out_weight, begin=0, stride=1, earlier=()):
    group_rows = rows * len(spread.names)
    width, deep = qkv_weight.shape
    units = out_weight.shape[0]
    block = min(256, group_rows)
    steps = group_rows // block
    per_group = len(spread.names)
    blocks = range(begin, steps, stride)
    once = pl.Buffered(1)

    def out_block(columns):
        return pl.BlockSpec((block, columns), lambda i: (i * stride + begin, 0))

    row = pl.BlockSpec((1, width), lambda i: (0, 0))
    anywhere = pl.BlockSpec(memory_space=pl.ANY)
    wide = jax.ShapeDtypeStruct((group_rows, width), bf16)
    first = len(spread.arrays) + 6
    return call(
        functools.partial(
            entry_body, spread=spread, rows=rows, block=block, blocks=blocks, earlier=len(earlier)
        ),
        "entry",
        grid=(len(blocks),),
        in_specs=[anywhere] * len(spread.arrays)
        + [row] * 4
        + [
            pl.BlockSpec(qkv_weight.shape, lambda i: (0, 0), pipeline_mode=once),
            pl.BlockSpec(out_weight.shape, lambda i: (0, 0), pipeline_mode=once),
        ]
        + [anywhere] * len(earlier),
        out_specs=[
            out_block(width),
            out_block(width),
            out_block(width),
            out_block(deep),
            out_block(units),
            anywhere,
        ],
        out_shape=[
            wide,
            wide,
            wide,
            jax.ShapeDtypeStruct((group_rows, deep), f32),
            jax.ShapeDtypeStruct((group_rows, units), bf16),
            wide,
        ],
        input_output_aliases={first + i: i for i in range(len(earlier))},
        scratch_shapes=[
            pltpu.VMEM((group_rows, width), bf16),
            pltpu.VMEM((group_rows, width), bf16),
            pltpu.SemaphoreType.DMA((per_group,)),
            pltpu.SemaphoreType.DMA((per_group,)),
            pltpu.SemaphoreType.DMA((steps,)),
        ],
    )(*spread.arrays, *gains, qkv_weight, out_weight, *earlier)


def pairs_body(input_ref, cot_ref, gain_ref, bias_ref, pair_ref, shared_ref):
    rows = input_ref.shape[0]
    values = input_ref[...].astype(f32)
    centred = values - jnp.mean(values, axis=1, keepdims=True)
    hat = centred * lax.rsqrt(jnp.mean(centred * centred, axis=1, keepdims=True) + norm_eps)
    pair_ref[:rows, :] = input_ref[...]
    pair_ref[rows:, :] = cot_ref[...]
    shared_ref[:rows, :] = (hat * gain_ref[...] + bias_ref[...]).astype(bf16)
    shared_ref[rows:, :] = cot_ref[...]


def pairs(layer_input, cotangent, gain, bias):
    rows, width = layer_input.shape
    return call(
        pairs_body,
        "pairs",
        out_shape=[jax.ShapeDtypeStruct((2 * rows, width), bf16)] * 2,
    )(layer_input, cotangent, gain, bias)


def fold_body(near_ref, came_ref, going_ref, kept_ref, *, rows, going, kept):
    for ref, places in ((going_ref, going), (kept_ref, kept)):
        for i, at in enumerate(places):
            here = slice(at * rows, (at + 1) * rows)
            total = near_ref[here, :].astype(f32) + came_ref[here, :].astype(f32)
            ref[i * rows : (i + 1) * rows, :] = total.astype(bf16)


def folds_body(*refs, count):
    for ref in range(2 * count):
        total = refs[2 * ref][...].astype(f32) + refs[2 * ref + 1][...].astype(f32)
        refs[4 * count + ref][...] = total.astype(bf16)


def fold(sums, rows):
    width = sums[0][0].shape[1]
    operands, in_specs = [], []
    for near, came, places in sums:
        for first, *more in places:
            apart = more[0] - first if more else 0
            spec = pl.BlockSpec((rows, width), lambda i, a=apart, f=first: (a * i + f, 0))
            operands += [near, came]
            in_specs += [spec, spec]
    per = len(sums[0][2][0])
    return call(
        functools.partial(folds_body, count=len(sums)),
        "fold",
        grid=(per,),
        in_specs=in_specs,
        out_specs=[pl.BlockSpec((rows, width), lambda i: (i, 0))] * (2 * len(sums)),
        out_shape=[jax.ShapeDtypeStruct((per * rows, width), bf16)] * (2 * len(sums)),
    )(*operands)


def cut_body(side_x, side_y, x_ref, y_ref, sems):
    rows = x_ref.shape[0]
    copies = [
        pltpu.make_async_copy(side_x.at[:rows, :], x_ref, sems.at[0]),
        pltpu.make_async_copy(side_y.at[rows:, :], y_ref, sems.at[1]),
    ]
    start(copies)
    wait(copies)


def cut(side_x, side_y):
    rows, width = side_x.shape
    anywhere = pl.BlockSpec(memory_space=pl.ANY)
    return call(
        cut_body,
        "cut",
        in_specs=[anywhere] * 2,
        out_specs=[anywhere] * 2,
        out_shape=[jax.ShapeDtypeStruct((rows // 2, width), side_x.dtype)] * 2,
        scratch_shapes=[pltpu.SemaphoreType.DMA((2,))],
    )(side_x, side_y)


def start(copies):
    for copy in copies:
        copy.start()


def wait(copies):
    for copy in copies:
        copy.wait()


class Branch:
    def __init__(self, arrays, weights, buffers, sems, spread, rows, block, tile):
        self.up_ref, self.shift_ref, self.down_ref = weights
        self.x_buf, self.c_buf, self.u_buf, self.d_buf = buffers
        sem_x, sem_c, sem_u, sem_d = sems
        self.block = block
        self.every = range(self.x_buf.shape[0] // block)
        units = self.u_buf.shape[1]
        self.x_copies = block_copies(spread, "a", arrays, self.x_buf, sem_x, rows, block, self.every)
        self.c_copies = block_copies(spread, "b", arrays, self.c_buf, sem_c, rows, block, self.every)
        self.tiles = [slice(i, i + tile) for i in range(0, units, tile)]
        ups = [
            pltpu.make_async_copy(self.up_ref.at[:, t], self.u_buf.at[:, t], sem_u.at[i])
            for i, t in enumerate(self.tiles)
        ]
        downs = [
            pltpu.make_async_copy(self.down_ref.at[t, :], self.d_buf.at[t, :], sem_d.at[i])
            for i, t in enumerate(self.tiles)
        ]
        self.needs = [self.x_copies[0] + ups, self.c_copies[0] + downs]

    def block_step(self, step, hidden_ref, grad_ref, sum_ref, to_rows, prior_ref, extra=()):
        @pl.when(step == 0)
        def _():
            start(self.needs[0])
            sum_ref[...] = jnp.zeros_like(sum_ref) if prior_ref is None else prior_ref[...]
            wait(self.needs[0])
            start(self.needs[1])

        for i in self.every[1:]:

            @pl.when(step == i)
            def _(i=i):
                wait(self.x_copies[i] + self.c_copies[i])

        here = pl.ds(pl.multiple_of(step * self.block, self.block), self.block)
        there = here if to_rows else slice(None)
        gates = [
            dot_plain(self.x_buf[here, :], self.u_buf[:, part]) + self.shift_ref[:, part]
            for part in self.tiles
        ]

        @pl.when(step == 0)
        def _():
            wait(self.needs[1])
            for later in self.every[1:]:
                start(self.x_copies[later] + self.c_copies[later])
            start(extra)

        for gate, part in zip(gates, self.tiles):
            grad_hidden = contract_cols(self.c_buf[here, :], self.d_buf[part, :])
            below = 0.5 * (1.0 + lax.erf(gate * inv_root_two))
            hidden_ref[there, part] = (gate * below).astype(bf16)
            slope = below + gate * jnp.exp(-0.5 * gate * gate) * inv_root_tau
            grad = (grad_hidden * slope).astype(bf16)
            grad_ref[there, part] = grad
            sum_ref[:, part] += jnp.sum(grad.astype(f32), axis=0, keepdims=True)


def branch_scratch(group_rows, width, units, blocks, tiles):
    dma = pltpu.SemaphoreType.DMA
    return [
        pltpu.VMEM((group_rows, width), bf16),
        pltpu.VMEM((group_rows, width), bf16),
        pltpu.VMEM((width, units), bf16),
        pltpu.VMEM((units, width), bf16),
        dma((blocks,)),
        dma((blocks,)),
        dma((tiles,)),
        dma((tiles,)),
    ]


def mlp_body(*refs, spread, rows, block, tile):
    count = len(spread.arrays)
    hidden_ref, grad_ref, sum_ref = refs[count + 3 : count + 6]
    scratch = refs[count + 6 :]
    branch = Branch(
        refs[:count], refs[count : count + 3], scratch[:4], scratch[4:], spread, rows, block, tile
    )
    branch.block_step(pl.program_id(0), hidden_ref, grad_ref, sum_ref, False, None)


def mlp(spread, rows, up_weight, up_bias, down_weight):
    width, units = up_weight.shape
    group_rows = rows * len(spread.names)
    block = min(512, group_rows)
    tile = min(512, units)
    steps, tiles, blocks = group_rows // block, units // tile, len(spread.names)
    anywhere = pl.BlockSpec(memory_space=pl.ANY)
    part = pl.BlockSpec((block, units), lambda i: (i, 0))
    low = jax.ShapeDtypeStruct((group_rows, units), bf16)
    row = pl.BlockSpec((1, units), lambda i: (0, 0))
    return call(
        functools.partial(mlp_body, spread=spread, rows=rows, block=block, tile=tile),
        "mlp",
        grid=(steps,),
        in_specs=[anywhere] * len(spread.arrays) + [anywhere, row, anywhere],
        out_specs=[part, part, row],
        out_shape=[low, low, jax.ShapeDtypeStruct((1, units), f32)],
        scratch_shapes=branch_scratch(group_rows, width, units, blocks, tiles),
    )(*spread.arrays, up_weight, up_bias, down_weight)


def group_body(*refs, spread, rows, block, tile, steps, ups, adds, more, places):
    count = len(spread.arrays)
    arrays, weights, refs = refs[:count], refs[count : count + 3], refs[count + 3 :]
    prior_ref, *refs = refs
    added, refs = refs[: 2 * adds], refs[2 * adds :]
    own, refs = refs[: 4 * more], refs[4 * more :]
    folds, refs = (refs[:2], refs[2:]) if places else ((), refs)
    up_out, down_out, sum_ref = refs[:3]
    folded, refs = (refs[3:5], refs[5:]) if places else ((), refs[3:])
    buffers, sems, (hidden_buf, grad_buf), refs = refs[:4], refs[4:8], refs[8:10], refs[10:]
    branch = Branch(arrays, weights, buffers, sems, spread, rows, block, tile)
    step = pl.program_id(0)
    at = jnp.where(step < steps + ups, step - steps, step - steps - ups)
    at = jnp.maximum(at, 0)
    here = pl.ds(pl.multiple_of(at * tile, tile), tile)
    later = []
    if adds:
        sum_up, sum_down, sem_sum_up, sem_sum_down, *refs = refs

        def up_copy(i):
            first = pl.multiple_of(i * tile, tile)
            return pltpu.make_async_copy(
                added[0].at[pl.ds(first, tile), :], sum_up.at[i % 2], sem_sum_up.at[i % 2]
            )

        def down_copy(i):
            first = pl.multiple_of(i * tile, tile)
            return pltpu.make_async_copy(
                added[1].at[:, pl.ds(first, tile)], sum_down.at[i % 2], sem_sum_down.at[i % 2]
            )

        later = later + [up_copy(0)]
    if more:
        own_bufs, sem_own = refs[:4], refs[4]
        own_copies = [
            pltpu.make_async_copy(ref, buf, sem_own.at[i])
            for i, (ref, buf) in enumerate(zip(own, own_bufs))
        ]
        later = later + own_copies
        rows_own, cot_own, hidden_own, grad_own = own_bufs

    @pl.when(step < steps)
    def _():
        branch.block_step(step, hidden_buf, grad_buf, sum_ref, True, prior_ref, later)

    if more:

        @pl.when(step == steps)
        def _():
            wait(own_copies)

    if places:

        @pl.when(step >= steps)
        def _():
            fold_body(*folds, *folded, rows=rows, going=places[0], kept=places[1])

    @pl.when((step >= steps) & (step < steps + ups))
    def _():
        if adds:

            @pl.when(at + 1 < ups)
            def _():
                up_copy(at + 1).start()

            @pl.when(at + 1 == ups)
            def _():
                down_copy(0).start()

            up_copy(at).wait()
        total = contract_rows(branch.x_buf[:, here], grad_buf[...])
        if more:
            total = total + contract_rows(rows_own[:, here], grad_own[...])
        if adds:
            total = total + sum_up[at % 2]
        up_out[...] = total

    @pl.when(step >= steps + ups)
    def _():
        if adds:

            @pl.when(at + 1 < ups)
            def _():
                down_copy(at + 1).start()

            down_copy(at).wait()
        total = contract_rows(hidden_buf[...], branch.c_buf[:, here])
        if more:
            total = total + contract_rows(hidden_own[...], cot_own[:, here])
        if adds:
            total = total + sum_down[at % 2]
        down_out[...] = total


def group(spread, rows, up_weight, up_bias, down_weight, prior, added=(), own=(), folds=(), places=()):
    width, units = up_weight.shape
    group_rows = rows * len(spread.names)
    block = min(512, group_rows)
    tile = min(512, units)
    steps, tiles, blocks = group_rows // block, units // tile, len(spread.names)
    ups = width // tile
    anywhere = pl.BlockSpec(memory_space=pl.ANY)
    row = pl.BlockSpec((1, units), lambda i: (0, 0))
    dma = pltpu.SemaphoreType.DMA
    scratch = branch_scratch(group_rows, width, units, blocks, tiles)
    scratch += [pltpu.VMEM((group_rows, units), bf16)] * 2
    if added:
        scratch += [
            pltpu.VMEM((2, tile, units), f32),
            pltpu.VMEM((2, units, tile), f32),
            dma((2,)),
            dma((2,)),
        ]
    if own:
        scratch += [pltpu.VMEM(array.shape, bf16) for array in own] + [dma((4,))]
    fold_in, fold_out, fold_shape = [], [], []
    if folds:
        strip = width // (2 * ups)
        half = folds[0].shape[0] // 2

        def column(i):
            return 0, jnp.clip(i - steps, 0, 2 * ups - 1)

        fold_in = [pl.BlockSpec((2 * half, strip), column)] * 2
        fold_out = [pl.BlockSpec((half, strip), column)] * 2
        fold_shape = [jax.ShapeDtypeStruct((half, width), bf16)] * 2
    return call(
        functools.partial(
            group_body,
            spread=spread,
            rows=rows,
            block=block,
            tile=tile,
            steps=steps,
            ups=ups,
            adds=bool(added),
            more=bool(own),
            places=places,
        ),
        "group",
        grid=(steps + 2 * ups,),
        in_specs=[anywhere] * len(spread.arrays)
        + [anywhere, row, anywhere, row]
        + [anywhere] * (len(added) + len(own))
        + fold_in,
        out_specs=[
            pl.BlockSpec((tile, units), lambda i: (jnp.clip(i - steps, 0, ups - 1), 0)),
            pl.BlockSpec((units, tile), lambda i: (0, jnp.clip(i - steps - ups, 0, ups - 1))),
            row,
        ]
        + fold_out,
        out_shape=[
            jax.ShapeDtypeStruct((width, units), f32),
            jax.ShapeDtypeStruct((units, width), f32),
            jax.ShapeDtypeStruct((1, units), f32),
        ]
        + fold_shape,
        scratch_shapes=scratch,
    )(*spread.arrays, up_weight, up_bias, down_weight, prior, *added, *own, *folds)


def weight_body(left_ref, right_ref, out_ref):
    out_ref[...] = contract_rows(left_ref[...], right_ref[...])


def weight_product(left, right):
    wide, deep = left.shape[1], right.shape[1]
    tile = min(512, wide)
    return call(
        weight_body,
        "weight_product",
        grid=(wide // tile,),
        in_specs=[
            pl.BlockSpec((left.shape[0], tile), lambda i: (0, i)),
            pl.BlockSpec(right.shape, lambda i: (0, 0), pipeline_mode=pl.Buffered(1)),
        ],
        out_specs=pl.BlockSpec((tile, deep), lambda i: (i, 0)),
        out_shape=jax.ShapeDtypeStruct((wide, deep), f32),
    )(left, right)


def attention_weights_body(normed_ref, grad_qkv_ref, attended_ref, grad_out_ref, sum_ref):
    deep = grad_qkv_ref.shape[1]
    sum_ref[:, :deep] = contract_rows(normed_ref[...], grad_qkv_ref[...]).astype(bf16)
    sum_ref[:, deep:] = contract_rows(attended_ref[...], grad_out_ref[...]).astype(bf16)


def attention_weights(normed, grad_qkv, attended, grad_out):
    group_rows, width = normed.shape
    deep, units = grad_qkv.shape[1], attended.shape[1]
    once = pl.Buffered(1)
    block = pl.BlockSpec((group_rows, units), lambda i: (0, i))
    return call(
        attention_weights_body,
        "attention_weights",
        grid=(width // units,),
        in_specs=[
            block,
            pl.BlockSpec(grad_qkv.shape, lambda i: (0, 0), pipeline_mode=once),
            pl.BlockSpec(attended.shape, lambda i: (0, 0), pipeline_mode=once),
            block,
        ],
        out_specs=pl.BlockSpec((units, deep + units), lambda i: (i, 0)),
        out_shape=jax.ShapeDtypeStruct((width, deep + units), bf16),
    )(normed, grad_qkv, attended, grad_out)


def widen_body(sum_ref, qkv_ref, out_ref):
    units, deep = out_ref.shape[0], qkv_ref.shape[1]
    qkv_ref[...] = sum_ref[:, :deep].astype(f32)
    for first in range(0, sum_ref.shape[0], units):
        out_ref[:, first : first + units] = sum_ref[first : first + units, deep:].astype(f32)


def widen(total, deep, units):
    width = total.shape[0]
    block = min(2 * units, width)
    return call(
        widen_body,
        "widen",
        grid=(width // block,),
        in_specs=[pl.BlockSpec((block, deep + units), lambda i: (i, 0))],
        out_specs=[
            pl.BlockSpec((block, deep), lambda i: (i, 0)),
            pl.BlockSpec((units, block), lambda i: (0, i)),
        ],
        out_shape=[
            jax.ShapeDtypeStruct((width, deep), f32),
            jax.ShapeDtypeStruct((units, width), f32),
        ],
    )(total)


def branch_body(attended_ref, hidden_ref, out_ref, down_ref, near_ref, far_ref):
    middle = near_ref.shape[0]
    total = dot_plain(attended_ref[...], out_ref[...]) + dot_plain(hidden_ref[...], down_ref[...])
    near_ref[...] = total[:middle].astype(bf16)
    far_ref[...] = total[middle:].astype(bf16)


def branch_sum(attended, hidden, out_weight, down_weight):
    group_rows = attended.shape[0]
    width = out_weight.shape[1]
    tile = min(512, width)
    once = pl.Buffered(1)
    half = pl.BlockSpec((group_rows // 2, tile), lambda i: (0, i))
    return call(
        branch_body,
        "branch_sum",
        grid=(width // tile,),
        in_specs=[
            pl.BlockSpec(attended.shape, lambda i: (0, 0), pipeline_mode=once),
            pl.BlockSpec(hidden.shape, lambda i: (0, 0), pipeline_mode=once),
            pl.BlockSpec((out_weight.shape[0], tile), lambda i: (0, i)),
            pl.BlockSpec((down_weight.shape[0], tile), lambda i: (0, i)),
        ],
        out_specs=[half, half],
        out_shape=[jax.ShapeDtypeStruct((group_rows // 2, width), bf16)] * 2,
    )(attended, hidden, out_weight, down_weight)


def input_body(
    qkv_grad_ref, gate_grad_ref, qkv_ref, up_ref, gain1, gain2, hat_ref, near_ref, far_ref, sum_ref
):
    middle = near_ref.shape[0]
    hat = hat_ref[...].astype(f32)
    first = contract_cols(qkv_grad_ref[...], qkv_ref[...])
    second = contract_cols(gate_grad_ref[...], up_ref[...])
    both = first * gain1[...] + second * gain2[...]
    near_ref[...] = both[:middle].astype(bf16)
    far_ref[...] = both[middle:].astype(bf16)
    sum_ref[0:1, :] = jnp.sum(first * hat, axis=0, keepdims=True)
    sum_ref[1:2, :] = jnp.sum(first, axis=0, keepdims=True)
    sum_ref[2:3, :] = jnp.sum(second * hat, axis=0, keepdims=True)
    sum_ref[3:4, :] = jnp.sum(second, axis=0, keepdims=True)


def input_sums(grad_qkv, grad_gate, qkv_weight, up_weight, gain1, gain2, hat):
    group_rows = grad_qkv.shape[0]
    width = qkv_weight.shape[0]
    tile = min(256, width)
    once = pl.Buffered(1)
    half = pl.BlockSpec((group_rows // 2, tile), lambda i: (0, i))
    row = pl.BlockSpec((1, tile), lambda i: (0, i))
    return call(
        input_body,
        "input_sums",
        grid=(width // tile,),
        in_specs=[
            pl.BlockSpec(grad_qkv.shape, lambda i: (0, 0), pipeline_mode=once),
            pl.BlockSpec(grad_gate.shape, lambda i: (0, 0), pipeline_mode=once),
            pl.BlockSpec((tile, qkv_weight.shape[1]), lambda i: (i, 0)),
            pl.BlockSpec((tile, up_weight.shape[1]), lambda i: (i, 0)),
            row,
            row,
            pl.BlockSpec((group_rows, tile), lambda i: (0, i)),
        ],
        out_specs=[half, half, pl.BlockSpec((4, tile), lambda i: (0, i))],
        out_shape=[jax.ShapeDtypeStruct((group_rows // 2, width), bf16)] * 2
        + [jax.ShapeDtypeStruct((4, width), f32)],
    )(grad_qkv, grad_gate, qkv_weight, up_weight, gain1, gain2, hat)


def attention_body(
    own_ref,
    starts_ref,
    raw_ref,
    bias_ref,
    cos_ref,
    sine_ref,
    slope_in_ref,
    attended_ref,
    grad_qkv_ref,
    bias_grad_ref,
    query_ref,
    key_ref,
    value_ref,
    slope_ref,
    query_sum_ref,
    key_sum_ref,
    value_sum_ref,
    *,
    rows,
    names,
    block_rows,
    longest,
):
    own = own_ref[0]
    group_rows = rows * len(names)
    lane = lax.broadcasted_iota(jnp.int32, (rows, HEAD_DIM), 1)
    half = ROTARY // 2
    scale = HEAD_DIM ** (-0.5)

    def turned(u):
        return jnp.where(lane < half, pltpu.roll(u, HEAD_DIM - half, 1), pltpu.roll(u, half, 1))

    def far_rows(name):
        return pl.ds(pl.multiple_of((own ^ name) * rows, rows), rows)

    for i, name in enumerate(names):
        near = slice(i * rows, (i + 1) * rows)
        far = far_rows(name)
        raw = raw_ref[near, :] + bias_ref[...]
        cos_table = cos_ref[near, :]
        sine_table = sine_ref[near, :]
        query = raw[:, :HEAD_DIM]
        key = raw[:, HEAD_DIM : 2 * HEAD_DIM]
        query_ref[far, :] = (query * cos_table + turned(query) * sine_table).astype(bf16)
        key_ref[far, :] = (key * cos_table + turned(key) * sine_table).astype(bf16)
        value_ref[far, :] = raw[:, 2 * HEAD_DIM :].astype(bf16)
        slope_ref[far, :] = slope_in_ref[near, :]
    key_sum_ref[...] = jnp.zeros_like(key_sum_ref)
    value_sum_ref[...] = jnp.zeros_like(value_sum_ref)
    for first in range(0, group_rows, block_rows):
        last = first + block_rows
        low = max(0, (first - longest + 1) // 128 * 128)
        query = query_ref[first:last, :]
        keys = key_ref[low:last, :]
        values = value_ref[low:last, :]
        slope = slope_ref[first:last, :]
        scores = contract_cols(query, keys) * scale
        row = first + lax.broadcasted_iota(jnp.int32, (block_rows, 1), 0)
        begin = jnp.zeros((block_rows, 1), jnp.int32)
        for slot in range(starts_ref.shape[0]):
            begin = jnp.where(starts_ref[slot] <= row, starts_ref[slot], begin)
        column = low + lax.broadcasted_iota(jnp.int32, scores.shape, 1)
        scores = jnp.where((column >= begin) & (column <= row), scores, masked_score)
        peak = jnp.max(scores, axis=1, keepdims=True)
        raised = jnp.exp(scores - peak)
        probs = raised * (1.0 / jnp.sum(raised, axis=1, keepdims=True))
        probs_low = probs.astype(bf16)
        query_ref[first:last, :] = dot_plain(probs_low, values).astype(bf16)
        grad_probs = contract_cols(slope, values)
        delta = jnp.sum(grad_probs * probs, axis=1, keepdims=True)
        grad_score = (probs * (grad_probs - delta)).astype(bf16)
        query_sum_ref[first:last, :] = dot_plain(grad_score, keys) * scale
        key_sum_ref[low:last, :] += contract_rows(grad_score, query) * scale
        value_sum_ref[low:last, :] += contract_rows(probs_low, slope)
    bias_grad = jnp.zeros(bias_grad_ref.shape, f32)
    for i, name in enumerate(names):
        near = slice(i * rows, (i + 1) * rows)
        far = far_rows(name)
        cos_table = cos_ref[near, :]
        sine_table = sine_ref[near, :]
        query_grad = query_sum_ref[far, :]
        key_grad = key_sum_ref[far, :]
        grads = jnp.concatenate(
            [
                query_grad * cos_table - turned(query_grad) * sine_table,
                key_grad * cos_table - turned(key_grad) * sine_table,
                value_sum_ref[far, :],
            ],
            axis=1,
        ).astype(bf16)
        grad_qkv_ref[near, :] = grads
        bias_grad = bias_grad + jnp.sum(grads.astype(f32), axis=0, keepdims=True)
        attended_ref[near, :] = query_ref[far, :]
    bias_grad_ref[...] = bias_grad


def attention(own, starts, raw, bias, cos_table, sine_table, slope, rows, names):
    group_rows, width = raw.shape
    part = 3 * HEAD_DIM
    heads = width // part
    whole = pl.BlockSpec((group_rows, HEAD_DIM), lambda h: (0, 0))
    scalars = pl.BlockSpec(memory_space=pltpu.SMEM)
    low = pltpu.VMEM((group_rows, HEAD_DIM), bf16)
    wide = pltpu.VMEM((group_rows, HEAD_DIM), f32)
    longest = group_rows // 2
    return pl.pallas_call(
        functools.partial(
            attention_body,
            rows=rows,
            names=names,
            block_rows=min(256, group_rows),
            longest=longest,
        ),
        grid=(heads,),
        in_specs=[
            scalars,
            scalars,
            pl.BlockSpec((group_rows, part), lambda h: (0, h)),
            pl.BlockSpec((1, part), lambda h: (0, h)),
            whole,
            whole,
            pl.BlockSpec((group_rows, HEAD_DIM), lambda h: (0, h)),
        ],
        out_specs=[
            pl.BlockSpec((group_rows, HEAD_DIM), lambda h: (0, h)),
            pl.BlockSpec((group_rows, part), lambda h: (0, h)),
            pl.BlockSpec((1, part), lambda h: (0, h)),
        ],
        out_shape=[
            jax.ShapeDtypeStruct((group_rows, heads * HEAD_DIM), bf16),
            jax.ShapeDtypeStruct((group_rows, width), bf16),
            jax.ShapeDtypeStruct((1, width), f32),
        ],
        scratch_shapes=[low, low, low, low, wide, wide, wide],
        compiler_params=pltpu.CompilerParams(vmem_limit_bytes=vmem_bytes),
        cost_estimate=pl.CostEstimate(flops=1, bytes_accessed=1, transcendentals=0),
        name="attention",
    )(own, starts, raw, bias, cos_table, sine_table, slope)


def rotary_tables(position):
    half_rot = ROTARY // 2
    frequency = 10000.0 ** (-2.0 * jnp.arange(half_rot, dtype=f32) / ROTARY)
    angles = position.astype(f32)[:, None] * frequency[None, :]
    cos_half = jnp.cos(angles)
    sine_half = jnp.sin(angles)
    rest = (position.shape[0], HEAD_DIM - ROTARY)
    return (
        jnp.concatenate([cos_half, cos_half, jnp.ones(rest, f32)], axis=1),
        jnp.concatenate([-sine_half, sine_half, jnp.zeros(rest, f32)], axis=1),
    )


def butterfly(value, axis, count, bit):
    return value + swap(value, axis, count, bit)


def fence(*values):
    return lax.optimization_barrier(values)


def norm_own(layer_input):
    values = layer_input.astype(f32)
    centred = values - jnp.mean(values, axis=-1, keepdims=True)
    inv_std = lax.rsqrt(jnp.mean(centred * centred, axis=-1, keepdims=True) + norm_eps)
    return centred * inv_std, inv_std


def tables(own, lengths, names, rows):
    seq_ends = jnp.cumsum(lengths)
    seq_starts = seq_ends - lengths
    places = (
        (own ^ jnp.array(names, jnp.int32))[:, None] * rows
        + jnp.arange(rows, dtype=jnp.int32)[None, :]
    ).reshape(-1)
    seq_first = jnp.max(
        jnp.where(seq_starts[None, :] <= places[:, None], seq_starts[None, :], 0), axis=1
    )
    return (seq_starts, *rotary_tables(places - seq_first))


def contiguous(first, second, names, rows):
    places = [{n: (which, i * rows) for i, n in enumerate(names)} for which in range(2)]
    return Spread([first, second], *places, names)


def ends(layer_input, cotangent, xhat, inv_std, branch, scaled, biases):
    layer_output = (layer_input.astype(f32) + branch + biases).astype(bf16)
    input_grad = cotangent.astype(f32) + inv_std * (
        scaled
        - jnp.mean(scaled, axis=-1, keepdims=True)
        - xhat * jnp.mean(scaled * xhat, axis=-1, keepdims=True)
    )
    return layer_output, input_grad


def per_device(
    layer_input,
    lengths,
    norm1_gain,
    norm1_bias,
    norm2_gain,
    norm2_bias,
    qkv_weight,
    qkv_bias,
    out_weight,
    out_bias,
    up_weight,
    up_bias,
    down_weight,
    down_bias,
    cotangent,
):
    dp = lax.axis_size("dp")
    mp = lax.axis_size("mp")
    own = lax.axis_index("mp")
    rows, width = layer_input.shape
    up_row = up_bias[None, :]
    gains = (norm1_gain[None, :], norm1_bias[None, :], norm2_gain[None, :], norm2_bias[None, :])
    gather_all = mp == 8 and dp == 4 and 4 * rows * mp * dp * (width + up_bias.shape[0]) < most_gathered

    pair, shared = pairs(layer_input, cotangent, *gains[2:])
    if gather_all:
        names = four_names
        sides = spread_sides(pair, mp)
        group_a = turn(shared, "dp", dp, 1)
        placed = tables(own, lengths[0], names, rows)
        far = spread_core([pair], mp)
        shared, pair, sides, placed, far, group_a = fence(shared, pair, sides, placed, far, group_a)
        group_b = turn(shared, "dp", dp, -1)
        corner = spread_corner(sides, mp)
        near = [pair, *sides]
        far = far + spread_core(sides, mp)
        begun = entry(spread_four(near, far), rows, gains, qkv_weight, out_weight, 0, 2)
        near, far, corner, group_a, begun = fence(near, far, corner, group_a, begun)
        near, far = near + corner, far + spread_core(corner, mp)
        sides_a = spread_sides(group_a, mp)
        entered = entry(spread_four(near, far), rows, gains, qkv_weight, out_weight, 1, 2, begun)
        entered, group_b, group_a = fence(entered, group_b, group_a)
        far_a = spread_core([group_a], mp)
        group_c = turn(group_a, "dp", dp, 1)
    else:
        spread = spread_any(pair, mp)
        names = spread.names
        placed = tables(own, lengths[0], names, rows)
        entered = entry(spread, rows, gains, qkv_weight, out_weight)
    seq_starts, cos_table, sine_table = placed

    first_all, second_all, hat, raw, grad_attended, grad_out = entered
    attended, grad_qkv, qkv_bias_part = attention(
        own.reshape(1),
        seq_starts,
        raw,
        qkv_bias[None, :],
        cos_table,
        sine_table,
        grad_attended,
        rows,
        names,
    )
    if gather_all:
        (first_all, second_all, hat, grad_out, attended, grad_qkv), near_a, far_a, group_b = fence(
            (first_all, second_all, hat, grad_out, attended, grad_qkv),
            [group_a, *sides_a],
            far_a,
            group_b,
        )

    weights_part = attention_weights(first_all, grad_qkv, attended, grad_out)
    if gather_all:
        corner_a = spread_corner(near_a[1:], mp)
        far_a = far_a + spread_core(near_a[1:], mp)
        (weights_part, second_all, hat, grad_out, attended), near_a, corner_a, far_a, group_b, group_c = (
            fence(
                (weights_part, second_all, hat, grad_out, attended),
                near_a,
                corner_a,
                far_a,
                group_b,
                group_c,
            )
        )
    weights_sum = lax.psum_scatter(weights_part, "dp", scatter_dimension=0, tiled=True)

    own_spread = contiguous(second_all, grad_out, names, rows)
    hidden, grad_gate, gate_sum = mlp(own_spread, rows, up_weight, up_row, down_weight)
    branch = branch_sum(attended, hidden, out_weight, down_weight)
    if gather_all:
        sides_b = spread_sides(group_b, mp)
        far_b = spread_core([group_b], mp)
        far_a = far_a + spread_core(corner_a, mp)
        near_a = near_a + corner_a
        (hidden, grad_gate, branch, grad_qkv, hat), near_a, far_a, near_b, far_b, group_c = fence(
            (hidden, grad_gate, branch, grad_qkv, hat),
            near_a,
            far_a,
            [group_b, *sides_b],
            far_b,
            group_c,
        )

    scaled = input_sums(grad_qkv, grad_gate, qkv_weight, up_weight, gains[0], gains[2], hat)
    cot_sum = jnp.sum(cotangent.astype(f32), axis=0)
    small = jnp.concatenate([scaled[2].reshape(-1), cot_sum, qkv_bias_part.reshape(-1)])
    small = small.reshape(-1, 128)
    five = 5 * width // 128
    biases = out_bias + down_bias
    xhat, inv_std = norm_own(layer_input)

    def over_mp(both, bit):
        return jnp.concatenate([butterfly(both[:five], "mp", mp, bit), both[five:]], axis=0)

    if not gather_all:
        own_branch = scatter_group(*branch, names, mp, rows)
        own_scaled = scatter_group(*scaled[:2], names, mp, rows)
        layer_output, input_grad = ends(
            layer_input, cotangent, xhat, inv_std, own_branch, own_scaled, biases
        )
        for bit in (1 << i for i in range(dp.bit_length() - 1)):
            small = butterfly(small, "dp", dp, bit)
        small, qkv_bias_grad = small[:five], small[five:]
        for bit in (1 << i for i in range(mp.bit_length() - 1)):
            small = butterfly(small, "mp", mp, bit)
        weights_sum = lax.all_gather(weights_sum, "dp", axis=0, tiled=True)
        up_weight_grad, down_weight_grad, up_bias_grad = lax.psum(
            (weight_product(second_all, grad_gate), weight_product(hidden, grad_out), gate_sum[0]),
            "dp",
        )
    else:
        corner_b = spread_corner(near_b[1:], mp)
        far_b = far_b + spread_core(near_b[1:], mp)
        branch_came = swap(branch[1], "mp", mp, 1)
        scaled, small, near_a, far_a, near_b, far_b, corner_b, branch_came, group_c = fence(
            scaled, small, near_a, far_a, near_b, far_b, corner_b, branch_came, group_c
        )

        own_branch = Scatter(branch[0], branch_came, names, mp, rows, True)
        small = over_mp(small, 1)
        sides_c = spread_sides(group_c, mp)
        scaled_came = swap(scaled[1], "mp", mp, 1)
        far_b = far_b + spread_core(corner_b, mp)
        near_b = near_b + corner_b
        up_sum, down_sum, sum_a, *branch_sent = group(
            spread_four(near_a, far_a),
            rows,
            up_weight,
            up_row,
            down_weight,
            gate_sum,
            folds=(branch[0], branch_came),
            places=own_branch.places(),
        )
        sums, near_b, far_b, near_c, branch_sent, scaled_came, small, weights_sum = fence(
            (up_sum, down_sum),
            near_b,
            far_b,
            [group_c, *sides_c],
            branch_sent,
            scaled_came,
            small,
            weights_sum,
        )

        weights_sum = lax.all_gather(weights_sum, "dp", axis=0, tiled=True)
        own_scaled = Scatter(scaled[0], scaled_came, names, mp, rows, False)
        scaled_sent = fold([(scaled[0], scaled_came, own_scaled.places())], rows)
        far_c = spread_core(near_c[:1], mp)
        corner_c = spread_corner(near_c[1:], mp)
        small = over_mp(small, 2)
        scaled_sent, branch_sent, far_c, small, sums = fence(
            scaled_sent, branch_sent, far_c, small, sums
        )
        up_sum, down_sum, sum_b = group(
            spread_four(near_b, far_b), rows, up_weight, up_row, down_weight, sum_a, sums
        )
        sums, near_c, far_c, corner_c, branch_came, branch_kept, scaled_came, scaled_kept, small = fence(
            (up_sum, down_sum),
            near_c,
            far_c,
            corner_c,
            own_branch.swapped(branch_sent[0]),
            branch_sent[1],
            own_scaled.swapped(scaled_sent[0]),
            scaled_sent[1],
            small,
        )

        far_c = far_c + spread_core(near_c[1:] + corner_c, mp)
        near_c = near_c + corner_c
        small = over_mp(small, 4)
        own_branch.take(own_branch.listed(branch_kept), branch_came)
        own_scaled.take(own_scaled.listed(scaled_kept), scaled_came)
        folded = fold(
            [
                (branch_kept, branch_came, own_branch.places()),
                (scaled_kept, scaled_came, own_scaled.places()),
            ],
            rows,
        )
        near_c, far_c, small, branch_sent, scaled_sent = fence(
            near_c, far_c, small, folded[:2], folded[2:]
        )
        up_weight_grad, down_weight_grad, sum_c = group(
            spread_four(near_c, far_c),
            rows,
            up_weight,
            up_row,
            down_weight,
            sum_b,
            sums,
            (second_all, grad_out, hidden, grad_gate),
        )
        up_weight_grad, branch_came, branch_kept, scaled_came, scaled_kept, z_sums = fence(
            up_weight_grad,
            own_branch.swapped(branch_sent[0]),
            branch_sent[1],
            own_scaled.swapped(scaled_sent[0]),
            scaled_sent[1],
            [small] + [swap(small, "dp", dp, bit) for bit in (1, 2, 3)],
        )
        own_branch.take([branch_kept], branch_came)
        own_scaled.take([scaled_kept], scaled_came)
        branch_total, scaled_total = own_branch.total(0), own_scaled.total(0)
        small = (z_sums[0] + z_sums[1]) + (z_sums[2] + z_sums[3])
        layer_output, input_grad = ends(
            layer_input, cotangent, xhat, inv_std, branch_total, scaled_total, biases
        )
        up_bias_grad = sum_c[0]
        small, qkv_bias_grad = small[:five], small[five:]
    qkv_weight_grad, out_weight_grad = widen(weights_sum, qkv_weight.shape[1], out_weight.shape[0])
    small = small.reshape(5, width)
    return (
        layer_output,
        input_grad,
        small[0],
        small[1],
        small[2],
        small[3],
        qkv_weight_grad,
        qkv_bias_grad.reshape(-1),
        out_weight_grad,
        small[4],
        up_weight_grad,
        up_bias_grad,
        down_weight_grad,
        small[4],
    )


def solution(mesh):
    in_specs = (
        P(("dp", "mp"), None),
        P("dp", None),
        P(),
        P(),
        P(),
        P(),
        P(None, "mp"),
        P("mp"),
        P("mp", None),
        P(),
        P(None, "mp"),
        P("mp"),
        P("mp", None),
        P(),
        P(("dp", "mp"), None),
    )
    out_specs = (
        P(("dp", "mp"), None),
        P(("dp", "mp"), None),
        P(),
        P(),
        P(),
        P(),
        P(None, "mp"),
        P("mp"),
        P("mp", None),
        P(),
        P(None, "mp"),
        P("mp"),
        P("mp", None),
        P(),
    )
    return jax.shard_map(
        per_device, mesh=mesh, in_specs=in_specs, out_specs=out_specs, check_vma=False
    )
```

```python
import functools

import jax
import jax.numpy as jnp
from jax import lax
from jax.experimental import pallas as pl
from jax.experimental.pallas import tpu as pltpu
from jax.sharding import PartitionSpec as P

HEAD_DIM = 128
ROTARY = 32

norm_eps = 1e-05
masked_score = -1e30
inv_root_two = 0.7071067811865476
inv_root_tau = 0.3989422804014327
vmem_bytes = 60 << 20
most_gathered = 128 << 20
bf16 = jnp.bfloat16
f32 = jnp.float32


def dot_plain(left, right):
    return jnp.dot(left, right, preferred_element_type=f32)


def contract_rows(left, right):
    return lax.dot_general(left, right, (((0,), (0,)), ((), ())), preferred_element_type=f32)


def contract_cols(left, right):
    return lax.dot_general(left, right, (((1,), (1,)), ((), ())), preferred_element_type=f32)


def swap(value, axis, count, bit):
    return lax.ppermute(value, axis, [(i, i ^ bit) for i in range(count)])


def turn(value, axis, count, step):
    return lax.ppermute(value, axis, [(i, (i + step) % count) for i in range(count)])


def chip_bits(count):
    return [1 << i for i in range(1, count.bit_length() - 1)]


def after(value, *earlier):
    return lax.optimization_barrier((value, *earlier))[0]


class Spread:
    def __init__(self, arrays, a, b, names):
        self.arrays, self.a, self.b, self.names = arrays, a, b, names


four_names = (0, 2, 4, 6, 1, 3, 5, 7)


def spread_sides(pair, count):
    return [swap(pair, "mp", count, 2), swap(pair, "mp", count, 4)]


def spread_corner(sides, count):
    a, b = cut(*sides)
    return [swap(a, "mp", count, 4), swap(b, "mp", count, 2)]


def spread_core(arrays, count):
    return [swap(array, "mp", count, 1) for array in arrays]


def spread_four(near, far):
    rows = near[0].shape[0] // 2
    a, b = {}, {}
    for core in range(2):
        base = len(near) * core
        for i, name in enumerate((0, 2, 4)):
            a[name + core] = (base + i, 0)
            b[name + core] = (base + i, rows)
        a[6 + core] = (base + 3, 0)
        b[6 + core] = (base + 4, 0)
    return Spread(near + far, a, b, four_names)


def spread_any(pair, count):
    rows = pair.shape[0] // 2
    held, names = pair.reshape(1, 2, rows, -1), [0]
    for bit in chip_bits(count) + [1]:
        held = jnp.concatenate([held, swap(held, "mp", count, bit)], axis=0)
        names = names + [n ^ bit for n in names]
    arrays = [held.reshape(2 * rows * count, -1)]
    a = {n: (0, 2 * rows * i) for i, n in enumerate(names)}
    b = {n: (0, 2 * rows * i + rows) for i, n in enumerate(names)}
    return Spread(arrays, a, b, tuple(names))


class Scatter:
    def __init__(self, near, came, names, count, rows, rising):
        self.count, self.rows = count, rows
        names = names[: len(names) // 2]
        self.blocks = {n: near[i * rows : (i + 1) * rows] for i, n in enumerate(names)}
        self.adds = {n: came[i * rows : (i + 1) * rows] for i, n in enumerate(names)}
        bits = chip_bits(count)
        self.bits = bits if rising else bits[::-1]

    def total(self, n):
        return self.blocks[n].astype(f32) + self.adds[n].astype(f32)

    def places(self):
        bit, order = self.bits[0], list(self.blocks)
        going = [i for i, n in enumerate(order) if n & bit]
        return going, [i for i, n in enumerate(order) if not n & bit]

    def listed(self, kept):
        return [kept[i : i + self.rows] for i in range(0, kept.shape[0], self.rows)]

    def sent(self):
        bit = self.bits[0]
        stay = [n for n in self.blocks if not n & bit]
        going = jnp.concatenate([self.total(n | bit).astype(bf16) for n in stay], axis=0)
        return going, [self.total(n).astype(bf16) for n in stay]

    def swapped(self, going):
        return swap(going, "mp", self.count, self.bits[0])

    def take(self, kept, came):
        bit, self.bits = self.bits[0], self.bits[1:]
        stay = [n for n in self.blocks if not n & bit]
        self.blocks = dict(zip(stay, kept))
        self.adds = {n: came[i * self.rows : (i + 1) * self.rows] for i, n in enumerate(stay)}


def scatter_group(near, far, names, count, rows):
    scatter = Scatter(near, swap(far, "mp", count, 1), names, count, rows, True)
    while scatter.bits:
        going, kept = scatter.sent()
        scatter.take(kept, scatter.swapped(going))
    return scatter.total(0)


def call(body, name, **kwargs):
    return pl.pallas_call(
        body,
        name=name,
        compiler_params=pltpu.CompilerParams(vmem_limit_bytes=vmem_bytes),
        cost_estimate=pl.CostEstimate(flops=1, bytes_accessed=1, transcendentals=0),
        **kwargs,
    )


def block_copies(spread, which, refs, buffer, sems, rows, block, blocks):
    per = block // rows
    listed = []
    for at in blocks:
        listed.append([])
        for i in range(at * per, (at + 1) * per):
            array, first = getattr(spread, which)[spread.names[i]]
            listed[-1].append(
                pltpu.make_async_copy(
                    refs[array].at[first : first + rows, :],
                    buffer.at[i * rows : (i + 1) * rows, :],
                    sems.at[i],
                )
            )
    return listed


def out_copies(buffer, ref, sems, block, blocks):
    return [
        pltpu.make_async_copy(
            buffer.at[i * block : (i + 1) * block, :],
            ref.at[i * block : (i + 1) * block, :],
            sems.at[i],
        )
        for i in blocks
    ]


def entry_body(*refs, spread, rows, block, blocks, earlier):
    count = len(spread.arrays)
    arrays = refs[:count]
    (gain1, bias1, gain2, bias2, qkv_ref, out_weight_ref) = refs[count : count + 6]
    count += 6 + earlier
    (one_ref, two_ref, hat_ref, raw_ref, grad_ref, cot_ref) = refs[count : count + 6]
    x_buf, c_buf, sem_x, sem_c, sem_out = refs[count + 6 :]
    step = pl.program_id(0)
    x_copies = block_copies(spread, "a", arrays, x_buf, sem_x, rows, block, blocks)
    c_copies = block_copies(spread, "b", arrays, c_buf, sem_c, rows, block, blocks)
    outs = out_copies(c_buf, cot_ref, sem_out, block, blocks)

    @pl.when(step == 0)
    def _():
        for x_list, c_list in zip(x_copies, c_copies):
            for copy in x_list + c_list:
                copy.start()

    for i in range(len(outs)):

        @pl.when(step == i)
        def _(i=i):
            for copy in x_copies[i] + c_copies[i]:
                copy.wait()
            outs[i].start()

    here = pl.ds(pl.multiple_of((step * blocks.step + blocks.start) * block, block), block)
    values = x_buf[here, :].astype(f32)
    centred = values - jnp.mean(values, axis=1, keepdims=True)
    hat = centred * lax.rsqrt(jnp.mean(centred * centred, axis=1, keepdims=True) + norm_eps)
    hat_ref[...] = hat.astype(bf16)
    one_ref[...] = (hat * gain1[...] + bias1[...]).astype(bf16)
    two_ref[...] = (hat * gain2[...] + bias2[...]).astype(bf16)
    raw_ref[...] = dot_plain(one_ref[...], qkv_ref[...])
    grad_ref[...] = contract_cols(c_buf[here, :], out_weight_ref[...]).astype(bf16)

    @pl.when(step == len(outs) - 1)
    def _():
        for copy in outs:
            copy.wait()


def entry(spread, rows, gains, qkv_weight, out_weight, begin=0, stride=1, earlier=()):
    group_rows = rows * len(spread.names)
    width, deep = qkv_weight.shape
    units = out_weight.shape[0]
    block = min(256, group_rows)
    steps = group_rows // block
    per_group = len(spread.names)
    blocks = range(begin, steps, stride)
    once = pl.Buffered(1)

    def out_block(columns):
        return pl.BlockSpec((block, columns), lambda i: (i * stride + begin, 0))

    row = pl.BlockSpec((1, width), lambda i: (0, 0))
    anywhere = pl.BlockSpec(memory_space=pl.ANY)
    wide = jax.ShapeDtypeStruct((group_rows, width), bf16)
    first = len(spread.arrays) + 6
    return call(
        functools.partial(
            entry_body, spread=spread, rows=rows, block=block, blocks=blocks, earlier=len(earlier)
        ),
        "entry",
        grid=(len(blocks),),
        in_specs=[anywhere] * len(spread.arrays)
        + [row] * 4
        + [
            pl.BlockSpec(qkv_weight.shape, lambda i: (0, 0), pipeline_mode=once),
            pl.BlockSpec(out_weight.shape, lambda i: (0, 0), pipeline_mode=once),
        ]
        + [anywhere] * len(earlier),
        out_specs=[
            out_block(width),
            out_block(width),
            out_block(width),
            out_block(deep),
            out_block(units),
            anywhere,
        ],
        out_shape=[
            wide,
            wide,
            wide,
            jax.ShapeDtypeStruct((group_rows, deep), f32),
            jax.ShapeDtypeStruct((group_rows, units), bf16),
            wide,
        ],
        input_output_aliases={first + i: i for i in range(len(earlier))},
        scratch_shapes=[
            pltpu.VMEM((group_rows, width), bf16),
            pltpu.VMEM((group_rows, width), bf16),
            pltpu.SemaphoreType.DMA((per_group,)),
            pltpu.SemaphoreType.DMA((per_group,)),
            pltpu.SemaphoreType.DMA((steps,)),
        ],
    )(*spread.arrays, *gains, qkv_weight, out_weight, *earlier)


def pairs_body(input_ref, cot_ref, gain_ref, bias_ref, pair_ref, shared_ref):
    rows = input_ref.shape[0]
    values = input_ref[...].astype(f32)
    centred = values - jnp.mean(values, axis=1, keepdims=True)
    hat = centred * lax.rsqrt(jnp.mean(centred * centred, axis=1, keepdims=True) + norm_eps)
    pair_ref[:rows, :] = input_ref[...]
    pair_ref[rows:, :] = cot_ref[...]
    shared_ref[:rows, :] = (hat * gain_ref[...] + bias_ref[...]).astype(bf16)
    shared_ref[rows:, :] = cot_ref[...]


def pairs(layer_input, cotangent, gain, bias):
    rows, width = layer_input.shape
    return call(
        pairs_body,
        "pairs",
        out_shape=[jax.ShapeDtypeStruct((2 * rows, width), bf16)] * 2,
    )(layer_input, cotangent, gain, bias)


def fold_body(near_ref, came_ref, going_ref, kept_ref, *, rows, going, kept):
    for ref, places in ((going_ref, going), (kept_ref, kept)):
        for i, at in enumerate(places):
            here = slice(at * rows, (at + 1) * rows)
            total = near_ref[here, :].astype(f32) + came_ref[here, :].astype(f32)
            ref[i * rows : (i + 1) * rows, :] = total.astype(bf16)


def folds_body(*refs, count):
    for ref in range(2 * count):
        total = refs[2 * ref][...].astype(f32) + refs[2 * ref + 1][...].astype(f32)
        refs[4 * count + ref][...] = total.astype(bf16)


def fold(sums, rows):
    width = sums[0][0].shape[1]
    operands, in_specs = [], []
    for near, came, places in sums:
        for first, *more in places:
            apart = more[0] - first if more else 0
            spec = pl.BlockSpec((rows, width), lambda i, a=apart, f=first: (a * i + f, 0))
            operands += [near, came]
            in_specs += [spec, spec]
    per = len(sums[0][2][0])
    return call(
        functools.partial(folds_body, count=len(sums)),
        "fold",
        grid=(per,),
        in_specs=in_specs,
        out_specs=[pl.BlockSpec((rows, width), lambda i: (i, 0))] * (2 * len(sums)),
        out_shape=[jax.ShapeDtypeStruct((per * rows, width), bf16)] * (2 * len(sums)),
    )(*operands)


def cut_body(side_x, side_y, x_ref, y_ref):
    x_ref[...] = side_x[...]
    y_ref[...] = side_y[...]


def cut(side_x, side_y):
    rows, width = side_x.shape[0] // 2, side_x.shape[1]
    tops = pl.BlockSpec((rows, width), lambda i: (0, 0))
    return call(
        cut_body,
        "cut",
        grid=(1,),
        in_specs=[tops, pl.BlockSpec((rows, width), lambda i: (1, 0))],
        out_specs=[tops] * 2,
        out_shape=[jax.ShapeDtypeStruct((rows, width), side_x.dtype)] * 2,
    )(side_x, side_y)


def start(copies):
    for copy in copies:
        copy.start()


def wait(copies):
    for copy in copies:
        copy.wait()


class Branch:
    def __init__(self, arrays, weights, buffers, sems, spread, rows, block, tile):
        self.up_ref, self.shift_ref, self.down_ref = weights
        self.x_buf, self.c_buf, self.u_buf, self.d_buf = buffers
        sem_x, sem_c, sem_u, sem_d = sems
        self.block = block
        self.every = range(self.x_buf.shape[0] // block)
        units = self.u_buf.shape[1]
        self.x_copies = block_copies(spread, "a", arrays, self.x_buf, sem_x, rows, block, self.every)
        self.c_copies = block_copies(spread, "b", arrays, self.c_buf, sem_c, rows, block, self.every)
        self.tiles = [slice(i, i + tile) for i in range(0, units, tile)]
        self.needs = self.x_copies[0] + self.c_copies[0]
        self.needs.append(pltpu.make_async_copy(self.up_ref, self.u_buf, sem_u))
        self.needs.append(pltpu.make_async_copy(self.down_ref, self.d_buf, sem_d))

    def block_step(self, step, hidden_ref, grad_ref, sum_ref, to_rows, prior_ref, extra=()):
        @pl.when(step == 0)
        def _():
            start(self.needs)
            sum_ref[...] = jnp.zeros_like(sum_ref) if prior_ref is None else prior_ref[...]
            wait(self.needs)
            for later in self.every[1:]:
                start(self.x_copies[later] + self.c_copies[later])
            start(extra)

        for i in self.every[1:]:

            @pl.when(step == i)
            def _(i=i):
                wait(self.x_copies[i] + self.c_copies[i])

        here = pl.ds(pl.multiple_of(step * self.block, self.block), self.block)
        there = here if to_rows else slice(None)
        gates = [
            dot_plain(self.x_buf[here, :], self.u_buf[:, part]) + self.shift_ref[:, part]
            for part in self.tiles
        ]

        for gate, part in zip(gates, self.tiles):
            grad_hidden = contract_cols(self.c_buf[here, :], self.d_buf[part, :])
            below = 0.5 * (1.0 + lax.erf(gate * inv_root_two))
            hidden_ref[there, part] = (gate * below).astype(bf16)
            slope = below + gate * jnp.exp(-0.5 * gate * gate) * inv_root_tau
            grad = (grad_hidden * slope).astype(bf16)
            grad_ref[there, part] = grad
            sum_ref[:, part] += jnp.sum(grad.astype(f32), axis=0, keepdims=True)


def branch_scratch(group_rows, width, units, blocks):
    dma = pltpu.SemaphoreType.DMA
    return [
        pltpu.VMEM((group_rows, width), bf16),
        pltpu.VMEM((group_rows, width), bf16),
        pltpu.VMEM((width, units), bf16),
        pltpu.VMEM((units, width), bf16),
        dma((blocks,)),
        dma((blocks,)),
        dma,
        dma,
    ]


def mlp_body(*refs, spread, rows, block, tile):
    count = len(spread.arrays)
    hidden_ref, grad_ref, sum_ref = refs[count + 3 : count + 6]
    scratch = refs[count + 6 :]
    branch = Branch(
        refs[:count], refs[count : count + 3], scratch[:4], scratch[4:], spread, rows, block, tile
    )
    branch.block_step(pl.program_id(0), hidden_ref, grad_ref, sum_ref, False, None)


def mlp(spread, rows, up_weight, up_bias, down_weight):
    width, units = up_weight.shape
    group_rows = rows * len(spread.names)
    block = min(512, group_rows)
    tile = min(512, units)
    steps, blocks = group_rows // block, len(spread.names)
    anywhere = pl.BlockSpec(memory_space=pl.ANY)
    part = pl.BlockSpec((block, units), lambda i: (i, 0))
    low = jax.ShapeDtypeStruct((group_rows, units), bf16)
    row = pl.BlockSpec((1, units), lambda i: (0, 0))
    return call(
        functools.partial(mlp_body, spread=spread, rows=rows, block=block, tile=tile),
        "mlp",
        grid=(steps,),
        in_specs=[anywhere] * len(spread.arrays) + [anywhere, row, anywhere],
        out_specs=[part, part, row],
        out_shape=[low, low, jax.ShapeDtypeStruct((1, units), f32)],
        scratch_shapes=branch_scratch(group_rows, width, units, blocks),
    )(*spread.arrays, up_weight, up_bias, down_weight)


def group_body(*refs, spread, rows, block, tile, steps, ups, adds, more, places):
    count = len(spread.arrays)
    arrays, weights, refs = refs[:count], refs[count : count + 3], refs[count + 3 :]
    prior_ref, *refs = refs
    added, refs = refs[: 2 * adds], refs[2 * adds :]
    own, refs = refs[: 4 * more], refs[4 * more :]
    folds, refs = (refs[:2], refs[2:]) if places else ((), refs)
    up_out, down_out, sum_ref = refs[:3]
    folded, refs = (refs[3:5], refs[5:]) if places else ((), refs[3:])
    buffers, sems, (hidden_buf, grad_buf), refs = refs[:4], refs[4:8], refs[8:10], refs[10:]
    branch = Branch(arrays, weights, buffers, sems, spread, rows, block, tile)
    step = pl.program_id(0)
    at = jnp.where(step < steps + ups, step - steps, step - steps - ups)
    at = jnp.maximum(at, 0)
    here = pl.ds(pl.multiple_of(at * tile, tile), tile)
    later = []
    if adds:
        sum_up, sum_down, sem_sum_up, sem_sum_down, *refs = refs

        def up_copy(i):
            first = pl.multiple_of(i * tile, tile)
            return pltpu.make_async_copy(
                added[0].at[pl.ds(first, tile), :], sum_up.at[i % 2], sem_sum_up.at[i % 2]
            )

        def down_copy(i):
            first = pl.multiple_of(i * tile, tile)
            return pltpu.make_async_copy(
                added[1].at[:, pl.ds(first, tile)], sum_down.at[i % 2], sem_sum_down.at[i % 2]
            )

        later = later + [up_copy(0)]
    if more:
        own_bufs, sem_own = refs[:4], refs[4]
        own_copies = [
            pltpu.make_async_copy(ref, buf, sem_own.at[i])
            for i, (ref, buf) in enumerate(zip(own, own_bufs))
        ]
        later = later + own_copies
        rows_own, cot_own, hidden_own, grad_own = own_bufs

    @pl.when(step < steps)
    def _():
        branch.block_step(step, hidden_buf, grad_buf, sum_ref, True, prior_ref, later)

    if more:

        @pl.when(step == steps)
        def _():
            wait(own_copies)

    if places:

        @pl.when(step >= steps)
        def _():
            fold_body(*folds, *folded, rows=rows, going=places[0], kept=places[1])

    @pl.when((step >= steps) & (step < steps + ups))
    def _():
        if adds:

            @pl.when(at + 1 < ups)
            def _():
                up_copy(at + 1).start()

            @pl.when(at + 1 == ups)
            def _():
                down_copy(0).start()

            up_copy(at).wait()
        total = contract_rows(branch.x_buf[:, here], grad_buf[...])
        if more:
            total = total + contract_rows(rows_own[:, here], grad_own[...])
        if adds:
            total = total + sum_up[at % 2]
        up_out[...] = total

    @pl.when(step >= steps + ups)
    def _():
        if adds:

            @pl.when(at + 1 < ups)
            def _():
                down_copy(at + 1).start()

            down_copy(at).wait()
        total = contract_rows(hidden_buf[...], branch.c_buf[:, here])
        if more:
            total = total + contract_rows(hidden_own[...], cot_own[:, here])
        if adds:
            total = total + sum_down[at % 2]
        down_out[...] = total


def group(spread, rows, up_weight, up_bias, down_weight, prior, added=(), own=(), folds=(), places=()):
    width, units = up_weight.shape
    group_rows = rows * len(spread.names)
    block = min(512, group_rows)
    tile = min(512, units)
    steps, blocks = group_rows // block, len(spread.names)
    ups = width // tile
    anywhere = pl.BlockSpec(memory_space=pl.ANY)
    row = pl.BlockSpec((1, units), lambda i: (0, 0))
    dma = pltpu.SemaphoreType.DMA
    scratch = branch_scratch(group_rows, width, units, blocks)
    scratch += [pltpu.VMEM((group_rows, units), bf16)] * 2
    if added:
        scratch += [
            pltpu.VMEM((2, tile, units), f32),
            pltpu.VMEM((2, units, tile), f32),
            dma((2,)),
            dma((2,)),
        ]
    if own:
        scratch += [pltpu.VMEM(array.shape, bf16) for array in own] + [dma((4,))]
    fold_in, fold_out, fold_shape = [], [], []
    if folds:
        strip = width // (2 * ups)
        half = folds[0].shape[0] // 2

        def column(i):
            return 0, jnp.clip(i - steps, 0, 2 * ups - 1)

        fold_in = [pl.BlockSpec((2 * half, strip), column)] * 2
        fold_out = [pl.BlockSpec((half, strip), column)] * 2
        fold_shape = [jax.ShapeDtypeStruct((half, width), bf16)] * 2
    return call(
        functools.partial(
            group_body,
            spread=spread,
            rows=rows,
            block=block,
            tile=tile,
            steps=steps,
            ups=ups,
            adds=bool(added),
            more=bool(own),
            places=places,
        ),
        "group",
        grid=(steps + 2 * ups,),
        in_specs=[anywhere] * len(spread.arrays)
        + [anywhere, row, anywhere, row]
        + [anywhere] * (len(added) + len(own))
        + fold_in,
        out_specs=[
            pl.BlockSpec((tile, units), lambda i: (jnp.clip(i - steps, 0, ups - 1), 0)),
            pl.BlockSpec((units, tile), lambda i: (0, jnp.clip(i - steps - ups, 0, ups - 1))),
            row,
        ]
        + fold_out,
        out_shape=[
            jax.ShapeDtypeStruct((width, units), f32),
            jax.ShapeDtypeStruct((units, width), f32),
            jax.ShapeDtypeStruct((1, units), f32),
        ]
        + fold_shape,
        scratch_shapes=scratch,
    )(*spread.arrays, up_weight, up_bias, down_weight, prior, *added, *own, *folds)


def weight_body(left_ref, right_ref, out_ref):
    out_ref[...] = contract_rows(left_ref[...], right_ref[...])


def weight_product(left, right):
    wide, deep = left.shape[1], right.shape[1]
    tile = min(512, wide)
    return call(
        weight_body,
        "weight_product",
        grid=(wide // tile,),
        in_specs=[
            pl.BlockSpec((left.shape[0], tile), lambda i: (0, i)),
            pl.BlockSpec(right.shape, lambda i: (0, 0), pipeline_mode=pl.Buffered(1)),
        ],
        out_specs=pl.BlockSpec((tile, deep), lambda i: (i, 0)),
        out_shape=jax.ShapeDtypeStruct((wide, deep), f32),
    )(left, right)


def attention_weights_body(normed_ref, grad_qkv_ref, attended_ref, grad_out_ref, sum_ref):
    deep = grad_qkv_ref.shape[1]
    sum_ref[:, :deep] = contract_rows(normed_ref[...], grad_qkv_ref[...]).astype(bf16)
    sum_ref[:, deep:] = contract_rows(attended_ref[...], grad_out_ref[...]).astype(bf16)


def attention_weights(normed, grad_qkv, attended, grad_out):
    group_rows, width = normed.shape
    deep, units = grad_qkv.shape[1], attended.shape[1]
    once = pl.Buffered(1)
    block = pl.BlockSpec((group_rows, units), lambda i: (0, i))
    return call(
        attention_weights_body,
        "attention_weights",
        grid=(width // units,),
        in_specs=[
            block,
            pl.BlockSpec(grad_qkv.shape, lambda i: (0, 0), pipeline_mode=once),
            pl.BlockSpec(attended.shape, lambda i: (0, 0), pipeline_mode=once),
            block,
        ],
        out_specs=pl.BlockSpec((units, deep + units), lambda i: (i, 0)),
        out_shape=jax.ShapeDtypeStruct((width, deep + units), bf16),
    )(normed, grad_qkv, attended, grad_out)


def widen_body(sum_ref, qkv_ref, out_ref):
    units, deep = out_ref.shape[0], qkv_ref.shape[1]
    qkv_ref[...] = sum_ref[:, :deep].astype(f32)
    for first in range(0, sum_ref.shape[0], units):
        out_ref[:, first : first + units] = sum_ref[first : first + units, deep:].astype(f32)


def widen(total, deep, units):
    width = total.shape[0]
    block = min(2 * units, width)
    return call(
        widen_body,
        "widen",
        grid=(width // block,),
        in_specs=[pl.BlockSpec((block, deep + units), lambda i: (i, 0))],
        out_specs=[
            pl.BlockSpec((block, deep), lambda i: (i, 0)),
            pl.BlockSpec((units, block), lambda i: (0, i)),
        ],
        out_shape=[
            jax.ShapeDtypeStruct((width, deep), f32),
            jax.ShapeDtypeStruct((units, width), f32),
        ],
    )(total)


def branch_body(attended_ref, hidden_ref, out_ref, down_ref, near_ref, far_ref):
    middle = near_ref.shape[0]
    total = dot_plain(attended_ref[...], out_ref[...]) + dot_plain(hidden_ref[...], down_ref[...])
    near_ref[...] = total[:middle].astype(bf16)
    far_ref[...] = total[middle:].astype(bf16)


def branch_sum(attended, hidden, out_weight, down_weight):
    group_rows = attended.shape[0]
    width = out_weight.shape[1]
    tile = min(512, width)
    once = pl.Buffered(1)
    half = pl.BlockSpec((group_rows // 2, tile), lambda i: (0, i))
    return call(
        branch_body,
        "branch_sum",
        grid=(width // tile,),
        in_specs=[
            pl.BlockSpec(attended.shape, lambda i: (0, 0), pipeline_mode=once),
            pl.BlockSpec(hidden.shape, lambda i: (0, 0), pipeline_mode=once),
            pl.BlockSpec((out_weight.shape[0], tile), lambda i: (0, i)),
            pl.BlockSpec((down_weight.shape[0], tile), lambda i: (0, i)),
        ],
        out_specs=[half, half],
        out_shape=[jax.ShapeDtypeStruct((group_rows // 2, width), bf16)] * 2,
    )(attended, hidden, out_weight, down_weight)


def input_body(
    qkv_grad_ref, gate_grad_ref, qkv_ref, up_ref, gain1, gain2, hat_ref, near_ref, far_ref, sum_ref
):
    middle = near_ref.shape[0]
    hat = hat_ref[...].astype(f32)
    first = contract_cols(qkv_grad_ref[...], qkv_ref[...])
    second = contract_cols(gate_grad_ref[...], up_ref[...])
    both = first * gain1[...] + second * gain2[...]
    near_ref[...] = both[:middle].astype(bf16)
    far_ref[...] = both[middle:].astype(bf16)
    sum_ref[0:1, :] = jnp.sum(first * hat, axis=0, keepdims=True)
    sum_ref[1:2, :] = jnp.sum(first, axis=0, keepdims=True)
    sum_ref[2:3, :] = jnp.sum(second * hat, axis=0, keepdims=True)
    sum_ref[3:4, :] = jnp.sum(second, axis=0, keepdims=True)


def input_sums(grad_qkv, grad_gate, qkv_weight, up_weight, gain1, gain2, hat):
    group_rows = grad_qkv.shape[0]
    width = qkv_weight.shape[0]
    tile = min(256, width)
    once = pl.Buffered(1)
    half = pl.BlockSpec((group_rows // 2, tile), lambda i: (0, i))
    row = pl.BlockSpec((1, tile), lambda i: (0, i))
    return call(
        input_body,
        "input_sums",
        grid=(width // tile,),
        in_specs=[
            pl.BlockSpec(grad_qkv.shape, lambda i: (0, 0), pipeline_mode=once),
            pl.BlockSpec(grad_gate.shape, lambda i: (0, 0), pipeline_mode=once),
            pl.BlockSpec((tile, qkv_weight.shape[1]), lambda i: (i, 0)),
            pl.BlockSpec((tile, up_weight.shape[1]), lambda i: (i, 0)),
            row,
            row,
            pl.BlockSpec((group_rows, tile), lambda i: (0, i)),
        ],
        out_specs=[half, half, pl.BlockSpec((4, tile), lambda i: (0, i))],
        out_shape=[jax.ShapeDtypeStruct((group_rows // 2, width), bf16)] * 2
        + [jax.ShapeDtypeStruct((4, width), f32)],
    )(grad_qkv, grad_gate, qkv_weight, up_weight, gain1, gain2, hat)


def attention_body(
    own_ref,
    starts_ref,
    raw_ref,
    bias_ref,
    cos_ref,
    sine_ref,
    slope_in_ref,
    attended_ref,
    grad_qkv_ref,
    bias_grad_ref,
    query_ref,
    key_ref,
    value_ref,
    slope_ref,
    query_sum_ref,
    key_sum_ref,
    value_sum_ref,
    *,
    rows,
    names,
    block_rows,
    longest,
):
    own = own_ref[0]
    group_rows = rows * len(names)
    lane = lax.broadcasted_iota(jnp.int32, (rows, HEAD_DIM), 1)
    half = ROTARY // 2
    scale = HEAD_DIM ** (-0.5)

    def turned(u):
        return jnp.where(lane < half, pltpu.roll(u, HEAD_DIM - half, 1), pltpu.roll(u, half, 1))

    def far_rows(name):
        return pl.ds(pl.multiple_of((own ^ name) * rows, rows), rows)

    for i, name in enumerate(names):
        near = slice(i * rows, (i + 1) * rows)
        far = far_rows(name)
        raw = raw_ref[near, :] + bias_ref[...]
        cos_table = cos_ref[near, :]
        sine_table = sine_ref[near, :]
        query = raw[:, :HEAD_DIM]
        key = raw[:, HEAD_DIM : 2 * HEAD_DIM]
        query_ref[far, :] = (query * cos_table + turned(query) * sine_table).astype(bf16)
        key_ref[far, :] = (key * cos_table + turned(key) * sine_table).astype(bf16)
        value_ref[far, :] = raw[:, 2 * HEAD_DIM :].astype(bf16)
        slope_ref[far, :] = slope_in_ref[near, :]
    key_sum_ref[...] = jnp.zeros_like(key_sum_ref)
    value_sum_ref[...] = jnp.zeros_like(value_sum_ref)
    for first in range(0, group_rows, block_rows):
        last = first + block_rows
        low = max(0, (first - longest + 1) // 128 * 128)
        query = query_ref[first:last, :]
        keys = key_ref[low:last, :]
        values = value_ref[low:last, :]
        slope = slope_ref[first:last, :]
        scores = contract_cols(query, keys) * scale
        row = first + lax.broadcasted_iota(jnp.int32, (block_rows, 1), 0)
        begin = jnp.zeros((block_rows, 1), jnp.int32)
        for slot in range(starts_ref.shape[0]):
            begin = jnp.where(starts_ref[slot] <= row, starts_ref[slot], begin)
        column = low + lax.broadcasted_iota(jnp.int32, scores.shape, 1)
        scores = jnp.where((column >= begin) & (column <= row), scores, masked_score)
        peak = jnp.max(scores, axis=1, keepdims=True)
        raised = jnp.exp(scores - peak)
        probs = raised * (1.0 / jnp.sum(raised, axis=1, keepdims=True))
        probs_low = probs.astype(bf16)
        query_ref[first:last, :] = dot_plain(probs_low, values).astype(bf16)
        grad_probs = contract_cols(slope, values)
        delta = jnp.sum(grad_probs * probs, axis=1, keepdims=True)
        grad_score = (probs * (grad_probs - delta)).astype(bf16)
        query_sum_ref[first:last, :] = dot_plain(grad_score, keys) * scale
        key_sum_ref[low:last, :] += contract_rows(grad_score, query) * scale
        value_sum_ref[low:last, :] += contract_rows(probs_low, slope)
    bias_grad = jnp.zeros(bias_grad_ref.shape, f32)
    for i, name in enumerate(names):
        near = slice(i * rows, (i + 1) * rows)
        far = far_rows(name)
        cos_table = cos_ref[near, :]
        sine_table = sine_ref[near, :]
        query_grad = query_sum_ref[far, :]
        key_grad = key_sum_ref[far, :]
        grads = jnp.concatenate(
            [
                query_grad * cos_table - turned(query_grad) * sine_table,
                key_grad * cos_table - turned(key_grad) * sine_table,
                value_sum_ref[far, :],
            ],
            axis=1,
        ).astype(bf16)
        grad_qkv_ref[near, :] = grads
        bias_grad = bias_grad + jnp.sum(grads.astype(f32), axis=0, keepdims=True)
        attended_ref[near, :] = query_ref[far, :]
    bias_grad_ref[...] = bias_grad


def attention(own, starts, raw, bias, cos_table, sine_table, slope, rows, names):
    group_rows, width = raw.shape
    part = 3 * HEAD_DIM
    heads = width // part
    whole = pl.BlockSpec((group_rows, HEAD_DIM), lambda h: (0, 0))
    scalars = pl.BlockSpec(memory_space=pltpu.SMEM)
    low = pltpu.VMEM((group_rows, HEAD_DIM), bf16)
    wide = pltpu.VMEM((group_rows, HEAD_DIM), f32)
    longest = group_rows // 2
    return pl.pallas_call(
        functools.partial(
            attention_body,
            rows=rows,
            names=names,
            block_rows=min(256, group_rows),
            longest=longest,
        ),
        grid=(heads,),
        in_specs=[
            scalars,
            scalars,
            pl.BlockSpec((group_rows, part), lambda h: (0, h)),
            pl.BlockSpec((1, part), lambda h: (0, h)),
            whole,
            whole,
            pl.BlockSpec((group_rows, HEAD_DIM), lambda h: (0, h)),
        ],
        out_specs=[
            pl.BlockSpec((group_rows, HEAD_DIM), lambda h: (0, h)),
            pl.BlockSpec((group_rows, part), lambda h: (0, h)),
            pl.BlockSpec((1, part), lambda h: (0, h)),
        ],
        out_shape=[
            jax.ShapeDtypeStruct((group_rows, heads * HEAD_DIM), bf16),
            jax.ShapeDtypeStruct((group_rows, width), bf16),
            jax.ShapeDtypeStruct((1, width), f32),
        ],
        scratch_shapes=[low, low, low, low, wide, wide, wide],
        compiler_params=pltpu.CompilerParams(vmem_limit_bytes=vmem_bytes),
        cost_estimate=pl.CostEstimate(flops=1, bytes_accessed=1, transcendentals=0),
        name="attention",
    )(own, starts, raw, bias, cos_table, sine_table, slope)


def rotary_tables(position):
    half_rot = ROTARY // 2
    frequency = 10000.0 ** (-2.0 * jnp.arange(half_rot, dtype=f32) / ROTARY)
    angles = position.astype(f32)[:, None] * frequency[None, :]
    cos_half = jnp.cos(angles)
    sine_half = jnp.sin(angles)
    rest = (position.shape[0], HEAD_DIM - ROTARY)
    return (
        jnp.concatenate([cos_half, cos_half, jnp.ones(rest, f32)], axis=1),
        jnp.concatenate([-sine_half, sine_half, jnp.zeros(rest, f32)], axis=1),
    )


def butterfly(value, axis, count, bit):
    return value + swap(value, axis, count, bit)


def fence(*values):
    return lax.optimization_barrier(values)


def norm_own(layer_input):
    values = layer_input.astype(f32)
    centred = values - jnp.mean(values, axis=-1, keepdims=True)
    inv_std = lax.rsqrt(jnp.mean(centred * centred, axis=-1, keepdims=True) + norm_eps)
    return centred * inv_std, inv_std


def tables(own, lengths, names, rows):
    seq_ends = jnp.cumsum(lengths)
    seq_starts = seq_ends - lengths
    places = (
        (own ^ jnp.array(names, jnp.int32))[:, None] * rows
        + jnp.arange(rows, dtype=jnp.int32)[None, :]
    ).reshape(-1)
    seq_first = jnp.max(
        jnp.where(seq_starts[None, :] <= places[:, None], seq_starts[None, :], 0), axis=1
    )
    return (seq_starts, *rotary_tables(places - seq_first))


def contiguous(first, second, names, rows):
    places = [{n: (which, i * rows) for i, n in enumerate(names)} for which in range(2)]
    return Spread([first, second], *places, names)


def ends(layer_input, cotangent, xhat, inv_std, branch, scaled, biases):
    layer_output = (layer_input.astype(f32) + branch + biases).astype(bf16)
    input_grad = cotangent.astype(f32) + inv_std * (
        scaled
        - jnp.mean(scaled, axis=-1, keepdims=True)
        - xhat * jnp.mean(scaled * xhat, axis=-1, keepdims=True)
    )
    return layer_output, input_grad


def per_device(
    layer_input,
    lengths,
    norm1_gain,
    norm1_bias,
    norm2_gain,
    norm2_bias,
    qkv_weight,
    qkv_bias,
    out_weight,
    out_bias,
    up_weight,
    up_bias,
    down_weight,
    down_bias,
    cotangent,
):
    dp = lax.axis_size("dp")
    mp = lax.axis_size("mp")
    own = lax.axis_index("mp")
    rows, width = layer_input.shape
    up_row = up_bias[None, :]
    gains = (norm1_gain[None, :], norm1_bias[None, :], norm2_gain[None, :], norm2_bias[None, :])
    gather_all = mp == 8 and dp == 4 and 4 * rows * mp * dp * (width + up_bias.shape[0]) < most_gathered

    pair, shared = pairs(layer_input, cotangent, *gains[2:])
    if gather_all:
        names = four_names
        sides = spread_sides(pair, mp)
        group_a = turn(shared, "dp", dp, 1)
        placed = tables(own, lengths[0], names, rows)
        far = spread_core([pair], mp)
        shared, pair, sides, placed, far, group_a = fence(shared, pair, sides, placed, far, group_a)
        group_b = turn(shared, "dp", dp, -1)
        corner = spread_corner(sides, mp)
        near = [pair, *sides]
        far = far + spread_core(sides, mp)
        begun = entry(spread_four(near, far), rows, gains, qkv_weight, out_weight, 0, 2)
        near, far, corner, group_a, begun = fence(near, far, corner, group_a, begun)
        near, far = near + corner, far + spread_core(corner, mp)
        sides_a = spread_sides(group_a, mp)
        entered = entry(spread_four(near, far), rows, gains, qkv_weight, out_weight, 1, 2, begun)
        entered, group_b, group_a = fence(entered, group_b, group_a)
        far_a = spread_core([group_a], mp)
        group_c = turn(group_a, "dp", dp, 1)
    else:
        spread = spread_any(pair, mp)
        names = spread.names
        placed = tables(own, lengths[0], names, rows)
        entered = entry(spread, rows, gains, qkv_weight, out_weight)
    seq_starts, cos_table, sine_table = placed

    first_all, second_all, hat, raw, grad_attended, grad_out = entered
    attended, grad_qkv, qkv_bias_part = attention(
        own.reshape(1),
        seq_starts,
        raw,
        qkv_bias[None, :],
        cos_table,
        sine_table,
        grad_attended,
        rows,
        names,
    )
    if gather_all:
        (first_all, second_all, hat, grad_out, attended, grad_qkv), near_a, far_a, group_b = fence(
            (first_all, second_all, hat, grad_out, attended, grad_qkv),
            [group_a, *sides_a],
            far_a,
            group_b,
        )

    weights_part = attention_weights(first_all, grad_qkv, attended, grad_out)
    if gather_all:
        corner_a = spread_corner(near_a[1:], mp)
        far_a = far_a + spread_core(near_a[1:], mp)
        (weights_part, second_all, hat, grad_out, attended), near_a, corner_a, far_a, group_b, group_c = (
            fence(
                (weights_part, second_all, hat, grad_out, attended),
                near_a,
                corner_a,
                far_a,
                group_b,
                group_c,
            )
        )
    weights_sum = lax.psum_scatter(weights_part, "dp", scatter_dimension=0, tiled=True)

    own_spread = contiguous(second_all, grad_out, names, rows)
    hidden, grad_gate, gate_sum = mlp(own_spread, rows, up_weight, up_row, down_weight)
    branch = branch_sum(attended, hidden, out_weight, down_weight)
    if gather_all:
        sides_b = spread_sides(group_b, mp)
        far_b = spread_core([group_b], mp)
        far_a = far_a + spread_core(corner_a, mp)
        near_a = near_a + corner_a
        (hidden, grad_gate, branch, grad_qkv, hat), near_a, far_a, near_b, far_b, group_c = fence(
            (hidden, grad_gate, branch, grad_qkv, hat),
            near_a,
            far_a,
            [group_b, *sides_b],
            far_b,
            group_c,
        )

    scaled = input_sums(grad_qkv, grad_gate, qkv_weight, up_weight, gains[0], gains[2], hat)
    cot_sum = jnp.sum(cotangent.astype(f32), axis=0)
    small = jnp.concatenate([scaled[2].reshape(-1), cot_sum, qkv_bias_part.reshape(-1)])
    small = small.reshape(-1, 128)
    five = 5 * width // 128
    biases = out_bias + down_bias
    xhat, inv_std = norm_own(layer_input)

    def over_mp(both, bit):
        return jnp.concatenate([butterfly(both[:five], "mp", mp, bit), both[five:]], axis=0)

    if not gather_all:
        own_branch = scatter_group(*branch, names, mp, rows)
        own_scaled = scatter_group(*scaled[:2], names, mp, rows)
        layer_output, input_grad = ends(
            layer_input, cotangent, xhat, inv_std, own_branch, own_scaled, biases
        )
        for bit in (1 << i for i in range(dp.bit_length() - 1)):
            small = butterfly(small, "dp", dp, bit)
        small, qkv_bias_grad = small[:five], small[five:]
        for bit in (1 << i for i in range(mp.bit_length() - 1)):
            small = butterfly(small, "mp", mp, bit)
        weights_sum = lax.all_gather(weights_sum, "dp", axis=0, tiled=True)
        up_weight_grad, down_weight_grad, up_bias_grad = lax.psum(
            (weight_product(second_all, grad_gate), weight_product(hidden, grad_out), gate_sum[0]),
            "dp",
        )
    else:
        corner_b = spread_corner(near_b[1:], mp)
        far_b = far_b + spread_core(near_b[1:], mp)
        branch_came = swap(branch[1], "mp", mp, 1)
        scaled, small, near_a, far_a, near_b, far_b, corner_b, branch_came, group_c = fence(
            scaled, small, near_a, far_a, near_b, far_b, corner_b, branch_came, group_c
        )

        own_branch = Scatter(branch[0], branch_came, names, mp, rows, True)
        small = over_mp(small, 1)
        sides_c = spread_sides(group_c, mp)
        scaled_came = swap(scaled[1], "mp", mp, 1)
        far_b = far_b + spread_core(corner_b, mp)
        near_b = near_b + corner_b
        up_sum, down_sum, sum_a, *branch_sent = group(
            spread_four(near_a, far_a),
            rows,
            up_weight,
            up_row,
            down_weight,
            gate_sum,
            folds=(branch[0], branch_came),
            places=own_branch.places(),
        )
        sums, near_b, far_b, near_c, branch_sent, scaled_came, small, weights_sum = fence(
            (up_sum, down_sum),
            near_b,
            far_b,
            [group_c, *sides_c],
            branch_sent,
            scaled_came,
            small,
            weights_sum,
        )

        weights_sum = lax.all_gather(weights_sum, "dp", axis=0, tiled=True)
        own_scaled = Scatter(scaled[0], scaled_came, names, mp, rows, False)
        scaled_sent = fold([(scaled[0], scaled_came, own_scaled.places())], rows)
        far_c = spread_core(near_c[:1], mp)
        corner_c = spread_corner(near_c[1:], mp)
        small = over_mp(small, 2)
        scaled_sent, branch_sent, far_c, small, sums = fence(
            scaled_sent, branch_sent, far_c, small, sums
        )
        up_sum, down_sum, sum_b = group(
            spread_four(near_b, far_b), rows, up_weight, up_row, down_weight, sum_a, sums
        )
        sums, near_c, far_c, corner_c, branch_came, branch_kept, scaled_came, scaled_kept, small = fence(
            (up_sum, down_sum),
            near_c,
            far_c,
            corner_c,
            own_branch.swapped(branch_sent[0]),
            branch_sent[1],
            own_scaled.swapped(scaled_sent[0]),
            scaled_sent[1],
            small,
        )

        far_c = far_c + spread_core(near_c[1:] + corner_c, mp)
        near_c = near_c + corner_c
        small = over_mp(small, 4)
        own_branch.take(own_branch.listed(branch_kept), branch_came)
        own_scaled.take(own_scaled.listed(scaled_kept), scaled_came)
        folded = fold(
            [
                (branch_kept, branch_came, own_branch.places()),
                (scaled_kept, scaled_came, own_scaled.places()),
            ],
            rows,
        )
        near_c, far_c, small, branch_sent, scaled_sent = fence(
            near_c, far_c, small, folded[:2], folded[2:]
        )
        up_weight_grad, down_weight_grad, sum_c = group(
            spread_four(near_c, far_c),
            rows,
            up_weight,
            up_row,
            down_weight,
            sum_b,
            sums,
            (second_all, grad_out, hidden, grad_gate),
        )
        up_weight_grad, branch_came, branch_kept, scaled_came, scaled_kept, z_sums = fence(
            up_weight_grad,
            own_branch.swapped(branch_sent[0]),
            branch_sent[1],
            own_scaled.swapped(scaled_sent[0]),
            scaled_sent[1],
            [small] + [swap(small, "dp", dp, bit) for bit in (1, 2, 3)],
        )
        own_branch.take([branch_kept], branch_came)
        own_scaled.take([scaled_kept], scaled_came)
        branch_total, scaled_total = own_branch.total(0), own_scaled.total(0)
        small = (z_sums[0] + z_sums[1]) + (z_sums[2] + z_sums[3])
        layer_output, input_grad = ends(
            layer_input, cotangent, xhat, inv_std, branch_total, scaled_total, biases
        )
        up_bias_grad = sum_c[0]
        small, qkv_bias_grad = small[:five], small[five:]
    qkv_weight_grad, out_weight_grad = widen(weights_sum, qkv_weight.shape[1], out_weight.shape[0])
    small = small.reshape(5, width)
    return (
        layer_output,
        input_grad,
        small[0],
        small[1],
        small[2],
        small[3],
        qkv_weight_grad,
        qkv_bias_grad.reshape(-1),
        out_weight_grad,
        small[4],
        up_weight_grad,
        up_bias_grad,
        down_weight_grad,
        small[4],
    )


def solution(mesh):
    in_specs = (
        P(("dp", "mp"), None),
        P("dp", None),
        P(),
        P(),
        P(),
        P(),
        P(None, "mp"),
        P("mp"),
        P("mp", None),
        P(),
        P(None, "mp"),
        P("mp"),
        P("mp", None),
        P(),
        P(("dp", "mp"), None),
    )
    out_specs = (
        P(("dp", "mp"), None),
        P(("dp", "mp"), None),
        P(),
        P(),
        P(),
        P(),
        P(None, "mp"),
        P("mp"),
        P("mp", None),
        P(),
        P(None, "mp"),
        P("mp"),
        P("mp", None),
        P(),
    )
    return jax.shard_map(
        per_device, mesh=mesh, in_specs=in_specs, out_specs=out_specs, check_vma=False
    )
```

```python
import functools

import jax
import jax.numpy as jnp
from jax import lax
from jax.experimental import pallas as pl
from jax.experimental.pallas import tpu as pltpu
from jax.sharding import PartitionSpec as P

HEAD_DIM = 128
ROTARY = 32

norm_eps = 1e-05
masked_score = -1e30
inv_root_two = 0.7071067811865476
inv_root_tau = 0.3989422804014327
vmem_bytes = 60 << 20
most_gathered = 128 << 20
bf16 = jnp.bfloat16
f32 = jnp.float32


def dot_plain(left, right):
    return jnp.dot(left, right, preferred_element_type=f32)


def contract_rows(left, right):
    return lax.dot_general(left, right, (((0,), (0,)), ((), ())), preferred_element_type=f32)


def contract_cols(left, right):
    return lax.dot_general(left, right, (((1,), (1,)), ((), ())), preferred_element_type=f32)


def swap(value, axis, count, bit):
    return lax.ppermute(value, axis, [(i, i ^ bit) for i in range(count)])


def turn(value, axis, count, step):
    return lax.ppermute(value, axis, [(i, (i + step) % count) for i in range(count)])


def chip_bits(count):
    return [1 << i for i in range(1, count.bit_length() - 1)]


def after(value, *earlier):
    return lax.optimization_barrier((value, *earlier))[0]


class Spread:
    def __init__(self, arrays, a, b, names):
        self.arrays, self.a, self.b, self.names = arrays, a, b, names


four_names = (0, 2, 4, 6, 1, 3, 5, 7)


def spread_sides(pair, count):
    return [swap(pair, "mp", count, 2), swap(pair, "mp", count, 4)]


def spread_corner(sides, count):
    a, b = cut(*sides)
    return [swap(a, "mp", count, 4), swap(b, "mp", count, 2)]


def spread_core(arrays, count):
    return [swap(array, "mp", count, 1) for array in arrays]


def spread_four(near, far):
    rows = near[0].shape[0] // 2
    a, b = {}, {}
    for core in range(2):
        base = len(near) * core
        for i, name in enumerate((0, 2, 4)):
            a[name + core] = (base + i, 0)
            b[name + core] = (base + i, rows)
        a[6 + core] = (base + 3, 0)
        b[6 + core] = (base + 4, 0)
    return Spread(near + far, a, b, four_names)


def spread_any(pair, count):
    rows = pair.shape[0] // 2
    held, names = pair.reshape(1, 2, rows, -1), [0]
    for bit in chip_bits(count) + [1]:
        held = jnp.concatenate([held, swap(held, "mp", count, bit)], axis=0)
        names = names + [n ^ bit for n in names]
    arrays = [held.reshape(2 * rows * count, -1)]
    a = {n: (0, 2 * rows * i) for i, n in enumerate(names)}
    b = {n: (0, 2 * rows * i + rows) for i, n in enumerate(names)}
    return Spread(arrays, a, b, tuple(names))


class Scatter:
    def __init__(self, near, came, names, count, rows, rising):
        self.count, self.rows = count, rows
        names = names[: len(names) // 2]
        self.blocks = {n: near[i * rows : (i + 1) * rows] for i, n in enumerate(names)}
        self.adds = {n: came[i * rows : (i + 1) * rows] for i, n in enumerate(names)}
        bits = chip_bits(count)
        self.bits = bits if rising else bits[::-1]

    def total(self, n):
        return self.blocks[n].astype(f32) + self.adds[n].astype(f32)

    def places(self):
        bit, order = self.bits[0], list(self.blocks)
        going = [i for i, n in enumerate(order) if n & bit]
        return going, [i for i, n in enumerate(order) if not n & bit]

    def listed(self, kept):
        return [kept[i : i + self.rows] for i in range(0, kept.shape[0], self.rows)]

    def sent(self):
        bit = self.bits[0]
        stay = [n for n in self.blocks if not n & bit]
        going = jnp.concatenate([self.total(n | bit).astype(bf16) for n in stay], axis=0)
        return going, [self.total(n).astype(bf16) for n in stay]

    def swapped(self, going):
        return swap(going, "mp", self.count, self.bits[0])

    def take(self, kept, came):
        bit, self.bits = self.bits[0], self.bits[1:]
        stay = [n for n in self.blocks if not n & bit]
        self.blocks = dict(zip(stay, kept))
        self.adds = {n: came[i * self.rows : (i + 1) * self.rows] for i, n in enumerate(stay)}


def scatter_group(near, far, names, count, rows):
    scatter = Scatter(near, swap(far, "mp", count, 1), names, count, rows, True)
    while scatter.bits:
        going, kept = scatter.sent()
        scatter.take(kept, scatter.swapped(going))
    return scatter.total(0)


def call(body, name, **kwargs):
    return pl.pallas_call(
        body,
        name=name,
        compiler_params=pltpu.CompilerParams(vmem_limit_bytes=vmem_bytes),
        cost_estimate=pl.CostEstimate(flops=1, bytes_accessed=1, transcendentals=0),
        **kwargs,
    )


def block_copies(spread, which, refs, buffer, sems, rows, block, blocks):
    per = block // rows
    listed = []
    for at in blocks:
        listed.append([])
        for i in range(at * per, (at + 1) * per):
            array, first = getattr(spread, which)[spread.names[i]]
            listed[-1].append(
                pltpu.make_async_copy(
                    refs[array].at[first : first + rows, :],
                    buffer.at[i * rows : (i + 1) * rows, :],
                    sems.at[i],
                )
            )
    return listed


def out_copies(buffer, ref, sems, block, blocks):
    return [
        pltpu.make_async_copy(
            buffer.at[i * block : (i + 1) * block, :],
            ref.at[i * block : (i + 1) * block, :],
            sems.at[i],
        )
        for i in blocks
    ]


def entry_body(*refs, spread, rows, block, blocks, earlier):
    count = len(spread.arrays)
    arrays = refs[:count]
    (gain1, bias1, gain2, bias2, qkv_ref, out_weight_ref) = refs[count : count + 6]
    count += 6 + earlier
    (one_ref, two_ref, hat_ref, raw_ref, grad_ref, cot_ref) = refs[count : count + 6]
    x_buf, c_buf, qkv_buf, out_buf, sem_x, sem_c, sem_out, sem_w = refs[count + 6 :]
    step = pl.program_id(0)
    x_copies = block_copies(spread, "a", arrays, x_buf, sem_x, rows, block, blocks)
    c_copies = block_copies(spread, "b", arrays, c_buf, sem_c, rows, block, blocks)
    outs = out_copies(c_buf, cot_ref, sem_out, block, blocks)

    weights = [
        pltpu.make_async_copy(qkv_ref, qkv_buf, sem_w.at[0]),
        pltpu.make_async_copy(out_weight_ref, out_buf, sem_w.at[1]),
    ]

    @pl.when(step == 0)
    def _():
        start(x_copies[0] + weights + c_copies[0])
        for x_list, c_list in zip(x_copies[1:], c_copies[1:]):
            start(x_list + c_list)

    for i in range(len(outs)):

        @pl.when(step == i)
        def _(i=i):
            wait(x_copies[i])

    here = pl.ds(pl.multiple_of((step * blocks.step + blocks.start) * block, block), block)
    values = x_buf[here, :].astype(f32)
    centred = values - jnp.mean(values, axis=1, keepdims=True)
    hat = centred * lax.rsqrt(jnp.mean(centred * centred, axis=1, keepdims=True) + norm_eps)
    hat_ref[...] = hat.astype(bf16)
    one_ref[...] = (hat * gain1[...] + bias1[...]).astype(bf16)
    two_ref[...] = (hat * gain2[...] + bias2[...]).astype(bf16)

    for i in range(len(outs)):

        @pl.when(step == i)
        def _(i=i):
            wait(c_copies[i])
            outs[i].start()
            if i == 0:
                wait(weights)

    raw_ref[...] = dot_plain(one_ref[...], qkv_buf[...])
    grad_ref[...] = contract_cols(c_buf[here, :], out_buf[...]).astype(bf16)

    @pl.when(step == len(outs) - 1)
    def _():
        for copy in outs:
            copy.wait()


def entry(spread, rows, gains, qkv_weight, out_weight, begin=0, stride=1, earlier=()):
    group_rows = rows * len(spread.names)
    width, deep = qkv_weight.shape
    units = out_weight.shape[0]
    block = min(256, group_rows)
    steps = group_rows // block
    per_group = len(spread.names)
    blocks = range(begin, steps, stride)

    def out_block(columns):
        return pl.BlockSpec((block, columns), lambda i: (i * stride + begin, 0))

    row = pl.BlockSpec((1, width), lambda i: (0, 0))
    anywhere = pl.BlockSpec(memory_space=pl.ANY)
    wide = jax.ShapeDtypeStruct((group_rows, width), bf16)
    first = len(spread.arrays) + 6
    return call(
        functools.partial(
            entry_body, spread=spread, rows=rows, block=block, blocks=blocks, earlier=len(earlier)
        ),
        "entry",
        grid=(len(blocks),),
        in_specs=[anywhere] * len(spread.arrays)
        + [row] * 4
        + [
            anywhere,
            anywhere,
        ]
        + [anywhere] * len(earlier),
        out_specs=[
            out_block(width),
            out_block(width),
            out_block(width),
            out_block(deep),
            out_block(units),
            anywhere,
        ],
        out_shape=[
            wide,
            wide,
            wide,
            jax.ShapeDtypeStruct((group_rows, deep), f32),
            jax.ShapeDtypeStruct((group_rows, units), bf16),
            wide,
        ],
        input_output_aliases={first + i: i for i in range(len(earlier))},
        scratch_shapes=[
            pltpu.VMEM((group_rows, width), bf16),
            pltpu.VMEM((group_rows, width), bf16),
            pltpu.VMEM(qkv_weight.shape, bf16),
            pltpu.VMEM(out_weight.shape, bf16),
            pltpu.SemaphoreType.DMA((per_group,)),
            pltpu.SemaphoreType.DMA((per_group,)),
            pltpu.SemaphoreType.DMA((steps,)),
            pltpu.SemaphoreType.DMA((2,)),
        ],
    )(*spread.arrays, *gains, qkv_weight, out_weight, *earlier)


def pairs_body(input_ref, cot_ref, gain_ref, bias_ref, pair_ref, shared_ref):
    rows = input_ref.shape[0]
    values = input_ref[...].astype(f32)
    centred = values - jnp.mean(values, axis=1, keepdims=True)
    hat = centred * lax.rsqrt(jnp.mean(centred * centred, axis=1, keepdims=True) + norm_eps)
    pair_ref[:rows, :] = input_ref[...]
    pair_ref[rows:, :] = cot_ref[...]
    shared_ref[:rows, :] = (hat * gain_ref[...] + bias_ref[...]).astype(bf16)
    shared_ref[rows:, :] = cot_ref[...]


def pairs(layer_input, cotangent, gain, bias):
    rows, width = layer_input.shape
    return call(
        pairs_body,
        "pairs",
        out_shape=[jax.ShapeDtypeStruct((2 * rows, width), bf16)] * 2,
    )(layer_input, cotangent, gain, bias)


def fold_body(near_ref, came_ref, going_ref, kept_ref, *, rows, going, kept):
    for ref, places in ((going_ref, going), (kept_ref, kept)):
        for i, at in enumerate(places):
            here = slice(at * rows, (at + 1) * rows)
            total = near_ref[here, :].astype(f32) + came_ref[here, :].astype(f32)
            ref[i * rows : (i + 1) * rows, :] = total.astype(bf16)


def folds_body(*refs, count):
    for ref in range(2 * count):
        total = refs[2 * ref][...].astype(f32) + refs[2 * ref + 1][...].astype(f32)
        refs[4 * count + ref][...] = total.astype(bf16)


def fold(sums, rows):
    width = sums[0][0].shape[1]
    operands, in_specs = [], []
    for near, came, places in sums:
        for first, *more in places:
            apart = more[0] - first if more else 0
            spec = pl.BlockSpec((rows, width), lambda i, a=apart, f=first: (a * i + f, 0))
            operands += [near, came]
            in_specs += [spec, spec]
    per = len(sums[0][2][0])
    return call(
        functools.partial(folds_body, count=len(sums)),
        "fold",
        grid=(per,),
        in_specs=in_specs,
        out_specs=[pl.BlockSpec((rows, width), lambda i: (i, 0))] * (2 * len(sums)),
        out_shape=[jax.ShapeDtypeStruct((per * rows, width), bf16)] * (2 * len(sums)),
    )(*operands)


def cut_body(side_x, side_y, x_ref, y_ref):
    x_ref[...] = side_x[...]
    y_ref[...] = side_y[...]


def cut(side_x, side_y):
    rows, width = side_x.shape[0] // 2, side_x.shape[1]
    tops = pl.BlockSpec((rows, width), lambda i: (0, 0))
    return call(
        cut_body,
        "cut",
        grid=(1,),
        in_specs=[tops, pl.BlockSpec((rows, width), lambda i: (1, 0))],
        out_specs=[tops] * 2,
        out_shape=[jax.ShapeDtypeStruct((rows, width), side_x.dtype)] * 2,
    )(side_x, side_y)


def start(copies):
    for copy in copies:
        copy.start()


def wait(copies):
    for copy in copies:
        copy.wait()


def products(x, c, up_ref, down_ref, shift_ref, tiles, hidden_ref, grad_ref, sum_ref):
    gates = [dot_plain(x, up_ref[:, part]) + shift_ref[:, part] for part in tiles]
    for gate, part in zip(gates, tiles):
        grad_hidden = contract_cols(c, down_ref[part, :])
        below = 0.5 * (1.0 + lax.erf(gate * inv_root_two))
        hidden_ref[:, part] = (gate * below).astype(bf16)
        slope = below + gate * jnp.exp(-0.5 * gate * gate) * inv_root_tau
        grad = (grad_hidden * slope).astype(bf16)
        grad_ref[:, part] = grad
        sum_ref[:, part] += jnp.sum(grad.astype(f32), axis=0, keepdims=True)


def column_tiles(units):
    tile = min(512, units)
    return [slice(i, i + tile) for i in range(0, units, tile)]


class Branch:
    def __init__(self, arrays, weights, buffers, sems, spread, rows, block):
        self.up_ref, self.shift_ref, self.down_ref = weights
        self.x_buf, self.c_buf, self.u_buf, self.d_buf = buffers
        sem_x, sem_c, sem_u, sem_d = sems
        self.block = block
        self.every = range(self.x_buf.shape[0] // block)
        self.x_copies = block_copies(spread, "a", arrays, self.x_buf, sem_x, rows, block, self.every)
        self.c_copies = block_copies(spread, "b", arrays, self.c_buf, sem_c, rows, block, self.every)
        self.tiles = column_tiles(self.u_buf.shape[1])
        self.needs = self.x_copies[0] + self.c_copies[0]
        self.needs.append(pltpu.make_async_copy(self.up_ref, self.u_buf, sem_u))
        self.needs.append(pltpu.make_async_copy(self.down_ref, self.d_buf, sem_d))

    def block_step(self, step, hidden_ref, grad_ref, sum_ref, prior_ref, extra=()):
        @pl.when(step == 0)
        def _():
            start(self.needs)
            sum_ref[...] = prior_ref[...]
            wait(self.needs)
            for later in self.every[1:]:
                start(self.x_copies[later] + self.c_copies[later])
            start(extra)

        for i in self.every[1:]:

            @pl.when(step == i)
            def _(i=i):
                wait(self.x_copies[i] + self.c_copies[i])

        here = pl.ds(pl.multiple_of(step * self.block, self.block), self.block)
        products(
            self.x_buf[here, :],
            self.c_buf[here, :],
            self.u_buf,
            self.d_buf,
            self.shift_ref,
            self.tiles,
            hidden_ref.at[here],
            grad_ref.at[here],
            sum_ref,
        )


def branch_scratch(group_rows, width, units, blocks):
    dma = pltpu.SemaphoreType.DMA
    return [
        pltpu.VMEM((group_rows, width), bf16),
        pltpu.VMEM((group_rows, width), bf16),
        pltpu.VMEM((width, units), bf16),
        pltpu.VMEM((units, width), bf16),
        dma((blocks,)),
        dma((blocks,)),
        dma,
        dma,
    ]


def mlp_body(x_ref, c_ref, up_ref, shift_ref, down_ref, hidden_ref, grad_ref, sum_ref):
    @pl.when(pl.program_id(0) == 0)
    def _():
        sum_ref[...] = jnp.zeros_like(sum_ref)

    tiles = column_tiles(up_ref.shape[1])
    products(
        x_ref[...], c_ref[...], up_ref, down_ref, shift_ref, tiles, hidden_ref, grad_ref, sum_ref
    )


def mlp(normed, cotangent, up_weight, up_bias, down_weight):
    width, units = up_weight.shape
    group_rows = normed.shape[0]
    block = min(256, group_rows)
    once = pl.Buffered(1)
    full = pl.BlockSpec((block, width), lambda i: (i, 0))
    part = pl.BlockSpec((block, units), lambda i: (i, 0))
    low = jax.ShapeDtypeStruct((group_rows, units), bf16)
    row = pl.BlockSpec((1, units), lambda i: (0, 0))
    return call(
        mlp_body,
        "mlp",
        grid=(group_rows // block,),
        in_specs=[
            full,
            full,
            pl.BlockSpec(up_weight.shape, lambda i: (0, 0), pipeline_mode=once),
            row,
            pl.BlockSpec(down_weight.shape, lambda i: (0, 0), pipeline_mode=once),
        ],
        out_specs=[part, part, row],
        out_shape=[low, low, jax.ShapeDtypeStruct((1, units), f32)],
    )(normed, cotangent, up_weight, up_bias, down_weight)


def group_body(*refs, spread, rows, block, tile, steps, ups, adds, more, places):
    count = len(spread.arrays)
    arrays, weights, refs = refs[:count], refs[count : count + 3], refs[count + 3 :]
    prior_ref, *refs = refs
    added, refs = refs[: 2 * adds], refs[2 * adds :]
    own, refs = refs[: 4 * more], refs[4 * more :]
    folds, refs = (refs[:2], refs[2:]) if places else ((), refs)
    up_out, down_out, sum_ref = refs[:3]
    folded, refs = (refs[3:5], refs[5:]) if places else ((), refs[3:])
    buffers, sems, (hidden_buf, grad_buf), refs = refs[:4], refs[4:8], refs[8:10], refs[10:]
    branch = Branch(arrays, weights, buffers, sems, spread, rows, block)
    step = pl.program_id(0)
    at = jnp.where(step < steps + ups, step - steps, step - steps - ups)
    at = jnp.maximum(at, 0)
    here = pl.ds(pl.multiple_of(at * tile, tile), tile)
    later = []
    if adds:
        sum_up, sum_down, sem_sum_up, sem_sum_down, *refs = refs

        def up_copy(i):
            first = pl.multiple_of(i * tile, tile)
            return pltpu.make_async_copy(
                added[0].at[pl.ds(first, tile), :], sum_up.at[i % 2], sem_sum_up.at[i % 2]
            )

        def down_copy(i):
            first = pl.multiple_of(i * tile, tile)
            return pltpu.make_async_copy(
                added[1].at[:, pl.ds(first, tile)], sum_down.at[i % 2], sem_sum_down.at[i % 2]
            )

        later = later + [up_copy(0)]
    if more:
        own_bufs, sem_own = refs[:4], refs[4]
        own_copies = [
            pltpu.make_async_copy(ref, buf, sem_own.at[i])
            for i, (ref, buf) in enumerate(zip(own, own_bufs))
        ]
        later = later + own_copies
        rows_own, cot_own, hidden_own, grad_own = own_bufs

    @pl.when(step < steps)
    def _():
        branch.block_step(step, hidden_buf, grad_buf, sum_ref, prior_ref, later)

    if more:

        @pl.when(step == steps)
        def _():
            wait(own_copies)

    if places:

        @pl.when(step >= steps)
        def _():
            fold_body(*folds, *folded, rows=rows, going=places[0], kept=places[1])

    @pl.when((step >= steps) & (step < steps + ups))
    def _():
        if adds:

            @pl.when(at + 1 < ups)
            def _():
                up_copy(at + 1).start()

            @pl.when(at + 1 == ups)
            def _():
                down_copy(0).start()

            up_copy(at).wait()
        total = contract_rows(branch.x_buf[:, here], grad_buf[...])
        if more:
            total = total + contract_rows(rows_own[:, here], grad_own[...])
        if adds:
            total = total + sum_up[at % 2]
        up_out[...] = total

    @pl.when(step >= steps + ups)
    def _():
        if adds:

            @pl.when(at + 1 < ups)
            def _():
                down_copy(at + 1).start()

            down_copy(at).wait()
        total = contract_rows(hidden_buf[...], branch.c_buf[:, here])
        if more:
            total = total + contract_rows(hidden_own[...], cot_own[:, here])
        if adds:
            total = total + sum_down[at % 2]
        down_out[...] = total


def group(spread, rows, up_weight, up_bias, down_weight, prior, added=(), own=(), folds=(), places=()):
    width, units = up_weight.shape
    group_rows = rows * len(spread.names)
    block = min(256, group_rows)
    tile = min(256, units)
    steps, blocks = group_rows // block, len(spread.names)
    ups = width // tile
    anywhere = pl.BlockSpec(memory_space=pl.ANY)
    row = pl.BlockSpec((1, units), lambda i: (0, 0))
    dma = pltpu.SemaphoreType.DMA
    scratch = branch_scratch(group_rows, width, units, blocks)
    scratch += [pltpu.VMEM((group_rows, units), bf16)] * 2
    if added:
        scratch += [
            pltpu.VMEM((2, tile, units), f32),
            pltpu.VMEM((2, units, tile), f32),
            dma((2,)),
            dma((2,)),
        ]
    if own:
        scratch += [pltpu.VMEM(array.shape, bf16) for array in own] + [dma((4,))]
    fold_in, fold_out, fold_shape = [], [], []
    if folds:
        strip = width // (2 * ups)
        half = folds[0].shape[0] // 2

        def column(i):
            return 0, jnp.clip(i - steps, 0, 2 * ups - 1)

        fold_in = [pl.BlockSpec((2 * half, strip), column)] * 2
        fold_out = [pl.BlockSpec((half, strip), column)] * 2
        fold_shape = [jax.ShapeDtypeStruct((half, width), bf16)] * 2
    return call(
        functools.partial(
            group_body,
            spread=spread,
            rows=rows,
            block=block,
            tile=tile,
            steps=steps,
            ups=ups,
            adds=bool(added),
            more=bool(own),
            places=places,
        ),
        "group",
        grid=(steps + 2 * ups,),
        in_specs=[anywhere] * len(spread.arrays)
        + [anywhere, row, anywhere, row]
        + [anywhere] * (len(added) + len(own))
        + fold_in,
        out_specs=[
            pl.BlockSpec((tile, units), lambda i: (jnp.clip(i - steps, 0, ups - 1), 0)),
            pl.BlockSpec((units, tile), lambda i: (0, jnp.clip(i - steps - ups, 0, ups - 1))),
            row,
        ]
        + fold_out,
        out_shape=[
            jax.ShapeDtypeStruct((width, units), f32),
            jax.ShapeDtypeStruct((units, width), f32),
            jax.ShapeDtypeStruct((1, units), f32),
        ]
        + fold_shape,
        scratch_shapes=scratch,
    )(*spread.arrays, up_weight, up_bias, down_weight, prior, *added, *own, *folds)


def weight_body(left_ref, right_ref, out_ref):
    out_ref[...] = contract_rows(left_ref[...], right_ref[...])


def weight_product(left, right):
    wide, deep = left.shape[1], right.shape[1]
    tile = min(512, wide)
    return call(
        weight_body,
        "weight_product",
        grid=(wide // tile,),
        in_specs=[
            pl.BlockSpec((left.shape[0], tile), lambda i: (0, i)),
            pl.BlockSpec(right.shape, lambda i: (0, 0), pipeline_mode=pl.Buffered(1)),
        ],
        out_specs=pl.BlockSpec((tile, deep), lambda i: (i, 0)),
        out_shape=jax.ShapeDtypeStruct((wide, deep), f32),
    )(left, right)


def attention_weights_body(normed_ref, grad_qkv_ref, attended_ref, grad_out_ref, sum_ref):
    deep = grad_qkv_ref.shape[1]
    sum_ref[:, :deep] = contract_rows(normed_ref[...], grad_qkv_ref[...]).astype(bf16)
    sum_ref[:, deep:] = contract_rows(attended_ref[...], grad_out_ref[...]).astype(bf16)


def attention_weights(normed, grad_qkv, attended, grad_out):
    group_rows, width = normed.shape
    deep, units = grad_qkv.shape[1], attended.shape[1]
    once = pl.Buffered(1)
    block = pl.BlockSpec((group_rows, units), lambda i: (0, i))
    return call(
        attention_weights_body,
        "attention_weights",
        grid=(width // units,),
        in_specs=[
            block,
            pl.BlockSpec(grad_qkv.shape, lambda i: (0, 0), pipeline_mode=once),
            pl.BlockSpec(attended.shape, lambda i: (0, 0), pipeline_mode=once),
            block,
        ],
        out_specs=pl.BlockSpec((units, deep + units), lambda i: (i, 0)),
        out_shape=jax.ShapeDtypeStruct((width, deep + units), bf16),
    )(normed, grad_qkv, attended, grad_out)


def widen_body(sum_ref, qkv_ref, out_ref):
    units, deep = out_ref.shape[0], qkv_ref.shape[1]
    qkv_ref[...] = sum_ref[:, :deep].astype(f32)
    for first in range(0, sum_ref.shape[0], units):
        out_ref[:, first : first + units] = sum_ref[first : first + units, deep:].astype(f32)


def widen(total, deep, units):
    width = total.shape[0]
    block = min(2 * units, width)
    return call(
        widen_body,
        "widen",
        grid=(width // block,),
        in_specs=[pl.BlockSpec((block, deep + units), lambda i: (i, 0))],
        out_specs=[
            pl.BlockSpec((block, deep), lambda i: (i, 0)),
            pl.BlockSpec((units, block), lambda i: (0, i)),
        ],
        out_shape=[
            jax.ShapeDtypeStruct((width, deep), f32),
            jax.ShapeDtypeStruct((units, width), f32),
        ],
    )(total)


def branch_body(attended_ref, hidden_ref, out_ref, down_ref, near_ref, far_ref):
    middle = near_ref.shape[0]
    total = dot_plain(attended_ref[...], out_ref[...]) + dot_plain(hidden_ref[...], down_ref[...])
    near_ref[...] = total[:middle].astype(bf16)
    far_ref[...] = total[middle:].astype(bf16)


def branch_sum(attended, hidden, out_weight, down_weight):
    group_rows = attended.shape[0]
    width = out_weight.shape[1]
    tile = min(512, width)
    once = pl.Buffered(1)
    half = pl.BlockSpec((group_rows // 2, tile), lambda i: (0, i))
    return call(
        branch_body,
        "branch_sum",
        grid=(width // tile,),
        in_specs=[
            pl.BlockSpec(attended.shape, lambda i: (0, 0), pipeline_mode=once),
            pl.BlockSpec(hidden.shape, lambda i: (0, 0), pipeline_mode=once),
            pl.BlockSpec((out_weight.shape[0], tile), lambda i: (0, i)),
            pl.BlockSpec((down_weight.shape[0], tile), lambda i: (0, i)),
        ],
        out_specs=[half, half],
        out_shape=[jax.ShapeDtypeStruct((group_rows // 2, width), bf16)] * 2,
    )(attended, hidden, out_weight, down_weight)


def input_body(
    qkv_grad_ref, gate_grad_ref, qkv_ref, up_ref, gain1, gain2, hat_ref, near_ref, far_ref, sum_ref
):
    middle = near_ref.shape[0]
    hat = hat_ref[...].astype(f32)
    first = contract_cols(qkv_grad_ref[...], qkv_ref[...])
    second = contract_cols(gate_grad_ref[...], up_ref[...])
    both = first * gain1[...] + second * gain2[...]
    near_ref[...] = both[:middle].astype(bf16)
    far_ref[...] = both[middle:].astype(bf16)
    sum_ref[0:1, :] = jnp.sum(first * hat, axis=0, keepdims=True)
    sum_ref[1:2, :] = jnp.sum(first, axis=0, keepdims=True)
    sum_ref[2:3, :] = jnp.sum(second * hat, axis=0, keepdims=True)
    sum_ref[3:4, :] = jnp.sum(second, axis=0, keepdims=True)


def input_sums(grad_qkv, grad_gate, qkv_weight, up_weight, gain1, gain2, hat):
    group_rows = grad_qkv.shape[0]
    width = qkv_weight.shape[0]
    tile = min(256, width)
    once = pl.Buffered(1)
    half = pl.BlockSpec((group_rows // 2, tile), lambda i: (0, i))
    row = pl.BlockSpec((1, tile), lambda i: (0, i))
    return call(
        input_body,
        "input_sums",
        grid=(width // tile,),
        in_specs=[
            pl.BlockSpec(grad_qkv.shape, lambda i: (0, 0), pipeline_mode=once),
            pl.BlockSpec(grad_gate.shape, lambda i: (0, 0), pipeline_mode=once),
            pl.BlockSpec((tile, qkv_weight.shape[1]), lambda i: (i, 0)),
            pl.BlockSpec((tile, up_weight.shape[1]), lambda i: (i, 0)),
            row,
            row,
            pl.BlockSpec((group_rows, tile), lambda i: (0, i)),
        ],
        out_specs=[half, half, pl.BlockSpec((4, tile), lambda i: (0, i))],
        out_shape=[jax.ShapeDtypeStruct((group_rows // 2, width), bf16)] * 2
        + [jax.ShapeDtypeStruct((4, width), f32)],
    )(grad_qkv, grad_gate, qkv_weight, up_weight, gain1, gain2, hat)


def attention_body(
    places_ref,
    starts_ref,
    raw_ref,
    bias_ref,
    cos_ref,
    sine_ref,
    slope_in_ref,
    attended_ref,
    grad_qkv_ref,
    bias_grad_ref,
    query_ref,
    key_ref,
    value_ref,
    slope_ref,
    query_sum_ref,
    key_sum_ref,
    value_sum_ref,
    *,
    rows,
    block_rows,
    longest,
):
    group_rows = raw_ref.shape[0]
    count = group_rows // rows
    lane = lax.broadcasted_iota(jnp.int32, (rows, HEAD_DIM), 1)
    half = ROTARY // 2
    scale = HEAD_DIM ** (-0.5)

    def turned(u):
        return jnp.where(lane < half, pltpu.roll(u, HEAD_DIM - half, 1), pltpu.roll(u, half, 1))

    def both_rows(i):
        near = pl.ds(pl.multiple_of(i * rows, rows), rows)
        return near, pl.ds(pl.multiple_of(places_ref[i] * rows, rows), rows)

    def arrange(i, _):
        near, far = both_rows(i)
        raw = raw_ref[near, :] + bias_ref[...]
        cos_table = cos_ref[near, :]
        sine_table = sine_ref[near, :]
        query = raw[:, :HEAD_DIM]
        key = raw[:, HEAD_DIM : 2 * HEAD_DIM]
        query_ref[far, :] = (query * cos_table + turned(query) * sine_table).astype(bf16)
        key_ref[far, :] = (key * cos_table + turned(key) * sine_table).astype(bf16)
        value_ref[far, :] = raw[:, 2 * HEAD_DIM :].astype(bf16)
        slope_ref[far, :] = slope_in_ref[near, :]
        return 0

    lax.fori_loop(0, count, arrange, 0)
    key_sum_ref[...] = jnp.zeros_like(key_sum_ref)
    value_sum_ref[...] = jnp.zeros_like(value_sum_ref)

    def block(first, low, span):
        here = pl.ds(first, block_rows)
        seen = pl.ds(low, span)
        query = query_ref[here, :]
        keys = key_ref[seen, :]
        values = value_ref[seen, :]
        slope = slope_ref[here, :]
        scores = contract_cols(query, keys) * scale
        row = first + lax.broadcasted_iota(jnp.int32, (block_rows, 1), 0)
        begin = jnp.zeros((block_rows, 1), jnp.int32)
        for slot in range(starts_ref.shape[0]):
            begin = jnp.where(starts_ref[slot] <= row, starts_ref[slot], begin)
        column = low + lax.broadcasted_iota(jnp.int32, scores.shape, 1)
        scores = jnp.where((column >= begin) & (column <= row), scores, masked_score)
        peak = jnp.max(scores, axis=1, keepdims=True)
        raised = jnp.exp(scores - peak)
        probs = raised * (1.0 / jnp.sum(raised, axis=1, keepdims=True))
        probs_low = probs.astype(bf16)
        query_ref[here, :] = dot_plain(probs_low, values).astype(bf16)
        grad_probs = contract_cols(slope, values)
        delta = jnp.sum(grad_probs * probs, axis=1, keepdims=True)
        grad_score = (probs * (grad_probs - delta)).astype(bf16)
        query_sum_ref[here, :] = dot_plain(grad_score, keys) * scale
        key_sum_ref[seen, :] += contract_rows(grad_score, query) * scale
        value_sum_ref[seen, :] += contract_rows(probs_low, slope)

    for first in range(0, longest, block_rows):
        block(first, 0, first + block_rows)

    def later(i, _):
        first = pl.multiple_of(longest + i * block_rows, block_rows)
        block(first, pl.multiple_of(i * block_rows, block_rows), longest + block_rows)
        return 0

    lax.fori_loop(0, (group_rows - longest) // block_rows, later, 0)

    def give_back(i, bias_grad):
        near, far = both_rows(i)
        cos_table = cos_ref[near, :]
        sine_table = sine_ref[near, :]
        query_grad = query_sum_ref[far, :]
        key_grad = key_sum_ref[far, :]
        grads = jnp.concatenate(
            [
                query_grad * cos_table - turned(query_grad) * sine_table,
                key_grad * cos_table - turned(key_grad) * sine_table,
                value_sum_ref[far, :],
            ],
            axis=1,
        ).astype(bf16)
        grad_qkv_ref[near, :] = grads
        attended_ref[near, :] = query_ref[far, :]
        return bias_grad + jnp.sum(grads.astype(f32), axis=0, keepdims=True)

    bias_grad_ref[...] = lax.fori_loop(
        0, count, give_back, jnp.zeros(bias_grad_ref.shape, f32)
    )


def attention(places, starts, raw, bias, cos_table, sine_table, slope, rows):
    group_rows, width = raw.shape
    part = 3 * HEAD_DIM
    heads = width // part
    whole = pl.BlockSpec((group_rows, HEAD_DIM), lambda h: (0, 0))
    scalars = pl.BlockSpec(memory_space=pltpu.SMEM)
    low = pltpu.VMEM((group_rows, HEAD_DIM), bf16)
    wide = pltpu.VMEM((group_rows, HEAD_DIM), f32)
    longest = group_rows // 2
    return pl.pallas_call(
        functools.partial(
            attention_body,
            rows=rows,
            block_rows=min(256, longest),
            longest=longest,
        ),
        grid=(heads,),
        in_specs=[
            scalars,
            scalars,
            pl.BlockSpec((group_rows, part), lambda h: (0, h)),
            pl.BlockSpec((1, part), lambda h: (0, h)),
            whole,
            whole,
            pl.BlockSpec((group_rows, HEAD_DIM), lambda h: (0, h)),
        ],
        out_specs=[
            pl.BlockSpec((group_rows, HEAD_DIM), lambda h: (0, h)),
            pl.BlockSpec((group_rows, part), lambda h: (0, h)),
            pl.BlockSpec((1, part), lambda h: (0, h)),
        ],
        out_shape=[
            jax.ShapeDtypeStruct((group_rows, heads * HEAD_DIM), bf16),
            jax.ShapeDtypeStruct((group_rows, width), bf16),
            jax.ShapeDtypeStruct((1, width), f32),
        ],
        scratch_shapes=[low, low, low, low, wide, wide, wide],
        compiler_params=pltpu.CompilerParams(vmem_limit_bytes=vmem_bytes),
        cost_estimate=pl.CostEstimate(flops=1, bytes_accessed=1, transcendentals=0),
        name="attention",
    )(places, starts, raw, bias, cos_table, sine_table, slope)


def rotary_tables(position):
    half_rot = ROTARY // 2
    frequency = 10000.0 ** (-2.0 * jnp.arange(half_rot, dtype=f32) / ROTARY)
    angles = frequency[:, None] * position.astype(f32)[None, :]
    cos_half, sine_half = lax.optimization_barrier((jnp.cos(angles), jnp.sin(angles)))
    rest = (HEAD_DIM - ROTARY, position.shape[0])
    return (
        jnp.concatenate([cos_half, cos_half, jnp.ones(rest, f32)], axis=0).T,
        jnp.concatenate([-sine_half, sine_half, jnp.zeros(rest, f32)], axis=0).T,
    )


def butterfly(value, axis, count, bit):
    return value + swap(value, axis, count, bit)


def fence(*values):
    return lax.optimization_barrier(values)


def norm_own(layer_input):
    values = layer_input.astype(f32)
    centred = values - jnp.mean(values, axis=-1, keepdims=True)
    inv_std = lax.rsqrt(jnp.mean(centred * centred, axis=-1, keepdims=True) + norm_eps)
    return centred * inv_std, inv_std


def tables(own, lengths, names, rows):
    seq_ends = jnp.cumsum(lengths)
    seq_starts = seq_ends - lengths
    places = (
        (own ^ jnp.array(names, jnp.int32))[:, None] * rows
        + jnp.arange(rows, dtype=jnp.int32)[None, :]
    ).reshape(-1)
    seq_first = jnp.max(
        jnp.where(seq_starts[None, :] <= places[:, None], seq_starts[None, :], 0), axis=1
    )
    return (seq_starts, *rotary_tables(places - seq_first))


def ends(layer_input, cotangent, xhat, inv_std, branch, scaled, biases):
    layer_output = (layer_input.astype(f32) + branch + biases).astype(bf16)
    input_grad = cotangent.astype(f32) + inv_std * (
        scaled
        - jnp.mean(scaled, axis=-1, keepdims=True)
        - xhat * jnp.mean(scaled * xhat, axis=-1, keepdims=True)
    )
    return layer_output, input_grad


def per_device(
    layer_input,
    lengths,
    norm1_gain,
    norm1_bias,
    norm2_gain,
    norm2_bias,
    qkv_weight,
    qkv_bias,
    out_weight,
    out_bias,
    up_weight,
    up_bias,
    down_weight,
    down_bias,
    cotangent,
):
    dp = lax.axis_size("dp")
    mp = lax.axis_size("mp")
    own = lax.axis_index("mp")
    rows, width = layer_input.shape
    up_row = up_bias[None, :]
    gains = (norm1_gain[None, :], norm1_bias[None, :], norm2_gain[None, :], norm2_bias[None, :])
    gather_all = mp == 8 and dp == 4 and 4 * rows * mp * dp * (width + up_bias.shape[0]) < most_gathered

    pair, shared = pairs(layer_input, cotangent, *gains[2:])
    if gather_all:
        names = four_names
        sides = spread_sides(pair, mp)
        group_a = turn(shared, "dp", dp, 1)
        placed = tables(own, lengths[0], names, rows)
        far = spread_core([pair], mp)
        shared, pair, sides, placed, far, group_a = fence(shared, pair, sides, placed, far, group_a)
        group_b = turn(shared, "dp", dp, -1)
        corner = spread_corner(sides, mp)
        near = [pair, *sides]
        far = far + spread_core(sides, mp)
        begun = entry(spread_four(near, far), rows, gains, qkv_weight, out_weight, 0, 2)
        near, far, corner, group_a, begun = fence(near, far, corner, group_a, begun)
        near, far = near + corner, far + spread_core(corner, mp)
        sides_a = spread_sides(group_a, mp)
        entered = entry(spread_four(near, far), rows, gains, qkv_weight, out_weight, 1, 2, begun)
        entered, group_b, group_a = fence(entered, group_b, group_a)
        far_a = spread_core([group_a], mp)
        group_c = turn(group_a, "dp", dp, 1)
    else:
        spread = spread_any(pair, mp)
        names = spread.names
        placed = tables(own, lengths[0], names, rows)
        entered = entry(spread, rows, gains, qkv_weight, out_weight)
    seq_starts, cos_table, sine_table = placed

    first_all, second_all, hat, raw, grad_attended, grad_out = entered
    attended, grad_qkv, qkv_bias_part = attention(
        own ^ jnp.array(names, jnp.int32),
        seq_starts,
        raw,
        qkv_bias[None, :],
        cos_table,
        sine_table,
        grad_attended,
        rows,
    )
    if gather_all:
        (first_all, second_all, hat, grad_out, attended, grad_qkv), near_a, far_a, group_b = fence(
            (first_all, second_all, hat, grad_out, attended, grad_qkv),
            [group_a, *sides_a],
            far_a,
            group_b,
        )

    weights_part = attention_weights(first_all, grad_qkv, attended, grad_out)
    if gather_all:
        corner_a = spread_corner(near_a[1:], mp)
        far_a = far_a + spread_core(near_a[1:], mp)
        (weights_part, second_all, hat, grad_out, attended), near_a, corner_a, far_a, group_b, group_c = (
            fence(
                (weights_part, second_all, hat, grad_out, attended),
                near_a,
                corner_a,
                far_a,
                group_b,
                group_c,
            )
        )
    weights_sum = lax.psum_scatter(weights_part, "dp", scatter_dimension=0, tiled=True)

    hidden, grad_gate, gate_sum = mlp(second_all, grad_out, up_weight, up_row, down_weight)
    branch = branch_sum(attended, hidden, out_weight, down_weight)
    if gather_all:
        sides_b = spread_sides(group_b, mp)
        far_b = spread_core([group_b], mp)
        far_a = far_a + spread_core(corner_a, mp)
        near_a = near_a + corner_a
        (hidden, grad_gate, branch, grad_qkv, hat), near_a, far_a, near_b, far_b, group_c = fence(
            (hidden, grad_gate, branch, grad_qkv, hat),
            near_a,
            far_a,
            [group_b, *sides_b],
            far_b,
            group_c,
        )

    scaled = input_sums(grad_qkv, grad_gate, qkv_weight, up_weight, gains[0], gains[2], hat)
    cot_sum = jnp.sum(cotangent.astype(f32), axis=0)
    small = jnp.concatenate([scaled[2].reshape(-1), cot_sum, qkv_bias_part.reshape(-1)])
    small = small.reshape(-1, 128)
    five = 5 * width // 128
    biases = out_bias + down_bias
    xhat, inv_std = norm_own(layer_input)

    def over_mp(both, bit):
        return jnp.concatenate([butterfly(both[:five], "mp", mp, bit), both[five:]], axis=0)

    if not gather_all:
        own_branch = scatter_group(*branch, names, mp, rows)
        own_scaled = scatter_group(*scaled[:2], names, mp, rows)
        layer_output, input_grad = ends(
            layer_input, cotangent, xhat, inv_std, own_branch, own_scaled, biases
        )
        for bit in (1 << i for i in range(dp.bit_length() - 1)):
            small = butterfly(small, "dp", dp, bit)
        small, qkv_bias_grad = small[:five], small[five:]
        for bit in (1 << i for i in range(mp.bit_length() - 1)):
            small = butterfly(small, "mp", mp, bit)
        weights_sum = lax.all_gather(weights_sum, "dp", axis=0, tiled=True)
        up_weight_grad, down_weight_grad, up_bias_grad = lax.psum(
            (weight_product(second_all, grad_gate), weight_product(hidden, grad_out), gate_sum[0]),
            "dp",
        )
    else:
        corner_b = spread_corner(near_b[1:], mp)
        far_b = far_b + spread_core(near_b[1:], mp)
        branch_came = swap(branch[1], "mp", mp, 1)
        scaled, small, near_a, far_a, near_b, far_b, corner_b, branch_came, group_c = fence(
            scaled, small, near_a, far_a, near_b, far_b, corner_b, branch_came, group_c
        )

        own_branch = Scatter(branch[0], branch_came, names, mp, rows, True)
        small = over_mp(small, 1)
        sides_c = spread_sides(group_c, mp)
        scaled_came = swap(scaled[1], "mp", mp, 1)
        far_b = far_b + spread_core(corner_b, mp)
        near_b = near_b + corner_b
        up_sum, down_sum, sum_a, *branch_sent = group(
            spread_four(near_a, far_a),
            rows,
            up_weight,
            up_row,
            down_weight,
            gate_sum,
            folds=(branch[0], branch_came),
            places=own_branch.places(),
        )
        sums, near_b, far_b, near_c, branch_sent, scaled_came, small, weights_sum = fence(
            (up_sum, down_sum),
            near_b,
            far_b,
            [group_c, *sides_c],
            branch_sent,
            scaled_came,
            small,
            weights_sum,
        )

        weights_sum = lax.all_gather(weights_sum, "dp", axis=0, tiled=True)
        own_scaled = Scatter(scaled[0], scaled_came, names, mp, rows, False)
        scaled_sent = fold([(scaled[0], scaled_came, own_scaled.places())], rows)
        far_c = spread_core(near_c[:1], mp)
        corner_c = spread_corner(near_c[1:], mp)
        small = over_mp(small, 2)
        scaled_sent, branch_sent, far_c, small, sums = fence(
            scaled_sent, branch_sent, far_c, small, sums
        )
        up_sum, down_sum, sum_b = group(
            spread_four(near_b, far_b), rows, up_weight, up_row, down_weight, sum_a, sums
        )
        sums, near_c, far_c, corner_c, branch_came, branch_kept, scaled_came, scaled_kept, small = fence(
            (up_sum, down_sum),
            near_c,
            far_c,
            corner_c,
            own_branch.swapped(branch_sent[0]),
            branch_sent[1],
            own_scaled.swapped(scaled_sent[0]),
            scaled_sent[1],
            small,
        )

        far_c = far_c + spread_core(near_c[1:] + corner_c, mp)
        near_c = near_c + corner_c
        small = over_mp(small, 4)
        own_branch.take(own_branch.listed(branch_kept), branch_came)
        own_scaled.take(own_scaled.listed(scaled_kept), scaled_came)
        folded = fold(
            [
                (branch_kept, branch_came, own_branch.places()),
                (scaled_kept, scaled_came, own_scaled.places()),
            ],
            rows,
        )
        near_c, far_c, small, branch_sent, scaled_sent = fence(
            near_c, far_c, small, folded[:2], folded[2:]
        )
        up_weight_grad, down_weight_grad, sum_c = group(
            spread_four(near_c, far_c),
            rows,
            up_weight,
            up_row,
            down_weight,
            sum_b,
            sums,
            (second_all, grad_out, hidden, grad_gate),
        )
        up_weight_grad, branch_came, branch_kept, scaled_came, scaled_kept, z_sums = fence(
            up_weight_grad,
            own_branch.swapped(branch_sent[0]),
            branch_sent[1],
            own_scaled.swapped(scaled_sent[0]),
            scaled_sent[1],
            [small] + [swap(small, "dp", dp, bit) for bit in (1, 2, 3)],
        )
        own_branch.take([branch_kept], branch_came)
        own_scaled.take([scaled_kept], scaled_came)
        branch_total, scaled_total = own_branch.total(0), own_scaled.total(0)
        small = (z_sums[0] + z_sums[1]) + (z_sums[2] + z_sums[3])
        layer_output, input_grad = ends(
            layer_input, cotangent, xhat, inv_std, branch_total, scaled_total, biases
        )
        up_bias_grad = sum_c[0]
        small, qkv_bias_grad = small[:five], small[five:]
    qkv_weight_grad, out_weight_grad = widen(weights_sum, qkv_weight.shape[1], out_weight.shape[0])
    small = small.reshape(5, width)
    return (
        layer_output,
        input_grad,
        small[0],
        small[1],
        small[2],
        small[3],
        qkv_weight_grad,
        qkv_bias_grad.reshape(-1),
        out_weight_grad,
        small[4],
        up_weight_grad,
        up_bias_grad,
        down_weight_grad,
        small[4],
    )


def solution(mesh):
    in_specs = (
        P(("dp", "mp"), None),
        P("dp", None),
        P(),
        P(),
        P(),
        P(),
        P(None, "mp"),
        P("mp"),
        P("mp", None),
        P(),
        P(None, "mp"),
        P("mp"),
        P("mp", None),
        P(),
        P(("dp", "mp"), None),
    )
    out_specs = (
        P(("dp", "mp"), None),
        P(("dp", "mp"), None),
        P(),
        P(),
        P(),
        P(),
        P(None, "mp"),
        P("mp"),
        P("mp", None),
        P(),
        P(None, "mp"),
        P("mp"),
        P("mp", None),
        P(),
    )
    return jax.shard_map(
        per_device, mesh=mesh, in_specs=in_specs, out_specs=out_specs, check_vma=False
    )
```

```python
import functools

import jax
import jax.numpy as jnp
from jax import lax
from jax.experimental import pallas as pl
from jax.experimental.pallas import tpu as pltpu
from jax.sharding import PartitionSpec as P

HEAD_DIM = 128
ROTARY = 32

norm_eps = 1e-05
masked_score = -1e30
inv_root_two = 0.7071067811865476
inv_root_tau = 0.3989422804014327
vmem_bytes = 60 << 20
most_gathered = 128 << 20
bf16 = jnp.bfloat16
f32 = jnp.float32


def dot_plain(left, right):
    return jnp.dot(left, right, preferred_element_type=f32)


def contract_rows(left, right):
    return lax.dot_general(left, right, (((0,), (0,)), ((), ())), preferred_element_type=f32)


def contract_cols(left, right):
    return lax.dot_general(left, right, (((1,), (1,)), ((), ())), preferred_element_type=f32)


def swap(value, axis, count, bit):
    return lax.ppermute(value, axis, [(i, i ^ bit) for i in range(count)])


def turn(value, axis, count, step):
    return lax.ppermute(value, axis, [(i, (i + step) % count) for i in range(count)])


def chip_bits(count):
    return [1 << i for i in range(1, count.bit_length() - 1)]


def after(value, *earlier):
    return lax.optimization_barrier((value, *earlier))[0]


class Spread:
    def __init__(self, arrays, a, b, names):
        self.arrays, self.a, self.b, self.names = arrays, a, b, names


four_names = (0, 2, 4, 6, 1, 3, 5, 7)


def spread_sides(pair, count):
    return [swap(pair, "mp", count, 2), swap(pair, "mp", count, 4)]


def spread_corner(sides, count):
    a, b = cut(*sides)
    return [swap(a, "mp", count, 4), swap(b, "mp", count, 2)]


def spread_core(arrays, count):
    return [swap(array, "mp", count, 1) for array in arrays]


def spread_four(near, far):
    rows = near[0].shape[0] // 2
    a, b = {}, {}
    for core in range(2):
        base = len(near) * core
        for i, name in enumerate((0, 2, 4)):
            a[name + core] = (base + i, 0)
            b[name + core] = (base + i, rows)
        a[6 + core] = (base + 3, 0)
        b[6 + core] = (base + 4, 0)
    return Spread(near + far, a, b, four_names)


def spread_any(pair, count):
    rows = pair.shape[0] // 2
    held, names = pair.reshape(1, 2, rows, -1), [0]
    for bit in chip_bits(count) + [1]:
        held = jnp.concatenate([held, swap(held, "mp", count, bit)], axis=0)
        names = names + [n ^ bit for n in names]
    arrays = [held.reshape(2 * rows * count, -1)]
    a = {n: (0, 2 * rows * i) for i, n in enumerate(names)}
    b = {n: (0, 2 * rows * i + rows) for i, n in enumerate(names)}
    return Spread(arrays, a, b, tuple(names))


class Scatter:
    def __init__(self, near, came, names, count, rows, rising):
        self.count, self.rows = count, rows
        names = names[: len(names) // 2]
        self.blocks = {n: near[i * rows : (i + 1) * rows] for i, n in enumerate(names)}
        self.adds = {n: came[i * rows : (i + 1) * rows] for i, n in enumerate(names)}
        bits = chip_bits(count)
        self.bits = bits if rising else bits[::-1]

    def total(self, n):
        return self.blocks[n].astype(f32) + self.adds[n].astype(f32)

    def places(self):
        bit, order = self.bits[0], list(self.blocks)
        going = [i for i, n in enumerate(order) if n & bit]
        return going, [i for i, n in enumerate(order) if not n & bit]

    def listed(self, kept):
        return [kept[i : i + self.rows] for i in range(0, kept.shape[0], self.rows)]

    def sent(self):
        bit = self.bits[0]
        stay = [n for n in self.blocks if not n & bit]
        going = jnp.concatenate([self.total(n | bit).astype(bf16) for n in stay], axis=0)
        return going, [self.total(n).astype(bf16) for n in stay]

    def swapped(self, going):
        return swap(going, "mp", self.count, self.bits[0])

    def take(self, kept, came):
        bit, self.bits = self.bits[0], self.bits[1:]
        stay = [n for n in self.blocks if not n & bit]
        self.blocks = dict(zip(stay, kept))
        self.adds = {n: came[i * self.rows : (i + 1) * self.rows] for i, n in enumerate(stay)}


def scatter_group(near, far, names, count, rows):
    scatter = Scatter(near, swap(far, "mp", count, 1), names, count, rows, True)
    while scatter.bits:
        going, kept = scatter.sent()
        scatter.take(kept, scatter.swapped(going))
    return scatter.total(0)


def call(body, name, **kwargs):
    return pl.pallas_call(
        body,
        name=name,
        compiler_params=pltpu.CompilerParams(vmem_limit_bytes=vmem_bytes),
        cost_estimate=pl.CostEstimate(flops=1, bytes_accessed=1, transcendentals=0),
        **kwargs,
    )


def block_copies(spread, which, refs, buffer, sems, rows, block, blocks):
    per = block // rows
    listed = []
    for at in blocks:
        listed.append([])
        for i in range(at * per, (at + 1) * per):
            array, first = getattr(spread, which)[spread.names[i]]
            listed[-1].append(
                pltpu.make_async_copy(
                    refs[array].at[first : first + rows, :],
                    buffer.at[i * rows : (i + 1) * rows, :],
                    sems.at[i],
                )
            )
    return listed


def out_copies(buffer, ref, sems, block, blocks):
    return [
        pltpu.make_async_copy(
            buffer.at[i * block : (i + 1) * block, :],
            ref.at[i * block : (i + 1) * block, :],
            sems.at[i],
        )
        for i in blocks
    ]


def entry_body(*refs, spread, rows, block, blocks, earlier):
    count = len(spread.arrays)
    arrays = refs[:count]
    (gain1, bias1, gain2, bias2, qkv_ref, out_weight_ref) = refs[count : count + 6]
    count += 6 + earlier
    (one_ref, two_ref, hat_ref, raw_ref, grad_ref, cot_ref) = refs[count : count + 6]
    x_buf, c_buf, qkv_buf, out_buf, sem_x, sem_c, sem_out, sem_w = refs[count + 6 :]
    step = pl.program_id(0)
    x_copies = block_copies(spread, "a", arrays, x_buf, sem_x, rows, block, blocks)
    c_copies = block_copies(spread, "b", arrays, c_buf, sem_c, rows, block, blocks)
    outs = out_copies(c_buf, cot_ref, sem_out, block, blocks)

    weights = [
        pltpu.make_async_copy(qkv_ref, qkv_buf, sem_w.at[0]),
        pltpu.make_async_copy(out_weight_ref, out_buf, sem_w.at[1]),
    ]

    @pl.when(step == 0)
    def _():
        start(x_copies[0] + weights + c_copies[0])
        for x_list, c_list in zip(x_copies[1:], c_copies[1:]):
            start(x_list + c_list)

    for i in range(len(outs)):

        @pl.when(step == i)
        def _(i=i):
            wait(x_copies[i])

    here = pl.ds(pl.multiple_of((step * blocks.step + blocks.start) * block, block), block)
    values = x_buf[here, :].astype(f32)
    centred = values - jnp.mean(values, axis=1, keepdims=True)
    hat = centred * lax.rsqrt(jnp.mean(centred * centred, axis=1, keepdims=True) + norm_eps)
    hat_ref[...] = hat.astype(bf16)
    one_ref[...] = (hat * gain1[...] + bias1[...]).astype(bf16)
    two_ref[...] = (hat * gain2[...] + bias2[...]).astype(bf16)

    for i in range(len(outs)):

        @pl.when(step == i)
        def _(i=i):
            wait(c_copies[i])
            outs[i].start()
            if i == 0:
                wait(weights)

    raw_ref[...] = dot_plain(one_ref[...], qkv_buf[...])
    grad_ref[...] = contract_cols(c_buf[here, :], out_buf[...]).astype(bf16)

    @pl.when(step == len(outs) - 1)
    def _():
        for copy in outs:
            copy.wait()


def entry(spread, rows, gains, qkv_weight, out_weight, begin=0, stride=1, earlier=()):
    group_rows = rows * len(spread.names)
    width, deep = qkv_weight.shape
    units = out_weight.shape[0]
    block = min(256, group_rows)
    steps = group_rows // block
    per_group = len(spread.names)
    blocks = range(begin, steps, stride)

    def out_block(columns):
        return pl.BlockSpec((block, columns), lambda i: (i * stride + begin, 0))

    row = pl.BlockSpec((1, width), lambda i: (0, 0))
    anywhere = pl.BlockSpec(memory_space=pl.ANY)
    wide = jax.ShapeDtypeStruct((group_rows, width), bf16)
    first = len(spread.arrays) + 6
    return call(
        functools.partial(
            entry_body, spread=spread, rows=rows, block=block, blocks=blocks, earlier=len(earlier)
        ),
        "entry",
        grid=(len(blocks),),
        in_specs=[anywhere] * len(spread.arrays)
        + [row] * 4
        + [
            anywhere,
            anywhere,
        ]
        + [anywhere] * len(earlier),
        out_specs=[
            out_block(width),
            out_block(width),
            out_block(width),
            out_block(deep),
            out_block(units),
            anywhere,
        ],
        out_shape=[
            wide,
            wide,
            wide,
            jax.ShapeDtypeStruct((group_rows, deep), f32),
            jax.ShapeDtypeStruct((group_rows, units), bf16),
            wide,
        ],
        input_output_aliases={first + i: i for i in range(len(earlier))},
        scratch_shapes=[
            pltpu.VMEM((group_rows, width), bf16),
            pltpu.VMEM((group_rows, width), bf16),
            pltpu.VMEM(qkv_weight.shape, bf16),
            pltpu.VMEM(out_weight.shape, bf16),
            pltpu.SemaphoreType.DMA((per_group,)),
            pltpu.SemaphoreType.DMA((per_group,)),
            pltpu.SemaphoreType.DMA((steps,)),
            pltpu.SemaphoreType.DMA((2,)),
        ],
    )(*spread.arrays, *gains, qkv_weight, out_weight, *earlier)


def pairs_body(input_ref, cot_ref, gain_ref, bias_ref, pair_ref, shared_ref):
    rows = input_ref.shape[0]
    values = input_ref[...].astype(f32)
    centred = values - jnp.mean(values, axis=1, keepdims=True)
    hat = centred * lax.rsqrt(jnp.mean(centred * centred, axis=1, keepdims=True) + norm_eps)
    pair_ref[:rows, :] = input_ref[...]
    pair_ref[rows:, :] = cot_ref[...]
    shared_ref[:rows, :] = (hat * gain_ref[...] + bias_ref[...]).astype(bf16)
    shared_ref[rows:, :] = cot_ref[...]


def pairs(layer_input, cotangent, gain, bias):
    rows, width = layer_input.shape
    return call(
        pairs_body,
        "pairs",
        out_shape=[jax.ShapeDtypeStruct((2 * rows, width), bf16)] * 2,
    )(layer_input, cotangent, gain, bias)


def fold_body(near_ref, came_ref, going_ref, kept_ref, *, rows, going, kept):
    for ref, places in ((going_ref, going), (kept_ref, kept)):
        for i, at in enumerate(places):
            here = slice(at * rows, (at + 1) * rows)
            total = near_ref[here, :].astype(f32) + came_ref[here, :].astype(f32)
            ref[i * rows : (i + 1) * rows, :] = total.astype(bf16)


def folds_body(*refs, count):
    for ref in range(2 * count):
        total = refs[2 * ref][...].astype(f32) + refs[2 * ref + 1][...].astype(f32)
        refs[4 * count + ref][...] = total.astype(bf16)


def fold(sums, rows):
    width = sums[0][0].shape[1]
    operands, in_specs = [], []
    for near, came, places in sums:
        for first, *more in places:
            apart = more[0] - first if more else 0
            spec = pl.BlockSpec((rows, width), lambda i, a=apart, f=first: (a * i + f, 0))
            operands += [near, came]
            in_specs += [spec, spec]
    per = len(sums[0][2][0])
    return call(
        functools.partial(folds_body, count=len(sums)),
        "fold",
        grid=(per,),
        in_specs=in_specs,
        out_specs=[pl.BlockSpec((rows, width), lambda i: (i, 0))] * (2 * len(sums)),
        out_shape=[jax.ShapeDtypeStruct((per * rows, width), bf16)] * (2 * len(sums)),
    )(*operands)


def cut_body(side_x, side_y, x_ref, y_ref):
    x_ref[...] = side_x[...]
    y_ref[...] = side_y[...]


def cut(side_x, side_y):
    rows, width = side_x.shape[0] // 2, side_x.shape[1]
    tops = pl.BlockSpec((rows, width), lambda i: (0, 0))
    return call(
        cut_body,
        "cut",
        grid=(1,),
        in_specs=[tops, pl.BlockSpec((rows, width), lambda i: (1, 0))],
        out_specs=[tops] * 2,
        out_shape=[jax.ShapeDtypeStruct((rows, width), side_x.dtype)] * 2,
    )(side_x, side_y)


def start(copies):
    for copy in copies:
        copy.start()


def wait(copies):
    for copy in copies:
        copy.wait()


def products(x, c, up_ref, down_ref, shift_ref, tiles, hidden_ref, grad_ref, sum_ref):
    gates = [dot_plain(x, up_ref[:, part]) + shift_ref[:, part] for part in tiles]
    for gate, part in zip(gates, tiles):
        grad_hidden = contract_cols(c, down_ref[part, :])
        below = 0.5 * (1.0 + lax.erf(gate * inv_root_two))
        hidden_ref[:, part] = (gate * below).astype(bf16)
        slope = below + gate * jnp.exp(-0.5 * gate * gate) * inv_root_tau
        grad = (grad_hidden * slope).astype(bf16)
        grad_ref[:, part] = grad
        sum_ref[:, part] += jnp.sum(grad.astype(f32), axis=0, keepdims=True)


def column_tiles(units):
    tile = min(512, units)
    return [slice(i, i + tile) for i in range(0, units, tile)]


class Branch:
    def __init__(self, arrays, weights, buffers, sems, spread, rows, block):
        self.up_ref, self.shift_ref, self.down_ref = weights
        self.x_buf, self.c_buf, self.u_buf, self.d_buf = buffers
        sem_x, sem_c, sem_u, sem_d = sems
        self.block = block
        self.every = range(self.x_buf.shape[0] // block)
        self.x_copies = block_copies(spread, "a", arrays, self.x_buf, sem_x, rows, block, self.every)
        self.c_copies = block_copies(spread, "b", arrays, self.c_buf, sem_c, rows, block, self.every)
        self.tiles = column_tiles(self.u_buf.shape[1])
        self.needs = self.x_copies[0] + self.c_copies[0]
        self.needs.append(pltpu.make_async_copy(self.up_ref, self.u_buf, sem_u))
        self.needs.append(pltpu.make_async_copy(self.down_ref, self.d_buf, sem_d))

    def block_step(self, step, hidden_ref, grad_ref, sum_ref, prior_ref, extra=()):
        @pl.when(step == 0)
        def _():
            start(self.needs)
            sum_ref[...] = prior_ref[...]
            wait(self.needs)
            for later in self.every[1:]:
                start(self.x_copies[later] + self.c_copies[later])
            start(extra)

        for i in self.every[1:]:

            @pl.when(step == i)
            def _(i=i):
                wait(self.x_copies[i] + self.c_copies[i])

        here = pl.ds(pl.multiple_of(step * self.block, self.block), self.block)
        products(
            self.x_buf[here, :],
            self.c_buf[here, :],
            self.u_buf,
            self.d_buf,
            self.shift_ref,
            self.tiles,
            hidden_ref.at[here],
            grad_ref.at[here],
            sum_ref,
        )


def branch_scratch(group_rows, width, units, blocks):
    dma = pltpu.SemaphoreType.DMA
    return [
        pltpu.VMEM((group_rows, width), bf16),
        pltpu.VMEM((group_rows, width), bf16),
        pltpu.VMEM((width, units), bf16),
        pltpu.VMEM((units, width), bf16),
        dma((blocks,)),
        dma((blocks,)),
        dma,
        dma,
    ]


def mlp_body(x_ref, c_ref, up_ref, shift_ref, down_ref, hidden_ref, grad_ref, sum_ref):
    @pl.when(pl.program_id(0) == 0)
    def _():
        sum_ref[...] = jnp.zeros_like(sum_ref)

    tiles = column_tiles(up_ref.shape[1])
    products(
        x_ref[...], c_ref[...], up_ref, down_ref, shift_ref, tiles, hidden_ref, grad_ref, sum_ref
    )


def mlp(normed, cotangent, up_weight, up_bias, down_weight):
    width, units = up_weight.shape
    group_rows = normed.shape[0]
    block = min(256, group_rows)
    once = pl.Buffered(1)
    full = pl.BlockSpec((block, width), lambda i: (i, 0))
    part = pl.BlockSpec((block, units), lambda i: (i, 0))
    low = jax.ShapeDtypeStruct((group_rows, units), bf16)
    row = pl.BlockSpec((1, units), lambda i: (0, 0))
    return call(
        mlp_body,
        "mlp",
        grid=(group_rows // block,),
        in_specs=[
            full,
            full,
            pl.BlockSpec(up_weight.shape, lambda i: (0, 0), pipeline_mode=once),
            row,
            pl.BlockSpec(down_weight.shape, lambda i: (0, 0), pipeline_mode=once),
        ],
        out_specs=[part, part, row],
        out_shape=[low, low, jax.ShapeDtypeStruct((1, units), f32)],
    )(normed, cotangent, up_weight, up_bias, down_weight)


def group_body(*refs, spread, rows, block, tile, steps, ups, adds, more, places):
    count = len(spread.arrays)
    arrays, weights, refs = refs[:count], refs[count : count + 3], refs[count + 3 :]
    prior_ref, *refs = refs
    added, refs = refs[: 2 * adds], refs[2 * adds :]
    own, refs = refs[: 4 * more], refs[4 * more :]
    folds, refs = (refs[:2], refs[2:]) if places else ((), refs)
    up_out, down_out, sum_ref = refs[:3]
    folded, refs = (refs[3:5], refs[5:]) if places else ((), refs[3:])
    buffers, sems, (hidden_buf, grad_buf), refs = refs[:4], refs[4:8], refs[8:10], refs[10:]
    branch = Branch(arrays, weights, buffers, sems, spread, rows, block)
    step = pl.program_id(0)
    at = jnp.where(step < steps + ups, step - steps, step - steps - ups)
    at = jnp.maximum(at, 0)
    here = pl.ds(pl.multiple_of(at * tile, tile), tile)
    later = []
    if adds:
        sum_up, sum_down, sem_sum_up, sem_sum_down, *refs = refs

        def up_copy(i):
            first = pl.multiple_of(i * tile, tile)
            return pltpu.make_async_copy(
                added[0].at[pl.ds(first, tile), :], sum_up.at[i % 2], sem_sum_up.at[i % 2]
            )

        def down_copy(i):
            first = pl.multiple_of(i * tile, tile)
            return pltpu.make_async_copy(
                added[1].at[:, pl.ds(first, tile)], sum_down.at[i % 2], sem_sum_down.at[i % 2]
            )

        later = later + [up_copy(0)]
    if more:
        own_bufs, sem_own = refs[:4], refs[4]
        own_copies = [
            pltpu.make_async_copy(ref, buf, sem_own.at[i])
            for i, (ref, buf) in enumerate(zip(own, own_bufs))
        ]
        later = later + own_copies
        rows_own, cot_own, hidden_own, grad_own = own_bufs

    @pl.when(step < steps)
    def _():
        branch.block_step(step, hidden_buf, grad_buf, sum_ref, prior_ref, later)

    if more:

        @pl.when(step == steps)
        def _():
            wait(own_copies)

    if places:

        @pl.when(step >= steps)
        def _():
            fold_body(*folds, *folded, rows=rows, going=places[0], kept=places[1])

    @pl.when((step >= steps) & (step < steps + ups))
    def _():
        if adds:

            @pl.when(at + 1 < ups)
            def _():
                up_copy(at + 1).start()

            @pl.when(at + 1 == ups)
            def _():
                down_copy(0).start()

            up_copy(at).wait()
        total = contract_rows(branch.x_buf[:, here], grad_buf[...])
        if more:
            total = total + contract_rows(rows_own[:, here], grad_own[...])
        if adds:
            total = total + sum_up[at % 2]
        up_out[...] = total

    @pl.when(step >= steps + ups)
    def _():
        if adds:

            @pl.when(at + 1 < ups)
            def _():
                down_copy(at + 1).start()

            down_copy(at).wait()
        total = contract_rows(hidden_buf[...], branch.c_buf[:, here])
        if more:
            total = total + contract_rows(hidden_own[...], cot_own[:, here])
        if adds:
            total = total + sum_down[at % 2]
        down_out[...] = total


def group(spread, rows, up_weight, up_bias, down_weight, prior, added=(), own=(), folds=(), places=()):
    width, units = up_weight.shape
    group_rows = rows * len(spread.names)
    block = min(256, group_rows)
    tile = min(512, units)
    steps, blocks = group_rows // block, len(spread.names)
    ups = width // tile
    anywhere = pl.BlockSpec(memory_space=pl.ANY)
    row = pl.BlockSpec((1, units), lambda i: (0, 0))
    dma = pltpu.SemaphoreType.DMA
    scratch = branch_scratch(group_rows, width, units, blocks)
    scratch += [pltpu.VMEM((group_rows, units), bf16)] * 2
    if added:
        scratch += [
            pltpu.VMEM((2, tile, units), f32),
            pltpu.VMEM((2, units, tile), f32),
            dma((2,)),
            dma((2,)),
        ]
    if own:
        scratch += [pltpu.VMEM(array.shape, bf16) for array in own] + [dma((4,))]
    fold_in, fold_out, fold_shape = [], [], []
    if folds:
        strip = width // (2 * ups)
        half = folds[0].shape[0] // 2

        def column(i):
            return 0, jnp.clip(i - steps, 0, 2 * ups - 1)

        fold_in = [pl.BlockSpec((2 * half, strip), column)] * 2
        fold_out = [pl.BlockSpec((half, strip), column)] * 2
        fold_shape = [jax.ShapeDtypeStruct((half, width), bf16)] * 2
    return call(
        functools.partial(
            group_body,
            spread=spread,
            rows=rows,
            block=block,
            tile=tile,
            steps=steps,
            ups=ups,
            adds=bool(added),
            more=bool(own),
            places=places,
        ),
        "group",
        grid=(steps + 2 * ups,),
        in_specs=[anywhere] * len(spread.arrays)
        + [anywhere, row, anywhere, row]
        + [anywhere] * (len(added) + len(own))
        + fold_in,
        out_specs=[
            pl.BlockSpec((tile, units), lambda i: (jnp.clip(i - steps, 0, ups - 1), 0)),
            pl.BlockSpec((units, tile), lambda i: (0, jnp.clip(i - steps - ups, 0, ups - 1))),
            row,
        ]
        + fold_out,
        out_shape=[
            jax.ShapeDtypeStruct((width, units), f32),
            jax.ShapeDtypeStruct((units, width), f32),
            jax.ShapeDtypeStruct((1, units), f32),
        ]
        + fold_shape,
        scratch_shapes=scratch,
    )(*spread.arrays, up_weight, up_bias, down_weight, prior, *added, *own, *folds)


def weight_body(left_ref, right_ref, out_ref):
    out_ref[...] = contract_rows(left_ref[...], right_ref[...])


def weight_product(left, right):
    wide, deep = left.shape[1], right.shape[1]
    tile = min(512, wide)
    return call(
        weight_body,
        "weight_product",
        grid=(wide // tile,),
        in_specs=[
            pl.BlockSpec((left.shape[0], tile), lambda i: (0, i)),
            pl.BlockSpec(right.shape, lambda i: (0, 0), pipeline_mode=pl.Buffered(1)),
        ],
        out_specs=pl.BlockSpec((tile, deep), lambda i: (i, 0)),
        out_shape=jax.ShapeDtypeStruct((wide, deep), f32),
    )(left, right)


def attention_weights_body(normed_ref, grad_qkv_ref, attended_ref, grad_out_ref, sum_ref):
    deep = grad_qkv_ref.shape[1]
    sum_ref[:, :deep] = contract_rows(normed_ref[...], grad_qkv_ref[...]).astype(bf16)
    sum_ref[:, deep:] = contract_rows(attended_ref[...], grad_out_ref[...]).astype(bf16)


def attention_weights(normed, grad_qkv, attended, grad_out):
    group_rows, width = normed.shape
    deep, units = grad_qkv.shape[1], attended.shape[1]
    once = pl.Buffered(1)
    block = pl.BlockSpec((group_rows, units), lambda i: (0, i))
    return call(
        attention_weights_body,
        "attention_weights",
        grid=(width // units,),
        in_specs=[
            block,
            pl.BlockSpec(grad_qkv.shape, lambda i: (0, 0), pipeline_mode=once),
            pl.BlockSpec(attended.shape, lambda i: (0, 0), pipeline_mode=once),
            block,
        ],
        out_specs=pl.BlockSpec((units, deep + units), lambda i: (i, 0)),
        out_shape=jax.ShapeDtypeStruct((width, deep + units), bf16),
    )(normed, grad_qkv, attended, grad_out)


def widen_body(sum_ref, qkv_ref, out_ref):
    units, deep = out_ref.shape[0], qkv_ref.shape[1]
    qkv_ref[...] = sum_ref[:, :deep].astype(f32)
    for first in range(0, sum_ref.shape[0], units):
        out_ref[:, first : first + units] = sum_ref[first : first + units, deep:].astype(f32)


def widen(total, deep, units):
    width = total.shape[0]
    block = min(2 * units, width)
    return call(
        widen_body,
        "widen",
        grid=(width // block,),
        in_specs=[pl.BlockSpec((block, deep + units), lambda i: (i, 0))],
        out_specs=[
            pl.BlockSpec((block, deep), lambda i: (i, 0)),
            pl.BlockSpec((units, block), lambda i: (0, i)),
        ],
        out_shape=[
            jax.ShapeDtypeStruct((width, deep), f32),
            jax.ShapeDtypeStruct((units, width), f32),
        ],
    )(total)


def branch_body(attended_ref, hidden_ref, out_ref, down_ref, near_ref, far_ref):
    middle = near_ref.shape[0]
    total = dot_plain(attended_ref[...], out_ref[...]) + dot_plain(hidden_ref[...], down_ref[...])
    near_ref[...] = total[:middle].astype(bf16)
    far_ref[...] = total[middle:].astype(bf16)


def branch_sum(attended, hidden, out_weight, down_weight):
    group_rows = attended.shape[0]
    width = out_weight.shape[1]
    tile = min(512, width)
    once = pl.Buffered(1)
    half = pl.BlockSpec((group_rows // 2, tile), lambda i: (0, i))
    return call(
        branch_body,
        "branch_sum",
        grid=(width // tile,),
        in_specs=[
            pl.BlockSpec(attended.shape, lambda i: (0, 0), pipeline_mode=once),
            pl.BlockSpec(hidden.shape, lambda i: (0, 0), pipeline_mode=once),
            pl.BlockSpec((out_weight.shape[0], tile), lambda i: (0, i)),
            pl.BlockSpec((down_weight.shape[0], tile), lambda i: (0, i)),
        ],
        out_specs=[half, half],
        out_shape=[jax.ShapeDtypeStruct((group_rows // 2, width), bf16)] * 2,
    )(attended, hidden, out_weight, down_weight)


def input_body(
    qkv_grad_ref, gate_grad_ref, qkv_ref, up_ref, gain1, gain2, hat_ref, near_ref, far_ref, sum_ref
):
    middle = near_ref.shape[0]
    hat = hat_ref[...].astype(f32)
    first = contract_cols(qkv_grad_ref[...], qkv_ref[...])
    second = contract_cols(gate_grad_ref[...], up_ref[...])
    both = first * gain1[...] + second * gain2[...]
    near_ref[...] = both[:middle].astype(bf16)
    far_ref[...] = both[middle:].astype(bf16)
    sum_ref[0:1, :] = jnp.sum(first * hat, axis=0, keepdims=True)
    sum_ref[1:2, :] = jnp.sum(first, axis=0, keepdims=True)
    sum_ref[2:3, :] = jnp.sum(second * hat, axis=0, keepdims=True)
    sum_ref[3:4, :] = jnp.sum(second, axis=0, keepdims=True)


def input_sums(grad_qkv, grad_gate, qkv_weight, up_weight, gain1, gain2, hat):
    group_rows = grad_qkv.shape[0]
    width = qkv_weight.shape[0]
    tile = min(256, width)
    once = pl.Buffered(1)
    half = pl.BlockSpec((group_rows // 2, tile), lambda i: (0, i))
    row = pl.BlockSpec((1, tile), lambda i: (0, i))
    return call(
        input_body,
        "input_sums",
        grid=(width // tile,),
        in_specs=[
            pl.BlockSpec(grad_qkv.shape, lambda i: (0, 0), pipeline_mode=once),
            pl.BlockSpec(grad_gate.shape, lambda i: (0, 0), pipeline_mode=once),
            pl.BlockSpec((tile, qkv_weight.shape[1]), lambda i: (i, 0)),
            pl.BlockSpec((tile, up_weight.shape[1]), lambda i: (i, 0)),
            row,
            row,
            pl.BlockSpec((group_rows, tile), lambda i: (0, i)),
        ],
        out_specs=[half, half, pl.BlockSpec((4, tile), lambda i: (0, i))],
        out_shape=[jax.ShapeDtypeStruct((group_rows // 2, width), bf16)] * 2
        + [jax.ShapeDtypeStruct((4, width), f32)],
    )(grad_qkv, grad_gate, qkv_weight, up_weight, gain1, gain2, hat)


def attention_body(
    own_ref,
    starts_ref,
    raw_ref,
    bias_ref,
    cos_ref,
    sine_ref,
    slope_in_ref,
    attended_ref,
    grad_qkv_ref,
    bias_grad_ref,
    query_ref,
    key_ref,
    value_ref,
    slope_ref,
    query_sum_ref,
    key_sum_ref,
    value_sum_ref,
    *,
    rows,
    names,
    block_rows,
    longest,
):
    own = own_ref[0]
    group_rows = rows * len(names)
    lane = lax.broadcasted_iota(jnp.int32, (rows, HEAD_DIM), 1)
    half = ROTARY // 2
    scale = HEAD_DIM ** (-0.5)

    def turned(u):
        return jnp.where(lane < half, pltpu.roll(u, HEAD_DIM - half, 1), pltpu.roll(u, half, 1))

    def far_rows(name):
        return pl.ds(pl.multiple_of((own ^ name) * rows, rows), rows)

    for i, name in enumerate(names):
        near = slice(i * rows, (i + 1) * rows)
        far = far_rows(name)
        raw = raw_ref[near, :] + bias_ref[...]
        cos_table = cos_ref[near, :]
        sine_table = sine_ref[near, :]
        query = raw[:, :HEAD_DIM]
        key = raw[:, HEAD_DIM : 2 * HEAD_DIM]
        query_ref[far, :] = (query * cos_table + turned(query) * sine_table).astype(bf16)
        key_ref[far, :] = (key * cos_table + turned(key) * sine_table).astype(bf16)
        value_ref[far, :] = raw[:, 2 * HEAD_DIM :].astype(bf16)
        slope_ref[far, :] = slope_in_ref[near, :]
    key_sum_ref[...] = jnp.zeros_like(key_sum_ref)
    value_sum_ref[...] = jnp.zeros_like(value_sum_ref)
    for first in range(0, group_rows, block_rows):
        last = first + block_rows
        low = max(0, (first - longest + 1) // 128 * 128)
        query = query_ref[first:last, :]
        keys = key_ref[low:last, :]
        values = value_ref[low:last, :]
        slope = slope_ref[first:last, :]
        scores = contract_cols(query, keys) * scale
        row = first + lax.broadcasted_iota(jnp.int32, (block_rows, 1), 0)
        begin = jnp.zeros((block_rows, 1), jnp.int32)
        for slot in range(starts_ref.shape[0]):
            begin = jnp.where(starts_ref[slot] <= row, starts_ref[slot], begin)
        column = low + lax.broadcasted_iota(jnp.int32, scores.shape, 1)
        scores = jnp.where((column >= begin) & (column <= row), scores, masked_score)
        peak = jnp.max(scores, axis=1, keepdims=True)
        raised = jnp.exp(scores - peak)
        probs = raised * (1.0 / jnp.sum(raised, axis=1, keepdims=True))
        probs_low = probs.astype(bf16)
        query_ref[first:last, :] = dot_plain(probs_low, values).astype(bf16)
        grad_probs = contract_cols(slope, values)
        delta = jnp.sum(grad_probs * probs, axis=1, keepdims=True)
        grad_score = (probs * (grad_probs - delta)).astype(bf16)
        query_sum_ref[first:last, :] = dot_plain(grad_score, keys) * scale
        key_sum_ref[low:last, :] += contract_rows(grad_score, query) * scale
        value_sum_ref[low:last, :] += contract_rows(probs_low, slope)
    bias_grad = jnp.zeros(bias_grad_ref.shape, f32)
    for i, name in enumerate(names):
        near = slice(i * rows, (i + 1) * rows)
        far = far_rows(name)
        cos_table = cos_ref[near, :]
        sine_table = sine_ref[near, :]
        query_grad = query_sum_ref[far, :]
        key_grad = key_sum_ref[far, :]
        grads = jnp.concatenate(
            [
                query_grad * cos_table - turned(query_grad) * sine_table,
                key_grad * cos_table - turned(key_grad) * sine_table,
                value_sum_ref[far, :],
            ],
            axis=1,
        ).astype(bf16)
        grad_qkv_ref[near, :] = grads
        bias_grad = bias_grad + jnp.sum(grads.astype(f32), axis=0, keepdims=True)
        attended_ref[near, :] = query_ref[far, :]
    bias_grad_ref[...] = bias_grad


def attention(own, starts, raw, bias, cos_table, sine_table, slope, rows, names):
    group_rows, width = raw.shape
    part = 3 * HEAD_DIM
    heads = width // part
    whole = pl.BlockSpec((group_rows, HEAD_DIM), lambda h: (0, 0))
    scalars = pl.BlockSpec(memory_space=pltpu.SMEM)
    low = pltpu.VMEM((group_rows, HEAD_DIM), bf16)
    wide = pltpu.VMEM((group_rows, HEAD_DIM), f32)
    longest = group_rows // 2
    return pl.pallas_call(
        functools.partial(
            attention_body,
            rows=rows,
            names=names,
            block_rows=min(256, group_rows),
            longest=longest,
        ),
        grid=(heads,),
        in_specs=[
            scalars,
            scalars,
            pl.BlockSpec((group_rows, part), lambda h: (0, h)),
            pl.BlockSpec((1, part), lambda h: (0, h)),
            whole,
            whole,
            pl.BlockSpec((group_rows, HEAD_DIM), lambda h: (0, h)),
        ],
        out_specs=[
            pl.BlockSpec((group_rows, HEAD_DIM), lambda h: (0, h)),
            pl.BlockSpec((group_rows, part), lambda h: (0, h)),
            pl.BlockSpec((1, part), lambda h: (0, h)),
        ],
        out_shape=[
            jax.ShapeDtypeStruct((group_rows, heads * HEAD_DIM), bf16),
            jax.ShapeDtypeStruct((group_rows, width), bf16),
            jax.ShapeDtypeStruct((1, width), f32),
        ],
        scratch_shapes=[low, low, low, low, wide, wide, wide],
        compiler_params=pltpu.CompilerParams(vmem_limit_bytes=vmem_bytes),
        cost_estimate=pl.CostEstimate(flops=1, bytes_accessed=1, transcendentals=0),
        name="attention",
    )(own, starts, raw, bias, cos_table, sine_table, slope)


def rotary_tables(position):
    half_rot = ROTARY // 2
    frequency = 10000.0 ** (-2.0 * jnp.arange(half_rot, dtype=f32) / ROTARY)
    angles = frequency[:, None] * position.astype(f32)[None, :]
    cos_half, sine_half = lax.optimization_barrier((jnp.cos(angles), jnp.sin(angles)))
    rest = (HEAD_DIM - ROTARY, position.shape[0])
    return (
        jnp.concatenate([cos_half, cos_half, jnp.ones(rest, f32)], axis=0).T,
        jnp.concatenate([-sine_half, sine_half, jnp.zeros(rest, f32)], axis=0).T,
    )


def butterfly(value, axis, count, bit):
    return value + swap(value, axis, count, bit)


def fence(*values):
    return lax.optimization_barrier(values)


def norm_own(layer_input):
    values = layer_input.astype(f32)
    centred = values - jnp.mean(values, axis=-1, keepdims=True)
    inv_std = lax.rsqrt(jnp.mean(centred * centred, axis=-1, keepdims=True) + norm_eps)
    return centred * inv_std, inv_std


def tables(own, lengths, names, rows):
    seq_ends = jnp.cumsum(lengths)
    seq_starts = seq_ends - lengths
    places = (
        (own ^ jnp.array(names, jnp.int32))[:, None] * rows
        + jnp.arange(rows, dtype=jnp.int32)[None, :]
    ).reshape(-1)
    seq_first = jnp.max(
        jnp.where(seq_starts[None, :] <= places[:, None], seq_starts[None, :], 0), axis=1
    )
    return (seq_starts, *rotary_tables(places - seq_first))


def ends(layer_input, cotangent, xhat, inv_std, branch, scaled, biases):
    layer_output = (layer_input.astype(f32) + branch + biases).astype(bf16)
    input_grad = cotangent.astype(f32) + inv_std * (
        scaled
        - jnp.mean(scaled, axis=-1, keepdims=True)
        - xhat * jnp.mean(scaled * xhat, axis=-1, keepdims=True)
    )
    return layer_output, input_grad


def per_device(
    layer_input,
    lengths,
    norm1_gain,
    norm1_bias,
    norm2_gain,
    norm2_bias,
    qkv_weight,
    qkv_bias,
    out_weight,
    out_bias,
    up_weight,
    up_bias,
    down_weight,
    down_bias,
    cotangent,
):
    dp = lax.axis_size("dp")
    mp = lax.axis_size("mp")
    own = lax.axis_index("mp")
    rows, width = layer_input.shape
    up_row = up_bias[None, :]
    gains = (norm1_gain[None, :], norm1_bias[None, :], norm2_gain[None, :], norm2_bias[None, :])
    gather_all = mp == 8 and dp == 4 and 4 * rows * mp * dp * (width + up_bias.shape[0]) < most_gathered

    pair, shared = pairs(layer_input, cotangent, *gains[2:])
    if gather_all:
        names = four_names
        sides = spread_sides(pair, mp)
        group_a = turn(shared, "dp", dp, 1)
        placed = tables(own, lengths[0], names, rows)
        far = spread_core([pair], mp)
        shared, pair, sides, placed, far, group_a = fence(shared, pair, sides, placed, far, group_a)
        group_b = turn(shared, "dp", dp, -1)
        corner = spread_corner(sides, mp)
        near = [pair, *sides]
        far = far + spread_core(sides, mp)
        begun = entry(spread_four(near, far), rows, gains, qkv_weight, out_weight, 0, 2)
        near, far, corner, group_a, begun = fence(near, far, corner, group_a, begun)
        near, far = near + corner, far + spread_core(corner, mp)
        sides_a = spread_sides(group_a, mp)
        entered = entry(spread_four(near, far), rows, gains, qkv_weight, out_weight, 1, 2, begun)
        entered, group_b, group_a = fence(entered, group_b, group_a)
        far_a = spread_core([group_a], mp)
        group_c = turn(group_a, "dp", dp, 1)
    else:
        spread = spread_any(pair, mp)
        names = spread.names
        placed = tables(own, lengths[0], names, rows)
        entered = entry(spread, rows, gains, qkv_weight, out_weight)
    seq_starts, cos_table, sine_table = placed

    first_all, second_all, hat, raw, grad_attended, grad_out = entered
    attended, grad_qkv, qkv_bias_part = attention(
        own.reshape(1),
        seq_starts,
        raw,
        qkv_bias[None, :],
        cos_table,
        sine_table,
        grad_attended,
        rows,
        names,
    )
    if gather_all:
        (first_all, second_all, hat, grad_out, attended, grad_qkv), near_a, far_a, group_b = fence(
            (first_all, second_all, hat, grad_out, attended, grad_qkv),
            [group_a, *sides_a],
            far_a,
            group_b,
        )

    weights_part = attention_weights(first_all, grad_qkv, attended, grad_out)
    if gather_all:
        corner_a = spread_corner(near_a[1:], mp)
        far_a = far_a + spread_core(near_a[1:], mp)
        (weights_part, second_all, hat, grad_out, attended), near_a, corner_a, far_a, group_b, group_c = (
            fence(
                (weights_part, second_all, hat, grad_out, attended),
                near_a,
                corner_a,
                far_a,
                group_b,
                group_c,
            )
        )
    weights_sum = lax.psum_scatter(weights_part, "dp", scatter_dimension=0, tiled=True)

    hidden, grad_gate, gate_sum = mlp(second_all, grad_out, up_weight, up_row, down_weight)
    branch = branch_sum(attended, hidden, out_weight, down_weight)
    if gather_all:
        sides_b = spread_sides(group_b, mp)
        far_b = spread_core([group_b], mp)
        far_a = far_a + spread_core(corner_a, mp)
        near_a = near_a + corner_a
        (hidden, grad_gate, branch, grad_qkv, hat), near_a, far_a, near_b, far_b, group_c = fence(
            (hidden, grad_gate, branch, grad_qkv, hat),
            near_a,
            far_a,
            [group_b, *sides_b],
            far_b,
            group_c,
        )

    scaled = input_sums(grad_qkv, grad_gate, qkv_weight, up_weight, gains[0], gains[2], hat)
    cot_sum = jnp.sum(cotangent.astype(f32), axis=0)
    small = jnp.concatenate([scaled[2].reshape(-1), cot_sum, qkv_bias_part.reshape(-1)])
    small = small.reshape(-1, 128)
    five = 5 * width // 128
    biases = out_bias + down_bias
    xhat, inv_std = norm_own(layer_input)

    def over_mp(both, bit):
        return jnp.concatenate([butterfly(both[:five], "mp", mp, bit), both[five:]], axis=0)

    if not gather_all:
        own_branch = scatter_group(*branch, names, mp, rows)
        own_scaled = scatter_group(*scaled[:2], names, mp, rows)
        layer_output, input_grad = ends(
            layer_input, cotangent, xhat, inv_std, own_branch, own_scaled, biases
        )
        for bit in (1 << i for i in range(dp.bit_length() - 1)):
            small = butterfly(small, "dp", dp, bit)
        small, qkv_bias_grad = small[:five], small[five:]
        for bit in (1 << i for i in range(mp.bit_length() - 1)):
            small = butterfly(small, "mp", mp, bit)
        weights_sum = lax.all_gather(weights_sum, "dp", axis=0, tiled=True)
        up_weight_grad, down_weight_grad, up_bias_grad = lax.psum(
            (weight_product(second_all, grad_gate), weight_product(hidden, grad_out), gate_sum[0]),
            "dp",
        )
    else:
        corner_b = spread_corner(near_b[1:], mp)
        far_b = far_b + spread_core(near_b[1:], mp)
        branch_came = swap(branch[1], "mp", mp, 1)
        scaled, small, near_a, far_a, near_b, far_b, corner_b, branch_came, group_c = fence(
            scaled, small, near_a, far_a, near_b, far_b, corner_b, branch_came, group_c
        )

        own_branch = Scatter(branch[0], branch_came, names, mp, rows, True)
        small = over_mp(small, 1)
        sides_c = spread_sides(group_c, mp)
        scaled_came = swap(scaled[1], "mp", mp, 1)
        far_b = far_b + spread_core(corner_b, mp)
        near_b = near_b + corner_b
        up_sum, down_sum, sum_a, *branch_sent = group(
            spread_four(near_a, far_a),
            rows,
            up_weight,
            up_row,
            down_weight,
            gate_sum,
            folds=(branch[0], branch_came),
            places=own_branch.places(),
        )
        sums, near_b, far_b, near_c, branch_sent, scaled_came, small, weights_sum = fence(
            (up_sum, down_sum),
            near_b,
            far_b,
            [group_c, *sides_c],
            branch_sent,
            scaled_came,
            small,
            weights_sum,
        )

        weights_sum = lax.all_gather(weights_sum, "dp", axis=0, tiled=True)
        own_scaled = Scatter(scaled[0], scaled_came, names, mp, rows, False)
        scaled_sent = fold([(scaled[0], scaled_came, own_scaled.places())], rows)
        far_c = spread_core(near_c[:1], mp)
        corner_c = spread_corner(near_c[1:], mp)
        small = over_mp(small, 2)
        scaled_sent, branch_sent, far_c, small, sums = fence(
            scaled_sent, branch_sent, far_c, small, sums
        )
        up_sum, down_sum, sum_b = group(
            spread_four(near_b, far_b), rows, up_weight, up_row, down_weight, sum_a, sums
        )
        sums, near_c, far_c, corner_c, branch_came, branch_kept, scaled_came, scaled_kept, small = fence(
            (up_sum, down_sum),
            near_c,
            far_c,
            corner_c,
            own_branch.swapped(branch_sent[0]),
            branch_sent[1],
            own_scaled.swapped(scaled_sent[0]),
            scaled_sent[1],
            small,
        )

        far_c = far_c + spread_core(near_c[1:] + corner_c, mp)
        near_c = near_c + corner_c
        small = over_mp(small, 4)
        own_branch.take(own_branch.listed(branch_kept), branch_came)
        own_scaled.take(own_scaled.listed(scaled_kept), scaled_came)
        folded = fold(
            [
                (branch_kept, branch_came, own_branch.places()),
                (scaled_kept, scaled_came, own_scaled.places()),
            ],
            rows,
        )
        near_c, far_c, small, branch_sent, scaled_sent = fence(
            near_c, far_c, small, folded[:2], folded[2:]
        )
        up_weight_grad, down_weight_grad, sum_c = group(
            spread_four(near_c, far_c),
            rows,
            up_weight,
            up_row,
            down_weight,
            sum_b,
            sums,
            (second_all, grad_out, hidden, grad_gate),
        )
        up_weight_grad, branch_came, branch_kept, scaled_came, scaled_kept, z_sums = fence(
            up_weight_grad,
            own_branch.swapped(branch_sent[0]),
            branch_sent[1],
            own_scaled.swapped(scaled_sent[0]),
            scaled_sent[1],
            [small] + [swap(small, "dp", dp, bit) for bit in (1, 2, 3)],
        )
        own_branch.take([branch_kept], branch_came)
        own_scaled.take([scaled_kept], scaled_came)
        branch_total, scaled_total = own_branch.total(0), own_scaled.total(0)
        small = (z_sums[0] + z_sums[1]) + (z_sums[2] + z_sums[3])
        layer_output, input_grad = ends(
            layer_input, cotangent, xhat, inv_std, branch_total, scaled_total, biases
        )
        up_bias_grad = sum_c[0]
        small, qkv_bias_grad = small[:five], small[five:]
    qkv_weight_grad, out_weight_grad = widen(weights_sum, qkv_weight.shape[1], out_weight.shape[0])
    small = small.reshape(5, width)
    return (
        layer_output,
        input_grad,
        small[0],
        small[1],
        small[2],
        small[3],
        qkv_weight_grad,
        qkv_bias_grad.reshape(-1),
        out_weight_grad,
        small[4],
        up_weight_grad,
        up_bias_grad,
        down_weight_grad,
        small[4],
    )


def solution(mesh):
    in_specs = (
        P(("dp", "mp"), None),
        P("dp", None),
        P(),
        P(),
        P(),
        P(),
        P(None, "mp"),
        P("mp"),
        P("mp", None),
        P(),
        P(None, "mp"),
        P("mp"),
        P("mp", None),
        P(),
        P(("dp", "mp"), None),
    )
    out_specs = (
        P(("dp", "mp"), None),
        P(("dp", "mp"), None),
        P(),
        P(),
        P(),
        P(),
        P(None, "mp"),
        P("mp"),
        P("mp", None),
        P(),
        P(None, "mp"),
        P("mp"),
        P("mp", None),
        P(),
    )
    return jax.shard_map(
        per_device, mesh=mesh, in_specs=in_specs, out_specs=out_specs, check_vma=False
    )
```

```python
import functools

import jax
import jax.numpy as jnp
from jax import lax
from jax.experimental import pallas as pl
from jax.experimental.pallas import tpu as pltpu
from jax.sharding import PartitionSpec as P

HEAD_DIM = 128
ROTARY = 32

norm_eps = 1e-05
masked_score = -1e30
inv_root_two = 0.7071067811865476
inv_root_tau = 0.3989422804014327
vmem_bytes = 60 << 20
most_gathered = 128 << 20
bf16 = jnp.bfloat16
f32 = jnp.float32


def dot_plain(left, right):
    return jnp.dot(left, right, preferred_element_type=f32)


def contract_rows(left, right):
    return lax.dot_general(left, right, (((0,), (0,)), ((), ())), preferred_element_type=f32)


def contract_cols(left, right):
    return lax.dot_general(left, right, (((1,), (1,)), ((), ())), preferred_element_type=f32)


def swap(value, axis, count, bit):
    return lax.ppermute(value, axis, [(i, i ^ bit) for i in range(count)])


def turn(value, axis, count, step):
    return lax.ppermute(value, axis, [(i, (i + step) % count) for i in range(count)])


def chip_bits(count):
    return [1 << i for i in range(1, count.bit_length() - 1)]


def after(value, *earlier):
    return lax.optimization_barrier((value, *earlier))[0]


class Spread:
    def __init__(self, arrays, a, b, names):
        self.arrays, self.a, self.b, self.names = arrays, a, b, names


four_names = (0, 2, 4, 6, 1, 3, 5, 7)


def spread_sides(pair, count):
    return [swap(pair, "mp", count, 2), swap(pair, "mp", count, 4)]


def spread_corner(sides, count):
    a, b = cut(*sides)
    return [swap(a, "mp", count, 4), swap(b, "mp", count, 2)]


def spread_core(arrays, count):
    return [swap(array, "mp", count, 1) for array in arrays]


def spread_four(near, far):
    rows = near[0].shape[0] // 2
    a, b = {}, {}
    for core in range(2):
        base = len(near) * core
        for i, name in enumerate((0, 2, 4)):
            a[name + core] = (base + i, 0)
            b[name + core] = (base + i, rows)
        a[6 + core] = (base + 3, 0)
        b[6 + core] = (base + 4, 0)
    return Spread(near + far, a, b, four_names)


def spread_any(pair, count):
    rows = pair.shape[0] // 2
    held, names = pair.reshape(1, 2, rows, -1), [0]
    for bit in chip_bits(count) + [1]:
        held = jnp.concatenate([held, swap(held, "mp", count, bit)], axis=0)
        names = names + [n ^ bit for n in names]
    arrays = [held.reshape(2 * rows * count, -1)]
    a = {n: (0, 2 * rows * i) for i, n in enumerate(names)}
    b = {n: (0, 2 * rows * i + rows) for i, n in enumerate(names)}
    return Spread(arrays, a, b, tuple(names))


class Scatter:
    def __init__(self, near, came, names, count, rows, rising):
        self.count, self.rows = count, rows
        names = names[: len(names) // 2]
        self.blocks = {n: near[i * rows : (i + 1) * rows] for i, n in enumerate(names)}
        self.adds = {n: came[i * rows : (i + 1) * rows] for i, n in enumerate(names)}
        bits = chip_bits(count)
        self.bits = bits if rising else bits[::-1]

    def total(self, n):
        return self.blocks[n].astype(f32) + self.adds[n].astype(f32)

    def places(self):
        bit, order = self.bits[0], list(self.blocks)
        going = [i for i, n in enumerate(order) if n & bit]
        return going, [i for i, n in enumerate(order) if not n & bit]

    def listed(self, kept):
        return [kept[i : i + self.rows] for i in range(0, kept.shape[0], self.rows)]

    def sent(self):
        bit = self.bits[0]
        stay = [n for n in self.blocks if not n & bit]
        going = jnp.concatenate([self.total(n | bit).astype(bf16) for n in stay], axis=0)
        return going, [self.total(n).astype(bf16) for n in stay]

    def swapped(self, going):
        return swap(going, "mp", self.count, self.bits[0])

    def take(self, kept, came):
        bit, self.bits = self.bits[0], self.bits[1:]
        stay = [n for n in self.blocks if not n & bit]
        self.blocks = dict(zip(stay, kept))
        self.adds = {n: came[i * self.rows : (i + 1) * self.rows] for i, n in enumerate(stay)}


def scatter_group(near, far, names, count, rows):
    scatter = Scatter(near, swap(far, "mp", count, 1), names, count, rows, True)
    while scatter.bits:
        going, kept = scatter.sent()
        scatter.take(kept, scatter.swapped(going))
    return scatter.total(0)


def call(body, name, **kwargs):
    return pl.pallas_call(
        body,
        name=name,
        compiler_params=pltpu.CompilerParams(vmem_limit_bytes=vmem_bytes),
        cost_estimate=pl.CostEstimate(flops=1, bytes_accessed=1, transcendentals=0),
        **kwargs,
    )


def block_copies(spread, which, refs, buffer, sems, rows, block, blocks):
    per = block // rows
    listed = []
    for at in blocks:
        listed.append([])
        for i in range(at * per, (at + 1) * per):
            array, first = getattr(spread, which)[spread.names[i]]
            listed[-1].append(
                pltpu.make_async_copy(
                    refs[array].at[first : first + rows, :],
                    buffer.at[i * rows : (i + 1) * rows, :],
                    sems.at[i],
                )
            )
    return listed


def out_copies(buffer, ref, sems, block, blocks):
    return [
        pltpu.make_async_copy(
            buffer.at[i * block : (i + 1) * block, :],
            ref.at[i * block : (i + 1) * block, :],
            sems.at[i],
        )
        for i in blocks
    ]


def entry_body(*refs, spread, rows, block, blocks, earlier):
    count = len(spread.arrays)
    arrays = refs[:count]
    (gain1, bias1, gain2, bias2, qkv_ref, out_weight_ref) = refs[count : count + 6]
    count += 6 + earlier
    (one_ref, two_ref, hat_ref, raw_ref, grad_ref, cot_ref) = refs[count : count + 6]
    x_buf, c_buf, qkv_buf, out_buf, sem_x, sem_c, sem_out, sem_w = refs[count + 6 :]
    step = pl.program_id(0)
    x_copies = block_copies(spread, "a", arrays, x_buf, sem_x, rows, block, blocks)
    c_copies = block_copies(spread, "b", arrays, c_buf, sem_c, rows, block, blocks)
    outs = out_copies(c_buf, cot_ref, sem_out, block, blocks)

    weights = [
        pltpu.make_async_copy(qkv_ref, qkv_buf, sem_w.at[0]),
        pltpu.make_async_copy(out_weight_ref, out_buf, sem_w.at[1]),
    ]

    @pl.when(step == 0)
    def _():
        start(x_copies[0] + weights + c_copies[0])
        for x_list, c_list in zip(x_copies[1:], c_copies[1:]):
            start(x_list + c_list)

    for i in range(len(outs)):

        @pl.when(step == i)
        def _(i=i):
            wait(x_copies[i])

    here = pl.ds(pl.multiple_of((step * blocks.step + blocks.start) * block, block), block)
    values = x_buf[here, :].astype(f32)
    centred = values - jnp.mean(values, axis=1, keepdims=True)
    hat = centred * lax.rsqrt(jnp.mean(centred * centred, axis=1, keepdims=True) + norm_eps)
    hat_ref[...] = hat.astype(bf16)
    one_ref[...] = (hat * gain1[...] + bias1[...]).astype(bf16)
    two_ref[...] = (hat * gain2[...] + bias2[...]).astype(bf16)

    for i in range(len(outs)):

        @pl.when(step == i)
        def _(i=i):
            wait(c_copies[i])
            outs[i].start()
            if i == 0:
                wait(weights)

    raw_ref[...] = dot_plain(one_ref[...], qkv_buf[...])
    grad_ref[...] = contract_cols(c_buf[here, :], out_buf[...]).astype(bf16)

    @pl.when(step == len(outs) - 1)
    def _():
        for copy in outs:
            copy.wait()


def entry(spread, rows, gains, qkv_weight, out_weight, begin=0, stride=1, earlier=()):
    group_rows = rows * len(spread.names)
    width, deep = qkv_weight.shape
    units = out_weight.shape[0]
    block = min(256, group_rows)
    steps = group_rows // block
    per_group = len(spread.names)
    blocks = range(begin, steps, stride)

    def out_block(columns):
        return pl.BlockSpec((block, columns), lambda i: (i * stride + begin, 0))

    row = pl.BlockSpec((1, width), lambda i: (0, 0))
    anywhere = pl.BlockSpec(memory_space=pl.ANY)
    wide = jax.ShapeDtypeStruct((group_rows, width), bf16)
    first = len(spread.arrays) + 6
    return call(
        functools.partial(
            entry_body, spread=spread, rows=rows, block=block, blocks=blocks, earlier=len(earlier)
        ),
        "entry",
        grid=(len(blocks),),
        in_specs=[anywhere] * len(spread.arrays)
        + [row] * 4
        + [
            anywhere,
            anywhere,
        ]
        + [anywhere] * len(earlier),
        out_specs=[
            out_block(width),
            out_block(width),
            out_block(width),
            out_block(deep),
            out_block(units),
            anywhere,
        ],
        out_shape=[
            wide,
            wide,
            wide,
            jax.ShapeDtypeStruct((group_rows, deep), f32),
            jax.ShapeDtypeStruct((group_rows, units), bf16),
            wide,
        ],
        input_output_aliases={first + i: i for i in range(len(earlier))},
        scratch_shapes=[
            pltpu.VMEM((group_rows, width), bf16),
            pltpu.VMEM((group_rows, width), bf16),
            pltpu.VMEM(qkv_weight.shape, bf16),
            pltpu.VMEM(out_weight.shape, bf16),
            pltpu.SemaphoreType.DMA((per_group,)),
            pltpu.SemaphoreType.DMA((per_group,)),
            pltpu.SemaphoreType.DMA((steps,)),
            pltpu.SemaphoreType.DMA((2,)),
        ],
    )(*spread.arrays, *gains, qkv_weight, out_weight, *earlier)


def pairs_body(input_ref, cot_ref, gain_ref, bias_ref, pair_ref, shared_ref):
    rows = input_ref.shape[0]
    values = input_ref[...].astype(f32)
    centred = values - jnp.mean(values, axis=1, keepdims=True)
    hat = centred * lax.rsqrt(jnp.mean(centred * centred, axis=1, keepdims=True) + norm_eps)
    pair_ref[:rows, :] = input_ref[...]
    pair_ref[rows:, :] = cot_ref[...]
    shared_ref[:rows, :] = (hat * gain_ref[...] + bias_ref[...]).astype(bf16)
    shared_ref[rows:, :] = cot_ref[...]


def pairs(layer_input, cotangent, gain, bias):
    rows, width = layer_input.shape
    return call(
        pairs_body,
        "pairs",
        out_shape=[jax.ShapeDtypeStruct((2 * rows, width), bf16)] * 2,
    )(layer_input, cotangent, gain, bias)


def fold_body(near_ref, came_ref, going_ref, kept_ref, *, rows, going, kept):
    for ref, places in ((going_ref, going), (kept_ref, kept)):
        for i, at in enumerate(places):
            here = slice(at * rows, (at + 1) * rows)
            total = near_ref[here, :].astype(f32) + came_ref[here, :].astype(f32)
            ref[i * rows : (i + 1) * rows, :] = total.astype(bf16)


def folds_body(*refs, count):
    for ref in range(2 * count):
        total = refs[2 * ref][...].astype(f32) + refs[2 * ref + 1][...].astype(f32)
        refs[4 * count + ref][...] = total.astype(bf16)


def fold(sums, rows):
    width = sums[0][0].shape[1]
    operands, in_specs = [], []
    for near, came, places in sums:
        for first, *more in places:
            apart = more[0] - first if more else 0
            spec = pl.BlockSpec((rows, width), lambda i, a=apart, f=first: (a * i + f, 0))
            operands += [near, came]
            in_specs += [spec, spec]
    per = len(sums[0][2][0])
    return call(
        functools.partial(folds_body, count=len(sums)),
        "fold",
        grid=(per,),
        in_specs=in_specs,
        out_specs=[pl.BlockSpec((rows, width), lambda i: (i, 0))] * (2 * len(sums)),
        out_shape=[jax.ShapeDtypeStruct((per * rows, width), bf16)] * (2 * len(sums)),
    )(*operands)


def cut_body(side_x, side_y, x_ref, y_ref):
    x_ref[...] = side_x[...]
    y_ref[...] = side_y[...]


def cut(side_x, side_y):
    rows, width = side_x.shape[0] // 2, side_x.shape[1]
    tops = pl.BlockSpec((rows, width), lambda i: (0, 0))
    return call(
        cut_body,
        "cut",
        grid=(1,),
        in_specs=[tops, pl.BlockSpec((rows, width), lambda i: (1, 0))],
        out_specs=[tops] * 2,
        out_shape=[jax.ShapeDtypeStruct((rows, width), side_x.dtype)] * 2,
    )(side_x, side_y)


def start(copies):
    for copy in copies:
        copy.start()


def wait(copies):
    for copy in copies:
        copy.wait()


def products(x, c, up_ref, down_ref, shift_ref, tiles, hidden_ref, grad_ref, sum_ref):
    gates = [dot_plain(x, up_ref[:, part]) + shift_ref[:, part] for part in tiles]
    for gate, part in zip(gates, tiles):
        grad_hidden = contract_cols(c, down_ref[part, :])
        below = 0.5 * (1.0 + lax.erf(gate * inv_root_two))
        hidden_ref[:, part] = (gate * below).astype(bf16)
        slope = below + gate * jnp.exp(-0.5 * gate * gate) * inv_root_tau
        grad = (grad_hidden * slope).astype(bf16)
        grad_ref[:, part] = grad
        sum_ref[:, part] += jnp.sum(grad.astype(f32), axis=0, keepdims=True)


def column_tiles(units):
    tile = min(512, units)
    return [slice(i, i + tile) for i in range(0, units, tile)]


class Branch:
    def __init__(self, arrays, weights, buffers, sems, spread, rows, block):
        self.up_ref, self.shift_ref, self.down_ref = weights
        self.x_buf, self.c_buf, self.u_buf, self.d_buf = buffers
        sem_x, sem_c, sem_u, sem_d = sems
        self.block = block
        self.every = range(self.x_buf.shape[0] // block)
        self.x_copies = block_copies(spread, "a", arrays, self.x_buf, sem_x, rows, block, self.every)
        self.c_copies = block_copies(spread, "b", arrays, self.c_buf, sem_c, rows, block, self.every)
        self.tiles = column_tiles(self.u_buf.shape[1])
        self.needs = self.x_copies[0] + self.c_copies[0]
        self.needs.append(pltpu.make_async_copy(self.up_ref, self.u_buf, sem_u))
        self.needs.append(pltpu.make_async_copy(self.down_ref, self.d_buf, sem_d))

    def block_step(self, step, hidden_ref, grad_ref, sum_ref, prior_ref, extra=()):
        @pl.when(step == 0)
        def _():
            start(self.needs)
            sum_ref[...] = prior_ref[...]
            wait(self.needs)
            for later in self.every[1:]:
                start(self.x_copies[later] + self.c_copies[later])
            start(extra)

        for i in self.every[1:]:

            @pl.when(step == i)
            def _(i=i):
                wait(self.x_copies[i] + self.c_copies[i])

        here = pl.ds(pl.multiple_of(step * self.block, self.block), self.block)
        products(
            self.x_buf[here, :],
            self.c_buf[here, :],
            self.u_buf,
            self.d_buf,
            self.shift_ref,
            self.tiles,
            hidden_ref.at[here],
            grad_ref.at[here],
            sum_ref,
        )


def branch_scratch(group_rows, width, units, blocks):
    dma = pltpu.SemaphoreType.DMA
    return [
        pltpu.VMEM((group_rows, width), bf16),
        pltpu.VMEM((group_rows, width), bf16),
        pltpu.VMEM((width, units), bf16),
        pltpu.VMEM((units, width), bf16),
        dma((blocks,)),
        dma((blocks,)),
        dma,
        dma,
    ]


def mlp_body(x_ref, c_ref, up_ref, shift_ref, down_ref, hidden_ref, grad_ref, sum_ref):
    @pl.when(pl.program_id(0) == 0)
    def _():
        sum_ref[...] = jnp.zeros_like(sum_ref)

    tiles = column_tiles(up_ref.shape[1])
    products(
        x_ref[...], c_ref[...], up_ref, down_ref, shift_ref, tiles, hidden_ref, grad_ref, sum_ref
    )


def mlp(normed, cotangent, up_weight, up_bias, down_weight):
    width, units = up_weight.shape
    group_rows = normed.shape[0]
    block = min(256, group_rows)
    once = pl.Buffered(1)
    full = pl.BlockSpec((block, width), lambda i: (i, 0))
    part = pl.BlockSpec((block, units), lambda i: (i, 0))
    low = jax.ShapeDtypeStruct((group_rows, units), bf16)
    row = pl.BlockSpec((1, units), lambda i: (0, 0))
    return call(
        mlp_body,
        "mlp",
        grid=(group_rows // block,),
        in_specs=[
            full,
            full,
            pl.BlockSpec(up_weight.shape, lambda i: (0, 0), pipeline_mode=once),
            row,
            pl.BlockSpec(down_weight.shape, lambda i: (0, 0), pipeline_mode=once),
        ],
        out_specs=[part, part, row],
        out_shape=[low, low, jax.ShapeDtypeStruct((1, units), f32)],
    )(normed, cotangent, up_weight, up_bias, down_weight)


def group_body(*refs, spread, rows, block, tile, steps, ups, adds, more, places):
    count = len(spread.arrays)
    arrays, weights, refs = refs[:count], refs[count : count + 3], refs[count + 3 :]
    prior_ref, *refs = refs
    added, refs = refs[: 2 * adds], refs[2 * adds :]
    own, refs = refs[: 4 * more], refs[4 * more :]
    folds, refs = (refs[:2], refs[2:]) if places else ((), refs)
    up_out, down_out, sum_ref = refs[:3]
    folded, refs = (refs[3:5], refs[5:]) if places else ((), refs[3:])
    buffers, sems, (hidden_buf, grad_buf), refs = refs[:4], refs[4:8], refs[8:10], refs[10:]
    branch = Branch(arrays, weights, buffers, sems, spread, rows, block)
    step = pl.program_id(0)
    at = jnp.where(step < steps + ups, step - steps, step - steps - ups)
    at = jnp.maximum(at, 0)
    here = pl.ds(pl.multiple_of(at * tile, tile), tile)
    later = []
    if adds:
        sum_up, sum_down, sem_sum_up, sem_sum_down, *refs = refs

        def up_copy(i):
            first = pl.multiple_of(i * tile, tile)
            return pltpu.make_async_copy(
                added[0].at[pl.ds(first, tile), :], sum_up.at[i % 2], sem_sum_up.at[i % 2]
            )

        def down_copy(i):
            first = pl.multiple_of(i * tile, tile)
            return pltpu.make_async_copy(
                added[1].at[:, pl.ds(first, tile)], sum_down.at[i % 2], sem_sum_down.at[i % 2]
            )

        later = later + [up_copy(0)]
    if more:
        own_bufs, sem_own = refs[:4], refs[4]
        own_copies = [
            pltpu.make_async_copy(ref, buf, sem_own.at[i])
            for i, (ref, buf) in enumerate(zip(own, own_bufs))
        ]
        later = later + own_copies
        rows_own, cot_own, hidden_own, grad_own = own_bufs

    @pl.when(step < steps)
    def _():
        branch.block_step(step, hidden_buf, grad_buf, sum_ref, prior_ref, later)

    if more:

        @pl.when(step == steps)
        def _():
            wait(own_copies)

    if places:

        @pl.when(step >= steps)
        def _():
            fold_body(*folds, *folded, rows=rows, going=places[0], kept=places[1])

    @pl.when((step >= steps) & (step < steps + ups))
    def _():
        if adds:

            @pl.when(at + 1 < ups)
            def _():
                up_copy(at + 1).start()

            @pl.when(at + 1 == ups)
            def _():
                down_copy(0).start()

            up_copy(at).wait()
        total = contract_rows(branch.x_buf[:, here], grad_buf[...])
        if more:
            total = total + contract_rows(rows_own[:, here], grad_own[...])
        if adds:
            total = total + sum_up[at % 2]
        up_out[...] = total

    @pl.when(step >= steps + ups)
    def _():
        if adds:

            @pl.when(at + 1 < ups)
            def _():
                down_copy(at + 1).start()

            down_copy(at).wait()
        total = contract_rows(hidden_buf[...], branch.c_buf[:, here])
        if more:
            total = total + contract_rows(hidden_own[...], cot_own[:, here])
        if adds:
            total = total + sum_down[at % 2]
        down_out[...] = total


def group(spread, rows, up_weight, up_bias, down_weight, prior, added=(), own=(), folds=(), places=()):
    width, units = up_weight.shape
    group_rows = rows * len(spread.names)
    block = min(256, group_rows)
    tile = min(512, units)
    steps, blocks = group_rows // block, len(spread.names)
    ups = width // tile
    anywhere = pl.BlockSpec(memory_space=pl.ANY)
    row = pl.BlockSpec((1, units), lambda i: (0, 0))
    dma = pltpu.SemaphoreType.DMA
    scratch = branch_scratch(group_rows, width, units, blocks)
    scratch += [pltpu.VMEM((group_rows, units), bf16)] * 2
    if added:
        scratch += [
            pltpu.VMEM((2, tile, units), f32),
            pltpu.VMEM((2, units, tile), f32),
            dma((2,)),
            dma((2,)),
        ]
    if own:
        scratch += [pltpu.VMEM(array.shape, bf16) for array in own] + [dma((4,))]
    fold_in, fold_out, fold_shape = [], [], []
    if folds:
        strip = width // (2 * ups)
        half = folds[0].shape[0] // 2

        def column(i):
            return 0, jnp.clip(i - steps, 0, 2 * ups - 1)

        fold_in = [pl.BlockSpec((2 * half, strip), column)] * 2
        fold_out = [pl.BlockSpec((half, strip), column)] * 2
        fold_shape = [jax.ShapeDtypeStruct((half, width), bf16)] * 2
    return call(
        functools.partial(
            group_body,
            spread=spread,
            rows=rows,
            block=block,
            tile=tile,
            steps=steps,
            ups=ups,
            adds=bool(added),
            more=bool(own),
            places=places,
        ),
        "group",
        grid=(steps + 2 * ups,),
        in_specs=[anywhere] * len(spread.arrays)
        + [anywhere, row, anywhere, row]
        + [anywhere] * (len(added) + len(own))
        + fold_in,
        out_specs=[
            pl.BlockSpec((tile, units), lambda i: (jnp.clip(i - steps, 0, ups - 1), 0)),
            pl.BlockSpec((units, tile), lambda i: (0, jnp.clip(i - steps - ups, 0, ups - 1))),
            row,
        ]
        + fold_out,
        out_shape=[
            jax.ShapeDtypeStruct((width, units), f32),
            jax.ShapeDtypeStruct((units, width), f32),
            jax.ShapeDtypeStruct((1, units), f32),
        ]
        + fold_shape,
        scratch_shapes=scratch,
    )(*spread.arrays, up_weight, up_bias, down_weight, prior, *added, *own, *folds)


def weight_body(left_ref, right_ref, out_ref):
    out_ref[...] = contract_rows(left_ref[...], right_ref[...])


def weight_product(left, right):
    wide, deep = left.shape[1], right.shape[1]
    tile = min(512, wide)
    return call(
        weight_body,
        "weight_product",
        grid=(wide // tile,),
        in_specs=[
            pl.BlockSpec((left.shape[0], tile), lambda i: (0, i)),
            pl.BlockSpec(right.shape, lambda i: (0, 0), pipeline_mode=pl.Buffered(1)),
        ],
        out_specs=pl.BlockSpec((tile, deep), lambda i: (i, 0)),
        out_shape=jax.ShapeDtypeStruct((wide, deep), f32),
    )(left, right)


def attention_weights_body(normed_ref, grad_qkv_ref, attended_ref, grad_out_ref, sum_ref):
    deep, units = grad_qkv_ref.shape[1], attended_ref.shape[1]
    sum_ref[:, :deep] = contract_rows(normed_ref[...], grad_qkv_ref[...]).astype(bf16)
    total = contract_rows(attended_ref[...], grad_out_ref[...]).astype(bf16)
    for first in range(0, sum_ref.shape[0], units):
        sum_ref[first : first + units, deep:] = total[:, first : first + units]


def attention_weights(normed, grad_qkv, attended, grad_out):
    group_rows, width = normed.shape
    deep, units = grad_qkv.shape[1], attended.shape[1]
    once = pl.Buffered(1)
    columns = min(2 * units, width)
    block = pl.BlockSpec((group_rows, columns), lambda i: (0, i))
    return call(
        attention_weights_body,
        "attention_weights",
        grid=(width // columns,),
        in_specs=[
            block,
            pl.BlockSpec(grad_qkv.shape, lambda i: (0, 0), pipeline_mode=once),
            pl.BlockSpec(attended.shape, lambda i: (0, 0), pipeline_mode=once),
            block,
        ],
        out_specs=pl.BlockSpec((columns, deep + units), lambda i: (i, 0)),
        out_shape=jax.ShapeDtypeStruct((width, deep + units), bf16),
    )(normed, grad_qkv, attended, grad_out)


def widen_body(sum_ref, qkv_ref, out_ref):
    units, deep = out_ref.shape[0], qkv_ref.shape[1]
    qkv_ref[...] = sum_ref[:, :deep].astype(f32)
    for first in range(0, sum_ref.shape[0], units):
        out_ref[:, first : first + units] = sum_ref[first : first + units, deep:].astype(f32)


def widen(total, deep, units):
    width = total.shape[0]
    block = min(2 * units, width)
    return call(
        widen_body,
        "widen",
        grid=(width // block,),
        in_specs=[pl.BlockSpec((block, deep + units), lambda i: (i, 0))],
        out_specs=[
            pl.BlockSpec((block, deep), lambda i: (i, 0)),
            pl.BlockSpec((units, block), lambda i: (0, i)),
        ],
        out_shape=[
            jax.ShapeDtypeStruct((width, deep), f32),
            jax.ShapeDtypeStruct((units, width), f32),
        ],
    )(total)


def branch_body(attended_ref, hidden_ref, out_ref, down_ref, near_ref, far_ref):
    middle = near_ref.shape[0]
    total = dot_plain(attended_ref[...], out_ref[...]) + dot_plain(hidden_ref[...], down_ref[...])
    near_ref[...] = total[:middle].astype(bf16)
    far_ref[...] = total[middle:].astype(bf16)


def branch_sum(attended, hidden, out_weight, down_weight):
    group_rows = attended.shape[0]
    width = out_weight.shape[1]
    tile = min(512, width)
    once = pl.Buffered(1)
    half = pl.BlockSpec((group_rows // 2, tile), lambda i: (0, i))
    return call(
        branch_body,
        "branch_sum",
        grid=(width // tile,),
        in_specs=[
            pl.BlockSpec(attended.shape, lambda i: (0, 0), pipeline_mode=once),
            pl.BlockSpec(hidden.shape, lambda i: (0, 0), pipeline_mode=once),
            pl.BlockSpec((out_weight.shape[0], tile), lambda i: (0, i)),
            pl.BlockSpec((down_weight.shape[0], tile), lambda i: (0, i)),
        ],
        out_specs=[half, half],
        out_shape=[jax.ShapeDtypeStruct((group_rows // 2, width), bf16)] * 2,
    )(attended, hidden, out_weight, down_weight)


def input_body(
    qkv_grad_ref, gate_grad_ref, qkv_ref, up_ref, gain1, gain2, hat_ref, near_ref, far_ref, sum_ref
):
    middle = near_ref.shape[0]
    hat = hat_ref[...].astype(f32)
    first = contract_cols(qkv_grad_ref[...], qkv_ref[...])
    second = contract_cols(gate_grad_ref[...], up_ref[...])
    both = first * gain1[...] + second * gain2[...]
    near_ref[...] = both[:middle].astype(bf16)
    far_ref[...] = both[middle:].astype(bf16)
    sum_ref[0:1, :] = jnp.sum(first * hat, axis=0, keepdims=True)
    sum_ref[1:2, :] = jnp.sum(first, axis=0, keepdims=True)
    sum_ref[2:3, :] = jnp.sum(second * hat, axis=0, keepdims=True)
    sum_ref[3:4, :] = jnp.sum(second, axis=0, keepdims=True)


def input_sums(grad_qkv, grad_gate, qkv_weight, up_weight, gain1, gain2, hat):
    group_rows = grad_qkv.shape[0]
    width = qkv_weight.shape[0]
    tile = min(512, width)
    once = pl.Buffered(1)
    half = pl.BlockSpec((group_rows // 2, tile), lambda i: (0, i))
    row = pl.BlockSpec((1, tile), lambda i: (0, i))
    return call(
        input_body,
        "input_sums",
        grid=(width // tile,),
        in_specs=[
            pl.BlockSpec(grad_qkv.shape, lambda i: (0, 0), pipeline_mode=once),
            pl.BlockSpec(grad_gate.shape, lambda i: (0, 0), pipeline_mode=once),
            pl.BlockSpec((tile, qkv_weight.shape[1]), lambda i: (i, 0)),
            pl.BlockSpec((tile, up_weight.shape[1]), lambda i: (i, 0)),
            row,
            row,
            pl.BlockSpec((group_rows, tile), lambda i: (0, i)),
        ],
        out_specs=[half, half, pl.BlockSpec((4, tile), lambda i: (0, i))],
        out_shape=[jax.ShapeDtypeStruct((group_rows // 2, width), bf16)] * 2
        + [jax.ShapeDtypeStruct((4, width), f32)],
    )(grad_qkv, grad_gate, qkv_weight, up_weight, gain1, gain2, hat)


def attention_body(
    own_ref,
    starts_ref,
    raw_ref,
    bias_ref,
    cos_ref,
    sine_ref,
    slope_in_ref,
    attended_ref,
    grad_qkv_ref,
    bias_grad_ref,
    query_ref,
    key_ref,
    value_ref,
    slope_ref,
    query_sum_ref,
    key_sum_ref,
    value_sum_ref,
    *,
    rows,
    names,
    block_rows,
    longest,
):
    own = own_ref[0]
    group_rows = rows * len(names)
    lane = lax.broadcasted_iota(jnp.int32, (rows, HEAD_DIM), 1)
    half = ROTARY // 2
    scale = HEAD_DIM ** (-0.5)

    def turned(u):
        return jnp.where(lane < half, pltpu.roll(u, HEAD_DIM - half, 1), pltpu.roll(u, half, 1))

    def far_rows(name):
        return pl.ds(pl.multiple_of((own ^ name) * rows, rows), rows)

    for i, name in enumerate(names):
        near = slice(i * rows, (i + 1) * rows)
        far = far_rows(name)
        raw = raw_ref[near, :] + bias_ref[...]
        cos_table = cos_ref[near, :]
        sine_table = sine_ref[near, :]
        query = raw[:, :HEAD_DIM]
        key = raw[:, HEAD_DIM : 2 * HEAD_DIM]
        query_ref[far, :] = (query * cos_table + turned(query) * sine_table).astype(bf16)
        key_ref[far, :] = (key * cos_table + turned(key) * sine_table).astype(bf16)
        value_ref[far, :] = raw[:, 2 * HEAD_DIM :].astype(bf16)
        slope_ref[far, :] = slope_in_ref[near, :]
    key_sum_ref[...] = jnp.zeros_like(key_sum_ref)
    value_sum_ref[...] = jnp.zeros_like(value_sum_ref)
    for first in range(0, group_rows, block_rows):
        last = first + block_rows
        low = max(0, (first - longest + 1) // 128 * 128)
        query = query_ref[first:last, :]
        keys = key_ref[low:last, :]
        values = value_ref[low:last, :]
        slope = slope_ref[first:last, :]
        scores = contract_cols(query, keys) * scale
        row = first + lax.broadcasted_iota(jnp.int32, (block_rows, 1), 0)
        begin = jnp.zeros((block_rows, 1), jnp.int32)
        for slot in range(starts_ref.shape[0]):
            begin = jnp.where(starts_ref[slot] <= row, starts_ref[slot], begin)
        column = low + lax.broadcasted_iota(jnp.int32, scores.shape, 1)
        scores = jnp.where((column >= begin) & (column <= row), scores, masked_score)
        peak = jnp.max(scores, axis=1, keepdims=True)
        raised = jnp.exp(scores - peak)
        probs = raised * (1.0 / jnp.sum(raised, axis=1, keepdims=True))
        probs_low = probs.astype(bf16)
        query_ref[first:last, :] = dot_plain(probs_low, values).astype(bf16)
        grad_probs = contract_cols(slope, values)
        delta = jnp.sum(grad_probs * probs, axis=1, keepdims=True)
        grad_score = (probs * (grad_probs - delta)).astype(bf16)
        query_sum_ref[first:last, :] = dot_plain(grad_score, keys) * scale
        key_sum_ref[low:last, :] += contract_rows(grad_score, query) * scale
        value_sum_ref[low:last, :] += contract_rows(probs_low, slope)
    bias_grad = jnp.zeros(bias_grad_ref.shape, f32)
    for i, name in enumerate(names):
        near = slice(i * rows, (i + 1) * rows)
        far = far_rows(name)
        cos_table = cos_ref[near, :]
        sine_table = sine_ref[near, :]
        query_grad = query_sum_ref[far, :]
        key_grad = key_sum_ref[far, :]
        grads = jnp.concatenate(
            [
                query_grad * cos_table - turned(query_grad) * sine_table,
                key_grad * cos_table - turned(key_grad) * sine_table,
                value_sum_ref[far, :],
            ],
            axis=1,
        ).astype(bf16)
        grad_qkv_ref[near, :] = grads
        bias_grad = bias_grad + jnp.sum(grads.astype(f32), axis=0, keepdims=True)
        attended_ref[near, :] = query_ref[far, :]
    bias_grad_ref[...] = bias_grad


def attention(own, starts, raw, bias, cos_table, sine_table, slope, rows, names):
    group_rows, width = raw.shape
    part = 3 * HEAD_DIM
    heads = width // part
    whole = pl.BlockSpec((group_rows, HEAD_DIM), lambda h: (0, 0))
    scalars = pl.BlockSpec(memory_space=pltpu.SMEM)
    low = pltpu.VMEM((group_rows, HEAD_DIM), bf16)
    wide = pltpu.VMEM((group_rows, HEAD_DIM), f32)
    longest = group_rows // 2
    return pl.pallas_call(
        functools.partial(
            attention_body,
            rows=rows,
            names=names,
            block_rows=min(256, group_rows),
            longest=longest,
        ),
        grid=(heads,),
        in_specs=[
            scalars,
            scalars,
            pl.BlockSpec((group_rows, part), lambda h: (0, h)),
            pl.BlockSpec((1, part), lambda h: (0, h)),
            whole,
            whole,
            pl.BlockSpec((group_rows, HEAD_DIM), lambda h: (0, h)),
        ],
        out_specs=[
            pl.BlockSpec((group_rows, HEAD_DIM), lambda h: (0, h)),
            pl.BlockSpec((group_rows, part), lambda h: (0, h)),
            pl.BlockSpec((1, part), lambda h: (0, h)),
        ],
        out_shape=[
            jax.ShapeDtypeStruct((group_rows, heads * HEAD_DIM), bf16),
            jax.ShapeDtypeStruct((group_rows, width), bf16),
            jax.ShapeDtypeStruct((1, width), f32),
        ],
        scratch_shapes=[low, low, low, low, wide, wide, wide],
        compiler_params=pltpu.CompilerParams(vmem_limit_bytes=vmem_bytes),
        cost_estimate=pl.CostEstimate(flops=1, bytes_accessed=1, transcendentals=0),
        name="attention",
    )(own, starts, raw, bias, cos_table, sine_table, slope)


def rotary_tables(position):
    half_rot = ROTARY // 2
    frequency = 10000.0 ** (-2.0 * jnp.arange(half_rot, dtype=f32) / ROTARY)
    angles = frequency[:, None] * position.astype(f32)[None, :]
    cos_half, sine_half = lax.optimization_barrier((jnp.cos(angles), jnp.sin(angles)))
    rest = (HEAD_DIM - ROTARY, position.shape[0])
    return (
        jnp.concatenate([cos_half, cos_half, jnp.ones(rest, f32)], axis=0).T,
        jnp.concatenate([-sine_half, sine_half, jnp.zeros(rest, f32)], axis=0).T,
    )


def butterfly(value, axis, count, bit):
    return value + swap(value, axis, count, bit)


def fence(*values):
    return lax.optimization_barrier(values)


def norm_own(layer_input):
    values = layer_input.astype(f32)
    centred = values - jnp.mean(values, axis=-1, keepdims=True)
    inv_std = lax.rsqrt(jnp.mean(centred * centred, axis=-1, keepdims=True) + norm_eps)
    return centred * inv_std, inv_std


def tables(own, lengths, names, rows):
    seq_ends = jnp.cumsum(lengths)
    seq_starts = seq_ends - lengths
    places = (
        (own ^ jnp.array(names, jnp.int32))[:, None] * rows
        + jnp.arange(rows, dtype=jnp.int32)[None, :]
    ).reshape(-1)
    seq_first = jnp.max(
        jnp.where(seq_starts[None, :] <= places[:, None], seq_starts[None, :], 0), axis=1
    )
    return (seq_starts, *rotary_tables(places - seq_first))


def ends(layer_input, cotangent, xhat, inv_std, branch, scaled, biases):
    layer_output = (layer_input.astype(f32) + branch + biases).astype(bf16)
    input_grad = cotangent.astype(f32) + inv_std * (
        scaled
        - jnp.mean(scaled, axis=-1, keepdims=True)
        - xhat * jnp.mean(scaled * xhat, axis=-1, keepdims=True)
    )
    return layer_output, input_grad


def per_device(
    layer_input,
    lengths,
    norm1_gain,
    norm1_bias,
    norm2_gain,
    norm2_bias,
    qkv_weight,
    qkv_bias,
    out_weight,
    out_bias,
    up_weight,
    up_bias,
    down_weight,
    down_bias,
    cotangent,
):
    dp = lax.axis_size("dp")
    mp = lax.axis_size("mp")
    own = lax.axis_index("mp")
    rows, width = layer_input.shape
    up_row = up_bias[None, :]
    gains = (norm1_gain[None, :], norm1_bias[None, :], norm2_gain[None, :], norm2_bias[None, :])
    gather_all = mp == 8 and dp == 4 and 4 * rows * mp * dp * (width + up_bias.shape[0]) < most_gathered

    pair, shared = pairs(layer_input, cotangent, *gains[2:])
    if gather_all:
        names = four_names
        sides = spread_sides(pair, mp)
        group_a = turn(shared, "dp", dp, 1)
        placed = tables(own, lengths[0], names, rows)
        far = spread_core([pair], mp)
        shared, pair, sides, placed, far, group_a = fence(shared, pair, sides, placed, far, group_a)
        group_b = turn(shared, "dp", dp, -1)
        corner = spread_corner(sides, mp)
        near = [pair, *sides]
        far = far + spread_core(sides, mp)
        begun = entry(spread_four(near, far), rows, gains, qkv_weight, out_weight, 0, 2)
        near, far, corner, group_a, begun = fence(near, far, corner, group_a, begun)
        near, far = near + corner, far + spread_core(corner, mp)
        sides_a = spread_sides(group_a, mp)
        entered = entry(spread_four(near, far), rows, gains, qkv_weight, out_weight, 1, 2, begun)
        entered, group_b, group_a = fence(entered, group_b, group_a)
        far_a = spread_core([group_a], mp)
        group_c = turn(group_a, "dp", dp, 1)
    else:
        spread = spread_any(pair, mp)
        names = spread.names
        placed = tables(own, lengths[0], names, rows)
        entered = entry(spread, rows, gains, qkv_weight, out_weight)
    seq_starts, cos_table, sine_table = placed

    first_all, second_all, hat, raw, grad_attended, grad_out = entered
    attended, grad_qkv, qkv_bias_part = attention(
        own.reshape(1),
        seq_starts,
        raw,
        qkv_bias[None, :],
        cos_table,
        sine_table,
        grad_attended,
        rows,
        names,
    )
    if gather_all:
        (first_all, second_all, hat, grad_out, attended, grad_qkv), near_a, far_a, group_b = fence(
            (first_all, second_all, hat, grad_out, attended, grad_qkv),
            [group_a, *sides_a],
            far_a,
            group_b,
        )

    weights_part = attention_weights(first_all, grad_qkv, attended, grad_out)
    if gather_all:
        corner_a = spread_corner(near_a[1:], mp)
        far_a = far_a + spread_core(near_a[1:], mp)
        (weights_part, second_all, hat, grad_out, attended), near_a, corner_a, far_a, group_b, group_c = (
            fence(
                (weights_part, second_all, hat, grad_out, attended),
                near_a,
                corner_a,
                far_a,
                group_b,
                group_c,
            )
        )
    weights_sum = lax.psum_scatter(weights_part, "dp", scatter_dimension=0, tiled=True)

    hidden, grad_gate, gate_sum = mlp(second_all, grad_out, up_weight, up_row, down_weight)
    branch = branch_sum(attended, hidden, out_weight, down_weight)
    if gather_all:
        sides_b = spread_sides(group_b, mp)
        far_b = spread_core([group_b], mp)
        far_a = far_a + spread_core(corner_a, mp)
        near_a = near_a + corner_a
        (hidden, grad_gate, branch, grad_qkv, hat), near_a, far_a, near_b, far_b, group_c = fence(
            (hidden, grad_gate, branch, grad_qkv, hat),
            near_a,
            far_a,
            [group_b, *sides_b],
            far_b,
            group_c,
        )

    scaled = input_sums(grad_qkv, grad_gate, qkv_weight, up_weight, gains[0], gains[2], hat)
    cot_sum = jnp.sum(cotangent.astype(f32), axis=0)
    small = jnp.concatenate([scaled[2].reshape(-1), cot_sum, qkv_bias_part.reshape(-1)])
    small = small.reshape(-1, 128)
    five = 5 * width // 128
    biases = out_bias + down_bias
    xhat, inv_std = norm_own(layer_input)

    def over_mp(both, bit):
        return jnp.concatenate([butterfly(both[:five], "mp", mp, bit), both[five:]], axis=0)

    if not gather_all:
        own_branch = scatter_group(*branch, names, mp, rows)
        own_scaled = scatter_group(*scaled[:2], names, mp, rows)
        layer_output, input_grad = ends(
            layer_input, cotangent, xhat, inv_std, own_branch, own_scaled, biases
        )
        for bit in (1 << i for i in range(dp.bit_length() - 1)):
            small = butterfly(small, "dp", dp, bit)
        small, qkv_bias_grad = small[:five], small[five:]
        for bit in (1 << i for i in range(mp.bit_length() - 1)):
            small = butterfly(small, "mp", mp, bit)
        weights_sum = lax.all_gather(weights_sum, "dp", axis=0, tiled=True)
        up_weight_grad, down_weight_grad, up_bias_grad = lax.psum(
            (weight_product(second_all, grad_gate), weight_product(hidden, grad_out), gate_sum[0]),
            "dp",
        )
    else:
        corner_b = spread_corner(near_b[1:], mp)
        far_b = far_b + spread_core(near_b[1:], mp)
        branch_came = swap(branch[1], "mp", mp, 1)
        scaled, small, near_a, far_a, near_b, far_b, corner_b, branch_came, group_c = fence(
            scaled, small, near_a, far_a, near_b, far_b, corner_b, branch_came, group_c
        )

        own_branch = Scatter(branch[0], branch_came, names, mp, rows, True)
        small = over_mp(small, 1)
        sides_c = spread_sides(group_c, mp)
        scaled_came = swap(scaled[1], "mp", mp, 1)
        far_b = far_b + spread_core(corner_b, mp)
        near_b = near_b + corner_b
        up_sum, down_sum, sum_a, *branch_sent = group(
            spread_four(near_a, far_a),
            rows,
            up_weight,
            up_row,
            down_weight,
            gate_sum,
            folds=(branch[0], branch_came),
            places=own_branch.places(),
        )
        sums, near_b, far_b, near_c, branch_sent, scaled_came, small, weights_sum = fence(
            (up_sum, down_sum),
            near_b,
            far_b,
            [group_c, *sides_c],
            branch_sent,
            scaled_came,
            small,
            weights_sum,
        )

        weights_sum = lax.all_gather(weights_sum, "dp", axis=0, tiled=True)
        own_scaled = Scatter(scaled[0], scaled_came, names, mp, rows, False)
        scaled_sent = fold([(scaled[0], scaled_came, own_scaled.places())], rows)
        far_c = spread_core(near_c[:1], mp)
        corner_c = spread_corner(near_c[1:], mp)
        small = over_mp(small, 2)
        scaled_sent, branch_sent, far_c, small, sums = fence(
            scaled_sent, branch_sent, far_c, small, sums
        )
        up_sum, down_sum, sum_b = group(
            spread_four(near_b, far_b), rows, up_weight, up_row, down_weight, sum_a, sums
        )
        sums, near_c, far_c, corner_c, branch_came, branch_kept, scaled_came, scaled_kept, small = fence(
            (up_sum, down_sum),
            near_c,
            far_c,
            corner_c,
            own_branch.swapped(branch_sent[0]),
            branch_sent[1],
            own_scaled.swapped(scaled_sent[0]),
            scaled_sent[1],
            small,
        )

        far_c = far_c + spread_core(near_c[1:] + corner_c, mp)
        near_c = near_c + corner_c
        small = over_mp(small, 4)
        own_branch.take(own_branch.listed(branch_kept), branch_came)
        own_scaled.take(own_scaled.listed(scaled_kept), scaled_came)
        folded = fold(
            [
                (branch_kept, branch_came, own_branch.places()),
                (scaled_kept, scaled_came, own_scaled.places()),
            ],
            rows,
        )
        near_c, far_c, small, branch_sent, scaled_sent = fence(
            near_c, far_c, small, folded[:2], folded[2:]
        )
        up_weight_grad, down_weight_grad, sum_c = group(
            spread_four(near_c, far_c),
            rows,
            up_weight,
            up_row,
            down_weight,
            sum_b,
            sums,
            (second_all, grad_out, hidden, grad_gate),
        )
        up_weight_grad, branch_came, branch_kept, scaled_came, scaled_kept, z_sums = fence(
            up_weight_grad,
            own_branch.swapped(branch_sent[0]),
            branch_sent[1],
            own_scaled.swapped(scaled_sent[0]),
            scaled_sent[1],
            [small] + [swap(small, "dp", dp, bit) for bit in (1, 2, 3)],
        )
        own_branch.take([branch_kept], branch_came)
        own_scaled.take([scaled_kept], scaled_came)
        branch_total, scaled_total = own_branch.total(0), own_scaled.total(0)
        small = (z_sums[0] + z_sums[1]) + (z_sums[2] + z_sums[3])
        layer_output, input_grad = ends(
            layer_input, cotangent, xhat, inv_std, branch_total, scaled_total, biases
        )
        up_bias_grad = sum_c[0]
        small, qkv_bias_grad = small[:five], small[five:]
    qkv_weight_grad, out_weight_grad = widen(weights_sum, qkv_weight.shape[1], out_weight.shape[0])
    small = small.reshape(5, width)
    return (
        layer_output,
        input_grad,
        small[0],
        small[1],
        small[2],
        small[3],
        qkv_weight_grad,
        qkv_bias_grad.reshape(-1),
        out_weight_grad,
        small[4],
        up_weight_grad,
        up_bias_grad,
        down_weight_grad,
        small[4],
    )


def solution(mesh):
    in_specs = (
        P(("dp", "mp"), None),
        P("dp", None),
        P(),
        P(),
        P(),
        P(),
        P(None, "mp"),
        P("mp"),
        P("mp", None),
        P(),
        P(None, "mp"),
        P("mp"),
        P("mp", None),
        P(),
        P(("dp", "mp"), None),
    )
    out_specs = (
        P(("dp", "mp"), None),
        P(("dp", "mp"), None),
        P(),
        P(),
        P(),
        P(),
        P(None, "mp"),
        P("mp"),
        P("mp", None),
        P(),
        P(None, "mp"),
        P("mp"),
        P("mp", None),
        P(),
    )
    return jax.shard_map(
        per_device, mesh=mesh, in_specs=in_specs, out_specs=out_specs, check_vma=False
    )
```

```python
import functools

import jax
import jax.numpy as jnp
from jax import lax
from jax.experimental import pallas as pl
from jax.experimental.pallas import tpu as pltpu
from jax.sharding import PartitionSpec as P

HEAD_DIM = 128
ROTARY = 32

norm_eps = 1e-05
masked_score = -1e30
inv_root_two = 0.7071067811865476
inv_root_tau = 0.3989422804014327
vmem_bytes = 60 << 20
most_gathered = 128 << 20
bf16 = jnp.bfloat16
f32 = jnp.float32


def dot_plain(left, right):
    return jnp.dot(left, right, preferred_element_type=f32)


def contract_rows(left, right):
    return lax.dot_general(left, right, (((0,), (0,)), ((), ())), preferred_element_type=f32)


def contract_cols(left, right):
    return lax.dot_general(left, right, (((1,), (1,)), ((), ())), preferred_element_type=f32)


def swap(value, axis, count, bit):
    return lax.ppermute(value, axis, [(i, i ^ bit) for i in range(count)])


def turn(value, axis, count, step):
    return lax.ppermute(value, axis, [(i, (i + step) % count) for i in range(count)])


def chip_bits(count):
    return [1 << i for i in range(1, count.bit_length() - 1)]


def after(value, *earlier):
    return lax.optimization_barrier((value, *earlier))[0]


class Spread:
    def __init__(self, arrays, a, b, names):
        self.arrays, self.a, self.b, self.names = arrays, a, b, names


four_names = (0, 2, 4, 6, 1, 3, 5, 7)


def spread_sides(pair, count):
    return [swap(pair, "mp", count, 2), swap(pair, "mp", count, 4)]


def spread_corner(sides, count):
    a, b = cut(*sides)
    return [swap(a, "mp", count, 4), swap(b, "mp", count, 2)]


def spread_core(arrays, count):
    return [swap(array, "mp", count, 1) for array in arrays]


def spread_four(near, far):
    rows = near[0].shape[0] // 2
    a, b = {}, {}
    for core in range(2):
        base = len(near) * core
        for i, name in enumerate((0, 2, 4)):
            a[name + core] = (base + i, 0)
            b[name + core] = (base + i, rows)
        a[6 + core] = (base + 3, 0)
        b[6 + core] = (base + 4, 0)
    return Spread(near + far, a, b, four_names)


def spread_any(pair, count):
    rows = pair.shape[0] // 2
    held, names = pair.reshape(1, 2, rows, -1), [0]
    for bit in chip_bits(count) + [1]:
        held = jnp.concatenate([held, swap(held, "mp", count, bit)], axis=0)
        names = names + [n ^ bit for n in names]
    arrays = [held.reshape(2 * rows * count, -1)]
    a = {n: (0, 2 * rows * i) for i, n in enumerate(names)}
    b = {n: (0, 2 * rows * i + rows) for i, n in enumerate(names)}
    return Spread(arrays, a, b, tuple(names))


class Scatter:
    def __init__(self, near, came, names, count, rows, rising):
        self.count, self.rows = count, rows
        names = names[: len(names) // 2]
        self.blocks = {n: near[i * rows : (i + 1) * rows] for i, n in enumerate(names)}
        self.adds = {n: came[i * rows : (i + 1) * rows] for i, n in enumerate(names)}
        bits = chip_bits(count)
        self.bits = bits if rising else bits[::-1]

    def total(self, n):
        return self.blocks[n].astype(f32) + self.adds[n].astype(f32)

    def places(self):
        bit, order = self.bits[0], list(self.blocks)
        going = [i for i, n in enumerate(order) if n & bit]
        return going, [i for i, n in enumerate(order) if not n & bit]

    def listed(self, kept):
        return [kept[i : i + self.rows] for i in range(0, kept.shape[0], self.rows)]

    def sent(self):
        bit = self.bits[0]
        stay = [n for n in self.blocks if not n & bit]
        going = jnp.concatenate([self.total(n | bit).astype(bf16) for n in stay], axis=0)
        return going, [self.total(n).astype(bf16) for n in stay]

    def swapped(self, going):
        return swap(going, "mp", self.count, self.bits[0])

    def take(self, kept, came):
        bit, self.bits = self.bits[0], self.bits[1:]
        stay = [n for n in self.blocks if not n & bit]
        self.blocks = dict(zip(stay, kept))
        self.adds = {n: came[i * self.rows : (i + 1) * self.rows] for i, n in enumerate(stay)}


def scatter_group(near, far, names, count, rows):
    scatter = Scatter(near, swap(far, "mp", count, 1), names, count, rows, True)
    while scatter.bits:
        going, kept = scatter.sent()
        scatter.take(kept, scatter.swapped(going))
    return scatter.total(0)


def call(body, name, **kwargs):
    return pl.pallas_call(
        body,
        name=name,
        compiler_params=pltpu.CompilerParams(vmem_limit_bytes=vmem_bytes),
        cost_estimate=pl.CostEstimate(flops=1, bytes_accessed=1, transcendentals=0),
        **kwargs,
    )


def block_copies(spread, which, refs, buffer, sems, rows, block, blocks):
    per = block // rows
    listed = []
    for at in blocks:
        listed.append([])
        for i in range(at * per, (at + 1) * per):
            array, first = getattr(spread, which)[spread.names[i]]
            listed[-1].append(
                pltpu.make_async_copy(
                    refs[array].at[first : first + rows, :],
                    buffer.at[i * rows : (i + 1) * rows, :],
                    sems.at[i],
                )
            )
    return listed


def out_copies(buffer, ref, sems, block, blocks):
    return [
        pltpu.make_async_copy(
            buffer.at[i * block : (i + 1) * block, :],
            ref.at[i * block : (i + 1) * block, :],
            sems.at[i],
        )
        for i in blocks
    ]


def entry_body(*refs, spread, rows, block, blocks, earlier):
    count = len(spread.arrays)
    arrays = refs[:count]
    (gain1, bias1, gain2, bias2, qkv_ref, out_weight_ref) = refs[count : count + 6]
    count += 6 + earlier
    (one_ref, two_ref, hat_ref, raw_ref, grad_ref, cot_ref) = refs[count : count + 6]
    x_buf, c_buf, qkv_buf, out_buf, sem_x, sem_c, sem_out, sem_w = refs[count + 6 :]
    step = pl.program_id(0)
    x_copies = block_copies(spread, "a", arrays, x_buf, sem_x, rows, block, blocks)
    c_copies = block_copies(spread, "b", arrays, c_buf, sem_c, rows, block, blocks)
    outs = out_copies(c_buf, cot_ref, sem_out, block, blocks)

    weights = [
        pltpu.make_async_copy(qkv_ref, qkv_buf, sem_w.at[0]),
        pltpu.make_async_copy(out_weight_ref, out_buf, sem_w.at[1]),
    ]

    @pl.when(step == 0)
    def _():
        start(x_copies[0] + weights + c_copies[0])
        for x_list, c_list in zip(x_copies[1:], c_copies[1:]):
            start(x_list + c_list)

    for i in range(len(outs)):

        @pl.when(step == i)
        def _(i=i):
            wait(x_copies[i])

    here = pl.ds(pl.multiple_of((step * blocks.step + blocks.start) * block, block), block)
    values = x_buf[here, :].astype(f32)
    centred = values - jnp.mean(values, axis=1, keepdims=True)
    hat = centred * lax.rsqrt(jnp.mean(centred * centred, axis=1, keepdims=True) + norm_eps)
    hat_ref[...] = hat.astype(bf16)
    one_ref[...] = (hat * gain1[...] + bias1[...]).astype(bf16)
    two_ref[...] = (hat * gain2[...] + bias2[...]).astype(bf16)

    for i in range(len(outs)):

        @pl.when(step == i)
        def _(i=i):
            wait(c_copies[i])
            outs[i].start()
            if i == 0:
                wait(weights)

    raw_ref[...] = dot_plain(one_ref[...], qkv_buf[...])
    grad_ref[...] = contract_cols(c_buf[here, :], out_buf[...]).astype(bf16)

    @pl.when(step == len(outs) - 1)
    def _():
        for copy in outs:
            copy.wait()


def entry(spread, rows, gains, qkv_weight, out_weight, begin=0, stride=1, earlier=()):
    group_rows = rows * len(spread.names)
    width, deep = qkv_weight.shape
    units = out_weight.shape[0]
    block = min(256, group_rows)
    steps = group_rows // block
    per_group = len(spread.names)
    blocks = range(begin, steps, stride)

    def out_block(columns):
        return pl.BlockSpec((block, columns), lambda i: (i * stride + begin, 0))

    row = pl.BlockSpec((1, width), lambda i: (0, 0))
    anywhere = pl.BlockSpec(memory_space=pl.ANY)
    wide = jax.ShapeDtypeStruct((group_rows, width), bf16)
    first = len(spread.arrays) + 6
    return call(
        functools.partial(
            entry_body, spread=spread, rows=rows, block=block, blocks=blocks, earlier=len(earlier)
        ),
        "entry",
        grid=(len(blocks),),
        in_specs=[anywhere] * len(spread.arrays)
        + [row] * 4
        + [
            anywhere,
            anywhere,
        ]
        + [anywhere] * len(earlier),
        out_specs=[
            out_block(width),
            out_block(width),
            out_block(width),
            out_block(deep),
            out_block(units),
            anywhere,
        ],
        out_shape=[
            wide,
            wide,
            wide,
            jax.ShapeDtypeStruct((group_rows, deep), f32),
            jax.ShapeDtypeStruct((group_rows, units), bf16),
            wide,
        ],
        input_output_aliases={first + i: i for i in range(len(earlier))},
        scratch_shapes=[
            pltpu.VMEM((group_rows, width), bf16),
            pltpu.VMEM((group_rows, width), bf16),
            pltpu.VMEM(qkv_weight.shape, bf16),
            pltpu.VMEM(out_weight.shape, bf16),
            pltpu.SemaphoreType.DMA((per_group,)),
            pltpu.SemaphoreType.DMA((per_group,)),
            pltpu.SemaphoreType.DMA((steps,)),
            pltpu.SemaphoreType.DMA((2,)),
        ],
    )(*spread.arrays, *gains, qkv_weight, out_weight, *earlier)


def pairs_body(input_ref, cot_ref, gain_ref, bias_ref, pair_ref, shared_ref):
    values = input_ref[...].astype(f32)
    centred = values - jnp.mean(values, axis=1, keepdims=True)
    hat = centred * lax.rsqrt(jnp.mean(centred * centred, axis=1, keepdims=True) + norm_eps)
    pair_ref[0] = input_ref[...]
    pair_ref[1] = cot_ref[...]
    shared_ref[0] = (hat * gain_ref[...] + bias_ref[...]).astype(bf16)
    shared_ref[1] = cot_ref[...]


def pairs(layer_input, cotangent, gain, bias):
    rows, width = layer_input.shape
    block = min(32, rows)
    some = pl.BlockSpec((block, width), lambda i: (i, 0))
    row = pl.BlockSpec((1, width), lambda i: (0, 0))
    both = call(
        pairs_body,
        "pairs",
        grid=(rows // block,),
        in_specs=[some, some, row, row],
        out_specs=[pl.BlockSpec((2, block, width), lambda i: (0, i, 0))] * 2,
        out_shape=[jax.ShapeDtypeStruct((2, rows, width), bf16)] * 2,
    )(layer_input, cotangent, gain, bias)
    return [array.reshape(2 * rows, width) for array in both]


def fold_body(near_ref, came_ref, going_ref, kept_ref, *, rows, going, kept):
    for ref, places in ((going_ref, going), (kept_ref, kept)):
        for i, at in enumerate(places):
            here = slice(at * rows, (at + 1) * rows)
            total = near_ref[here, :].astype(f32) + came_ref[here, :].astype(f32)
            ref[i * rows : (i + 1) * rows, :] = total.astype(bf16)


def folds_body(*refs, count):
    for ref in range(2 * count):
        total = refs[2 * ref][...].astype(f32) + refs[2 * ref + 1][...].astype(f32)
        refs[4 * count + ref][...] = total.astype(bf16)


def fold(sums, rows):
    width = sums[0][0].shape[1]
    operands, in_specs = [], []
    for near, came, places in sums:
        for first, *more in places:
            apart = more[0] - first if more else 0
            spec = pl.BlockSpec((rows, width), lambda i, a=apart, f=first: (a * i + f, 0))
            operands += [near, came]
            in_specs += [spec, spec]
    per = len(sums[0][2][0])
    return call(
        functools.partial(folds_body, count=len(sums)),
        "fold",
        grid=(per,),
        in_specs=in_specs,
        out_specs=[pl.BlockSpec((rows, width), lambda i: (i, 0))] * (2 * len(sums)),
        out_shape=[jax.ShapeDtypeStruct((per * rows, width), bf16)] * (2 * len(sums)),
    )(*operands)


def cut_body(side_x, side_y, x_ref, y_ref):
    x_ref[...] = side_x[...]
    y_ref[...] = side_y[...]


def cut(side_x, side_y):
    rows, width = side_x.shape[0] // 2, side_x.shape[1]
    tops = pl.BlockSpec((rows, width), lambda i: (0, 0))
    return call(
        cut_body,
        "cut",
        grid=(1,),
        in_specs=[tops, pl.BlockSpec((rows, width), lambda i: (1, 0))],
        out_specs=[tops] * 2,
        out_shape=[jax.ShapeDtypeStruct((rows, width), side_x.dtype)] * 2,
    )(side_x, side_y)


def start(copies):
    for copy in copies:
        copy.start()


def wait(copies):
    for copy in copies:
        copy.wait()


def products(x, c, up_ref, down_ref, shift_ref, tiles, hidden_ref, grad_ref, sum_ref):
    gates = [dot_plain(x, up_ref[:, part]) + shift_ref[:, part] for part in tiles]
    for gate, part in zip(gates, tiles):
        grad_hidden = contract_cols(c, down_ref[part, :])
        below = 0.5 * (1.0 + lax.erf(gate * inv_root_two))
        hidden_ref[:, part] = (gate * below).astype(bf16)
        slope = below + gate * jnp.exp(-0.5 * gate * gate) * inv_root_tau
        grad = (grad_hidden * slope).astype(bf16)
        grad_ref[:, part] = grad
        sum_ref[:, part] += jnp.sum(grad.astype(f32), axis=0, keepdims=True)


def column_tiles(units):
    tile = min(512, units)
    return [slice(i, i + tile) for i in range(0, units, tile)]


class Branch:
    def __init__(self, arrays, weights, buffers, sems, spread, rows, block):
        self.up_ref, self.shift_ref, self.down_ref = weights
        self.x_buf, self.c_buf, self.u_buf, self.d_buf = buffers
        sem_x, sem_c, sem_u, sem_d = sems
        self.block = block
        self.every = range(self.x_buf.shape[0] // block)
        self.x_copies = block_copies(spread, "a", arrays, self.x_buf, sem_x, rows, block, self.every)
        self.c_copies = block_copies(spread, "b", arrays, self.c_buf, sem_c, rows, block, self.every)
        self.tiles = column_tiles(self.u_buf.shape[1])
        self.needs = self.x_copies[0] + self.c_copies[0]
        self.needs.append(pltpu.make_async_copy(self.up_ref, self.u_buf, sem_u))
        self.needs.append(pltpu.make_async_copy(self.down_ref, self.d_buf, sem_d))

    def block_step(self, step, hidden_ref, grad_ref, sum_ref, prior_ref, extra=()):
        @pl.when(step == 0)
        def _():
            start(self.needs)
            sum_ref[...] = prior_ref[...]
            wait(self.needs)
            for later in self.every[1:]:
                start(self.x_copies[later] + self.c_copies[later])
            start(extra)

        for i in self.every[1:]:

            @pl.when(step == i)
            def _(i=i):
                wait(self.x_copies[i] + self.c_copies[i])

        here = pl.ds(pl.multiple_of(step * self.block, self.block), self.block)
        products(
            self.x_buf[here, :],
            self.c_buf[here, :],
            self.u_buf,
            self.d_buf,
            self.shift_ref,
            self.tiles,
            hidden_ref.at[here],
            grad_ref.at[here],
            sum_ref,
        )


def branch_scratch(group_rows, width, units, blocks):
    dma = pltpu.SemaphoreType.DMA
    return [
        pltpu.VMEM((group_rows, width), bf16),
        pltpu.VMEM((group_rows, width), bf16),
        pltpu.VMEM((width, units), bf16),
        pltpu.VMEM((units, width), bf16),
        dma((blocks,)),
        dma((blocks,)),
        dma,
        dma,
    ]


def mlp_body(x_ref, c_ref, up_ref, shift_ref, down_ref, hidden_ref, grad_ref, sum_ref):
    @pl.when(pl.program_id(0) == 0)
    def _():
        sum_ref[...] = jnp.zeros_like(sum_ref)

    tiles = column_tiles(up_ref.shape[1])
    products(
        x_ref[...], c_ref[...], up_ref, down_ref, shift_ref, tiles, hidden_ref, grad_ref, sum_ref
    )


def mlp(normed, cotangent, up_weight, up_bias, down_weight):
    width, units = up_weight.shape
    group_rows = normed.shape[0]
    block = min(256, group_rows)
    once = pl.Buffered(1)
    full = pl.BlockSpec((block, width), lambda i: (i, 0))
    part = pl.BlockSpec((block, units), lambda i: (i, 0))
    low = jax.ShapeDtypeStruct((group_rows, units), bf16)
    row = pl.BlockSpec((1, units), lambda i: (0, 0))
    return call(
        mlp_body,
        "mlp",
        grid=(group_rows // block,),
        in_specs=[
            full,
            full,
            pl.BlockSpec(up_weight.shape, lambda i: (0, 0), pipeline_mode=once),
            row,
            pl.BlockSpec(down_weight.shape, lambda i: (0, 0), pipeline_mode=once),
        ],
        out_specs=[part, part, row],
        out_shape=[low, low, jax.ShapeDtypeStruct((1, units), f32)],
    )(normed, cotangent, up_weight, up_bias, down_weight)


def group_body(*refs, spread, rows, block, tile, steps, ups, adds, more, places):
    count = len(spread.arrays)
    arrays, weights, refs = refs[:count], refs[count : count + 3], refs[count + 3 :]
    prior_ref, *refs = refs
    added, refs = refs[: 2 * adds], refs[2 * adds :]
    own, refs = refs[: 4 * more], refs[4 * more :]
    folds, refs = (refs[:2], refs[2:]) if places else ((), refs)
    up_out, down_out, sum_ref = refs[:3]
    folded, refs = (refs[3:5], refs[5:]) if places else ((), refs[3:])
    buffers, sems, (hidden_buf, grad_buf), refs = refs[:4], refs[4:8], refs[8:10], refs[10:]
    branch = Branch(arrays, weights, buffers, sems, spread, rows, block)
    step = pl.program_id(0)
    at = jnp.where(step < steps + ups, step - steps, step - steps - ups)
    at = jnp.maximum(at, 0)
    here = pl.ds(pl.multiple_of(at * tile, tile), tile)
    later = []
    if adds:
        sum_up, sum_down, sem_sum_up, sem_sum_down, *refs = refs

        def up_copy(i):
            first = pl.multiple_of(i * tile, tile)
            return pltpu.make_async_copy(
                added[0].at[pl.ds(first, tile), :], sum_up.at[i % 2], sem_sum_up.at[i % 2]
            )

        def down_copy(i):
            first = pl.multiple_of(i * tile, tile)
            return pltpu.make_async_copy(
                added[1].at[:, pl.ds(first, tile)], sum_down.at[i % 2], sem_sum_down.at[i % 2]
            )

        later = later + [up_copy(0)]
    if more:
        own_bufs, sem_own = refs[:4], refs[4]
        own_copies = [
            pltpu.make_async_copy(ref, buf, sem_own.at[i])
            for i, (ref, buf) in enumerate(zip(own, own_bufs))
        ]
        later = later + own_copies
        rows_own, cot_own, hidden_own, grad_own = own_bufs

    @pl.when(step < steps)
    def _():
        branch.block_step(step, hidden_buf, grad_buf, sum_ref, prior_ref, later)

    if more:

        @pl.when(step == steps)
        def _():
            wait(own_copies)

    if places:

        @pl.when(step >= steps)
        def _():
            fold_body(*folds, *folded, rows=rows, going=places[0], kept=places[1])

    @pl.when((step >= steps) & (step < steps + ups))
    def _():
        if adds:

            @pl.when(at + 1 < ups)
            def _():
                up_copy(at + 1).start()

            @pl.when(at + 1 == ups)
            def _():
                down_copy(0).start()

            up_copy(at).wait()
        total = contract_rows(branch.x_buf[:, here], grad_buf[...])
        if more:
            total = total + contract_rows(rows_own[:, here], grad_own[...])
        if adds:
            total = total + sum_up[at % 2]
        up_out[...] = total

    @pl.when(step >= steps + ups)
    def _():
        if adds:

            @pl.when(at + 1 < ups)
            def _():
                down_copy(at + 1).start()

            down_copy(at).wait()
        total = contract_rows(hidden_buf[...], branch.c_buf[:, here])
        if more:
            total = total + contract_rows(hidden_own[...], cot_own[:, here])
        if adds:
            total = total + sum_down[at % 2]
        down_out[...] = total


def group(spread, rows, up_weight, up_bias, down_weight, prior, added=(), own=(), folds=(), places=()):
    width, units = up_weight.shape
    group_rows = rows * len(spread.names)
    block = min(256, group_rows)
    tile = min(512, units)
    steps, blocks = group_rows // block, len(spread.names)
    ups = width // tile
    anywhere = pl.BlockSpec(memory_space=pl.ANY)
    row = pl.BlockSpec((1, units), lambda i: (0, 0))
    dma = pltpu.SemaphoreType.DMA
    scratch = branch_scratch(group_rows, width, units, blocks)
    scratch += [pltpu.VMEM((group_rows, units), bf16)] * 2
    if added:
        scratch += [
            pltpu.VMEM((2, tile, units), f32),
            pltpu.VMEM((2, units, tile), f32),
            dma((2,)),
            dma((2,)),
        ]
    if own:
        scratch += [pltpu.VMEM(array.shape, bf16) for array in own] + [dma((4,))]
    fold_in, fold_out, fold_shape = [], [], []
    if folds:
        strip = width // (2 * ups)
        half = folds[0].shape[0] // 2

        def column(i):
            return 0, jnp.clip(i - steps, 0, 2 * ups - 1)

        fold_in = [pl.BlockSpec((2 * half, strip), column)] * 2
        fold_out = [pl.BlockSpec((half, strip), column)] * 2
        fold_shape = [jax.ShapeDtypeStruct((half, width), bf16)] * 2
    return call(
        functools.partial(
            group_body,
            spread=spread,
            rows=rows,
            block=block,
            tile=tile,
            steps=steps,
            ups=ups,
            adds=bool(added),
            more=bool(own),
            places=places,
        ),
        "group",
        grid=(steps + 2 * ups,),
        in_specs=[anywhere] * len(spread.arrays)
        + [anywhere, row, anywhere, row]
        + [anywhere] * (len(added) + len(own))
        + fold_in,
        out_specs=[
            pl.BlockSpec((tile, units), lambda i: (jnp.clip(i - steps, 0, ups - 1), 0)),
            pl.BlockSpec((units, tile), lambda i: (0, jnp.clip(i - steps - ups, 0, ups - 1))),
            row,
        ]
        + fold_out,
        out_shape=[
            jax.ShapeDtypeStruct((width, units), f32),
            jax.ShapeDtypeStruct((units, width), f32),
            jax.ShapeDtypeStruct((1, units), f32),
        ]
        + fold_shape,
        scratch_shapes=scratch,
    )(*spread.arrays, up_weight, up_bias, down_weight, prior, *added, *own, *folds)


def weight_body(left_ref, right_ref, out_ref):
    out_ref[...] = contract_rows(left_ref[...], right_ref[...])


def weight_product(left, right):
    wide, deep = left.shape[1], right.shape[1]
    tile = min(512, wide)
    return call(
        weight_body,
        "weight_product",
        grid=(wide // tile,),
        in_specs=[
            pl.BlockSpec((left.shape[0], tile), lambda i: (0, i)),
            pl.BlockSpec(right.shape, lambda i: (0, 0), pipeline_mode=pl.Buffered(1)),
        ],
        out_specs=pl.BlockSpec((tile, deep), lambda i: (i, 0)),
        out_shape=jax.ShapeDtypeStruct((wide, deep), f32),
    )(left, right)


def attention_weights_body(normed_ref, grad_qkv_ref, attended_ref, grad_out_ref, sum_ref):
    deep, units = grad_qkv_ref.shape[1], attended_ref.shape[1]
    sum_ref[:, :deep] = contract_rows(normed_ref[...], grad_qkv_ref[...]).astype(bf16)
    total = contract_rows(attended_ref[...], grad_out_ref[...]).astype(bf16)
    for first in range(0, sum_ref.shape[0], units):
        sum_ref[first : first + units, deep:] = total[:, first : first + units]


def attention_weights(normed, grad_qkv, attended, grad_out):
    group_rows, width = normed.shape
    deep, units = grad_qkv.shape[1], attended.shape[1]
    once = pl.Buffered(1)
    columns = min(2 * units, width)
    block = pl.BlockSpec((group_rows, columns), lambda i: (0, i))
    return call(
        attention_weights_body,
        "attention_weights",
        grid=(width // columns,),
        in_specs=[
            block,
            pl.BlockSpec(grad_qkv.shape, lambda i: (0, 0), pipeline_mode=once),
            pl.BlockSpec(attended.shape, lambda i: (0, 0), pipeline_mode=once),
            block,
        ],
        out_specs=pl.BlockSpec((columns, deep + units), lambda i: (i, 0)),
        out_shape=jax.ShapeDtypeStruct((width, deep + units), bf16),
    )(normed, grad_qkv, attended, grad_out)


def widen_body(sum_ref, qkv_ref, out_ref):
    units, deep = out_ref.shape[0], qkv_ref.shape[1]
    qkv_ref[...] = sum_ref[:, :deep].astype(f32)
    for first in range(0, sum_ref.shape[0], units):
        out_ref[:, first : first + units] = sum_ref[first : first + units, deep:].astype(f32)


def widen(total, deep, units):
    width = total.shape[0]
    block = min(2 * units, width)
    return call(
        widen_body,
        "widen",
        grid=(width // block,),
        in_specs=[pl.BlockSpec((block, deep + units), lambda i: (i, 0))],
        out_specs=[
            pl.BlockSpec((block, deep), lambda i: (i, 0)),
            pl.BlockSpec((units, block), lambda i: (0, i)),
        ],
        out_shape=[
            jax.ShapeDtypeStruct((width, deep), f32),
            jax.ShapeDtypeStruct((units, width), f32),
        ],
    )(total)


def branch_body(attended_ref, hidden_ref, out_ref, down_ref, near_ref, far_ref):
    middle = near_ref.shape[0]
    total = dot_plain(attended_ref[...], out_ref[...]) + dot_plain(hidden_ref[...], down_ref[...])
    near_ref[...] = total[:middle].astype(bf16)
    far_ref[...] = total[middle:].astype(bf16)


def branch_sum(attended, hidden, out_weight, down_weight):
    group_rows = attended.shape[0]
    width = out_weight.shape[1]
    tile = min(512, width)
    once = pl.Buffered(1)
    half = pl.BlockSpec((group_rows // 2, tile), lambda i: (0, i))
    return call(
        branch_body,
        "branch_sum",
        grid=(width // tile,),
        in_specs=[
            pl.BlockSpec(attended.shape, lambda i: (0, 0), pipeline_mode=once),
            pl.BlockSpec(hidden.shape, lambda i: (0, 0), pipeline_mode=once),
            pl.BlockSpec((out_weight.shape[0], tile), lambda i: (0, i)),
            pl.BlockSpec((down_weight.shape[0], tile), lambda i: (0, i)),
        ],
        out_specs=[half, half],
        out_shape=[jax.ShapeDtypeStruct((group_rows // 2, width), bf16)] * 2,
    )(attended, hidden, out_weight, down_weight)


def input_body(
    qkv_grad_ref, gate_grad_ref, qkv_ref, up_ref, gain1, gain2, hat_ref, near_ref, far_ref, sum_ref
):
    middle = near_ref.shape[0]
    hat = hat_ref[...].astype(f32)
    first = contract_cols(qkv_grad_ref[...], qkv_ref[...])
    second = contract_cols(gate_grad_ref[...], up_ref[...])
    both = first * gain1[...] + second * gain2[...]
    near_ref[...] = both[:middle].astype(bf16)
    far_ref[...] = both[middle:].astype(bf16)
    sum_ref[0:1, :] = jnp.sum(first * hat, axis=0, keepdims=True)
    sum_ref[1:2, :] = jnp.sum(first, axis=0, keepdims=True)
    sum_ref[2:3, :] = jnp.sum(second * hat, axis=0, keepdims=True)
    sum_ref[3:4, :] = jnp.sum(second, axis=0, keepdims=True)


def input_sums(grad_qkv, grad_gate, qkv_weight, up_weight, gain1, gain2, hat):
    group_rows = grad_qkv.shape[0]
    width = qkv_weight.shape[0]
    tile = min(512, width)
    once = pl.Buffered(1)
    half = pl.BlockSpec((group_rows // 2, tile), lambda i: (0, i))
    row = pl.BlockSpec((1, tile), lambda i: (0, i))
    return call(
        input_body,
        "input_sums",
        grid=(width // tile,),
        in_specs=[
            pl.BlockSpec(grad_qkv.shape, lambda i: (0, 0), pipeline_mode=once),
            pl.BlockSpec(grad_gate.shape, lambda i: (0, 0), pipeline_mode=once),
            pl.BlockSpec((tile, qkv_weight.shape[1]), lambda i: (i, 0)),
            pl.BlockSpec((tile, up_weight.shape[1]), lambda i: (i, 0)),
            row,
            row,
            pl.BlockSpec((group_rows, tile), lambda i: (0, i)),
        ],
        out_specs=[half, half, pl.BlockSpec((4, tile), lambda i: (0, i))],
        out_shape=[jax.ShapeDtypeStruct((group_rows // 2, width), bf16)] * 2
        + [jax.ShapeDtypeStruct((4, width), f32)],
    )(grad_qkv, grad_gate, qkv_weight, up_weight, gain1, gain2, hat)


def attention_body(
    own_ref,
    starts_ref,
    raw_ref,
    bias_ref,
    cos_ref,
    sine_ref,
    slope_in_ref,
    attended_ref,
    grad_qkv_ref,
    bias_grad_ref,
    query_ref,
    key_ref,
    value_ref,
    slope_ref,
    query_sum_ref,
    key_sum_ref,
    value_sum_ref,
    *,
    rows,
    names,
    block_rows,
    longest,
):
    own = own_ref[0]
    group_rows = rows * len(names)
    lane = lax.broadcasted_iota(jnp.int32, (rows, HEAD_DIM), 1)
    half = ROTARY // 2
    scale = HEAD_DIM ** (-0.5)

    def turned(u):
        return jnp.where(lane < half, pltpu.roll(u, HEAD_DIM - half, 1), pltpu.roll(u, half, 1))

    def far_rows(name):
        return pl.ds(pl.multiple_of((own ^ name) * rows, rows), rows)

    for i, name in enumerate(names):
        near = slice(i * rows, (i + 1) * rows)
        far = far_rows(name)
        raw = raw_ref[near, :] + bias_ref[...]
        cos_table = cos_ref[near, :]
        sine_table = sine_ref[near, :]
        query = raw[:, :HEAD_DIM]
        key = raw[:, HEAD_DIM : 2 * HEAD_DIM]
        query_ref[far, :] = (query * cos_table + turned(query) * sine_table).astype(bf16)
        key_ref[far, :] = (key * cos_table + turned(key) * sine_table).astype(bf16)
        value_ref[far, :] = raw[:, 2 * HEAD_DIM :].astype(bf16)
        slope_ref[far, :] = slope_in_ref[near, :]
    key_sum_ref[...] = jnp.zeros_like(key_sum_ref)
    value_sum_ref[...] = jnp.zeros_like(value_sum_ref)
    for first in range(0, group_rows, block_rows):
        last = first + block_rows
        low = max(0, (first - longest + 1) // 128 * 128)
        query = query_ref[first:last, :]
        keys = key_ref[low:last, :]
        values = value_ref[low:last, :]
        slope = slope_ref[first:last, :]
        scores = contract_cols(query, keys) * scale
        row = first + lax.broadcasted_iota(jnp.int32, (block_rows, 1), 0)
        begin = jnp.zeros((block_rows, 1), jnp.int32)
        for slot in range(starts_ref.shape[0]):
            begin = jnp.where(starts_ref[slot] <= row, starts_ref[slot], begin)
        column = low + lax.broadcasted_iota(jnp.int32, scores.shape, 1)
        scores = jnp.where((column >= begin) & (column <= row), scores, masked_score)
        peak = jnp.max(scores, axis=1, keepdims=True)
        raised = jnp.exp(scores - peak)
        probs = raised * (1.0 / jnp.sum(raised, axis=1, keepdims=True))
        probs_low = probs.astype(bf16)
        query_ref[first:last, :] = dot_plain(probs_low, values).astype(bf16)
        grad_probs = contract_cols(slope, values)
        delta = jnp.sum(grad_probs * probs, axis=1, keepdims=True)
        grad_score = (probs * (grad_probs - delta)).astype(bf16)
        query_sum_ref[first:last, :] = dot_plain(grad_score, keys) * scale
        key_sum_ref[low:last, :] += contract_rows(grad_score, query) * scale
        value_sum_ref[low:last, :] += contract_rows(probs_low, slope)
    bias_grad = jnp.zeros(bias_grad_ref.shape, f32)
    for i, name in enumerate(names):
        near = slice(i * rows, (i + 1) * rows)
        far = far_rows(name)
        cos_table = cos_ref[near, :]
        sine_table = sine_ref[near, :]
        query_grad = query_sum_ref[far, :]
        key_grad = key_sum_ref[far, :]
        grads = jnp.concatenate(
            [
                query_grad * cos_table - turned(query_grad) * sine_table,
                key_grad * cos_table - turned(key_grad) * sine_table,
                value_sum_ref[far, :],
            ],
            axis=1,
        ).astype(bf16)
        grad_qkv_ref[near, :] = grads
        bias_grad = bias_grad + jnp.sum(grads.astype(f32), axis=0, keepdims=True)
        attended_ref[near, :] = query_ref[far, :]
    bias_grad_ref[...] = bias_grad


def attention(own, starts, raw, bias, cos_table, sine_table, slope, rows, names):
    group_rows, width = raw.shape
    part = 3 * HEAD_DIM
    heads = width // part
    whole = pl.BlockSpec((group_rows, HEAD_DIM), lambda h: (0, 0))
    scalars = pl.BlockSpec(memory_space=pltpu.SMEM)
    low = pltpu.VMEM((group_rows, HEAD_DIM), bf16)
    wide = pltpu.VMEM((group_rows, HEAD_DIM), f32)
    longest = group_rows // 2
    return pl.pallas_call(
        functools.partial(
            attention_body,
            rows=rows,
            names=names,
            block_rows=min(256, group_rows),
            longest=longest,
        ),
        grid=(heads,),
        in_specs=[
            scalars,
            scalars,
            pl.BlockSpec((group_rows, part), lambda h: (0, h)),
            pl.BlockSpec((1, part), lambda h: (0, h)),
            whole,
            whole,
            pl.BlockSpec((group_rows, HEAD_DIM), lambda h: (0, h)),
        ],
        out_specs=[
            pl.BlockSpec((group_rows, HEAD_DIM), lambda h: (0, h)),
            pl.BlockSpec((group_rows, part), lambda h: (0, h)),
            pl.BlockSpec((1, part), lambda h: (0, h)),
        ],
        out_shape=[
            jax.ShapeDtypeStruct((group_rows, heads * HEAD_DIM), bf16),
            jax.ShapeDtypeStruct((group_rows, width), bf16),
            jax.ShapeDtypeStruct((1, width), f32),
        ],
        scratch_shapes=[low, low, low, low, wide, wide, wide],
        compiler_params=pltpu.CompilerParams(vmem_limit_bytes=vmem_bytes),
        cost_estimate=pl.CostEstimate(flops=1, bytes_accessed=1, transcendentals=0),
        name="attention",
    )(own, starts, raw, bias, cos_table, sine_table, slope)


def rotary_tables(position):
    half_rot = ROTARY // 2
    frequency = 10000.0 ** (-2.0 * jnp.arange(half_rot, dtype=f32) / ROTARY)
    angles = frequency[:, None] * position.astype(f32)[None, :]
    cos_half, sine_half = lax.optimization_barrier((jnp.cos(angles), jnp.sin(angles)))
    rest = (HEAD_DIM - ROTARY, position.shape[0])
    return (
        jnp.concatenate([cos_half, cos_half, jnp.ones(rest, f32)], axis=0).T,
        jnp.concatenate([-sine_half, sine_half, jnp.zeros(rest, f32)], axis=0).T,
    )


def butterfly(value, axis, count, bit):
    return value + swap(value, axis, count, bit)


def fence(*values):
    return lax.optimization_barrier(values)


def norm_own(layer_input):
    values = layer_input.astype(f32)
    centred = values - jnp.mean(values, axis=-1, keepdims=True)
    inv_std = lax.rsqrt(jnp.mean(centred * centred, axis=-1, keepdims=True) + norm_eps)
    return centred * inv_std, inv_std


def tables(own, lengths, names, rows):
    seq_ends = jnp.cumsum(lengths)
    seq_starts = seq_ends - lengths
    places = (
        (own ^ jnp.array(names, jnp.int32))[:, None] * rows
        + jnp.arange(rows, dtype=jnp.int32)[None, :]
    ).reshape(-1)
    seq_first = jnp.max(
        jnp.where(seq_starts[None, :] <= places[:, None], seq_starts[None, :], 0), axis=1
    )
    return (seq_starts, *rotary_tables(places - seq_first))


def ends(layer_input, cotangent, xhat, inv_std, branch, scaled, biases):
    layer_output = (layer_input.astype(f32) + branch + biases).astype(bf16)
    input_grad = cotangent.astype(f32) + inv_std * (
        scaled
        - jnp.mean(scaled, axis=-1, keepdims=True)
        - xhat * jnp.mean(scaled * xhat, axis=-1, keepdims=True)
    )
    return layer_output, input_grad


def per_device(
    layer_input,
    lengths,
    norm1_gain,
    norm1_bias,
    norm2_gain,
    norm2_bias,
    qkv_weight,
    qkv_bias,
    out_weight,
    out_bias,
    up_weight,
    up_bias,
    down_weight,
    down_bias,
    cotangent,
):
    dp = lax.axis_size("dp")
    mp = lax.axis_size("mp")
    own = lax.axis_index("mp")
    rows, width = layer_input.shape
    up_row = up_bias[None, :]
    gains = (norm1_gain[None, :], norm1_bias[None, :], norm2_gain[None, :], norm2_bias[None, :])
    gather_all = mp == 8 and dp == 4 and 4 * rows * mp * dp * (width + up_bias.shape[0]) < most_gathered

    pair, shared = pairs(layer_input, cotangent, *gains[2:])
    if gather_all:
        names = four_names
        sides = spread_sides(pair, mp)
        group_a = turn(shared, "dp", dp, 1)
        placed = tables(own, lengths[0], names, rows)
        far = spread_core([pair], mp)
        shared, pair, sides, placed, far, group_a = fence(shared, pair, sides, placed, far, group_a)
        group_b = turn(shared, "dp", dp, -1)
        corner = spread_corner(sides, mp)
        near = [pair, *sides]
        far = far + spread_core(sides, mp)
        begun = entry(spread_four(near, far), rows, gains, qkv_weight, out_weight, 0, 2)
        near, far, corner, group_a, begun = fence(near, far, corner, group_a, begun)
        near, far = near + corner, far + spread_core(corner, mp)
        sides_a = spread_sides(group_a, mp)
        entered = entry(spread_four(near, far), rows, gains, qkv_weight, out_weight, 1, 2, begun)
        entered, group_b, group_a = fence(entered, group_b, group_a)
        far_a = spread_core([group_a], mp)
        group_c = turn(group_a, "dp", dp, 1)
    else:
        spread = spread_any(pair, mp)
        names = spread.names
        placed = tables(own, lengths[0], names, rows)
        entered = entry(spread, rows, gains, qkv_weight, out_weight)
    seq_starts, cos_table, sine_table = placed

    first_all, second_all, hat, raw, grad_attended, grad_out = entered
    attended, grad_qkv, qkv_bias_part = attention(
        own.reshape(1),
        seq_starts,
        raw,
        qkv_bias[None, :],
        cos_table,
        sine_table,
        grad_attended,
        rows,
        names,
    )
    if gather_all:
        (first_all, second_all, hat, grad_out, attended, grad_qkv), near_a, far_a, group_b = fence(
            (first_all, second_all, hat, grad_out, attended, grad_qkv),
            [group_a, *sides_a],
            far_a,
            group_b,
        )

    weights_part = attention_weights(first_all, grad_qkv, attended, grad_out)
    if gather_all:
        corner_a = spread_corner(near_a[1:], mp)
        far_a = far_a + spread_core(near_a[1:], mp)
        (weights_part, second_all, hat, grad_out, attended), near_a, corner_a, far_a, group_b, group_c = (
            fence(
                (weights_part, second_all, hat, grad_out, attended),
                near_a,
                corner_a,
                far_a,
                group_b,
                group_c,
            )
        )
    weights_sum = lax.psum_scatter(weights_part, "dp", scatter_dimension=0, tiled=True)

    hidden, grad_gate, gate_sum = mlp(second_all, grad_out, up_weight, up_row, down_weight)
    branch = branch_sum(attended, hidden, out_weight, down_weight)
    if gather_all:
        sides_b = spread_sides(group_b, mp)
        far_b = spread_core([group_b], mp)
        far_a = far_a + spread_core(corner_a, mp)
        near_a = near_a + corner_a
        (hidden, grad_gate, branch, grad_qkv, hat), near_a, far_a, near_b, far_b, group_c = fence(
            (hidden, grad_gate, branch, grad_qkv, hat),
            near_a,
            far_a,
            [group_b, *sides_b],
            far_b,
            group_c,
        )

    scaled = input_sums(grad_qkv, grad_gate, qkv_weight, up_weight, gains[0], gains[2], hat)
    cot_sum = jnp.sum(cotangent.astype(f32), axis=0)
    small = jnp.concatenate([scaled[2].reshape(-1), cot_sum, qkv_bias_part.reshape(-1)])
    small = small.reshape(-1, 128)
    five = 5 * width // 128
    biases = out_bias + down_bias
    xhat, inv_std = norm_own(layer_input)

    def over_mp(both, bit):
        return jnp.concatenate([butterfly(both[:five], "mp", mp, bit), both[five:]], axis=0)

    if not gather_all:
        own_branch = scatter_group(*branch, names, mp, rows)
        own_scaled = scatter_group(*scaled[:2], names, mp, rows)
        layer_output, input_grad = ends(
            layer_input, cotangent, xhat, inv_std, own_branch, own_scaled, biases
        )
        for bit in (1 << i for i in range(dp.bit_length() - 1)):
            small = butterfly(small, "dp", dp, bit)
        small, qkv_bias_grad = small[:five], small[five:]
        for bit in (1 << i for i in range(mp.bit_length() - 1)):
            small = butterfly(small, "mp", mp, bit)
        weights_sum = lax.all_gather(weights_sum, "dp", axis=0, tiled=True)
        up_weight_grad, down_weight_grad, up_bias_grad = lax.psum(
            (weight_product(second_all, grad_gate), weight_product(hidden, grad_out), gate_sum[0]),
            "dp",
        )
    else:
        corner_b = spread_corner(near_b[1:], mp)
        far_b = far_b + spread_core(near_b[1:], mp)
        branch_came = swap(branch[1], "mp", mp, 1)
        scaled, small, near_a, far_a, near_b, far_b, corner_b, branch_came, group_c = fence(
            scaled, small, near_a, far_a, near_b, far_b, corner_b, branch_came, group_c
        )

        own_branch = Scatter(branch[0], branch_came, names, mp, rows, True)
        small = over_mp(small, 1)
        sides_c = spread_sides(group_c, mp)
        scaled_came = swap(scaled[1], "mp", mp, 1)
        far_b = far_b + spread_core(corner_b, mp)
        near_b = near_b + corner_b
        up_sum, down_sum, sum_a, *branch_sent = group(
            spread_four(near_a, far_a),
            rows,
            up_weight,
            up_row,
            down_weight,
            gate_sum,
            folds=(branch[0], branch_came),
            places=own_branch.places(),
        )
        sums, near_b, far_b, near_c, branch_sent, scaled_came, small, weights_sum = fence(
            (up_sum, down_sum),
            near_b,
            far_b,
            [group_c, *sides_c],
            branch_sent,
            scaled_came,
            small,
            weights_sum,
        )

        weights_sum = lax.all_gather(weights_sum, "dp", axis=0, tiled=True)
        own_scaled = Scatter(scaled[0], scaled_came, names, mp, rows, False)
        scaled_sent = fold([(scaled[0], scaled_came, own_scaled.places())], rows)
        far_c = spread_core(near_c[:1], mp)
        corner_c = spread_corner(near_c[1:], mp)
        small = over_mp(small, 2)
        scaled_sent, branch_sent, far_c, small, sums = fence(
            scaled_sent, branch_sent, far_c, small, sums
        )
        up_sum, down_sum, sum_b = group(
            spread_four(near_b, far_b), rows, up_weight, up_row, down_weight, sum_a, sums
        )
        sums, near_c, far_c, corner_c, branch_came, branch_kept, scaled_came, scaled_kept, small = fence(
            (up_sum, down_sum),
            near_c,
            far_c,
            corner_c,
            own_branch.swapped(branch_sent[0]),
            branch_sent[1],
            own_scaled.swapped(scaled_sent[0]),
            scaled_sent[1],
            small,
        )

        far_c = far_c + spread_core(near_c[1:] + corner_c, mp)
        near_c = near_c + corner_c
        small = over_mp(small, 4)
        own_branch.take(own_branch.listed(branch_kept), branch_came)
        own_scaled.take(own_scaled.listed(scaled_kept), scaled_came)
        folded = fold(
            [
                (branch_kept, branch_came, own_branch.places()),
                (scaled_kept, scaled_came, own_scaled.places()),
            ],
            rows,
        )
        near_c, far_c, small, branch_sent, scaled_sent = fence(
            near_c, far_c, small, folded[:2], folded[2:]
        )
        up_weight_grad, down_weight_grad, sum_c = group(
            spread_four(near_c, far_c),
            rows,
            up_weight,
            up_row,
            down_weight,
            sum_b,
            sums,
            (second_all, grad_out, hidden, grad_gate),
        )
        up_weight_grad, branch_came, branch_kept, scaled_came, scaled_kept, z_sums = fence(
            up_weight_grad,
            own_branch.swapped(branch_sent[0]),
            branch_sent[1],
            own_scaled.swapped(scaled_sent[0]),
            scaled_sent[1],
            [small] + [swap(small, "dp", dp, bit) for bit in (1, 2, 3)],
        )
        own_branch.take([branch_kept], branch_came)
        own_scaled.take([scaled_kept], scaled_came)
        branch_total, scaled_total = own_branch.total(0), own_scaled.total(0)
        small = (z_sums[0] + z_sums[1]) + (z_sums[2] + z_sums[3])
        layer_output, input_grad = ends(
            layer_input, cotangent, xhat, inv_std, branch_total, scaled_total, biases
        )
        up_bias_grad = sum_c[0]
        small, qkv_bias_grad = small[:five], small[five:]
    qkv_weight_grad, out_weight_grad = widen(weights_sum, qkv_weight.shape[1], out_weight.shape[0])
    small = small.reshape(5, width)
    return (
        layer_output,
        input_grad,
        small[0],
        small[1],
        small[2],
        small[3],
        qkv_weight_grad,
        qkv_bias_grad.reshape(-1),
        out_weight_grad,
        small[4],
        up_weight_grad,
        up_bias_grad,
        down_weight_grad,
        small[4],
    )


def solution(mesh):
    in_specs = (
        P(("dp", "mp"), None),
        P("dp", None),
        P(),
        P(),
        P(),
        P(),
        P(None, "mp"),
        P("mp"),
        P("mp", None),
        P(),
        P(None, "mp"),
        P("mp"),
        P("mp", None),
        P(),
        P(("dp", "mp"), None),
    )
    out_specs = (
        P(("dp", "mp"), None),
        P(("dp", "mp"), None),
        P(),
        P(),
        P(),
        P(),
        P(None, "mp"),
        P("mp"),
        P("mp", None),
        P(),
        P(None, "mp"),
        P("mp"),
        P("mp", None),
        P(),
    )
    return jax.shard_map(
        per_device, mesh=mesh, in_specs=in_specs, out_specs=out_specs, check_vma=False
    )
```
